32 devices in a mesh: dp: 8 (over y, x, core), tensor: 4 (over z).
Axes of the slice: x: 2, y: 2, z: 4, core: 2. Of those that a mesh axis runs over, the one named last changes fastest.
Arguments:
- tokens: bfloat16 [12288, 1024], P(('dp', 'tensor')), may hold values from -0.19921875 to 0.19921875
- w_query: bfloat16 [1024, 1024], P('dp', 'tensor'), may hold values from -0.1875 to 0.1875
- w_key: bfloat16 [1024, 1024], P('dp', 'tensor'), may hold values from -0.1875 to 0.1875
- w_value: bfloat16 [1024, 1024], P('dp', 'tensor'), may hold values from -0.1875 to 0.1875
- w_out_t: bfloat16 [1024, 1024], P('dp', 'tensor'), may hold values from -0.1875 to 0.1875
- w_up: bfloat16 [1024, 4096], P('dp', 'tensor'), may hold values from -0.1875 to 0.1875
- w_gate: bfloat16 [1024, 4096], P('dp', 'tensor'), may hold values from -0.1875 to 0.1875
- w_down_t: bfloat16 [1024, 4096], P('dp', 'tensor'), may hold values from -0.09375 to 0.09375
- scale_qk: float32 [1024], replicated, may hold values from 0.6 to 1.8
- alpha_attn: float32 [1024], replicated, may hold values from 0.1 to 0.6
- scale_up: float32 [4096], replicated, may hold values from 0.5 to 2
- scale_gate: float32 [4096], replicated, may hold values from 0.5 to 2
- alpha_mlp: float32 [1024], replicated, may hold values from 0.1 to 0.6
- order: int32 [8, 1536], P('dp'), may hold values from 0 to 1535, each once within a row
- lengths: int32 [8, 3], P('dp'), may hold values from 1 to 1024, 1536 in all within a row
- cotangent: bfloat16 [12288, 1024], P(('dp', 'tensor')), may hold values from -6 to 6
Outputs:
- out: bfloat16 [12288, 1024], P(('dp', 'tensor'))
- grad_tokens: float32 [12288, 1024], P(('dp', 'tensor'))
- grad_w_query: float32 [1024, 1024], P('dp', 'tensor')
- grad_w_key: float32 [1024, 1024], P('dp', 'tensor')
- grad_w_value: float32 [1024, 1024], P('dp', 'tensor')
- grad_w_out_t: float32 [1024, 1024], P('dp', 'tensor')
- grad_w_up: float32 [1024, 4096], P('dp', 'tensor')
- grad_w_gate: float32 [1024, 4096], P('dp', 'tensor')
- grad_w_down_t: float32 [1024, 4096], P('dp', 'tensor')
- grad_scale_qk: float32 [1024], replicated
- grad_alpha_attn: float32 [1024], replicated
- grad_scale_up: float32 [4096], replicated
- grad_scale_gate: float32 [4096], replicated
- grad_alpha_mlp: float32 [1024], replicated
The draws below stay inside these ranges and needn't reach their ends.
Inputs may be any that keep to these rules, and one draw needn't show every extreme that they name: Each row of order holds every place 0 to 1535 once. Each row of lengths sums to 1536, and its largest entry is exactly 1024.
All inputs are finite; a program needn't handle non-finite values.
Results may differ from the reference program's by a relative error of at most 0.017.
Values may be sent and summed in bfloat16 or wider, within the bound.
A program may use at most 192 MiB of HBM per device.

```python
import math
import jax
import jax.numpy as jnp
import numpy as np
from jax import lax

D = 1024
HEADS = 16
HD = 64
FF = 4096
TOK_G = 1536
MAXLEN = 1024
SEQS = 3
GROUPS = 8
TOKENS = 12288


def shard_levels(stream_key, dims, shards, low, high):
    def one(position, shards_of):
        draws = jax.random.uniform(jax.random.fold_in(jax.random.fold_in(stream_key, 6), position), (shards_of,), jnp.float32, low / len(shards), high / len(shards))
        return jnp.repeat(jnp.exp(draws), dims[position] // shards_of).reshape((-1,) + (1,) * (len(dims) - position - 1))

    level = one(*shards[0])
    for cut in shards[1:]:
        level = level * one(*cut)
    return level


def length_profile(number_of, total, reach, skew):
    portions = [(1 << 20) // math.isqrt(grade ** skew) + 1 for grade in range(2, number_of + 1)]
    spare, given = total - reach - (number_of - 1), [1] * (number_of - 1)
    while spare > 0:
        movable = [i for i in range(number_of - 1) if given[i] < reach]
        whole, budget = sum([portions[i] for i in movable]), spare
        for i in movable:
            extra = min(reach - given[i], max(1, budget * portions[i] // whole), spare)
            given[i] = given[i] + extra
            spare = spare - extra
    return np.array([reach] + given)


def ragged_sizes(stream_key, count, total, reach, skew):
    if count == 2:
        one = jax.random.randint(stream_key, (), max(1, total - reach), min(reach, total - 1) + 1)
        return jnp.stack([one, total - one])
    sizes = jnp.asarray(length_profile(count, total, reach, skew), jnp.int32)
    couples = (count - 1) // 2
    donor, taker = sizes[1:1 + 2 * couples:2], sizes[2:2 + 2 * couples:2]
    slack = jnp.minimum(donor - 1, reach - taker)
    moved = jax.random.randint(jax.random.fold_in(stream_key, 1), (couples,), 0, 1 << 20) % (slack + 1)
    sizes = sizes.at[1:1 + 2 * couples:2].set(donor - moved).at[2:2 + 2 * couples:2].set(taker + moved)
    return sizes[jax.random.permutation(jax.random.fold_in(stream_key, 2), count)]


def scatter_about(stream_key, shape, deviation, limit, shards=(), held_as=jnp.bfloat16):
    loudness = shard_levels(stream_key, shape, shards, -0.22, 0.18) if shards else 1.0
    entries = jax.random.normal(stream_key, shape, jnp.float32) * deviation * loudness
    return jnp.minimum(jnp.maximum(entries, -limit), limit).astype(held_as)


def setup_inputs(seed: int = 0) -> dict:
    seeds = jax.random.split(jax.random.key(seed), 17)
    return {
        "tokens": scatter_about(seeds[0], (TOKENS, D), 0.03125, 0.19921875, ((0, 32),)),
        "w_query": scatter_about(seeds[1], (D, D), D ** -0.5, 0.1875, ((0, 8), (1, 4))),
        "w_key": scatter_about(seeds[2], (D, D), D ** -0.5, 0.1875, ((0, 8), (1, 4))),
        "w_value": scatter_about(seeds[3], (D, D), D ** -0.5, 0.1875, ((0, 8), (1, 4))),
        "w_out_t": scatter_about(seeds[4], (D, D), D ** -0.5, 0.1875, ((0, 8), (1, 4))),
        "w_up": scatter_about(seeds[5], (D, FF), D ** -0.5, 0.1875, ((0, 8), (1, 4))),
        "w_gate": scatter_about(seeds[6], (D, FF), D ** -0.5, 0.1875, ((0, 8), (1, 4))),
        "w_down_t": scatter_about(seeds[7], (D, FF), FF ** -0.5, 0.09375, ((0, 8), (1, 4))),
        "scale_qk": jnp.clip(jnp.exp(jax.random.uniform(seeds[8], (D,), jnp.float32, math.log(0.6), math.log(1.8))), 0.6, 1.8),
        "alpha_attn": jnp.clip(jax.random.uniform(seeds[9], (D,), jnp.float32, 0.1, 0.6), 0.1, 0.6),
        "scale_up": jnp.clip(jnp.exp(jax.random.uniform(seeds[10], (FF,), jnp.float32, math.log(0.5), math.log(2.0))), 0.5, 2.0),
        "scale_gate": jnp.clip(jnp.exp(jax.random.uniform(seeds[11], (FF,), jnp.float32, math.log(0.5), math.log(2.0))), 0.5, 2.0),
        "alpha_mlp": jnp.clip(jax.random.uniform(seeds[12], (D,), jnp.float32, 0.1, 0.6), 0.1, 0.6),
        "order": jax.vmap(lambda own: jax.random.permutation(own, TOK_G))(jax.random.split(seeds[13], GROUPS)).reshape((GROUPS, TOK_G)).astype(jnp.int32),
        "lengths": jax.vmap(lambda own: ragged_sizes(own, SEQS, TOK_G, MAXLEN, 2))(jax.random.split(seeds[14], GROUPS)).reshape((GROUPS, SEQS)).astype(jnp.int32),
        "cotangent": scatter_about(seeds[15], (TOKENS, D), 1.0, 6.0, ((0, 32),)),
    }


@jax.custom_vjp
def low(v):
    return lax.optimization_barrier(v.astype(jnp.bfloat16)).astype(jnp.float32)

@jax.custom_vjp
def low_back(v):
    return v

def low_keep(v):
    return (low(v), None)

def low_pass(kept, grad):
    return (grad,)

def back_keep(v):
    return (v, None)

def back_low(kept, grad):
    return (low(grad),)
low.defvjp(low_keep, low_pass)
low_back.defvjp(back_keep, back_low)

def matmul_ab(first_op, second_op):
    return jnp.dot(first_op, second_op, precision=lax.Precision.HIGHEST)

def matmul_abt(first_op, second_op):
    return lax.dot_general(first_op, second_op, (((1,), (1,)), ((), ())), precision=lax.Precision.HIGHEST)

def unit_rows(matrix):
    return matrix * lax.rsqrt(lax.optimization_barrier(jnp.sum(matrix * matrix, axis=-1, keepdims=True)) + 1e-06)

def rotate(matrix, angles):
    half_width = matrix.shape[-1] // 2
    cosine = jnp.cos(angles)[:, None, :]
    sine_part = jnp.sin(angles)[:, None, :]
    lead_half = matrix[..., :half_width]
    tail_half = matrix[..., half_width:]
    return jnp.concatenate([lead_half * cosine - tail_half * sine_part, tail_half * cosine + lead_half * sine_part], axis=-1)

def layout(order_row, length_row):
    group_rows = order_row.shape[0]
    places = jnp.arange(group_rows, dtype=jnp.int32)
    seg_ends = jnp.cumsum(length_row, dtype=jnp.int32)
    seg_starts = seg_ends - length_row
    segment = lax.optimization_barrier(jnp.sum((places[:, None] >= seg_ends[None, :]).astype(jnp.int32), axis=1, dtype=jnp.int32))
    seg_first = lax.optimization_barrier(jnp.max(jnp.where(seg_starts[None, :] <= places[:, None], seg_starts[None, :], 0), axis=1))
    half_width = HD // 2
    inv_freq = jnp.exp(jnp.arange(half_width, dtype=jnp.float32) * (-math.log(10000.0) / half_width))
    angles = (places - seg_first).astype(jnp.float32)[:, None] * inv_freq[None, :]
    inverse = jnp.zeros((group_rows,), jnp.int32).at[order_row].set(places)
    return (segment, places, angles, inverse)

def group_layer(weights, tokens_g, order_row, length_row):
    w_query, w_key, w_value, w_out_t, w_up, w_gate, w_down_t, scale_qk, alpha_attn, scale_up, scale_gate, alpha_mlp = weights
    segment, places, angles, inverse = layout(order_row, length_row)
    group_rows = tokens_g.shape[0]
    packed = tokens_g[order_row]
    qk_gains = scale_qk.reshape(HEADS, HD)

    def project(weight):
        raw_heads = low_back(matmul_ab(packed, weight)).reshape(group_rows, HEADS, HD)
        return low(rotate(unit_rows(raw_heads) * qk_gains, angles))
    queries = project(w_query)
    key_rows = project(w_key)
    value_rows = low(low_back(matmul_ab(packed, w_value))).reshape(group_rows, HEADS, HD)
    scores = low_back(jnp.einsum('qhd,khd->hqk', queries, key_rows, precision=lax.Precision.HIGHEST) * math.sqrt(HD))
    allowed = (segment[:, None] == segment[None, :]) & (places[None, :] <= places[:, None])
    scores = jnp.where(allowed[None], scores, -1e+30)
    attn_probs = low(jax.nn.softmax(scores, axis=-1))
    attended = jnp.einsum('hqk,khd->qhd', attn_probs, value_rows, precision=lax.Precision.HIGHEST).reshape(group_rows, D)
    attended = low(low_back(attended))
    branch_a = low_back(matmul_abt(attended, w_out_t)[inverse])
    norm_a = unit_rows(branch_a)
    middle = unit_rows(tokens_g + alpha_attn * (norm_a - tokens_g))
    middle_in = low(middle)
    up_proj = low_back(matmul_ab(middle_in, w_up)) * scale_up
    gate_proj = low_back(matmul_ab(middle_in, w_gate)) * (scale_gate * math.sqrt(D))
    mixed_b = low(up_proj * jax.nn.silu(gate_proj))
    branch_m = low_back(matmul_abt(mixed_b, w_down_t))
    norm_m = unit_rows(branch_m)
    return unit_rows(middle + alpha_mlp * (norm_m - middle))

def reference(tokens, w_query, w_key, w_value, w_out_t, w_up, w_gate, w_down_t, scale_qk, alpha_attn, scale_up, scale_gate, alpha_mlp, order, lengths, cotangent):
    weights = tuple((member.astype(jnp.float32) for member in (w_query, w_key, w_value, w_out_t, w_up, w_gate, w_down_t, scale_qk, alpha_attn, scale_up, scale_gate, alpha_mlp)))
    groups = order.shape[0]
    inputs = tokens.astype(jnp.float32).reshape(groups, -1, D)

    def forward(weight_set, input_set):

        def one_group(member):
            return group_layer(weight_set, member[0], member[1], member[2])
        return lax.map(jax.checkpoint(one_group), (input_set, order, lengths))
    result, pullback = jax.vjp(forward, weights, inputs)
    grad_weights, grad_inputs = pullback(cotangent.astype(jnp.float32).reshape(result.shape))
    return (result.reshape(-1, D).astype(jnp.bfloat16), grad_inputs.reshape(-1, D), grad_weights[0], grad_weights[1], grad_weights[2], grad_weights[3], grad_weights[4], grad_weights[5], grad_weights[6], grad_weights[7], grad_weights[8], grad_weights[9], grad_weights[10], grad_weights[11])
```

```python
import math

import jax
import jax.numpy as jnp
from jax import lax
from jax.experimental import pallas as pl
from jax.experimental.pallas import tpu as pltpu
from jax.sharding import PartitionSpec as P

D = 1024
HD = 64
BLK = 256
LOG2E = 1.4426950408889634
VMEM_LIMIT = 60 * 1024 * 1024


def dot_ab(a, b):
    return lax.dot_general(a, b, (((1,), (0,)), ((), ())), preferred_element_type=jnp.float32)


def dot_abt(a, b):
    return lax.dot_general(a, b, (((1,), (1,)), ((), ())), preferred_element_type=jnp.float32)


def split_heads(block, heads):
    lane_head = lax.broadcasted_iota(jnp.int32, block.shape, 1) // HD
    zero = jnp.zeros_like(block)
    return jnp.concatenate([jnp.where(lane_head == h, block, zero) for h in range(heads)], axis=0)


def attn_fwd_body(low_ref, start_ref, q_ref, k_ref, v_ref, out_ref, lse_ref, vt_ref, qs_ref, acc_ref, sum_ref):
    rows, cols = q_ref.shape
    heads = cols // HD
    scale = math.sqrt(HD) * LOG2E
    for b in range(rows // BLK):
        vt_ref[:, b * BLK : (b + 1) * BLK] = v_ref[b * BLK : (b + 1) * BLK, :].T

    def one_block(i, _):
        base = pl.multiple_of(i * BLK, BLK)
        qs_ref[...] = split_heads(q_ref[pl.ds(base, BLK), :], heads)
        acc_ref[...] = jnp.zeros_like(acc_ref)
        sum_ref[...] = jnp.zeros_like(sum_ref)
        start = jnp.concatenate([start_ref[:, pl.ds(base, BLK)]] * heads, axis=1)
        own = lax.broadcasted_iota(jnp.int32, (1, heads * BLK), 1) % BLK + base

        def step(j, causal):
            at = pl.multiple_of(j * BLK, BLK)
            scores = dot_abt(k_ref[pl.ds(at, BLK), :], qs_ref[...])
            place = lax.broadcasted_iota(jnp.int32, scores.shape, 0) + at
            keep = place >= start
            if causal:
                keep = keep & (place <= own)
            probs = jnp.where(keep, jnp.exp2(scores * scale), 0.0)
            sum_ref[...] += jnp.sum(probs, axis=0, keepdims=True)
            probs_b = probs.astype(jnp.bfloat16)
            for h in range(heads):
                acc_ref[h * HD : (h + 1) * HD, :] += dot_ab(
                    vt_ref[h * HD : (h + 1) * HD, pl.ds(at, BLK)], probs_b[:, h * BLK : (h + 1) * BLK]
                )

        lax.fori_loop(low_ref[i], i, lambda j, c: (step(j, False), c)[1], 0)
        step(i, True)
        total = sum_ref[...]
        inv = 1.0 / total
        logs = jnp.log2(total)
        for h in range(heads):
            lse_ref[h : h + 1, pl.ds(base, BLK)] = logs[:, h * BLK : (h + 1) * BLK]
            acc_ref[h * HD : (h + 1) * HD, :] *= inv[:, h * BLK : (h + 1) * BLK]
        out_ref[pl.ds(base, BLK), :] = acc_ref[...].T.astype(jnp.bfloat16)
        return 0

    lax.fori_loop(0, rows // BLK, one_block, 0)


def vmem():
    return pl.BlockSpec(memory_space=pltpu.VMEM)


def attn_fwd(low, start, q, k, v):
    rows, cols = q.shape
    heads = cols // HD
    return pl.pallas_call(
        attn_fwd_body,
        out_shape=(
            jax.ShapeDtypeStruct((rows, cols), jnp.bfloat16),
            jax.ShapeDtypeStruct((8, rows), jnp.float32),
        ),
        in_specs=[pl.BlockSpec(memory_space=pltpu.SMEM)] + [vmem()] * 4,
        out_specs=(vmem(), vmem()),
        scratch_shapes=[
            pltpu.VMEM((cols, rows), jnp.bfloat16),
            pltpu.VMEM((heads * BLK, cols), jnp.bfloat16),
            pltpu.VMEM((cols, BLK), jnp.float32),
            pltpu.VMEM((1, heads * BLK), jnp.float32),
        ],
        compiler_params=pltpu.CompilerParams(vmem_limit_bytes=VMEM_LIMIT),
        cost_estimate=pl.CostEstimate(flops=4 * rows * rows * cols, bytes_accessed=8 * rows * cols, transcendentals=rows * rows * heads),
        name="attn_fwd",
    )(low, start, q, k, v)


def attn_bwd_body(
    low_ref, start_ref, lse_ref, q_ref, k_ref, v_ref, o_ref, g_ref,
    dq_ref, dk_ref, dv_ref, kt_ref, qs_ref, gs_ref, dqt_ref, dk_acc, dv_acc,
):
    rows, cols = q_ref.shape
    heads = cols // HD
    root = math.sqrt(HD)
    scale = root * LOG2E
    for b in range(rows // BLK):
        kt_ref[:, b * BLK : (b + 1) * BLK] = k_ref[b * BLK : (b + 1) * BLK, :].T
    dk_acc[...] = jnp.zeros_like(dk_acc)
    dv_acc[...] = jnp.zeros_like(dv_acc)

    def one_block(i, _):
        base = pl.multiple_of(i * BLK, BLK)
        qs_ref[...] = split_heads(q_ref[pl.ds(base, BLK), :], heads)
        grads = g_ref[pl.ds(base, BLK), :]
        gs_ref[...] = split_heads(grads, heads)
        dqt_ref[...] = jnp.zeros_like(dqt_ref)
        start = jnp.concatenate([start_ref[:, pl.ds(base, BLK)]] * heads, axis=1)
        own = lax.broadcasted_iota(jnp.int32, (1, heads * BLK), 1) % BLK + base
        prod = (grads.astype(jnp.float32) * o_ref[pl.ds(base, BLK), :].astype(jnp.float32)).T
        delta = jnp.concatenate(
            [jnp.sum(prod[h * HD : (h + 1) * HD, :], axis=0, keepdims=True) for h in range(heads)], axis=1
        )
        lse = jnp.concatenate([lse_ref[h : h + 1, pl.ds(base, BLK)] for h in range(heads)], axis=1)

        def step(j, causal):
            at = pl.multiple_of(j * BLK, BLK)
            scores = dot_abt(k_ref[pl.ds(at, BLK), :], qs_ref[...])
            dprobs = dot_abt(v_ref[pl.ds(at, BLK), :], gs_ref[...])
            place = lax.broadcasted_iota(jnp.int32, scores.shape, 0) + at
            keep = place >= start
            if causal:
                keep = keep & (place <= own)
            probs = jnp.where(keep, jnp.exp2(scores * scale - lse), 0.0)
            dsc = (probs * (dprobs - delta)).astype(jnp.bfloat16)
            dv_acc[pl.ds(at, BLK), :] += dot_ab(probs.astype(jnp.bfloat16), gs_ref[...])
            dk_acc[pl.ds(at, BLK), :] += dot_ab(dsc, qs_ref[...])
            for h in range(heads):
                dqt_ref[h * HD : (h + 1) * HD, :] += dot_ab(
                    kt_ref[h * HD : (h + 1) * HD, pl.ds(at, BLK)], dsc[:, h * BLK : (h + 1) * BLK]
                )

        lax.fori_loop(low_ref[i], i, lambda j, c: (step(j, False), c)[1], 0)
        step(i, True)
        dq_ref[pl.ds(base, BLK), :] = (dqt_ref[...].T * root).astype(dq_ref.dtype)
        return 0

    lax.fori_loop(0, rows // BLK, one_block, 0)
    dk_ref[...] = (dk_acc[...] * root).astype(dk_ref.dtype)
    dv_ref[...] = dv_acc[...].astype(dv_ref.dtype)


def attn_bwd(low, start, lse, q, k, v, o, g):
    rows, cols = q.shape
    heads = cols // HD
    return pl.pallas_call(
        attn_bwd_body,
        out_shape=(jax.ShapeDtypeStruct((rows, cols), jnp.bfloat16),) * 3,
        in_specs=[pl.BlockSpec(memory_space=pltpu.SMEM)] + [vmem()] * 7,
        out_specs=(vmem(),) * 3,
        scratch_shapes=[
            pltpu.VMEM((cols, rows), jnp.bfloat16),
            pltpu.VMEM((heads * BLK, cols), jnp.bfloat16),
            pltpu.VMEM((heads * BLK, cols), jnp.bfloat16),
            pltpu.VMEM((cols, BLK), jnp.float32),
            pltpu.VMEM((rows, cols), jnp.float32),
            pltpu.VMEM((rows, cols), jnp.float32),
        ],
        compiler_params=pltpu.CompilerParams(vmem_limit_bytes=VMEM_LIMIT),
        cost_estimate=pl.CostEstimate(flops=10 * rows * rows * cols, bytes_accessed=16 * rows * cols, transcendentals=rows * rows * heads),
        name="attn_bwd",
    )(low, start, lse, q, k, v, o, g)


def matmul_ab(first_op, second_op):
    return jnp.dot(first_op, second_op, preferred_element_type=jnp.float32)


def matmul_abt(first_op, second_op):
    return lax.dot_general(
        first_op, second_op, (((1,), (1,)), ((), ())), preferred_element_type=jnp.float32
    )


def matmul_atb(first_op, second_op):
    return lax.dot_general(
        first_op, second_op, (((0,), (0,)), ((), ())), preferred_element_type=jnp.float32
    )


def unit_pair(matrix):
    factor = lax.rsqrt(jnp.sum(matrix * matrix, axis=-1, keepdims=True) + 1e-06)
    return (matrix * factor, factor)


def unit_back(normed, factor, grad_out):
    return factor * (grad_out - normed * jnp.sum(normed * grad_out, axis=-1, keepdims=True))


def rotate(matrix, angles, direction):
    half_width = matrix.shape[-1] // 2
    cosine = jnp.cos(angles)[:, None, :]
    sine_part = direction * jnp.sin(angles)[:, None, :]
    lead_half = matrix[..., :half_width]
    tail_half = matrix[..., half_width:]
    return jnp.concatenate(
        [lead_half * cosine - tail_half * sine_part, tail_half * cosine + lead_half * sine_part],
        axis=-1,
    )


def layout(order_row, length_row):
    group_rows = order_row.shape[0]
    places = jnp.arange(group_rows, dtype=jnp.int32)
    seg_ends = jnp.cumsum(length_row, dtype=jnp.int32)
    seg_starts = seg_ends - length_row
    seg_first = jnp.max(
        jnp.where(seg_starts[None, :] <= places[:, None], seg_starts[None, :], 0), axis=1
    )
    half_width = HD // 2
    inv_freq = jnp.exp(
        jnp.arange(half_width, dtype=jnp.float32) * (-math.log(10000.0) / half_width)
    )
    angles = (places - seg_first).astype(jnp.float32)[:, None] * inv_freq[None, :]
    inverse = jnp.zeros((group_rows,), jnp.int32).at[order_row].set(places)
    return (seg_first, angles, inverse)


def on_device(
    tokens,
    w_query,
    w_key,
    w_value,
    w_out_t,
    w_up,
    w_gate,
    w_down_t,
    scale_qk,
    alpha_attn,
    scale_up,
    scale_gate,
    alpha_mlp,
    order,
    lengths,
    cotangent,
):
    tensor_rank = lax.axis_index("tensor")
    head_cols = w_query.shape[1]
    hidden_cols = w_up.shape[1]
    local_heads = head_cols // HD
    qk_gains = lax.dynamic_slice_in_dim(scale_qk, tensor_rank * head_cols, head_cols).reshape(
        local_heads, HD
    )
    up_gains = lax.dynamic_slice_in_dim(scale_up, tensor_rank * hidden_cols, hidden_cols)
    gate_gains = lax.dynamic_slice_in_dim(
        scale_gate, tensor_rank * hidden_cols, hidden_cols
    ) * math.sqrt(D)
    order_row = order[0]
    seg_first, angles, inverse = layout(order_row, lengths[0])
    group_rows = order_row.shape[0]
    attn_full = (
        lax.all_gather(w_query, "dp", axis=0, tiled=True),
        lax.all_gather(w_key, "dp", axis=0, tiled=True),
        lax.all_gather(w_value, "dp", axis=0, tiled=True),
        lax.all_gather(w_out_t, "dp", axis=0, tiled=True),
    )
    mlp_full = (
        lax.all_gather(w_up, "dp", axis=0, tiled=True),
        lax.all_gather(w_gate, "dp", axis=0, tiled=True),
        lax.all_gather(w_down_t, "dp", axis=0, tiled=True),
    )
    wq_full, wk_full, wv_full, wo_full = attn_full
    wu_full, wg_full, wd_full = mlp_full
    gathered = lax.all_gather(tokens, "tensor", axis=0, tiled=True)
    packed = gathered[order_row]
    query_n, query_f = unit_pair(matmul_ab(packed, wq_full).reshape(group_rows, local_heads, HD))
    key_n, key_f = unit_pair(matmul_ab(packed, wk_full).reshape(group_rows, local_heads, HD))
    queries = rotate(query_n * qk_gains, angles, 1.0).astype(jnp.bfloat16)
    key_rows = rotate(key_n * qk_gains, angles, 1.0).astype(jnp.bfloat16)
    value_rows = (
        matmul_ab(packed, wv_full).astype(jnp.bfloat16).reshape(group_rows, local_heads, HD)
    )

    low = lax.slice(seg_first, (0,), (group_rows,), (BLK,)) // BLK
    start = seg_first[None, :]
    queries = queries.reshape(group_rows, head_cols)
    key_rows = key_rows.reshape(group_rows, head_cols)
    value_rows = value_rows.reshape(group_rows, head_cols)
    attended, log_totals = attn_fwd(low, start, queries, key_rows, value_rows)
    attended_mine = lax.all_to_all(
        attended[inverse], "tensor", split_axis=0, concat_axis=1, tiled=True
    )
    wo_every = lax.all_gather(wo_full, "tensor", axis=1, tiled=True)
    branch_a = matmul_abt(attended_mine, wo_every)
    inputs_f = tokens.astype(jnp.float32)
    norm_a, factor_a = unit_pair(branch_a)
    middle, factor_mid = unit_pair(inputs_f + alpha_attn * (norm_a - inputs_f))
    middle_rows = lax.all_gather(middle.astype(jnp.bfloat16), "tensor", axis=0, tiled=True)
    up_raw = matmul_ab(middle_rows, wu_full)
    gate_raw = matmul_ab(middle_rows, wg_full)
    up_proj = up_raw * up_gains
    gate_proj = gate_raw * gate_gains
    sigmoid_g = jax.nn.sigmoid(gate_proj)
    silu_g = jax.nn.silu(gate_proj)
    mixed_b = (up_proj * silu_g).astype(jnp.bfloat16)
    branch_m = lax.psum_scatter(
        matmul_abt(mixed_b, wd_full).astype(jnp.bfloat16), "tensor", scatter_dimension=0, tiled=True
    ).astype(jnp.float32)
    norm_m, factor_m = unit_pair(branch_m)
    outputs, factor_out = unit_pair(middle + alpha_mlp * (norm_m - middle))
    mlp_back = (
        lax.all_gather(w_up, "dp", axis=0, tiled=True),
        lax.all_gather(w_gate, "dp", axis=0, tiled=True),
        lax.all_gather(w_down_t, "dp", axis=0, tiled=True),
    )
    attn_back = (
        lax.all_gather(w_query, "dp", axis=0, tiled=True),
        lax.all_gather(w_key, "dp", axis=0, tiled=True),
        lax.all_gather(w_value, "dp", axis=0, tiled=True),
        lax.all_gather(w_out_t, "dp", axis=0, tiled=True),
    )
    wu_back, wg_back, wd_back = mlp_back
    wq_back, wk_back, wv_back, wo_back = attn_back
    grad_out = cotangent.astype(jnp.float32)
    grad_h2 = unit_back(outputs, factor_out, grad_out)
    grad_alpha_m = jnp.sum(grad_h2 * (norm_m - middle), axis=0)
    grad_bm = unit_back(norm_m, factor_m, alpha_mlp * grad_h2).astype(jnp.bfloat16)
    grad_bm_rows = lax.all_gather(grad_bm, "tensor", axis=0, tiled=True)
    grad_mixed = matmul_ab(grad_bm_rows, wd_back)
    grad_wd = matmul_atb(grad_bm_rows, mixed_b)
    grad_upp = grad_mixed * silu_g
    grad_gatep = grad_mixed * up_proj * sigmoid_g * (1.0 + gate_proj * (1.0 - sigmoid_g))
    grad_su = jnp.sum(grad_upp * up_raw, axis=0)
    grad_sv = jnp.sum(grad_gatep * gate_raw, axis=0) * math.sqrt(D)
    grad_up_b = (grad_upp * up_gains).astype(jnp.bfloat16)
    grad_gate_b = (grad_gatep * gate_gains).astype(jnp.bfloat16)
    grad_wu = matmul_atb(middle_rows, grad_up_b)
    grad_wg = matmul_atb(middle_rows, grad_gate_b)
    back_terms = matmul_abt(grad_up_b, wu_back) + matmul_abt(grad_gate_b, wg_back)
    grad_middle = (1.0 - alpha_mlp) * grad_h2 + lax.psum_scatter(
        back_terms.astype(jnp.bfloat16), "tensor", scatter_dimension=0, tiled=True
    ).astype(jnp.float32)
    grad_h1 = unit_back(middle, factor_mid, grad_middle)
    grad_alpha_a = jnp.sum(grad_h1 * (norm_a - inputs_f), axis=0)
    grad_ba = unit_back(norm_a, factor_a, alpha_attn * grad_h1).astype(jnp.bfloat16)
    grad_ba_rows = lax.all_gather(grad_ba, "tensor", axis=0, tiled=True)[order_row]
    grad_att = matmul_ab(grad_ba_rows, wo_back).astype(jnp.bfloat16)
    grad_wo = matmul_atb(grad_ba_rows, attended)
    grad_queries, grad_keys, grad_vals = attn_bwd(
        low, start, log_totals, queries, key_rows, value_rows, attended, grad_att
    )
    grad_queries = grad_queries.astype(jnp.float32).reshape(group_rows, local_heads, HD)
    grad_keys = grad_keys.astype(jnp.float32).reshape(group_rows, local_heads, HD)
    grad_qs = rotate(grad_queries, angles, -1.0)
    grad_ks = rotate(grad_keys, angles, -1.0)
    grad_gain = jnp.sum(grad_qs * query_n + grad_ks * key_n, axis=0).reshape(head_cols)
    grad_qraw = (
        unit_back(query_n, query_f, grad_qs * qk_gains)
        .astype(jnp.bfloat16)
        .reshape(group_rows, head_cols)
    )
    grad_kraw = (
        unit_back(key_n, key_f, grad_ks * qk_gains)
        .astype(jnp.bfloat16)
        .reshape(group_rows, head_cols)
    )
    grad_vraw = grad_vals.astype(jnp.bfloat16).reshape(group_rows, head_cols)
    grad_wq = matmul_atb(packed, grad_qraw)
    grad_wk = matmul_atb(packed, grad_kraw)
    grad_wv = matmul_atb(packed, grad_vraw)
    query_mine, key_mine, value_mine = (
        lax.all_to_all(grad_qraw[inverse], "tensor", split_axis=0, concat_axis=1, tiled=True),
        lax.all_to_all(grad_kraw[inverse], "tensor", split_axis=0, concat_axis=1, tiled=True),
        lax.all_to_all(grad_vraw[inverse], "tensor", split_axis=0, concat_axis=1, tiled=True),
    )
    wq_every, wk_every, wv_every = (
        lax.all_gather(wq_back, "tensor", axis=1, tiled=True),
        lax.all_gather(wk_back, "tensor", axis=1, tiled=True),
        lax.all_gather(wv_back, "tensor", axis=1, tiled=True),
    )
    attn_part = (
        matmul_abt(query_mine, wq_every)
        + matmul_abt(key_mine, wk_every)
        + matmul_abt(value_mine, wv_every)
    )
    grad_tokens = (1.0 - alpha_attn) * grad_h1 + attn_part
    grad_qk_full = lax.dynamic_update_slice_in_dim(
        jnp.zeros(scale_qk.shape, jnp.float32), grad_gain, tensor_rank * head_cols, 0
    )
    grad_su_full = lax.dynamic_update_slice_in_dim(
        jnp.zeros(scale_up.shape, jnp.float32), grad_su, tensor_rank * hidden_cols, 0
    )
    grad_sv_full = lax.dynamic_update_slice_in_dim(
        jnp.zeros(scale_gate.shape, jnp.float32), grad_sv, tensor_rank * hidden_cols, 0
    )
    vector_sums = lax.psum(
        (grad_qk_full, grad_alpha_a, grad_su_full, grad_sv_full, grad_alpha_m), ("dp", "tensor")
    )
    mlp_sums = lax.psum_scatter(
        jnp.concatenate([grad_wu, grad_wg, grad_wd], axis=1).astype(jnp.bfloat16), "dp", scatter_dimension=0, tiled=True
    ).astype(jnp.float32)
    attn_sums = lax.psum_scatter(
        jnp.concatenate([grad_wq, grad_wk, grad_wv, grad_wo], axis=1).astype(jnp.bfloat16), "dp", scatter_dimension=0, tiled=True
    ).astype(jnp.float32)
    weight_sums = [attn_sums[:, i * head_cols : (i + 1) * head_cols] for i in range(4)] + [
        mlp_sums[:, i * hidden_cols : (i + 1) * hidden_cols] for i in range(3)
    ]
    return (
        outputs.astype(jnp.bfloat16),
        grad_tokens,
        weight_sums[0],
        weight_sums[1],
        weight_sums[2],
        weight_sums[3],
        weight_sums[4],
        weight_sums[5],
        weight_sums[6],
        vector_sums[0],
        vector_sums[1],
        vector_sums[2],
        vector_sums[3],
        vector_sums[4],
    )


def solution(mesh):
    return jax.shard_map(
        on_device,
        mesh=mesh,
        in_specs=(
            P(("dp", "tensor"), None),
            P("dp", "tensor"),
            P("dp", "tensor"),
            P("dp", "tensor"),
            P("dp", "tensor"),
            P("dp", "tensor"),
            P("dp", "tensor"),
            P("dp", "tensor"),
            P(),
            P(),
            P(),
            P(),
            P(),
            P("dp", None),
            P("dp", None),
            P(("dp", "tensor"), None),
        ),
        out_specs=(
            P(("dp", "tensor"), None),
            P(("dp", "tensor"), None),
            P("dp", "tensor"),
            P("dp", "tensor"),
            P("dp", "tensor"),
            P("dp", "tensor"),
            P("dp", "tensor"),
            P("dp", "tensor"),
            P("dp", "tensor"),
            P(),
            P(),
            P(),
            P(),
            P(),
        ),
        check_vma=False,
    )
```

```python
import math

import jax
import jax.numpy as jnp
from jax import lax
from jax.experimental import pallas as pl
from jax.experimental.pallas import tpu as pltpu
from jax.sharding import PartitionSpec as P

D = 1024
HD = 64
BLK = 256
LOG2E = 1.4426950408889634
VMEM_LIMIT = 60 * 1024 * 1024


def dot_ab(a, b):
    return lax.dot_general(a, b, (((1,), (0,)), ((), ())), preferred_element_type=jnp.float32)


def dot_abt(a, b):
    return lax.dot_general(a, b, (((1,), (1,)), ((), ())), preferred_element_type=jnp.float32)


def split_heads(block, heads):
    lane_head = lax.broadcasted_iota(jnp.int32, block.shape, 1) // HD
    zero = jnp.zeros_like(block)
    return jnp.concatenate([jnp.where(lane_head == h, block, zero) for h in range(heads)], axis=0)


def attn_fwd_body(low_ref, start_ref, q_ref, k_ref, v_ref, out_ref, lse_ref, vt_ref, qs_ref, acc_ref, sum_ref):
    rows, cols = q_ref.shape
    heads = cols // HD
    scale = math.sqrt(HD) * LOG2E
    for b in range(rows // BLK):
        vt_ref[:, b * BLK : (b + 1) * BLK] = v_ref[b * BLK : (b + 1) * BLK, :].T

    def one_block(i, _):
        base = pl.multiple_of(i * BLK, BLK)
        qs_ref[...] = split_heads(q_ref[pl.ds(base, BLK), :], heads)
        acc_ref[...] = jnp.zeros_like(acc_ref)
        sum_ref[...] = jnp.zeros_like(sum_ref)
        start = jnp.concatenate([start_ref[:, pl.ds(base, BLK)]] * heads, axis=1)
        own = lax.broadcasted_iota(jnp.int32, (1, heads * BLK), 1) % BLK + base

        def step(j, causal):
            at = pl.multiple_of(j * BLK, BLK)
            scores = dot_abt(k_ref[pl.ds(at, BLK), :], qs_ref[...])
            place = lax.broadcasted_iota(jnp.int32, scores.shape, 0) + at
            keep = place >= start
            if causal:
                keep = keep & (place <= own)
            probs = jnp.where(keep, jnp.exp2(scores * scale), 0.0)
            sum_ref[...] += jnp.sum(probs, axis=0, keepdims=True)
            probs_b = probs.astype(jnp.bfloat16)
            for h in range(heads):
                acc_ref[h * HD : (h + 1) * HD, :] += dot_ab(
                    vt_ref[h * HD : (h + 1) * HD, pl.ds(at, BLK)], probs_b[:, h * BLK : (h + 1) * BLK]
                )

        lax.fori_loop(low_ref[i], i, lambda j, c: (step(j, False), c)[1], 0)
        step(i, True)
        total = sum_ref[...]
        inv = 1.0 / total
        logs = jnp.log2(total)
        for h in range(heads):
            lse_ref[h : h + 1, pl.ds(base, BLK)] = logs[:, h * BLK : (h + 1) * BLK]
            acc_ref[h * HD : (h + 1) * HD, :] *= inv[:, h * BLK : (h + 1) * BLK]
        out_ref[pl.ds(base, BLK), :] = acc_ref[...].T.astype(jnp.bfloat16)
        return 0

    lax.fori_loop(0, rows // BLK, one_block, 0)


def vmem():
    return pl.BlockSpec(memory_space=pltpu.VMEM)


def attn_fwd(low, start, q, k, v):
    rows, cols = q.shape
    heads = cols // HD
    return pl.pallas_call(
        attn_fwd_body,
        out_shape=(
            jax.ShapeDtypeStruct((rows, cols), jnp.bfloat16),
            jax.ShapeDtypeStruct((8, rows), jnp.float32),
        ),
        in_specs=[pl.BlockSpec(memory_space=pltpu.SMEM)] + [vmem()] * 4,
        out_specs=(vmem(), vmem()),
        scratch_shapes=[
            pltpu.VMEM((cols, rows), jnp.bfloat16),
            pltpu.VMEM((heads * BLK, cols), jnp.bfloat16),
            pltpu.VMEM((cols, BLK), jnp.float32),
            pltpu.VMEM((1, heads * BLK), jnp.float32),
        ],
        compiler_params=pltpu.CompilerParams(vmem_limit_bytes=VMEM_LIMIT),
        cost_estimate=pl.CostEstimate(flops=4 * rows * rows * cols, bytes_accessed=8 * rows * cols, transcendentals=rows * rows * heads),
        name="attn_fwd",
    )(low, start, q, k, v)


def attn_bwd_body(
    low_ref, start_ref, lse_ref, q_ref, k_ref, v_ref, o_ref, g_ref,
    dq_ref, dk_ref, dv_ref, kt_ref, qs_ref, gs_ref, dqt_ref, dk_acc, dv_acc,
):
    rows, cols = q_ref.shape
    heads = cols // HD
    root = math.sqrt(HD)
    scale = root * LOG2E
    for b in range(rows // BLK):
        kt_ref[:, b * BLK : (b + 1) * BLK] = k_ref[b * BLK : (b + 1) * BLK, :].T
    dk_acc[...] = jnp.zeros_like(dk_acc)
    dv_acc[...] = jnp.zeros_like(dv_acc)

    def one_block(i, _):
        base = pl.multiple_of(i * BLK, BLK)
        qs_ref[...] = split_heads(q_ref[pl.ds(base, BLK), :], heads)
        grads = g_ref[pl.ds(base, BLK), :]
        gs_ref[...] = split_heads(grads, heads)
        dqt_ref[...] = jnp.zeros_like(dqt_ref)
        start = jnp.concatenate([start_ref[:, pl.ds(base, BLK)]] * heads, axis=1)
        own = lax.broadcasted_iota(jnp.int32, (1, heads * BLK), 1) % BLK + base
        prod = (grads.astype(jnp.float32) * o_ref[pl.ds(base, BLK), :].astype(jnp.float32)).T
        delta = jnp.concatenate(
            [jnp.sum(prod[h * HD : (h + 1) * HD, :], axis=0, keepdims=True) for h in range(heads)], axis=1
        )
        lse = jnp.concatenate([lse_ref[h : h + 1, pl.ds(base, BLK)] for h in range(heads)], axis=1)

        def step(j, causal):
            at = pl.multiple_of(j * BLK, BLK)
            scores = dot_abt(k_ref[pl.ds(at, BLK), :], qs_ref[...])
            dprobs = dot_abt(v_ref[pl.ds(at, BLK), :], gs_ref[...])
            place = lax.broadcasted_iota(jnp.int32, scores.shape, 0) + at
            keep = place >= start
            if causal:
                keep = keep & (place <= own)
            probs = jnp.where(keep, jnp.exp2(scores * scale - lse), 0.0)
            dsc = (probs * (dprobs - delta)).astype(jnp.bfloat16)
            dv_acc[pl.ds(at, BLK), :] += dot_ab(probs.astype(jnp.bfloat16), gs_ref[...])
            dk_acc[pl.ds(at, BLK), :] += dot_ab(dsc, qs_ref[...])
            for h in range(heads):
                dqt_ref[h * HD : (h + 1) * HD, :] += dot_ab(
                    kt_ref[h * HD : (h + 1) * HD, pl.ds(at, BLK)], dsc[:, h * BLK : (h + 1) * BLK]
                )

        lax.fori_loop(low_ref[i], i, lambda j, c: (step(j, False), c)[1], 0)
        step(i, True)
        dq_ref[pl.ds(base, BLK), :] = (dqt_ref[...].T * root).astype(dq_ref.dtype)
        return 0

    lax.fori_loop(0, rows // BLK, one_block, 0)
    dk_ref[...] = (dk_acc[...] * root).astype(dk_ref.dtype)
    dv_ref[...] = dv_acc[...].astype(dv_ref.dtype)


def attn_bwd(low, start, lse, q, k, v, o, g):
    rows, cols = q.shape
    heads = cols // HD
    return pl.pallas_call(
        attn_bwd_body,
        out_shape=(jax.ShapeDtypeStruct((rows, cols), jnp.bfloat16),) * 3,
        in_specs=[pl.BlockSpec(memory_space=pltpu.SMEM)] + [vmem()] * 7,
        out_specs=(vmem(),) * 3,
        scratch_shapes=[
            pltpu.VMEM((cols, rows), jnp.bfloat16),
            pltpu.VMEM((heads * BLK, cols), jnp.bfloat16),
            pltpu.VMEM((heads * BLK, cols), jnp.bfloat16),
            pltpu.VMEM((cols, BLK), jnp.float32),
            pltpu.VMEM((rows, cols), jnp.float32),
            pltpu.VMEM((rows, cols), jnp.float32),
        ],
        compiler_params=pltpu.CompilerParams(vmem_limit_bytes=VMEM_LIMIT),
        cost_estimate=pl.CostEstimate(flops=10 * rows * rows * cols, bytes_accessed=16 * rows * cols, transcendentals=rows * rows * heads),
        name="attn_bwd",
    )(low, start, lse, q, k, v, o, g)


MESH_ID = pl.DeviceIdType.MESH
EPS = 1e-06
TILE = 256
STRIP = 64


def flip1(index):
    return index + 1 - 2 * lax.rem(index, 2)


def flip2(index):
    return index + 2 - 4 * (index // 2)


def over(count, body):
    lax.fori_loop(0, count, lambda i, carry: (body(i), carry)[1], 0)


def tile_at(index, size):
    return pl.ds(pl.multiple_of(index * size, size), size)


def row_sum(value):
    return jnp.sum(value, axis=-1, keepdims=True)


def middle_body(
    att_ref, wo_hbm, w_hbm, tok_hbm, cot_hbm, aa_ref, am_ref, su_ref, sg_ref,
    out_ref, datt_ref, gw_hbm, gwo_hbm, dh1_ref, gaa_ref, gam_ref, gsu_ref, gsg_ref,
    wo, wall, tok, cot, parts, mids, dbms, mid_t, dbm_t, ups, gates, mixed,
    middle, branch, dh2, own_part, send_a, recv_a, send_d, recv_d, send_z, recv_z,
    gw, gwo, dparts, load_sems, store_sems, hop_send, hop_recv, a2a_send, a2a_recv, d2a_send, d2a_recv, part_send, part_recv,
):
    d = lax.axis_index("dp")
    t = lax.axis_index("tensor")
    rows, width = tok.shape
    heads_w = att_ref.shape[1]
    hid = wall.shape[2]
    nq = w_hbm.shape[0]
    qrows = w_hbm.shape[2]
    chunks = hop_send.shape[0] // 6
    crow = rows // chunks
    core_peer = (flip1(d), t)
    z_peer = (d, flip1(t))
    line = [t, flip1(t), flip2(t), 3 - t]

    barrier = pltpu.get_barrier_semaphore()
    for peer in [core_peer] + [(d, line[k]) for k in (1, 2, 3)]:
        pl.semaphore_signal(barrier, inc=1, device_id=peer, device_id_type=MESH_ID)
    pl.semaphore_wait(barrier, 4)

    def remote(src, dst, ssem, rsem, peer):
        return pltpu.make_async_remote_copy(
            src_ref=src, dst_ref=dst, send_sem=ssem, recv_sem=rsem, device_id=peer, device_id_type=MESH_ID
        )

    a2a = [
        remote(att_ref.at[tile_at(line[k], rows), :], parts.at[k - 1], a2a_send.at[k - 1], a2a_recv.at[k - 1], (d, line[k]))
        for k in (1, 2, 3)
    ]
    for copy in a2a:
        copy.start()
    loads = [
        pltpu.make_async_copy(wo_hbm, wo, load_sems.at[0]),
        pltpu.make_async_copy(tok_hbm, tok, load_sems.at[1]),
        pltpu.make_async_copy(cot_hbm, cot, load_sems.at[2]),
    ]
    wloads = [
        [
            pltpu.make_async_copy(w_hbm.at[q, m], wall.at[m, pl.ds(q * qrows, qrows), :], load_sems.at[3 + m * nq + q])
            for q in range(nq)
        ]
        for m in range(3)
    ]
    for copy in loads + wloads[0] + wloads[1] + wloads[2]:
        copy.start()

    gsu_ref[...] = jnp.zeros_like(gsu_ref)
    gsg_ref[...] = jnp.zeros_like(gsg_ref)
    gam_ref[...] = jnp.zeros_like(gam_ref)
    gaa_ref[...] = jnp.zeros_like(gaa_ref)

    loads[0].wait()
    for copy in a2a:
        copy.wait_recv()

    def project(n):
        cols = tile_at(n, TILE)
        total = dot_abt(att_ref[tile_at(t, rows), :], wo[cols, tile_at(t, heads_w)])
        for k in (1, 2, 3):
            total += dot_abt(parts[k - 1], wo[cols, tile_at(line[k], heads_w)])
        branch[:, cols] = total

    over(width // TILE, project)
    loads[1].wait()

    def hop(buf, phase, ch, kind):
        part = pl.ds(ch * crow, crow)
        index = (phase * chunks + ch) * 3 + kind
        src, dst, peer = ((0, 2, z_peer), (0, 1, core_peer), (2, 3, core_peer))[kind]
        return remote(buf.at[src, part, :], buf.at[dst, part, :], hop_send.at[index], hop_recv.at[index], peer)

    def strips(ch, body):
        over(crow // STRIP, lambda i: body(tile_at(i + ch * (crow // STRIP), STRIP)))

    def unit_of(value):
        factor = lax.rsqrt(row_sum(value * value) + EPS)
        return value * factor, factor

    def make_middle(at):
        inputs = tok[at, :].astype(jnp.float32)
        norm_a, factor_a = unit_of(branch[at, :])
        mid, factor_mid = unit_of(inputs + aa_ref[...] * (norm_a - inputs))
        return inputs, norm_a, factor_a, mid, factor_mid

    def first(at):
        mid = make_middle(at)[3]
        middle[at, :] = mid
        mids[0, at, :] = mid.astype(jnp.bfloat16)

    for ch in range(chunks):
        strips(ch, first)
        hop(mids, 0, ch, 0).start()
        hop(mids, 0, ch, 1).start()

    for m in range(3):
        for copy in wloads[m]:
            copy.wait()

    def forward_rows(slot, at, store, ready):
        base = slot * rows

        def hidden(n):
            cols = tile_at(n, TILE)
            x = mids[slot, at, :]
            up = dot_ab(x, wall[0, :, cols])
            gate_raw = dot_ab(x, wall[1, :, cols])
            gate = gate_raw * sg_ref[:, cols]
            silu = gate / (1.0 + jnp.exp(-gate))
            where = pl.ds(base + at.start, at.size)
            ups[where, cols] = up.astype(jnp.bfloat16)
            gates[where, cols] = gate_raw.astype(jnp.bfloat16)
            mixed[where, cols] = (up * su_ref[:, cols] * silu).astype(jnp.bfloat16)

        over(hid // TILE, hidden)
        ready()

        def down(n):
            cols = tile_at(n, TILE)
            store(at, cols, dot_abt(mixed[pl.ds(base + at.start, at.size), :], wall[2, cols, :]))

        over(width // TILE, down)

    def backward_rows(slot, at, store, ready):
        base = slot * rows
        where = pl.ds(base + at.start, at.size)

        def hidden(n):
            cols = tile_at(n, TILE)
            dmix = dot_ab(dbms[slot, at, :], wall[2, :, cols])
            up_raw = ups[where, cols].astype(jnp.float32)
            gate_raw = gates[where, cols].astype(jnp.float32)
            gate = gate_raw * sg_ref[:, cols]
            sig = 1.0 / (1.0 + jnp.exp(-gate))
            d_up = dmix * (gate * sig)
            d_gate = dmix * (up_raw * su_ref[:, cols]) * (sig * (1.0 + gate * (1.0 - sig)))
            gsu_ref[:, cols] += jnp.sum(d_up * up_raw, axis=0, keepdims=True)
            gsg_ref[:, cols] += jnp.sum(d_gate * gate_raw, axis=0, keepdims=True)
            ups[where, cols] = (d_up * su_ref[:, cols]).astype(jnp.bfloat16)
            gates[where, cols] = (d_gate * sg_ref[:, cols]).astype(jnp.bfloat16)

        over(hid // TILE, hidden)
        ready()

        def down(n):
            cols = tile_at(n, TILE)
            store(at, cols, dot_abt(ups[where, :], wall[0, cols, :]) + dot_abt(gates[where, :], wall[1, cols, :]))

        over(width // TILE, down)

    def part_copy(phase, kind, ch):
        part = pl.ds(ch * crow, crow)
        index = (phase * 3 + kind) * chunks + ch
        src, dst, peer = ((send_a, recv_a, core_peer), (send_d, recv_d, core_peer), (send_z, recv_z, z_peer))[kind]
        return remote(src.at[part, :], dst.at[part, :], part_send.at[index], part_recv.at[index], peer)

    everything = pl.ds(0, rows)

    def nothing():
        pass

    def tensor_pass(phase, buf, rows_fn, fillers):
        def keep_own(at, cols, value):
            own_part[at, cols] = value

        def to(ref):
            def store(at, cols, value):
                ref[at, cols] = value.astype(jnp.bfloat16)

            return store

        def to_z(at, cols, value):
            send_z[at, cols] = (value + recv_d[at, cols].astype(jnp.float32)).astype(jnp.bfloat16)

        rows_fn(0, everything, keep_own, nothing)
        for ch in range(chunks):
            hop(buf, phase, ch, 1).wait_recv()
        if phase == 1:
            for ch in range(chunks):
                part_copy(0, 0, ch).wait_send()
        rows_fn(1, everything, to(send_a), nothing)
        for ch in range(chunks):
            part_copy(phase, 0, ch).start()
        fillers[0]()
        for ch in range(chunks):
            hop(buf, phase, ch, 0).wait_recv()
            hop(buf, phase, ch, 2).start()
            at = pl.ds(ch * crow, crow)
            hop(buf, phase, ch, 2).wait_recv()
            if phase == 1:
                part_copy(0, 1, ch).wait_send()
            rows_fn(3, at, to(send_d), nothing)
            part_copy(phase, 1, ch).start()

            def ready():
                part_copy(phase, 1, ch).wait_recv()
                if phase == 1:
                    part_copy(0, 2, ch).wait_send()

            rows_fn(2, at, to_z, ready)
            part_copy(phase, 2, ch).start()
        fillers[1]()

    def transpose_into(dst, buf, slots):
        for slot in slots:
            for b in range(rows // 128):
                for n in range(width // TILE):
                    dst[n * TILE : (n + 1) * TILE, slot * rows + b * 128 : slot * rows + (b + 1) * 128] = buf[
                        slot, b * 128 : (b + 1) * 128, n * TILE : (n + 1) * TILE
                    ].T

    tensor_pass(
        0, mids, forward_rows,
        [lambda: transpose_into(mid_t, mids, (0, 1)), lambda: transpose_into(mid_t, mids, (2, 3))],
    )

    loads[2].wait()

    def turn(at):
        mid = middle[at, :]
        branch_m = own_part[at, :] + recv_a[at, :].astype(jnp.float32) + recv_z[at, :].astype(jnp.float32)
        norm_m, factor_m = unit_of(branch_m)
        alpha = am_ref[...]
        y, factor_y = unit_of(mid + alpha * (norm_m - mid))
        out_ref[at, :] = y.astype(jnp.bfloat16)
        dy = cot[at, :].astype(jnp.float32)
        grad = factor_y * (dy - y * row_sum(y * dy))
        gam_ref[...] += jnp.sum(grad * (norm_m - mid), axis=0, keepdims=True)
        back = alpha * grad
        dbms[0, at, :] = (factor_m * (back - norm_m * row_sum(norm_m * back))).astype(jnp.bfloat16)
        dh2[at, :] = grad - back

    for ch in range(chunks):
        part_copy(0, 0, ch).wait_recv()
        part_copy(0, 2, ch).wait_recv()
        strips(ch, turn)
        hop(dbms, 1, ch, 0).start()
        hop(dbms, 1, ch, 1).start()

    def weight_grads():
        transpose_into(dbm_t, dbms, (2, 3))
        for m, (lhs, rhs) in enumerate(((mid_t, ups), (mid_t, gates), (dbm_t, mixed))):

            def block(i):
                q = i // (hid // TILE)
                cols = tile_at(lax.rem(i, hid // TILE), TILE)
                value = dot_ab(lhs[tile_at(q, TILE), :], rhs[:, cols])
                gw[m, tile_at(q, TILE), cols] = value.astype(jnp.bfloat16)

            over((width // TILE) * (hid // TILE), block)
            for q in range(nq):
                grad_store(m, q).start()

    def grad_store(m, q):
        return pltpu.make_async_copy(gw.at[m, pl.ds(q * qrows, qrows), :], gw_hbm.at[q, m], store_sems.at[m * nq + q])

    tensor_pass(1, dbms, backward_rows, [lambda: transpose_into(dbm_t, dbms, (0, 1)), weight_grads])

    def last(at):
        inputs, norm_a, factor_a, mid, factor_mid = make_middle(at)
        grad_mid = dh2[at, :] + own_part[at, :] + recv_a[at, :].astype(jnp.float32) + recv_z[at, :].astype(jnp.float32)
        grad = factor_mid * (grad_mid - mid * row_sum(mid * grad_mid))
        gaa_ref[...] += jnp.sum(grad * (norm_a - inputs), axis=0, keepdims=True)
        back = aa_ref[...] * grad
        dh1_ref[at, :] = grad - back
        mids[0, at, :] = (factor_a * (back - norm_a * row_sum(norm_a * back))).astype(jnp.bfloat16)

    for ch in range(chunks):
        hop(mids, 0, ch, 0).wait_send()
        hop(mids, 0, ch, 1).wait_send()
        part_copy(1, 0, ch).wait_recv()
        part_copy(1, 2, ch).wait_recv()
        strips(ch, last)

    dback = [
        remote(dparts.at[k], datt_ref.at[tile_at(t, rows), :], d2a_send.at[k - 1], d2a_recv.at[k - 1], (d, line[k]))
        for k in (1, 2, 3)
    ]
    for k in (3, 2, 1, 0):
        value = dot_ab(mids[0], wo[:, tile_at(line[k], heads_w)]).astype(jnp.bfloat16)
        if k:
            dparts[k] = value
            dback[k - 1].start()
        else:
            datt_ref[tile_at(t, rows), :] = value

    for b in range(rows // 128):
        for n in range(width // TILE):
            mid_t[n * TILE : (n + 1) * TILE, b * 128 : (b + 1) * 128] = mids[
                0, b * 128 : (b + 1) * 128, n * TILE : (n + 1) * TILE
            ].T

    def out_grad(n):
        at = tile_at(n, TILE)
        lhs = mid_t[at, 0:rows]
        gwo[at, tile_at(t, heads_w)] = dot_ab(lhs, att_ref[tile_at(t, rows), :]).astype(jnp.bfloat16)
        for k in (1, 2, 3):
            gwo[at, tile_at(line[k], heads_w)] = dot_ab(lhs, parts[k - 1]).astype(jnp.bfloat16)

    over(width // TILE, out_grad)
    wo_store = pltpu.make_async_copy(gwo, gwo_hbm, store_sems.at[3 * nq])
    wo_store.start()

    for k in (1, 2, 3):
        remote(
            dparts.at[k], datt_ref.at[tile_at(line[k], rows), :], d2a_send.at[k - 1], d2a_recv.at[k - 1], (d, line[k])
        ).wait()
    for copy in a2a:
        copy.wait_send()
    for ch in range(chunks):
        hop(mids, 0, ch, 2).wait_send()
        for kind in range(3):
            hop(dbms, 1, ch, kind).wait_send()
            part_copy(1, kind, ch).wait_send()
    for m in range(3):
        for q in range(nq):
            grad_store(m, q).wait()
    wo_store.wait()


def middle_call(chunks, attended, wo, w_parts, tokens, cotangent, alpha_a, alpha_m, su, sg):
    rows, width = tokens.shape
    group, heads_w = attended.shape
    nq, _, qrows, hid = w_parts.shape
    bf, f32 = jnp.bfloat16, jnp.float32
    anywhere = pl.BlockSpec(memory_space=pl.ANY)
    dma = pltpu.SemaphoreType.DMA
    return pl.pallas_call(
        middle_body,
        out_shape=(
            jax.ShapeDtypeStruct((rows, width), bf),
            jax.ShapeDtypeStruct((group, heads_w), bf),
            jax.ShapeDtypeStruct((nq, 3, qrows, hid), bf),
            jax.ShapeDtypeStruct((width, width), bf),
            jax.ShapeDtypeStruct((rows, width), f32),
            jax.ShapeDtypeStruct((1, width), f32),
            jax.ShapeDtypeStruct((1, width), f32),
            jax.ShapeDtypeStruct((1, hid), f32),
            jax.ShapeDtypeStruct((1, hid), f32),
        ),
        in_specs=[vmem(), anywhere, anywhere, anywhere, anywhere] + [vmem()] * 4,
        out_specs=(vmem(), vmem(), anywhere, anywhere) + (vmem(),) * 5,
        scratch_shapes=[
            pltpu.VMEM((width, width), bf),
            pltpu.VMEM((3, width, hid), bf),
            pltpu.VMEM((rows, width), bf),
            pltpu.VMEM((rows, width), bf),
            pltpu.VMEM((3, rows, heads_w), bf),
            pltpu.VMEM((4, rows, width), bf),
            pltpu.VMEM((4, rows, width), bf),
            pltpu.VMEM((width, 4 * rows), bf),
            pltpu.VMEM((width, 4 * rows), bf),
            pltpu.VMEM((4 * rows, hid), bf),
            pltpu.VMEM((4 * rows, hid), bf),
            pltpu.VMEM((4 * rows, hid), bf),
            pltpu.VMEM((rows, width), f32),
            pltpu.VMEM((rows, width), f32),
            pltpu.VMEM((rows, width), f32),
            pltpu.VMEM((rows, width), f32),
        ]
        + [pltpu.VMEM((rows, width), bf)] * 6
        + [
            pltpu.VMEM((3, width, hid), bf),
            pltpu.VMEM((width, width), bf),
            pltpu.VMEM((4, rows, heads_w), bf),
            dma((3 + 3 * nq,)),
            dma((3 * nq + 1,)),
            dma((6 * chunks,)),
            dma((6 * chunks,)),
            dma((3,)),
            dma((3,)),
            dma((3,)),
            dma((3,)),
            dma((6 * chunks,)),
            dma((6 * chunks,)),
        ],
        compiler_params=pltpu.CompilerParams(vmem_limit_bytes=67000000, collective_id=1, has_side_effects=True),
        cost_estimate=pl.CostEstimate(flops=10**11, bytes_accessed=10**8, transcendentals=10**6),
        name="middle",
    )(attended, wo, w_parts, tokens, cotangent, alpha_a, alpha_m, su, sg)


def flat(dp_index, tensor_index, tensor_count):
    return dp_index * tensor_count + tensor_index


def hidden_routes(dp_count, tensor_count):
    near, far = [], []
    for d in range(dp_count):
        for t in range(tensor_count):
            own = flat(d, t, tensor_count)
            if d % 2 != t // 2:
                near.append((own, flat(d ^ 1, t, tensor_count)))
                far.append((own, flat(d ^ 1, t ^ 2, tensor_count)))
            else:
                near.append((own, flat(d, t ^ 2, tensor_count)))
    return near, far


def same_core_groups(dp_count):
    return [list(range(parity, dp_count, 2)) for parity in range(2)]


def gather_hidden(own, dp_count, tensor_count):
    near, far = hidden_routes(dp_count, tensor_count)
    axes = ("dp", "tensor")
    core = lax.rem(lax.axis_index("dp"), 2)
    home = core == lax.axis_index("tensor") // 2
    first = lax.ppermute(own, axes, near)
    second = lax.ppermute(own, axes, far)
    mine = jnp.where(home, own, first)
    other = jnp.where(home, first, second)
    pair = jnp.where(core == 0, jnp.stack([mine, other], 1), jnp.stack([other, mine], 1))
    kinds, _, rows, cols = pair.shape
    return lax.all_gather(
        pair.reshape(kinds, 2 * rows, cols), "dp", axis=0, tiled=False, axis_index_groups=same_core_groups(dp_count)
    )


def scatter_hidden(parts, dp_count, tensor_count):
    near, far = hidden_routes(dp_count, tensor_count)
    axes = ("dp", "tensor")
    core = lax.rem(lax.axis_index("dp"), 2)
    home = core == lax.axis_index("tensor") // 2
    summed = lax.psum_scatter(
        parts, "dp", scatter_dimension=0, tiled=False, axis_index_groups=same_core_groups(dp_count)
    )
    kinds, rows, cols = summed.shape
    halves = summed.reshape(kinds, 2, rows // 2, cols)
    mine = jnp.where(core == 0, halves[:, 0], halves[:, 1])
    other = jnp.where(core == 0, halves[:, 1], halves[:, 0])
    first = lax.ppermute(jnp.where(home, other, mine), axes, [(b, a) for a, b in near])
    second = lax.ppermute(other, axes, [(b, a) for a, b in far])
    f32 = jnp.float32
    return jnp.where(home, mine.astype(f32), second.astype(f32)) + first.astype(f32)


def matmul_ab(first_op, second_op):
    return jnp.dot(first_op, second_op, preferred_element_type=jnp.float32)


def matmul_abt(first_op, second_op):
    return lax.dot_general(
        first_op, second_op, (((1,), (1,)), ((), ())), preferred_element_type=jnp.float32
    )


def matmul_atb(first_op, second_op):
    return lax.dot_general(
        first_op, second_op, (((0,), (0,)), ((), ())), preferred_element_type=jnp.float32
    )


def unit_pair(matrix):
    factor = lax.rsqrt(jnp.sum(matrix * matrix, axis=-1, keepdims=True) + 1e-06)
    return (matrix * factor, factor)


def unit_back(normed, factor, grad_out):
    return factor * (grad_out - normed * jnp.sum(normed * grad_out, axis=-1, keepdims=True))


def rotate(matrix, angles, direction):
    half_width = matrix.shape[-1] // 2
    cosine = jnp.cos(angles)[:, None, :]
    sine_part = direction * jnp.sin(angles)[:, None, :]
    lead_half = matrix[..., :half_width]
    tail_half = matrix[..., half_width:]
    return jnp.concatenate(
        [lead_half * cosine - tail_half * sine_part, tail_half * cosine + lead_half * sine_part],
        axis=-1,
    )


def layout(order_row, length_row):
    group_rows = order_row.shape[0]
    places = jnp.arange(group_rows, dtype=jnp.int32)
    seg_ends = jnp.cumsum(length_row, dtype=jnp.int32)
    seg_starts = seg_ends - length_row
    seg_first = jnp.max(
        jnp.where(seg_starts[None, :] <= places[:, None], seg_starts[None, :], 0), axis=1
    )
    half_width = HD // 2
    inv_freq = jnp.exp(
        jnp.arange(half_width, dtype=jnp.float32) * (-math.log(10000.0) / half_width)
    )
    angles = (places - seg_first).astype(jnp.float32)[:, None] * inv_freq[None, :]
    inverse = jnp.zeros((group_rows,), jnp.int32).at[order_row].set(places)
    return (seg_first, angles, inverse)


def on_device(
    tokens,
    w_query,
    w_key,
    w_value,
    w_out_t,
    w_up,
    w_gate,
    w_down_t,
    scale_qk,
    alpha_attn,
    scale_up,
    scale_gate,
    alpha_mlp,
    order,
    lengths,
    cotangent,
):
    tensor_rank = lax.axis_index("tensor")
    head_cols = w_query.shape[1]
    hidden_cols = w_up.shape[1]
    local_heads = head_cols // HD
    qk_gains = lax.dynamic_slice_in_dim(scale_qk, tensor_rank * head_cols, head_cols).reshape(
        local_heads, HD
    )
    dp_count, tensor_count = lax.axis_size("dp"), lax.axis_size("tensor")
    hidden_rank = lax.rem(tensor_rank, 2) + 2 * lax.rem(lax.axis_index("dp"), 2)
    up_gains = lax.dynamic_slice_in_dim(scale_up, hidden_rank * hidden_cols, hidden_cols)[None, :]
    gate_gains = lax.dynamic_slice_in_dim(
        scale_gate, hidden_rank * hidden_cols, hidden_cols
    )[None, :] * math.sqrt(D)
    order_row = order[0]
    seg_first, angles, inverse = layout(order_row, lengths[0])
    group_rows = order_row.shape[0]
    attn_full = (
        lax.all_gather(w_query, "dp", axis=0, tiled=True),
        lax.all_gather(w_key, "dp", axis=0, tiled=True),
        lax.all_gather(w_value, "dp", axis=0, tiled=True),
        lax.all_gather(w_out_t, "dp", axis=0, tiled=True),
    )
    wq_full, wk_full, wv_full, wo_full = attn_full
    mlp_parts = gather_hidden(jnp.stack([w_up, w_gate, w_down_t]), dp_count, tensor_count)
    gathered = lax.all_gather(tokens, "tensor", axis=0, tiled=True)
    packed = gathered[order_row]
    query_n, query_f = unit_pair(matmul_ab(packed, wq_full).reshape(group_rows, local_heads, HD))
    key_n, key_f = unit_pair(matmul_ab(packed, wk_full).reshape(group_rows, local_heads, HD))
    queries = rotate(query_n * qk_gains, angles, 1.0).astype(jnp.bfloat16)
    key_rows = rotate(key_n * qk_gains, angles, 1.0).astype(jnp.bfloat16)
    value_rows = (
        matmul_ab(packed, wv_full).astype(jnp.bfloat16).reshape(group_rows, local_heads, HD)
    )

    low = lax.slice(seg_first, (0,), (group_rows,), (BLK,)) // BLK
    start = seg_first[None, :]
    queries = queries.reshape(group_rows, head_cols)
    key_rows = key_rows.reshape(group_rows, head_cols)
    value_rows = value_rows.reshape(group_rows, head_cols)
    attended, log_totals = attn_fwd(low, start, queries, key_rows, value_rows)
    wo_every = lax.all_gather(wo_full, "tensor", axis=1, tiled=True)
    out_rows, grad_att_rows, mlp_grads, wo_grads, grad_h1_kept, grad_alpha_a, grad_alpha_m, grad_su, grad_sv = middle_call(
        2,
        attended[inverse],
        wo_every,
        mlp_parts,
        tokens,
        cotangent,
        alpha_attn[None, :],
        alpha_mlp[None, :],
        up_gains,
        gate_gains,
    )
    grad_att = grad_att_rows[order_row]
    grad_queries, grad_keys, grad_vals = attn_bwd(
        low, start, log_totals, queries, key_rows, value_rows, attended, grad_att
    )
    grad_queries = grad_queries.astype(jnp.float32).reshape(group_rows, local_heads, HD)
    grad_keys = grad_keys.astype(jnp.float32).reshape(group_rows, local_heads, HD)
    grad_qs = rotate(grad_queries, angles, -1.0)
    grad_ks = rotate(grad_keys, angles, -1.0)
    grad_gain = jnp.sum(grad_qs * query_n + grad_ks * key_n, axis=0).reshape(head_cols)
    grad_qraw = (
        unit_back(query_n, query_f, grad_qs * qk_gains)
        .astype(jnp.bfloat16)
        .reshape(group_rows, head_cols)
    )
    grad_kraw = (
        unit_back(key_n, key_f, grad_ks * qk_gains)
        .astype(jnp.bfloat16)
        .reshape(group_rows, head_cols)
    )
    grad_vraw = grad_vals.astype(jnp.bfloat16).reshape(group_rows, head_cols)
    grad_wq = matmul_atb(packed, grad_qraw)
    grad_wk = matmul_atb(packed, grad_kraw)
    grad_wv = matmul_atb(packed, grad_vraw)
    back_rows = jnp.concatenate([grad_qraw, grad_kraw, grad_vraw], axis=1)[inverse]
    back_weights = jnp.concatenate([wq_full, wk_full, wv_full], axis=1)
    attn_part = lax.psum_scatter(
        matmul_abt(back_rows, back_weights).astype(jnp.bfloat16), "tensor", scatter_dimension=0, tiled=True
    ).astype(jnp.float32)
    grad_tokens = grad_h1_kept + attn_part
    grad_qk_full = lax.dynamic_update_slice_in_dim(
        jnp.zeros(scale_qk.shape, jnp.float32), grad_gain, tensor_rank * head_cols, 0
    )
    grad_su_full = lax.dynamic_update_slice_in_dim(
        jnp.zeros(scale_up.shape, jnp.float32), grad_su[0], hidden_rank * hidden_cols, 0
    )
    grad_sv_full = lax.dynamic_update_slice_in_dim(
        jnp.zeros(scale_gate.shape, jnp.float32), grad_sv[0] * math.sqrt(D), hidden_rank * hidden_cols, 0
    )
    vector_sums = lax.psum(
        (grad_qk_full, grad_alpha_a[0], grad_su_full, grad_sv_full, grad_alpha_m[0]), ("dp", "tensor")
    )
    mlp_sums = scatter_hidden(mlp_grads, dp_count, tensor_count)
    attn_sums = lax.psum_scatter(
        jnp.concatenate([grad_wq, grad_wk, grad_wv], axis=1).astype(jnp.bfloat16), "dp", scatter_dimension=0, tiled=True
    ).astype(jnp.float32)
    wo_sums = lax.psum_scatter(
        lax.psum_scatter(wo_grads, "dp", scatter_dimension=0, tiled=True), "tensor", scatter_dimension=1, tiled=True
    ).astype(jnp.float32)
    weight_sums = [attn_sums[:, i * head_cols : (i + 1) * head_cols] for i in range(3)] + [wo_sums, *mlp_sums]
    return (
        out_rows,
        grad_tokens,
        weight_sums[0],
        weight_sums[1],
        weight_sums[2],
        weight_sums[3],
        weight_sums[4],
        weight_sums[5],
        weight_sums[6],
        vector_sums[0],
        vector_sums[1],
        vector_sums[2],
        vector_sums[3],
        vector_sums[4],
    )


def solution(mesh):
    return jax.shard_map(
        on_device,
        mesh=mesh,
        in_specs=(
            P(("dp", "tensor"), None),
            P("dp", "tensor"),
            P("dp", "tensor"),
            P("dp", "tensor"),
            P("dp", "tensor"),
            P("dp", "tensor"),
            P("dp", "tensor"),
            P("dp", "tensor"),
            P(),
            P(),
            P(),
            P(),
            P(),
            P("dp", None),
            P("dp", None),
            P(("dp", "tensor"), None),
        ),
        out_specs=(
            P(("dp", "tensor"), None),
            P(("dp", "tensor"), None),
            P("dp", "tensor"),
            P("dp", "tensor"),
            P("dp", "tensor"),
            P("dp", "tensor"),
            P("dp", "tensor"),
            P("dp", "tensor"),
            P("dp", "tensor"),
            P(),
            P(),
            P(),
            P(),
            P(),
        ),
        check_vma=False,
    )
```

```python
import functools
import math

import jax
import jax.numpy as jnp
from jax import lax
from jax.experimental import pallas as pl
from jax.experimental.pallas import tpu as pltpu
from jax.sharding import PartitionSpec as P

D = 1024
HD = 64
BLK = 256
LOG2E = 1.4426950408889634
VMEM_LIMIT = 60 * 1024 * 1024


def dot_ab(a, b):
    return lax.dot_general(a, b, (((1,), (0,)), ((), ())), preferred_element_type=jnp.float32)


def dot_abt(a, b):
    return lax.dot_general(a, b, (((1,), (1,)), ((), ())), preferred_element_type=jnp.float32)


def split_heads(block, heads):
    lane_head = lax.broadcasted_iota(jnp.int32, block.shape, 1) // HD
    zero = jnp.zeros_like(block)
    return jnp.concatenate([jnp.where(lane_head == h, block, zero) for h in range(heads)], axis=0)


def attn_fwd_body(
    low_ref, start_ref, order_row, q_ref, k_ref, v_ref, out_ref, lse_ref, plain_ref, vt_ref, qs_ref, acc_ref, sum_ref
):
    rows, cols = q_ref.shape
    heads = cols // HD
    scale = math.sqrt(HD) * LOG2E
    for b in range(rows // BLK):
        vt_ref[:, b * BLK : (b + 1) * BLK] = v_ref[b * BLK : (b + 1) * BLK, :].T

    def one_block(i, _):
        base = pl.multiple_of(i * BLK, BLK)
        qs_ref[...] = split_heads(q_ref[pl.ds(base, BLK), :], heads)
        acc_ref[...] = jnp.zeros_like(acc_ref)
        sum_ref[...] = jnp.zeros_like(sum_ref)
        start = jnp.concatenate([start_ref[:, pl.ds(base, BLK)]] * heads, axis=1)
        own = lax.broadcasted_iota(jnp.int32, (1, heads * BLK), 1) % BLK + base

        def step(j, causal):
            at = pl.multiple_of(j * BLK, BLK)
            scores = dot_abt(k_ref[pl.ds(at, BLK), :], qs_ref[...])
            place = lax.broadcasted_iota(jnp.int32, scores.shape, 0) + at
            keep = place >= start
            if causal:
                keep = keep & (place <= own)
            probs = jnp.where(keep, jnp.exp2(scores * scale), 0.0)
            sum_ref[...] += jnp.sum(probs, axis=0, keepdims=True)
            probs_b = probs.astype(jnp.bfloat16)
            for h in range(heads):
                acc_ref[h * HD : (h + 1) * HD, :] += dot_ab(
                    vt_ref[h * HD : (h + 1) * HD, pl.ds(at, BLK)], probs_b[:, h * BLK : (h + 1) * BLK]
                )

        lax.fori_loop(low_ref[i], i, lambda j, c: (step(j, False), c)[1], 0)
        step(i, True)
        total = sum_ref[...]
        inv = 1.0 / total
        logs = jnp.log2(total)
        for h in range(heads):
            lse_ref[h : h + 1, pl.ds(base, BLK)] = logs[:, h * BLK : (h + 1) * BLK]
            acc_ref[h * HD : (h + 1) * HD, :] *= inv[:, h * BLK : (h + 1) * BLK]
        out_ref[pl.ds(base, BLK), :] = acc_ref[...].T.astype(jnp.bfloat16)
        return 0

    lax.fori_loop(0, rows // BLK, one_block, 0)
    over(rows // BLK, lambda b: to_token_order(b, order_row, out_ref, plain_ref))


def to_token_order(b, order_row, src, dst):
    at = pl.ds(pl.multiple_of(b * BLK, BLK), BLK)
    hot = lax.broadcasted_iota(jnp.int32, (BLK, src.shape[0]), 0) + b * BLK == order_row[...]
    dst[at, :] = dot_ab(hot.astype(jnp.float32).astype(jnp.bfloat16), src[...]).astype(dst.dtype)


def to_packed_order(b, order_col, src, dst):
    at = pl.ds(pl.multiple_of(b * BLK, BLK), BLK)
    hot = lax.broadcasted_iota(jnp.int32, (BLK, src.shape[0]), 1) == order_col[at, :]
    dst[at, :] = dot_ab(hot.astype(jnp.float32).astype(jnp.bfloat16), src[...]).astype(dst.dtype)


def over(count, body):
    lax.fori_loop(0, count, lambda i, carry: (body(i), carry)[1], 0)


def vmem():
    return pl.BlockSpec(memory_space=pltpu.VMEM)


def attn_fwd(low, start, order_row, q, k, v):
    rows, cols = q.shape
    heads = cols // HD
    return pl.pallas_call(
        attn_fwd_body,
        out_shape=(
            jax.ShapeDtypeStruct((rows, cols), jnp.bfloat16),
            jax.ShapeDtypeStruct((8, rows), jnp.float32),
            jax.ShapeDtypeStruct((rows, cols), jnp.bfloat16),
        ),
        in_specs=[pl.BlockSpec(memory_space=pltpu.SMEM)] + [vmem()] * 5,
        out_specs=(vmem(),) * 3,
        scratch_shapes=[
            pltpu.VMEM((cols, rows), jnp.bfloat16),
            pltpu.VMEM((heads * BLK, cols), jnp.bfloat16),
            pltpu.VMEM((cols, BLK), jnp.float32),
            pltpu.VMEM((1, heads * BLK), jnp.float32),
        ],
        compiler_params=pltpu.CompilerParams(vmem_limit_bytes=VMEM_LIMIT),
        cost_estimate=pl.CostEstimate(flops=4 * rows * rows * cols, bytes_accessed=8 * rows * cols, transcendentals=rows * rows * heads),
        name="attn_fwd",
    )(low, start, order_row, q, k, v)


def attn_bwd_body(
    low_ref, start_ref, order_row, order_col, lse_ref, q_ref, k_ref, v_ref, o_ref, grad_ref,
    plain_ref, kt_ref, qs_ref, gs_ref, dqt_ref, dk_acc, dv_acc, g_ref, packed,
):
    rows, cols = q_ref.shape
    heads = cols // HD
    root = math.sqrt(HD)
    scale = root * LOG2E
    for b in range(rows // BLK):
        kt_ref[:, b * BLK : (b + 1) * BLK] = k_ref[b * BLK : (b + 1) * BLK, :].T
    over(rows // BLK, lambda b: to_packed_order(b, order_col, grad_ref, g_ref))
    dk_acc[...] = jnp.zeros_like(dk_acc)
    dv_acc[...] = jnp.zeros_like(dv_acc)

    def one_block(i, _):
        base = pl.multiple_of(i * BLK, BLK)
        qs_ref[...] = split_heads(q_ref[pl.ds(base, BLK), :], heads)
        grads = g_ref[pl.ds(base, BLK), :]
        gs_ref[...] = split_heads(grads, heads)
        dqt_ref[...] = jnp.zeros_like(dqt_ref)
        start = jnp.concatenate([start_ref[:, pl.ds(base, BLK)]] * heads, axis=1)
        own = lax.broadcasted_iota(jnp.int32, (1, heads * BLK), 1) % BLK + base
        prod = (grads.astype(jnp.float32) * o_ref[pl.ds(base, BLK), :].astype(jnp.float32)).T
        delta = jnp.concatenate(
            [jnp.sum(prod[h * HD : (h + 1) * HD, :], axis=0, keepdims=True) for h in range(heads)], axis=1
        )
        lse = jnp.concatenate([lse_ref[h : h + 1, pl.ds(base, BLK)] for h in range(heads)], axis=1)

        def step(j, causal):
            at = pl.multiple_of(j * BLK, BLK)
            scores = dot_abt(k_ref[pl.ds(at, BLK), :], qs_ref[...])
            dprobs = dot_abt(v_ref[pl.ds(at, BLK), :], gs_ref[...])
            place = lax.broadcasted_iota(jnp.int32, scores.shape, 0) + at
            keep = place >= start
            if causal:
                keep = keep & (place <= own)
            probs = jnp.where(keep, jnp.exp2(scores * scale - lse), 0.0)
            dsc = (probs * (dprobs - delta)).astype(jnp.bfloat16)
            dv_acc[pl.ds(at, BLK), :] += dot_ab(probs.astype(jnp.bfloat16), gs_ref[...])
            dk_acc[pl.ds(at, BLK), :] += dot_ab(dsc, qs_ref[...])
            for h in range(heads):
                dqt_ref[h * HD : (h + 1) * HD, :] += dot_ab(
                    kt_ref[h * HD : (h + 1) * HD, pl.ds(at, BLK)], dsc[:, h * BLK : (h + 1) * BLK]
                )

        lax.fori_loop(low_ref[i], i, lambda j, c: (step(j, False), c)[1], 0)
        step(i, True)
        packed[pl.ds(base, BLK), 0:cols] = (dqt_ref[...].T * root).astype(packed.dtype)
        return 0

    lax.fori_loop(0, rows // BLK, one_block, 0)
    packed[:, cols : 2 * cols] = (dk_acc[...] * root).astype(packed.dtype)
    packed[:, 2 * cols : 3 * cols] = dv_acc[...].astype(packed.dtype)
    over(rows // BLK, lambda b: to_token_order(b, order_row, packed, plain_ref))


def attn_bwd(low, start, order_row, order_col, lse, q, k, v, o, g):
    rows, cols = q.shape
    heads = cols // HD
    return pl.pallas_call(
        attn_bwd_body,
        out_shape=jax.ShapeDtypeStruct((rows, 3 * cols), jnp.bfloat16),
        in_specs=[pl.BlockSpec(memory_space=pltpu.SMEM)] + [vmem()] * 9,
        out_specs=vmem(),
        scratch_shapes=[
            pltpu.VMEM((cols, rows), jnp.bfloat16),
            pltpu.VMEM((heads * BLK, cols), jnp.bfloat16),
            pltpu.VMEM((heads * BLK, cols), jnp.bfloat16),
            pltpu.VMEM((cols, BLK), jnp.float32),
            pltpu.VMEM((rows, cols), jnp.float32),
            pltpu.VMEM((rows, cols), jnp.float32),
            pltpu.VMEM((rows, cols), jnp.bfloat16),
            pltpu.VMEM((rows, 3 * cols), jnp.bfloat16),
        ],
        compiler_params=pltpu.CompilerParams(vmem_limit_bytes=VMEM_LIMIT),
        cost_estimate=pl.CostEstimate(flops=10 * rows * rows * cols, bytes_accessed=16 * rows * cols, transcendentals=rows * rows * heads),
        name="attn_bwd",
    )(low, start, order_row, order_col, lse, q, k, v, o, g)


MESH_ID = pl.DeviceIdType.MESH
EPS = 1e-06
TILE = 256
STRIP = 64


def flip1(index):
    return index + 1 - 2 * lax.rem(index, 2)


def flip2(index):
    return index + 2 - 4 * (index // 2)


def tile_at(index, size):
    return pl.ds(pl.multiple_of(index * size, size), size)


def row_sum(value):
    return jnp.sum(value, axis=-1, keepdims=True)


def middle_body(
    att_ref, wo_hbm, w_hbm, tok_hbm, cot_hbm, aa_ref, am_ref, su_ref, sg_ref,
    out_ref, datt_ref, gw_hbm, gwo_hbm, dh1_ref, gaa_ref, gam_ref, gsu_ref, gsg_ref,
    wo, wall, tok, cot, parts, mids, dbms, mid_t, dbm_t, ups, gates, mixed,
    middle, branch, dh2, own_part, send_a, recv_a, send_d, recv_d, send_z, recv_z,
    gw, gwo, dparts, load_sems, store_sems, hop_send, hop_recv, a2a_send, a2a_recv, d2a_send, d2a_recv, part_send, part_recv,
):
    d = lax.axis_index("dp")
    t = lax.axis_index("tensor")
    rows, width = tok.shape
    heads_w = att_ref.shape[1]
    hid = wall.shape[2]
    nq = w_hbm.shape[0]
    qrows = w_hbm.shape[2]
    chunks = hop_send.shape[0] // 6
    crow = rows // chunks
    core_peer = (flip1(d), t)
    z_peer = (d, flip1(t))
    line = [t, flip1(t), flip2(t), 3 - t]

    barrier = pltpu.get_barrier_semaphore()
    for peer in [core_peer] + [(d, line[k]) for k in (1, 2, 3)]:
        pl.semaphore_signal(barrier, inc=1, device_id=peer, device_id_type=MESH_ID)
    pl.semaphore_wait(barrier, 4)

    def remote(src, dst, ssem, rsem, peer):
        return pltpu.make_async_remote_copy(
            src_ref=src, dst_ref=dst, send_sem=ssem, recv_sem=rsem, device_id=peer, device_id_type=MESH_ID
        )

    a2a = [
        remote(att_ref.at[tile_at(line[k], rows), :], parts.at[k - 1], a2a_send.at[k - 1], a2a_recv.at[k - 1], (d, line[k]))
        for k in (1, 2, 3)
    ]
    for copy in a2a:
        copy.start()
    loads = [
        pltpu.make_async_copy(wo_hbm, wo, load_sems.at[0]),
        pltpu.make_async_copy(tok_hbm, tok, load_sems.at[1]),
        pltpu.make_async_copy(cot_hbm, cot, load_sems.at[2]),
    ]
    wloads = [
        [
            pltpu.make_async_copy(w_hbm.at[q, m], wall.at[m, pl.ds(q * qrows, qrows), :], load_sems.at[3 + m * nq + q])
            for q in range(nq)
        ]
        for m in range(3)
    ]
    for copy in loads + wloads[0] + wloads[1] + wloads[2]:
        copy.start()

    gsu_ref[...] = jnp.zeros_like(gsu_ref)
    gsg_ref[...] = jnp.zeros_like(gsg_ref)
    gam_ref[...] = jnp.zeros_like(gam_ref)
    gaa_ref[...] = jnp.zeros_like(gaa_ref)

    loads[0].wait()
    for copy in a2a:
        copy.wait_recv()

    def project(n):
        cols = tile_at(n, TILE)
        total = dot_abt(att_ref[tile_at(t, rows), :], wo[cols, tile_at(t, heads_w)])
        for k in (1, 2, 3):
            total += dot_abt(parts[k - 1], wo[cols, tile_at(line[k], heads_w)])
        branch[:, cols] = total

    over(width // TILE, project)
    loads[1].wait()

    def hop(buf, phase, ch, kind):
        part = pl.ds(ch * crow, crow)
        index = (phase * chunks + ch) * 3 + kind
        src, dst, peer = ((0, 2, z_peer), (0, 1, core_peer), (2, 3, core_peer))[kind]
        return remote(buf.at[src, part, :], buf.at[dst, part, :], hop_send.at[index], hop_recv.at[index], peer)

    def strips(ch, body):
        over(crow // STRIP, lambda i: body(tile_at(i + ch * (crow // STRIP), STRIP)))

    def unit_of(value):
        factor = lax.rsqrt(row_sum(value * value) + EPS)
        return value * factor, factor

    def make_middle(at):
        inputs = tok[at, :].astype(jnp.float32)
        norm_a, factor_a = unit_of(branch[at, :])
        mid, factor_mid = unit_of(inputs + aa_ref[...] * (norm_a - inputs))
        return inputs, norm_a, factor_a, mid, factor_mid

    def first(at):
        mid = make_middle(at)[3]
        middle[at, :] = mid
        mids[0, at, :] = mid.astype(jnp.bfloat16)

    for ch in range(chunks):
        strips(ch, first)
        hop(mids, 0, ch, 0).start()
        hop(mids, 0, ch, 1).start()

    for m in range(3):
        for copy in wloads[m]:
            copy.wait()

    def forward_rows(slot, at, store, ready):
        base = slot * rows

        def hidden(n):
            cols = tile_at(n, TILE)
            x = mids[slot, at, :]
            up = dot_ab(x, wall[0, :, cols])
            gate_raw = dot_ab(x, wall[1, :, cols])
            gate = gate_raw * sg_ref[:, cols]
            silu = gate / (1.0 + jnp.exp(-gate))
            where = pl.ds(base + at.start, at.size)
            ups[where, cols] = up.astype(jnp.bfloat16)
            gates[where, cols] = gate_raw.astype(jnp.bfloat16)
            mixed[where, cols] = (up * su_ref[:, cols] * silu).astype(jnp.bfloat16)

        over(hid // TILE, hidden)
        ready()

        def down(n):
            cols = tile_at(n, TILE)
            store(at, cols, dot_abt(mixed[pl.ds(base + at.start, at.size), :], wall[2, cols, :]))

        over(width // TILE, down)

    def backward_rows(slot, at, store, ready):
        base = slot * rows
        where = pl.ds(base + at.start, at.size)

        def hidden(n):
            cols = tile_at(n, TILE)
            dmix = dot_ab(dbms[slot, at, :], wall[2, :, cols])
            up_raw = ups[where, cols].astype(jnp.float32)
            gate_raw = gates[where, cols].astype(jnp.float32)
            gate = gate_raw * sg_ref[:, cols]
            sig = 1.0 / (1.0 + jnp.exp(-gate))
            d_up = dmix * (gate * sig)
            d_gate = dmix * (up_raw * su_ref[:, cols]) * (sig * (1.0 + gate * (1.0 - sig)))
            gsu_ref[:, cols] += jnp.sum(d_up * up_raw, axis=0, keepdims=True)
            gsg_ref[:, cols] += jnp.sum(d_gate * gate_raw, axis=0, keepdims=True)
            ups[where, cols] = (d_up * su_ref[:, cols]).astype(jnp.bfloat16)
            gates[where, cols] = (d_gate * sg_ref[:, cols]).astype(jnp.bfloat16)

        over(hid // TILE, hidden)
        ready()

        def down(n):
            cols = tile_at(n, TILE)
            store(at, cols, dot_abt(ups[where, :], wall[0, cols, :]) + dot_abt(gates[where, :], wall[1, cols, :]))

        over(width // TILE, down)

    def part_copy(phase, kind, ch):
        part = pl.ds(ch * crow, crow)
        index = (phase * 3 + kind) * chunks + ch
        src, dst, peer = ((send_a, recv_a, core_peer), (send_d, recv_d, core_peer), (send_z, recv_z, z_peer))[kind]
        return remote(src.at[part, :], dst.at[part, :], part_send.at[index], part_recv.at[index], peer)

    everything = pl.ds(0, rows)

    def nothing():
        pass

    def tensor_pass(phase, buf, rows_fn, fillers):
        def keep_own(at, cols, value):
            own_part[at, cols] = value

        def to(ref):
            def store(at, cols, value):
                ref[at, cols] = value.astype(jnp.bfloat16)

            return store

        def to_z(at, cols, value):
            send_z[at, cols] = (value + recv_d[at, cols].astype(jnp.float32)).astype(jnp.bfloat16)

        rows_fn(0, everything, keep_own, nothing)
        for ch in range(chunks):
            hop(buf, phase, ch, 1).wait_recv()
        if phase == 1:
            for ch in range(chunks):
                part_copy(0, 0, ch).wait_send()
        rows_fn(1, everything, to(send_a), nothing)
        for ch in range(chunks):
            part_copy(phase, 0, ch).start()
        fillers[0]()
        for ch in range(chunks):
            hop(buf, phase, ch, 0).wait_recv()
            hop(buf, phase, ch, 2).start()
            at = pl.ds(ch * crow, crow)
            hop(buf, phase, ch, 2).wait_recv()
            if phase == 1:
                part_copy(0, 1, ch).wait_send()
            rows_fn(3, at, to(send_d), nothing)
            part_copy(phase, 1, ch).start()

            def ready():
                part_copy(phase, 1, ch).wait_recv()
                if phase == 1:
                    part_copy(0, 2, ch).wait_send()

            rows_fn(2, at, to_z, ready)
            part_copy(phase, 2, ch).start()
        fillers[1]()

    def transpose_into(dst, buf, slots):
        for slot in slots:
            for b in range(rows // 128):
                for n in range(width // TILE):
                    dst[n * TILE : (n + 1) * TILE, slot * rows + b * 128 : slot * rows + (b + 1) * 128] = buf[
                        slot, b * 128 : (b + 1) * 128, n * TILE : (n + 1) * TILE
                    ].T

    tensor_pass(
        0, mids, forward_rows,
        [lambda: transpose_into(mid_t, mids, (0, 1)), lambda: transpose_into(mid_t, mids, (2, 3))],
    )

    loads[2].wait()

    def turn(at):
        mid = middle[at, :]
        branch_m = own_part[at, :] + recv_a[at, :].astype(jnp.float32) + recv_z[at, :].astype(jnp.float32)
        norm_m, factor_m = unit_of(branch_m)
        alpha = am_ref[...]
        y, factor_y = unit_of(mid + alpha * (norm_m - mid))
        out_ref[at, :] = y.astype(jnp.bfloat16)
        dy = cot[at, :].astype(jnp.float32)
        grad = factor_y * (dy - y * row_sum(y * dy))
        gam_ref[...] += jnp.sum(grad * (norm_m - mid), axis=0, keepdims=True)
        back = alpha * grad
        dbms[0, at, :] = (factor_m * (back - norm_m * row_sum(norm_m * back))).astype(jnp.bfloat16)
        dh2[at, :] = grad - back

    for ch in range(chunks):
        part_copy(0, 0, ch).wait_recv()
        part_copy(0, 2, ch).wait_recv()
        strips(ch, turn)
        hop(dbms, 1, ch, 0).start()
        hop(dbms, 1, ch, 1).start()

    def weight_grads():
        transpose_into(dbm_t, dbms, (2, 3))
        for m, (lhs, rhs) in enumerate(((mid_t, ups), (mid_t, gates), (dbm_t, mixed))):

            def block(i):
                q = i // (hid // TILE)
                cols = tile_at(lax.rem(i, hid // TILE), TILE)
                value = dot_ab(lhs[tile_at(q, TILE), :], rhs[:, cols])
                gw[m, tile_at(q, TILE), cols] = value.astype(jnp.bfloat16)

            over((width // TILE) * (hid // TILE), block)
            for q in range(nq):
                grad_store(m, q).start()

    def grad_store(m, q):
        return pltpu.make_async_copy(gw.at[m, pl.ds(q * qrows, qrows), :], gw_hbm.at[q, m], store_sems.at[m * nq + q])

    tensor_pass(1, dbms, backward_rows, [lambda: transpose_into(dbm_t, dbms, (0, 1)), weight_grads])

    def last(at):
        inputs, norm_a, factor_a, mid, factor_mid = make_middle(at)
        grad_mid = dh2[at, :] + own_part[at, :] + recv_a[at, :].astype(jnp.float32) + recv_z[at, :].astype(jnp.float32)
        grad = factor_mid * (grad_mid - mid * row_sum(mid * grad_mid))
        gaa_ref[...] += jnp.sum(grad * (norm_a - inputs), axis=0, keepdims=True)
        back = aa_ref[...] * grad
        dh1_ref[at, :] = grad - back
        mids[0, at, :] = (factor_a * (back - norm_a * row_sum(norm_a * back))).astype(jnp.bfloat16)

    for ch in range(chunks):
        hop(mids, 0, ch, 0).wait_send()
        hop(mids, 0, ch, 1).wait_send()
        part_copy(1, 0, ch).wait_recv()
        part_copy(1, 2, ch).wait_recv()
        strips(ch, last)

    dback = [
        remote(dparts.at[k], datt_ref.at[tile_at(t, rows), :], d2a_send.at[k - 1], d2a_recv.at[k - 1], (d, line[k]))
        for k in (1, 2, 3)
    ]
    for k in (3, 2, 1, 0):
        value = dot_ab(mids[0], wo[:, tile_at(line[k], heads_w)]).astype(jnp.bfloat16)
        if k:
            dparts[k] = value
            dback[k - 1].start()
        else:
            datt_ref[tile_at(t, rows), :] = value

    for b in range(rows // 128):
        for n in range(width // TILE):
            mid_t[n * TILE : (n + 1) * TILE, b * 128 : (b + 1) * 128] = mids[
                0, b * 128 : (b + 1) * 128, n * TILE : (n + 1) * TILE
            ].T

    def out_grad(n):
        at = tile_at(n, TILE)
        lhs = mid_t[at, 0:rows]
        gwo[at, tile_at(t, heads_w)] = dot_ab(lhs, att_ref[tile_at(t, rows), :]).astype(jnp.bfloat16)
        for k in (1, 2, 3):
            gwo[at, tile_at(line[k], heads_w)] = dot_ab(lhs, parts[k - 1]).astype(jnp.bfloat16)

    over(width // TILE, out_grad)
    wo_store = pltpu.make_async_copy(gwo, gwo_hbm, store_sems.at[3 * nq])
    wo_store.start()

    for k in (1, 2, 3):
        remote(
            dparts.at[k], datt_ref.at[tile_at(line[k], rows), :], d2a_send.at[k - 1], d2a_recv.at[k - 1], (d, line[k])
        ).wait()
    for copy in a2a:
        copy.wait_send()
    for ch in range(chunks):
        hop(mids, 0, ch, 2).wait_send()
        for kind in range(3):
            hop(dbms, 1, ch, kind).wait_send()
            part_copy(1, kind, ch).wait_send()
    for m in range(3):
        for q in range(nq):
            grad_store(m, q).wait()
    wo_store.wait()


def middle_call(chunks, attended, wo, w_parts, tokens, cotangent, alpha_a, alpha_m, su, sg):
    rows, width = tokens.shape
    group, heads_w = attended.shape
    nq, _, qrows, hid = w_parts.shape
    bf, f32 = jnp.bfloat16, jnp.float32
    anywhere = pl.BlockSpec(memory_space=pl.ANY)
    dma = pltpu.SemaphoreType.DMA
    return pl.pallas_call(
        middle_body,
        out_shape=(
            jax.ShapeDtypeStruct((rows, width), bf),
            jax.ShapeDtypeStruct((group, heads_w), bf),
            jax.ShapeDtypeStruct((nq, 3, qrows, hid), bf),
            jax.ShapeDtypeStruct((width, width), bf),
            jax.ShapeDtypeStruct((rows, width), f32),
            jax.ShapeDtypeStruct((1, width), f32),
            jax.ShapeDtypeStruct((1, width), f32),
            jax.ShapeDtypeStruct((1, hid), f32),
            jax.ShapeDtypeStruct((1, hid), f32),
        ),
        in_specs=[vmem(), anywhere, anywhere, anywhere, anywhere] + [vmem()] * 4,
        out_specs=(vmem(), vmem(), anywhere, anywhere) + (vmem(),) * 5,
        scratch_shapes=[
            pltpu.VMEM((width, width), bf),
            pltpu.VMEM((3, width, hid), bf),
            pltpu.VMEM((rows, width), bf),
            pltpu.VMEM((rows, width), bf),
            pltpu.VMEM((3, rows, heads_w), bf),
            pltpu.VMEM((4, rows, width), bf),
            pltpu.VMEM((4, rows, width), bf),
            pltpu.VMEM((width, 4 * rows), bf),
            pltpu.VMEM((width, 4 * rows), bf),
            pltpu.VMEM((4 * rows, hid), bf),
            pltpu.VMEM((4 * rows, hid), bf),
            pltpu.VMEM((4 * rows, hid), bf),
            pltpu.VMEM((rows, width), f32),
            pltpu.VMEM((rows, width), f32),
            pltpu.VMEM((rows, width), f32),
            pltpu.VMEM((rows, width), f32),
        ]
        + [pltpu.VMEM((rows, width), bf)] * 6
        + [
            pltpu.VMEM((3, width, hid), bf),
            pltpu.VMEM((width, width), bf),
            pltpu.VMEM((4, rows, heads_w), bf),
            dma((3 + 3 * nq,)),
            dma((3 * nq + 1,)),
            dma((6 * chunks,)),
            dma((6 * chunks,)),
            dma((3,)),
            dma((3,)),
            dma((3,)),
            dma((3,)),
            dma((6 * chunks,)),
            dma((6 * chunks,)),
        ],
        compiler_params=pltpu.CompilerParams(vmem_limit_bytes=67000000, collective_id=1, has_side_effects=True),
        cost_estimate=pl.CostEstimate(flops=10**11, bytes_accessed=10**8, transcendentals=10**6),
        name="middle",
    )(attended, wo, w_parts, tokens, cotangent, alpha_a, alpha_m, su, sg)


def remote_copy(src, dst, send_sem, recv_sem, peer):
    return pltpu.make_async_remote_copy(
        src_ref=src, dst_ref=dst, send_sem=send_sem, recv_sem=recv_sem, device_id=peer, device_id_type=MESH_ID
    )


def greet(peers):
    barrier = pltpu.get_barrier_semaphore()
    for peer in peers:
        pl.semaphore_signal(barrier, inc=1, device_id=peer, device_id_type=MESH_ID)
    pl.semaphore_wait(barrier, len(peers))


def spread_body(
    count, tok, w_up, w_gate, w_down, wq, wk, wv, wo, pair, tok2, wqkv, wo_all,
    own_mlp, own_att, wo_rows, load_sem, keep_sem, a_send, a_recv, b_send, b_recv, tok_send, tok_recv,
    qkv_send, qkv_recv, oz_send, oz_recv, oq_send, oq_recv, oc_send, oc_recv,
):
    d = lax.axis_index("dp")
    t = lax.axis_index("tensor")
    core = lax.rem(d, 2)
    home = core == t // 2
    far = (d - core + t // 2, flip2(t))
    wrows, wcols = wq.shape
    half = count // 2
    mlp = (w_up, w_gate, w_down)
    att = (wq, wk, wv)
    mine = tile_at(d, wrows)
    side = tile_at(core, wrows)
    other_side = tile_at(1 - core, wrows)

    barrier = pltpu.get_barrier_semaphore()

    def dp_peer(i):
        return lax.rem(d + 1 + i, count)

    def hello(i):
        pl.semaphore_signal(barrier, inc=1, device_id=(dp_peer(i), t), device_id_type=MESH_ID)

    over(count - 1, hello)
    for k in (1, 2, 3):
        pl.semaphore_signal(barrier, inc=1, device_id=(d, lax.rem(t + k, 4)), device_id_type=MESH_ID)
    pl.semaphore_signal(barrier, inc=1, device_id=(flip1(d), flip2(t)), device_id_type=MESH_ID)
    pl.semaphore_wait(barrier, count + 3)

    def b_copy(m):
        return remote_copy(mlp[m], pair.at[m, side, :], b_send.at[m], b_recv.at[core * 3 + m], far)

    def a_copy(m):
        return remote_copy(mlp[m], pair.at[m, side, :], a_send.at[m], a_recv.at[m], (flip1(d), t))

    tok_copy = remote_copy(tok, tok2, tok_send, tok_recv, (d, flip1(t)))
    for m in range(3):
        b_copy(m).start()
    tok_copy.start()

    def oz_copy(k):
        return remote_copy(wo, wo_rows.at[:, tile_at(t, wcols)], oz_send.at[k - 1], oz_recv.at[k - 1], (d, lax.rem(t + k, 4)))

    for k in (1, 2, 3):
        oz_copy(k).start()
    load_o = pltpu.make_async_copy(wo, wo_rows.at[:, tile_at(t, wcols)], load_sem.at[0])
    load_o.start()

    def qkv_copy(i, m):
        return remote_copy(
            att[m], wqkv.at[mine, pl.ds(m * wcols, wcols)], qkv_send.at[i, m], qkv_recv.at[i, m], (dp_peer(i), t)
        )

    def qkv_start(i):
        for m in range(3):
            qkv_copy(i, m).start()

    over(count - 1, qkv_start)

    @pl.when(jnp.logical_not(home))
    def _():
        for m in range(3):
            a_copy(m).start()

    loads = [pltpu.make_async_copy(mlp[m], own_mlp.at[m], load_sem.at[1 + m]) for m in range(3)]
    loads += [pltpu.make_async_copy(att[m], own_att.at[m], load_sem.at[4 + m]) for m in range(3)]
    for copy in loads:
        copy.start()
    for copy in loads:
        copy.wait()
    keeps = [
        pltpu.make_async_copy(own_att.at[m], wqkv.at[mine, pl.ds(m * wcols, wcols)], keep_sem.at[m]) for m in range(3)
    ]
    for copy in keeps:
        copy.start()
    pair_keeps = [pltpu.make_async_copy(own_mlp.at[m], pair.at[m, side, :], keep_sem.at[3 + m]) for m in range(3)]

    @pl.when(home)
    def _():
        for copy in pair_keeps:
            copy.start()

    load_o.wait()
    for k in (1, 2, 3):
        oz_copy(k).wait_recv()
    keep_o = pltpu.make_async_copy(wo_rows, wo_all.at[mine, :], keep_sem.at[6])
    keep_o.start()

    def oq_copy(j):
        return remote_copy(wo_rows, wo_all.at[mine, :], oq_send.at[j], oq_recv.at[j], (lax.rem(d + 2 + 2 * j, count), t))

    def oc_own():
        return remote_copy(wo_rows, wo_all.at[mine, :], oc_send.at[half - 1], oc_recv.at[half - 1], (flip1(d), t))

    def oc_copy(j):
        rows = tile_at(lax.rem(d + count - 2 - 2 * j, count), wrows)
        return remote_copy(wo_all.at[rows, :], wo_all.at[rows, :], oc_send.at[j], oc_recv.at[j], (flip1(d), t))

    over(half - 1, lambda j: oq_copy(j).start())
    oc_own().start()

    def oq_next(j):
        oq_copy(j).wait_recv()
        oc_copy(j).start()

    over(half - 1, oq_next)

    def qkv_wait(i):
        for m in range(3):
            qkv_copy(i, m).wait()

    over(count - 1, qkv_wait)
    over(half - 1, lambda j: oq_copy(j).wait_send())
    over(half - 1, lambda j: oc_copy(j).wait())
    oc_own().wait()
    for k in (1, 2, 3):
        oz_copy(k).wait_send()
    keep_o.wait()
    for copy in keeps:
        copy.wait()
    tok_copy.wait()
    for m in range(3):
        b_copy(m).wait_send()

    @pl.when(home)
    def _():
        for m in range(3):
            pair_keeps[m].wait()
            remote_copy(mlp[m], pair.at[m, other_side, :], a_send.at[m], a_recv.at[m], (flip1(d), t)).wait_recv()

    @pl.when(jnp.logical_not(home))
    def _():
        for m in range(3):
            a_copy(m).wait_send()
            for c in range(2):
                remote_copy(
                    mlp[m], pair.at[m, pl.ds(c * wrows, wrows), :], b_send.at[m], b_recv.at[c * 3 + m], far
                ).wait_recv()


def spread_call(count, tokens, w_up, w_gate, w_down, wq, wk, wv, wo):
    rows, width = tokens.shape
    wrows, wcols = wq.shape
    hid = w_up.shape[1]
    bf = jnp.bfloat16
    anywhere = pl.BlockSpec(memory_space=pl.ANY)
    dma = pltpu.SemaphoreType.DMA
    return pl.pallas_call(
        functools.partial(spread_body, count),
        out_shape=(
            jax.ShapeDtypeStruct((3, 2 * wrows, hid), bf),
            jax.ShapeDtypeStruct((rows, width), bf),
            jax.ShapeDtypeStruct((width, 3 * wcols), bf),
            jax.ShapeDtypeStruct((width, width), bf),
        ),
        in_specs=[anywhere] * 8,
        out_specs=(anywhere,) * 4,
        scratch_shapes=[
            pltpu.VMEM((3, wrows, hid), bf),
            pltpu.VMEM((3, wrows, wcols), bf),
            pltpu.VMEM((wrows, width), bf),
            dma((7,)), dma((7,)), dma((3,)), dma((3,)), dma((3,)), dma((6,)), dma, dma,
            dma((count - 1, 3)), dma((count - 1, 3)), dma((3,)), dma((3,)),
            dma((count // 2,)), dma((count // 2,)), dma((count // 2,)), dma((count // 2,)),
        ],
        compiler_params=pltpu.CompilerParams(vmem_limit_bytes=VMEM_LIMIT, collective_id=2, has_side_effects=True),
        name="spread",
    )(tokens, w_up, w_gate, w_down, wq, wk, wv, wo)


def head_sums(value):
    width = value.shape[1]
    same = (
        lax.broadcasted_iota(jnp.int32, (width, width), 0) // HD == lax.broadcasted_iota(jnp.int32, (width, width), 1) // HD
    )
    ones = jnp.where(same, 1.0, 0.0).astype(jnp.bfloat16)
    high = value.astype(jnp.bfloat16)
    low = (value - high.astype(jnp.float32)).astype(jnp.bfloat16)
    return dot_ab(high, ones) + dot_ab(low, ones)


def swap_halves(value):
    width = value.shape[1]
    lane = lax.broadcasted_iota(jnp.int32, value.shape, 1) % HD
    return jnp.where(lane < HD // 2, pltpu.roll(value, width - HD // 2, 1), pltpu.roll(value, HD // 2, 1))


def project_body(
    tok, tok2, wqkv, cos_ref, sin_ref, order_col, gain_ref, q_ref, k_ref, v_ref, raw_ref, x_hbm,
    xs, plain, load_sem, keep_sem, mid_send, recv, on_send,
):
    t = lax.axis_index("tensor")
    d = lax.axis_index("dp")
    _, rows, width = xs.shape
    group, cols = q_ref.shape
    near = flip1(t)
    across = 3 - t
    inner = (t + 1) // 2 == 1
    arrive = (2 - t // 2, 3 - 3 * (t // 2))
    part = rows // 2
    greet([(d, near), (d, across)])

    def mid_copy(k):
        src = (tok, tok2)[k // 2].at[pl.ds((k % 2) * part, part), :]
        dst = xs.at[(t, near)[k // 2], pl.ds((k % 2) * part, part), :]
        return remote_copy(src, dst, mid_send.at[k], recv.at[k], (d, across))

    def on_copy(k):
        ref = xs.at[arrive[k // 2], pl.ds((k % 2) * part, part), :]
        return remote_copy(ref, ref, on_send.at[k], recv.at[k], (d, near))

    @pl.when(inner)
    def _():
        for k in range(4):
            mid_copy(k).start()

    loads = [
        pltpu.make_async_copy(tok, xs.at[t], load_sem.at[0]),
        pltpu.make_async_copy(tok2, xs.at[near], load_sem.at[1]),
    ]
    for copy in loads:
        copy.start()

    def keep(index, slot):
        return pltpu.make_async_copy(xs.at[slot], x_hbm.at[tile_at(slot, rows), :], keep_sem.at[index])

    def work(index, slot):
        keep(index, slot).start()
        at = tile_at(slot, rows)
        x = xs[slot]
        cos = jnp.concatenate([cos_ref[at, :]] * (cols // cos_ref.shape[1]), axis=1)
        sin = jnp.concatenate([sin_ref[at, :]] * (cols // sin_ref.shape[1]), axis=1)
        for m in range(2):
            raw = dot_ab(x, wqkv[:, m * cols : (m + 1) * cols])
            raw_ref[at, m * cols : (m + 1) * cols] = raw.astype(jnp.bfloat16)
            normed = raw * lax.rsqrt(head_sums(raw * raw) + EPS) * gain_ref[...]
            plain[at, m * cols : (m + 1) * cols] = (normed * cos + swap_halves(normed) * sin).astype(jnp.bfloat16)
        plain[at, 2 * cols : 3 * cols] = dot_ab(x, wqkv[:, 2 * cols : 3 * cols]).astype(jnp.bfloat16)

    loads[0].wait()
    work(0, t)
    loads[1].wait()
    work(1, near)
    for k in range(4):
        slot = arrive[k // 2]
        ref = xs.at[slot, pl.ds((k % 2) * part, part), :]
        remote_copy(ref, ref, on_send.at[k], recv.at[k], (d, near)).wait_recv()

        @pl.when(inner)
        def _():
            on_copy(k).start()

        if k % 2:
            work(2 + k // 2, slot)

    def permute(b):
        at = tile_at(b, BLK)
        hot = (lax.broadcasted_iota(jnp.int32, (BLK, group), 1) == order_col[at, :]).astype(jnp.float32)
        value = dot_ab(hot.astype(jnp.bfloat16), plain[...])
        for m, ref in enumerate((q_ref, k_ref, v_ref)):
            ref[at, :] = value[:, m * cols : (m + 1) * cols].astype(jnp.bfloat16)

    over(group // BLK, permute)
    for index, slot in enumerate((t, near, *arrive)):
        keep(index, slot).wait()

    @pl.when(inner)
    def _():
        for k in range(4):
            mid_copy(k).wait_send()
            on_copy(k).wait_send()


def project_call(tokens, tok2, wqkv, cos, sin, order_col, gains):
    rows, width = tokens.shape
    group = order_col.shape[0]
    cols = wqkv.shape[1] // 3
    bf = jnp.bfloat16
    anywhere = pl.BlockSpec(memory_space=pl.ANY)
    dma = pltpu.SemaphoreType.DMA
    return pl.pallas_call(
        project_body,
        out_shape=(jax.ShapeDtypeStruct((group, cols), bf),) * 3
        + (jax.ShapeDtypeStruct((group, 2 * cols), bf), jax.ShapeDtypeStruct((group, width), bf)),
        in_specs=[anywhere, anywhere] + [vmem()] * 5,
        out_specs=(vmem(),) * 4 + (anywhere,),
        scratch_shapes=[
            pltpu.VMEM((group // rows, rows, width), bf),
            pltpu.VMEM((group, 3 * cols), bf),
            dma((2,)), dma((4,)), dma((4,)), dma((4,)), dma((4,)),
        ],
        compiler_params=pltpu.CompilerParams(vmem_limit_bytes=VMEM_LIMIT, collective_id=3, has_side_effects=True),
        cost_estimate=pl.CostEstimate(flops=6 * 10**10, bytes_accessed=10**7, transcendentals=10**6),
        name="project",
    )(tokens, tok2, wqkv, cos, sin, order_col, gains)


def flat(dp_index, tensor_index, tensor_count):
    return dp_index * tensor_count + tensor_index


def hidden_routes(dp_count, tensor_count):
    near, far = [], []
    for d in range(dp_count):
        for t in range(tensor_count):
            own = flat(d, t, tensor_count)
            if d % 2 != t // 2:
                near.append((own, flat(d ^ 1, t, tensor_count)))
                far.append((own, flat(d ^ 1, t ^ 2, tensor_count)))
            else:
                near.append((own, flat(d, t ^ 2, tensor_count)))
    return near, far


def same_core_groups(dp_count):
    return [list(range(parity, dp_count, 2)) for parity in range(2)]


def scatter_hidden(parts, dp_count, tensor_count):
    near, far = hidden_routes(dp_count, tensor_count)
    axes = ("dp", "tensor")
    core = lax.rem(lax.axis_index("dp"), 2)
    home = core == lax.axis_index("tensor") // 2
    summed = lax.psum_scatter(
        parts, "dp", scatter_dimension=0, tiled=False, axis_index_groups=same_core_groups(dp_count)
    )
    kinds, rows, cols = summed.shape
    halves = summed.reshape(kinds, 2, rows // 2, cols)
    mine = jnp.where(core == 0, halves[:, 0], halves[:, 1])
    other = jnp.where(core == 0, halves[:, 1], halves[:, 0])
    first = lax.ppermute(jnp.where(home, other, mine), axes, [(b, a) for a, b in near])
    second = lax.ppermute(other, axes, [(b, a) for a, b in far])
    f32 = jnp.float32
    return jnp.where(home, mine.astype(f32), second.astype(f32)) + first.astype(f32)


def matmul_abt(first_op, second_op):
    return dot_abt(first_op, second_op)


def matmul_atb(first_op, second_op):
    return lax.dot_general(
        first_op, second_op, (((0,), (0,)), ((), ())), preferred_element_type=jnp.float32
    )


def unit_pair(matrix):
    factor = lax.rsqrt(jnp.sum(matrix * matrix, axis=-1, keepdims=True) + 1e-06)
    return (matrix * factor, factor)


def unit_back(normed, factor, grad_out):
    return factor * (grad_out - normed * jnp.sum(normed * grad_out, axis=-1, keepdims=True))


def rotate_back(matrix, angles):
    half_width = matrix.shape[-1] // 2
    cosine = jnp.cos(angles)[:, None, :]
    sine_part = -jnp.sin(angles)[:, None, :]
    lead_half = matrix[..., :half_width]
    tail_half = matrix[..., half_width:]
    return jnp.concatenate(
        [lead_half * cosine - tail_half * sine_part, tail_half * cosine + lead_half * sine_part],
        axis=-1,
    )


def layout(order_row, length_row):
    group_rows = order_row.shape[0]
    places = jnp.arange(group_rows, dtype=jnp.int32)
    seg_ends = jnp.cumsum(length_row, dtype=jnp.int32)
    seg_starts = seg_ends - length_row
    seg_first = jnp.max(
        jnp.where(seg_starts[None, :] <= places[:, None], seg_starts[None, :], 0), axis=1
    )
    half_width = HD // 2
    inv_freq = jnp.exp(
        jnp.arange(half_width, dtype=jnp.float32) * (-math.log(10000.0) / half_width)
    )
    depth = jnp.sum(
        jnp.where(order_row[None, :] == places[:, None], (places - seg_first)[None, :], 0), axis=1, dtype=jnp.int32
    )
    angles = depth.astype(jnp.float32)[:, None] * inv_freq[None, :]
    return (seg_first, angles)


def on_device(
    tokens,
    w_query,
    w_key,
    w_value,
    w_out_t,
    w_up,
    w_gate,
    w_down_t,
    scale_qk,
    alpha_attn,
    scale_up,
    scale_gate,
    alpha_mlp,
    order,
    lengths,
    cotangent,
):
    tensor_rank = lax.axis_index("tensor")
    head_cols = w_query.shape[1]
    hidden_cols = w_up.shape[1]
    local_heads = head_cols // HD
    qk_gains = lax.dynamic_slice_in_dim(scale_qk, tensor_rank * head_cols, head_cols)
    dp_count, tensor_count = lax.axis_size("dp"), lax.axis_size("tensor")
    hidden_rank = lax.rem(tensor_rank, 2) + 2 * lax.rem(lax.axis_index("dp"), 2)
    up_gains = lax.dynamic_slice_in_dim(scale_up, hidden_rank * hidden_cols, hidden_cols)[None, :]
    gate_gains = lax.dynamic_slice_in_dim(
        scale_gate, hidden_rank * hidden_cols, hidden_cols
    )[None, :] * math.sqrt(D)
    order_row = order[0]
    seg_first, angles = layout(order_row, lengths[0])
    group_rows = order_row.shape[0]
    low = lax.slice(seg_first, (0,), (group_rows,), (BLK,)) // BLK
    start = seg_first[None, :]
    order_col = order_row[:, None]
    cosine, sine = jnp.cos(angles), jnp.sin(angles)
    cos_table = jnp.concatenate([cosine] * 4, axis=1)
    sin_table = jnp.concatenate([-sine, sine] * 2, axis=1)

    pair, near_tokens, wqkv, wo_every = spread_call(
        dp_count, tokens, w_up, w_gate, w_down_t, w_query, w_key, w_value, w_out_t
    )
    mlp_parts = lax.all_gather(
        pair, "dp", axis=0, tiled=False, axis_index_groups=same_core_groups(dp_count)
    )
    queries, key_rows, value_rows, raw, all_tokens = project_call(
        tokens, near_tokens, wqkv, cos_table, sin_table, order_col, qk_gains[None, :]
    )
    attended, log_totals, attended_plain = attn_fwd(low, start, order, queries, key_rows, value_rows)
    out_rows, grad_att_rows, mlp_grads, wo_grads, grad_h1_kept, grad_alpha_a, grad_alpha_m, grad_su, grad_sv = middle_call(
        2,
        attended_plain,
        wo_every,
        mlp_parts,
        tokens,
        cotangent,
        alpha_attn[None, :],
        alpha_mlp[None, :],
        up_gains,
        gate_gains,
    )
    grad_qkv = attn_bwd(
        low, start, order, order_col, log_totals, queries, key_rows, value_rows, attended, grad_att_rows
    )
    gains = qk_gains.reshape(local_heads, HD)
    parts = []
    grad_gain = 0.0
    for m in range(2):
        cols = slice(m * head_cols, (m + 1) * head_cols)
        normed, factor = unit_pair(raw[:, cols].astype(jnp.float32).reshape(group_rows, local_heads, HD))
        grad = rotate_back(grad_qkv[:, cols].astype(jnp.float32).reshape(group_rows, local_heads, HD), angles)
        grad_gain = grad_gain + jnp.sum(grad * normed, axis=0).reshape(head_cols)
        parts.append(unit_back(normed, factor, grad * gains).astype(jnp.bfloat16).reshape(group_rows, head_cols))
    grad_raw = jnp.concatenate(parts + [grad_qkv[:, 2 * head_cols :]], axis=1)
    attn_part = lax.psum_scatter(
        matmul_abt(grad_raw, wqkv).astype(jnp.bfloat16), "tensor", scatter_dimension=0, tiled=True
    ).astype(jnp.float32)
    grad_tokens = grad_h1_kept + attn_part
    grad_qk_full = lax.dynamic_update_slice_in_dim(
        jnp.zeros(scale_qk.shape, jnp.float32), grad_gain, tensor_rank * head_cols, 0
    )
    grad_su_full = lax.dynamic_update_slice_in_dim(
        jnp.zeros(scale_up.shape, jnp.float32), grad_su[0], hidden_rank * hidden_cols, 0
    )
    grad_sv_full = lax.dynamic_update_slice_in_dim(
        jnp.zeros(scale_gate.shape, jnp.float32), grad_sv[0] * math.sqrt(D), hidden_rank * hidden_cols, 0
    )
    vector_sums = lax.psum(
        (grad_qk_full, grad_alpha_a[0], grad_su_full, grad_sv_full, grad_alpha_m[0]), ("dp", "tensor")
    )
    mlp_sums = scatter_hidden(mlp_grads, dp_count, tensor_count)
    attn_sums = lax.psum_scatter(
        matmul_atb(all_tokens, grad_raw).astype(jnp.bfloat16), "dp", scatter_dimension=0, tiled=True
    ).astype(jnp.float32)
    wo_sums = lax.psum_scatter(
        lax.psum_scatter(wo_grads, "dp", scatter_dimension=0, tiled=True), "tensor", scatter_dimension=1, tiled=True
    ).astype(jnp.float32)
    weight_sums = [attn_sums[:, i * head_cols : (i + 1) * head_cols] for i in range(3)] + [wo_sums, *mlp_sums]
    return (
        out_rows,
        grad_tokens,
        weight_sums[0],
        weight_sums[1],
        weight_sums[2],
        weight_sums[3],
        weight_sums[4],
        weight_sums[5],
        weight_sums[6],
        vector_sums[0],
        vector_sums[1],
        vector_sums[2],
        vector_sums[3],
        vector_sums[4],
    )


def solution(mesh):
    return jax.shard_map(
        on_device,
        mesh=mesh,
        in_specs=(
            P(("dp", "tensor"), None),
            P("dp", "tensor"),
            P("dp", "tensor"),
            P("dp", "tensor"),
            P("dp", "tensor"),
            P("dp", "tensor"),
            P("dp", "tensor"),
            P("dp", "tensor"),
            P(),
            P(),
            P(),
            P(),
            P(),
            P("dp", None),
            P("dp", None),
            P(("dp", "tensor"), None),
        ),
        out_specs=(
            P(("dp", "tensor"), None),
            P(("dp", "tensor"), None),
            P("dp", "tensor"),
            P("dp", "tensor"),
            P("dp", "tensor"),
            P("dp", "tensor"),
            P("dp", "tensor"),
            P("dp", "tensor"),
            P("dp", "tensor"),
            P(),
            P(),
            P(),
            P(),
            P(),
        ),
        check_vma=False,
    )
```

```python
import functools
import math

import jax
import jax.numpy as jnp
from jax import lax
from jax.experimental import pallas as pl
from jax.experimental.pallas import tpu as pltpu
from jax.sharding import PartitionSpec as P

D = 1024
HD = 64
BLK = 256
LOG2E = 1.4426950408889634
VMEM_LIMIT = 60 * 1024 * 1024


def dot_ab(a, b):
    return lax.dot_general(a, b, (((1,), (0,)), ((), ())), preferred_element_type=jnp.float32)


def dot_abt(a, b):
    return lax.dot_general(a, b, (((1,), (1,)), ((), ())), preferred_element_type=jnp.float32)


def split_heads(block, heads):
    lane_head = lax.broadcasted_iota(jnp.int32, block.shape, 1) // HD
    zero = jnp.zeros_like(block)
    return jnp.concatenate([jnp.where(lane_head == h, block, zero) for h in range(heads)], axis=0)


def attn_fwd_body(
    low_ref, start_ref, order_row, q_ref, k_ref, v_ref, out_ref, lse_ref, plain_ref, vt_ref, qs_ref, acc_ref, sum_ref
):
    rows, cols = q_ref.shape
    heads = cols // HD
    scale = math.sqrt(HD) * LOG2E
    for b in range(rows // BLK):
        vt_ref[:, b * BLK : (b + 1) * BLK] = v_ref[b * BLK : (b + 1) * BLK, :].T

    def one_block(i, _):
        base = pl.multiple_of(i * BLK, BLK)
        qs_ref[...] = split_heads(q_ref[pl.ds(base, BLK), :], heads)
        acc_ref[...] = jnp.zeros_like(acc_ref)
        sum_ref[...] = jnp.zeros_like(sum_ref)
        start = jnp.concatenate([start_ref[:, pl.ds(base, BLK)]] * heads, axis=1)
        own = lax.broadcasted_iota(jnp.int32, (1, heads * BLK), 1) % BLK + base

        def step(j, causal):
            at = pl.multiple_of(j * BLK, BLK)
            scores = dot_abt(k_ref[pl.ds(at, BLK), :], qs_ref[...])
            place = lax.broadcasted_iota(jnp.int32, scores.shape, 0) + at
            keep = place >= start
            if causal:
                keep = keep & (place <= own)
            probs = jnp.where(keep, jnp.exp2(scores * scale), 0.0)
            sum_ref[...] += jnp.sum(probs, axis=0, keepdims=True)
            probs_b = probs.astype(jnp.bfloat16)
            for h in range(heads):
                acc_ref[h * HD : (h + 1) * HD, :] += dot_ab(
                    vt_ref[h * HD : (h + 1) * HD, pl.ds(at, BLK)], probs_b[:, h * BLK : (h + 1) * BLK]
                )

        lax.fori_loop(low_ref[i], i, lambda j, c: (step(j, False), c)[1], 0)
        step(i, True)
        total = sum_ref[...]
        inv = 1.0 / total
        logs = jnp.log2(total)
        for h in range(heads):
            lse_ref[h : h + 1, pl.ds(base, BLK)] = logs[:, h * BLK : (h + 1) * BLK]
            acc_ref[h * HD : (h + 1) * HD, :] *= inv[:, h * BLK : (h + 1) * BLK]
        out_ref[pl.ds(base, BLK), :] = acc_ref[...].T.astype(jnp.bfloat16)
        return 0

    lax.fori_loop(0, rows // BLK, one_block, 0)
    over(rows // BLK, lambda b: to_token_order(b, order_row, out_ref, plain_ref))


def to_token_order(b, order_row, src, dst):
    at = pl.ds(pl.multiple_of(b * BLK, BLK), BLK)
    hot = lax.broadcasted_iota(jnp.int32, (BLK, src.shape[0]), 0) + b * BLK == order_row[...]
    dst[at, :] = dot_ab(hot.astype(jnp.float32).astype(jnp.bfloat16), src[...]).astype(dst.dtype)


def to_packed_order(b, order_col, src, dst):
    at = pl.ds(pl.multiple_of(b * BLK, BLK), BLK)
    hot = lax.broadcasted_iota(jnp.int32, (BLK, src.shape[0]), 1) == order_col[at, :]
    dst[at, :] = dot_ab(hot.astype(jnp.float32).astype(jnp.bfloat16), src[...]).astype(dst.dtype)


def over(count, body):
    lax.fori_loop(0, count, lambda i, carry: (body(i), carry)[1], 0)


def vmem():
    return pl.BlockSpec(memory_space=pltpu.VMEM)


def attn_fwd(low, start, order_row, q, k, v):
    rows, cols = q.shape
    heads = cols // HD
    return pl.pallas_call(
        attn_fwd_body,
        out_shape=(
            jax.ShapeDtypeStruct((rows, cols), jnp.bfloat16),
            jax.ShapeDtypeStruct((8, rows), jnp.float32),
            jax.ShapeDtypeStruct((rows, cols), jnp.bfloat16),
        ),
        in_specs=[pl.BlockSpec(memory_space=pltpu.SMEM)] + [vmem()] * 5,
        out_specs=(vmem(),) * 3,
        scratch_shapes=[
            pltpu.VMEM((cols, rows), jnp.bfloat16),
            pltpu.VMEM((heads * BLK, cols), jnp.bfloat16),
            pltpu.VMEM((cols, BLK), jnp.float32),
            pltpu.VMEM((1, heads * BLK), jnp.float32),
        ],
        compiler_params=pltpu.CompilerParams(vmem_limit_bytes=VMEM_LIMIT),
        cost_estimate=pl.CostEstimate(flops=4 * rows * rows * cols, bytes_accessed=8 * rows * cols, transcendentals=rows * rows * heads),
        name="attn_fwd",
    )(low, start, order_row, q, k, v)


def attn_bwd_body(
    low_ref, start_ref, order_row, order_col, lse_ref, q_ref, k_ref, v_ref, o_ref, grad_ref,
    plain_ref, kt_ref, qs_ref, gs_ref, dqt_ref, dk_acc, dv_acc, g_ref, packed,
):
    rows, cols = q_ref.shape
    heads = cols // HD
    root = math.sqrt(HD)
    scale = root * LOG2E
    for b in range(rows // BLK):
        kt_ref[:, b * BLK : (b + 1) * BLK] = k_ref[b * BLK : (b + 1) * BLK, :].T
    over(rows // BLK, lambda b: to_packed_order(b, order_col, grad_ref, g_ref))
    dk_acc[...] = jnp.zeros_like(dk_acc)
    dv_acc[...] = jnp.zeros_like(dv_acc)

    def one_block(i, _):
        base = pl.multiple_of(i * BLK, BLK)
        qs_ref[...] = split_heads(q_ref[pl.ds(base, BLK), :], heads)
        grads = g_ref[pl.ds(base, BLK), :]
        gs_ref[...] = split_heads(grads, heads)
        dqt_ref[...] = jnp.zeros_like(dqt_ref)
        start = jnp.concatenate([start_ref[:, pl.ds(base, BLK)]] * heads, axis=1)
        own = lax.broadcasted_iota(jnp.int32, (1, heads * BLK), 1) % BLK + base
        prod = (grads.astype(jnp.float32) * o_ref[pl.ds(base, BLK), :].astype(jnp.float32)).T
        delta = jnp.concatenate(
            [jnp.sum(prod[h * HD : (h + 1) * HD, :], axis=0, keepdims=True) for h in range(heads)], axis=1
        )
        lse = jnp.concatenate([lse_ref[h : h + 1, pl.ds(base, BLK)] for h in range(heads)], axis=1)

        def step(j, causal):
            at = pl.multiple_of(j * BLK, BLK)
            scores = dot_abt(k_ref[pl.ds(at, BLK), :], qs_ref[...])
            dprobs = dot_abt(v_ref[pl.ds(at, BLK), :], gs_ref[...])
            place = lax.broadcasted_iota(jnp.int32, scores.shape, 0) + at
            keep = place >= start
            if causal:
                keep = keep & (place <= own)
            probs = jnp.where(keep, jnp.exp2(scores * scale - lse), 0.0)
            dsc = (probs * (dprobs - delta)).astype(jnp.bfloat16)
            dv_acc[pl.ds(at, BLK), :] += dot_ab(probs.astype(jnp.bfloat16), gs_ref[...])
            dk_acc[pl.ds(at, BLK), :] += dot_ab(dsc, qs_ref[...])
            for h in range(heads):
                dqt_ref[h * HD : (h + 1) * HD, :] += dot_ab(
                    kt_ref[h * HD : (h + 1) * HD, pl.ds(at, BLK)], dsc[:, h * BLK : (h + 1) * BLK]
                )

        lax.fori_loop(low_ref[i], i, lambda j, c: (step(j, False), c)[1], 0)
        step(i, True)
        packed[pl.ds(base, BLK), 0:cols] = (dqt_ref[...].T * root).astype(packed.dtype)
        return 0

    lax.fori_loop(0, rows // BLK, one_block, 0)
    packed[:, cols : 2 * cols] = (dk_acc[...] * root).astype(packed.dtype)
    packed[:, 2 * cols : 3 * cols] = dv_acc[...].astype(packed.dtype)
    over(rows // BLK, lambda b: to_token_order(b, order_row, packed, plain_ref))


def attn_bwd(low, start, order_row, order_col, lse, q, k, v, o, g):
    rows, cols = q.shape
    heads = cols // HD
    return pl.pallas_call(
        attn_bwd_body,
        out_shape=jax.ShapeDtypeStruct((rows, 3 * cols), jnp.bfloat16),
        in_specs=[pl.BlockSpec(memory_space=pltpu.SMEM)] + [vmem()] * 9,
        out_specs=vmem(),
        scratch_shapes=[
            pltpu.VMEM((cols, rows), jnp.bfloat16),
            pltpu.VMEM((heads * BLK, cols), jnp.bfloat16),
            pltpu.VMEM((heads * BLK, cols), jnp.bfloat16),
            pltpu.VMEM((cols, BLK), jnp.float32),
            pltpu.VMEM((rows, cols), jnp.float32),
            pltpu.VMEM((rows, cols), jnp.float32),
            pltpu.VMEM((rows, cols), jnp.bfloat16),
            pltpu.VMEM((rows, 3 * cols), jnp.bfloat16),
        ],
        compiler_params=pltpu.CompilerParams(vmem_limit_bytes=VMEM_LIMIT),
        cost_estimate=pl.CostEstimate(flops=10 * rows * rows * cols, bytes_accessed=16 * rows * cols, transcendentals=rows * rows * heads),
        name="attn_bwd",
    )(low, start, order_row, order_col, lse, q, k, v, o, g)


MESH_ID = pl.DeviceIdType.MESH
EPS = 1e-06
TILE = 256
STRIP = 64


def flip1(index):
    return index + 1 - 2 * lax.rem(index, 2)


def flip2(index):
    return index + 2 - 4 * (index // 2)


def tile_at(index, size):
    return pl.ds(pl.multiple_of(index * size, size), size)


def row_sum(value):
    return jnp.sum(value, axis=-1, keepdims=True)


def middle_body(
    att_ref, wo_hbm, w_hbm, tok_hbm, cot_hbm, aa_ref, am_ref, su_ref, sg_ref,
    out_ref, datt_ref, gw_hbm, gwo_hbm, dh1_ref, gaa_ref, gam_ref, gsu_ref, gsg_ref,
    wo, wall, tok, cot, parts, mids, dbms, mid_t, dbm_t, ups, gates, mixed,
    middle, branch, dh2, own_part, send_a, recv_a, send_d, recv_d, send_z, recv_z,
    gw, gwo, dparts, load_sems, store_sems, hop_send, hop_recv, a2a_send, a2a_recv, d2a_send, d2a_recv, part_send, part_recv,
):
    d = lax.axis_index("dp")
    t = lax.axis_index("tensor")
    rows, width = tok.shape
    heads_w = att_ref.shape[1]
    hid = wall.shape[2]
    nq = w_hbm.shape[0]
    qrows = w_hbm.shape[2]
    chunks = hop_send.shape[0] // 6
    crow = rows // chunks
    core_peer = (flip1(d), t)
    z_peer = (d, flip1(t))
    line = [t, flip1(t), flip2(t), 3 - t]

    barrier = pltpu.get_barrier_semaphore()
    for peer in [core_peer] + [(d, line[k]) for k in (1, 2, 3)]:
        pl.semaphore_signal(barrier, inc=1, device_id=peer, device_id_type=MESH_ID)
    pl.semaphore_wait(barrier, 4)

    def remote(src, dst, ssem, rsem, peer):
        return pltpu.make_async_remote_copy(
            src_ref=src, dst_ref=dst, send_sem=ssem, recv_sem=rsem, device_id=peer, device_id_type=MESH_ID
        )

    a2a = [
        remote(att_ref.at[tile_at(line[k], rows), :], parts.at[k - 1], a2a_send.at[k - 1], a2a_recv.at[k - 1], (d, line[k]))
        for k in (1, 2, 3)
    ]
    for copy in a2a:
        copy.start()
    loads = [
        pltpu.make_async_copy(wo_hbm, wo, load_sems.at[0]),
        pltpu.make_async_copy(tok_hbm, tok, load_sems.at[1]),
        pltpu.make_async_copy(cot_hbm, cot, load_sems.at[2]),
    ]
    wloads = [
        [
            pltpu.make_async_copy(w_hbm.at[q, m], wall.at[m, pl.ds(q * qrows, qrows), :], load_sems.at[3 + m * nq + q])
            for q in range(nq)
        ]
        for m in range(3)
    ]
    for copy in loads + wloads[0] + wloads[1] + wloads[2]:
        copy.start()

    gsu_ref[...] = jnp.zeros_like(gsu_ref)
    gsg_ref[...] = jnp.zeros_like(gsg_ref)
    gam_ref[...] = jnp.zeros_like(gam_ref)
    gaa_ref[...] = jnp.zeros_like(gaa_ref)

    loads[0].wait()
    for copy in a2a:
        copy.wait_recv()

    def project(n):
        cols = tile_at(n, TILE)
        total = dot_abt(att_ref[tile_at(t, rows), :], wo[cols, tile_at(t, heads_w)])
        for k in (1, 2, 3):
            total += dot_abt(parts[k - 1], wo[cols, tile_at(line[k], heads_w)])
        branch[:, cols] = total

    over(width // TILE, project)
    loads[1].wait()

    def hop(buf, phase, ch, kind):
        part = pl.ds(ch * crow, crow)
        index = (phase * chunks + ch) * 3 + kind
        src, dst, peer = ((0, 2, z_peer), (0, 1, core_peer), (2, 3, core_peer))[kind]
        return remote(buf.at[src, part, :], buf.at[dst, part, :], hop_send.at[index], hop_recv.at[index], peer)

    def strips(ch, body):
        over(crow // STRIP, lambda i: body(tile_at(i + ch * (crow // STRIP), STRIP)))

    def unit_of(value):
        factor = lax.rsqrt(row_sum(value * value) + EPS)
        return value * factor, factor

    def make_middle(at):
        inputs = tok[at, :].astype(jnp.float32)
        norm_a, factor_a = unit_of(branch[at, :])
        mid, factor_mid = unit_of(inputs + aa_ref[...] * (norm_a - inputs))
        return inputs, norm_a, factor_a, mid, factor_mid

    def first(at):
        mid = make_middle(at)[3]
        middle[at, :] = mid
        mids[0, at, :] = mid.astype(jnp.bfloat16)

    for ch in range(chunks):
        strips(ch, first)
        hop(mids, 0, ch, 0).start()
        hop(mids, 0, ch, 1).start()

    for m in range(3):
        for copy in wloads[m]:
            copy.wait()

    def forward_rows(slot, at, store, ready):
        base = slot * rows

        def hidden(n):
            cols = tile_at(n, TILE)
            x = mids[slot, at, :]
            up = dot_ab(x, wall[0, :, cols])
            gate_raw = dot_ab(x, wall[1, :, cols])
            gate = gate_raw * sg_ref[:, cols]
            silu = gate / (1.0 + jnp.exp(-gate))
            where = pl.ds(base + at.start, at.size)
            ups[where, cols] = up.astype(jnp.bfloat16)
            gates[where, cols] = gate_raw.astype(jnp.bfloat16)
            mixed[where, cols] = (up * su_ref[:, cols] * silu).astype(jnp.bfloat16)

        over(hid // TILE, hidden)
        ready()

        def down(n):
            cols = tile_at(n, TILE)
            store(at, cols, dot_abt(mixed[pl.ds(base + at.start, at.size), :], wall[2, cols, :]))

        over(width // TILE, down)

    def backward_rows(slot, at, store, ready):
        base = slot * rows
        where = pl.ds(base + at.start, at.size)

        def hidden(n):
            cols = tile_at(n, TILE)
            dmix = dot_ab(dbms[slot, at, :], wall[2, :, cols])
            up_raw = ups[where, cols].astype(jnp.float32)
            gate_raw = gates[where, cols].astype(jnp.float32)
            gate = gate_raw * sg_ref[:, cols]
            sig = 1.0 / (1.0 + jnp.exp(-gate))
            d_up = dmix * (gate * sig)
            d_gate = dmix * (up_raw * su_ref[:, cols]) * (sig * (1.0 + gate * (1.0 - sig)))
            gsu_ref[:, cols] += jnp.sum(d_up * up_raw, axis=0, keepdims=True)
            gsg_ref[:, cols] += jnp.sum(d_gate * gate_raw, axis=0, keepdims=True)
            ups[where, cols] = (d_up * su_ref[:, cols]).astype(jnp.bfloat16)
            gates[where, cols] = (d_gate * sg_ref[:, cols]).astype(jnp.bfloat16)

        over(hid // TILE, hidden)
        ready()

        def down(n):
            cols = tile_at(n, TILE)
            store(at, cols, dot_abt(ups[where, :], wall[0, cols, :]) + dot_abt(gates[where, :], wall[1, cols, :]))

        over(width // TILE, down)

    def part_copy(phase, kind, ch):
        part = pl.ds(ch * crow, crow)
        index = (phase * 3 + kind) * chunks + ch
        src, dst, peer = ((send_a, recv_a, core_peer), (send_d, recv_d, core_peer), (send_z, recv_z, z_peer))[kind]
        return remote(src.at[part, :], dst.at[part, :], part_send.at[index], part_recv.at[index], peer)

    everything = pl.ds(0, rows)

    def nothing():
        pass

    def tensor_pass(phase, buf, rows_fn, fillers):
        def keep_own(at, cols, value):
            own_part[at, cols] = value

        def to(ref):
            def store(at, cols, value):
                ref[at, cols] = value.astype(jnp.bfloat16)

            return store

        def to_z(at, cols, value):
            send_z[at, cols] = (value + recv_d[at, cols].astype(jnp.float32)).astype(jnp.bfloat16)

        rows_fn(0, everything, keep_own, nothing)
        for ch in range(chunks):
            hop(buf, phase, ch, 1).wait_recv()
        if phase == 1:
            for ch in range(chunks):
                part_copy(0, 0, ch).wait_send()
        rows_fn(1, everything, to(send_a), nothing)
        for ch in range(chunks):
            part_copy(phase, 0, ch).start()
        fillers[0]()
        for ch in range(chunks):
            hop(buf, phase, ch, 0).wait_recv()
            hop(buf, phase, ch, 2).start()
            at = pl.ds(ch * crow, crow)
            hop(buf, phase, ch, 2).wait_recv()
            if phase == 1:
                part_copy(0, 1, ch).wait_send()
            rows_fn(3, at, to(send_d), nothing)
            part_copy(phase, 1, ch).start()

            def ready():
                part_copy(phase, 1, ch).wait_recv()
                if phase == 1:
                    part_copy(0, 2, ch).wait_send()

            rows_fn(2, at, to_z, ready)
            part_copy(phase, 2, ch).start()
        fillers[1]()

    def transpose_into(dst, buf, slots):
        for slot in slots:
            for b in range(rows // 128):
                for n in range(width // TILE):
                    dst[n * TILE : (n + 1) * TILE, slot * rows + b * 128 : slot * rows + (b + 1) * 128] = buf[
                        slot, b * 128 : (b + 1) * 128, n * TILE : (n + 1) * TILE
                    ].T

    tensor_pass(
        0, mids, forward_rows,
        [lambda: transpose_into(mid_t, mids, (0, 1)), lambda: transpose_into(mid_t, mids, (2, 3))],
    )

    loads[2].wait()

    def turn(at):
        mid = middle[at, :]
        branch_m = own_part[at, :] + recv_a[at, :].astype(jnp.float32) + recv_z[at, :].astype(jnp.float32)
        norm_m, factor_m = unit_of(branch_m)
        alpha = am_ref[...]
        y, factor_y = unit_of(mid + alpha * (norm_m - mid))
        out_ref[at, :] = y.astype(jnp.bfloat16)
        dy = cot[at, :].astype(jnp.float32)
        grad = factor_y * (dy - y * row_sum(y * dy))
        gam_ref[...] += jnp.sum(grad * (norm_m - mid), axis=0, keepdims=True)
        back = alpha * grad
        dbms[0, at, :] = (factor_m * (back - norm_m * row_sum(norm_m * back))).astype(jnp.bfloat16)
        dh2[at, :] = grad - back

    for ch in range(chunks):
        part_copy(0, 0, ch).wait_recv()
        part_copy(0, 2, ch).wait_recv()
        strips(ch, turn)
        hop(dbms, 1, ch, 0).start()
        hop(dbms, 1, ch, 1).start()

    def weight_grads():
        transpose_into(dbm_t, dbms, (2, 3))
        for m, (lhs, rhs) in enumerate(((mid_t, ups), (mid_t, gates), (dbm_t, mixed))):

            def block(i):
                q = i // (hid // TILE)
                cols = tile_at(lax.rem(i, hid // TILE), TILE)
                value = dot_ab(lhs[tile_at(q, TILE), :], rhs[:, cols])
                gw[m, tile_at(q, TILE), cols] = value.astype(jnp.bfloat16)

            over((width // TILE) * (hid // TILE), block)
            for q in range(nq):
                grad_store(m, q).start()

    def grad_store(m, q):
        return pltpu.make_async_copy(gw.at[m, pl.ds(q * qrows, qrows), :], gw_hbm.at[q, m], store_sems.at[m * nq + q])

    tensor_pass(1, dbms, backward_rows, [lambda: transpose_into(dbm_t, dbms, (0, 1)), weight_grads])

    def last(at):
        inputs, norm_a, factor_a, mid, factor_mid = make_middle(at)
        grad_mid = dh2[at, :] + own_part[at, :] + recv_a[at, :].astype(jnp.float32) + recv_z[at, :].astype(jnp.float32)
        grad = factor_mid * (grad_mid - mid * row_sum(mid * grad_mid))
        gaa_ref[...] += jnp.sum(grad * (norm_a - inputs), axis=0, keepdims=True)
        back = aa_ref[...] * grad
        dh1_ref[at, :] = grad - back
        mids[0, at, :] = (factor_a * (back - norm_a * row_sum(norm_a * back))).astype(jnp.bfloat16)

    for ch in range(chunks):
        hop(mids, 0, ch, 0).wait_send()
        hop(mids, 0, ch, 1).wait_send()
        part_copy(1, 0, ch).wait_recv()
        part_copy(1, 2, ch).wait_recv()
        strips(ch, last)

    dback = [
        remote(dparts.at[k], datt_ref.at[tile_at(t, rows), :], d2a_send.at[k - 1], d2a_recv.at[k - 1], (d, line[k]))
        for k in (1, 2, 3)
    ]
    for k in (3, 2, 1, 0):
        value = dot_ab(mids[0], wo[:, tile_at(line[k], heads_w)]).astype(jnp.bfloat16)
        if k:
            dparts[k] = value
            dback[k - 1].start()
        else:
            datt_ref[tile_at(t, rows), :] = value

    for b in range(rows // 128):
        for n in range(width // TILE):
            mid_t[n * TILE : (n + 1) * TILE, b * 128 : (b + 1) * 128] = mids[
                0, b * 128 : (b + 1) * 128, n * TILE : (n + 1) * TILE
            ].T

    def out_grad(n):
        at = tile_at(n, TILE)
        lhs = mid_t[at, 0:rows]
        gwo[at, tile_at(t, heads_w)] = dot_ab(lhs, att_ref[tile_at(t, rows), :]).astype(jnp.bfloat16)
        for k in (1, 2, 3):
            gwo[at, tile_at(line[k], heads_w)] = dot_ab(lhs, parts[k - 1]).astype(jnp.bfloat16)

    over(width // TILE, out_grad)
    wo_store = pltpu.make_async_copy(gwo, gwo_hbm, store_sems.at[3 * nq])
    wo_store.start()

    for k in (1, 2, 3):
        remote(
            dparts.at[k], datt_ref.at[tile_at(line[k], rows), :], d2a_send.at[k - 1], d2a_recv.at[k - 1], (d, line[k])
        ).wait()
    for copy in a2a:
        copy.wait_send()
    for ch in range(chunks):
        hop(mids, 0, ch, 2).wait_send()
        for kind in range(3):
            hop(dbms, 1, ch, kind).wait_send()
            part_copy(1, kind, ch).wait_send()
    for m in range(3):
        for q in range(nq):
            grad_store(m, q).wait()
    wo_store.wait()


def middle_call(chunks, attended, wo, w_parts, tokens, cotangent, alpha_a, alpha_m, su, sg):
    rows, width = tokens.shape
    group, heads_w = attended.shape
    nq, _, qrows, hid = w_parts.shape
    bf, f32 = jnp.bfloat16, jnp.float32
    anywhere = pl.BlockSpec(memory_space=pl.ANY)
    dma = pltpu.SemaphoreType.DMA
    return pl.pallas_call(
        middle_body,
        out_shape=(
            jax.ShapeDtypeStruct((rows, width), bf),
            jax.ShapeDtypeStruct((group, heads_w), bf),
            jax.ShapeDtypeStruct((nq, 3, qrows, hid), bf),
            jax.ShapeDtypeStruct((width, width), bf),
            jax.ShapeDtypeStruct((rows, width), f32),
            jax.ShapeDtypeStruct((1, width), f32),
            jax.ShapeDtypeStruct((1, width), f32),
            jax.ShapeDtypeStruct((1, hid), f32),
            jax.ShapeDtypeStruct((1, hid), f32),
        ),
        in_specs=[vmem(), anywhere, anywhere, anywhere, anywhere] + [vmem()] * 4,
        out_specs=(vmem(), vmem(), anywhere, anywhere) + (vmem(),) * 5,
        scratch_shapes=[
            pltpu.VMEM((width, width), bf),
            pltpu.VMEM((3, width, hid), bf),
            pltpu.VMEM((rows, width), bf),
            pltpu.VMEM((rows, width), bf),
            pltpu.VMEM((3, rows, heads_w), bf),
            pltpu.VMEM((4, rows, width), bf),
            pltpu.VMEM((4, rows, width), bf),
            pltpu.VMEM((width, 4 * rows), bf),
            pltpu.VMEM((width, 4 * rows), bf),
            pltpu.VMEM((4 * rows, hid), bf),
            pltpu.VMEM((4 * rows, hid), bf),
            pltpu.VMEM((4 * rows, hid), bf),
            pltpu.VMEM((rows, width), f32),
            pltpu.VMEM((rows, width), f32),
            pltpu.VMEM((rows, width), f32),
            pltpu.VMEM((rows, width), f32),
        ]
        + [pltpu.VMEM((rows, width), bf)] * 6
        + [
            pltpu.VMEM((3, width, hid), bf),
            pltpu.VMEM((width, width), bf),
            pltpu.VMEM((4, rows, heads_w), bf),
            dma((3 + 3 * nq,)),
            dma((3 * nq + 1,)),
            dma((6 * chunks,)),
            dma((6 * chunks,)),
            dma((3,)),
            dma((3,)),
            dma((3,)),
            dma((3,)),
            dma((6 * chunks,)),
            dma((6 * chunks,)),
        ],
        compiler_params=pltpu.CompilerParams(vmem_limit_bytes=67000000, collective_id=1, has_side_effects=True),
        cost_estimate=pl.CostEstimate(flops=10**11, bytes_accessed=10**8, transcendentals=10**6),
        name="middle",
    )(attended, wo, w_parts, tokens, cotangent, alpha_a, alpha_m, su, sg)


def remote_copy(src, dst, send_sem, recv_sem, peer):
    return pltpu.make_async_remote_copy(
        src_ref=src, dst_ref=dst, send_sem=send_sem, recv_sem=recv_sem, device_id=peer, device_id_type=MESH_ID
    )


def greet(peers):
    barrier = pltpu.get_barrier_semaphore()
    for peer in peers:
        pl.semaphore_signal(barrier, inc=1, device_id=peer, device_id_type=MESH_ID)
    pl.semaphore_wait(barrier, len(peers))


def spread_body(
    count, tok, w_up, w_gate, w_down, wq, wk, wv, wo, pair, tok2, wqkv, wo_all,
    own_mlp, own_att, wo_rows, load_sem, keep_sem, a_send, a_recv, b_send, b_recv, tok_send, tok_recv,
    qkv_send, qkv_recv, oz_send, oz_recv, oq_send, oq_recv, oc_send, oc_recv,
):
    d = lax.axis_index("dp")
    t = lax.axis_index("tensor")
    core = lax.rem(d, 2)
    home = core == t // 2
    far = (d - core + t // 2, flip2(t))
    wrows, wcols = wq.shape
    half = count // 2
    mlp = (w_up, w_gate, w_down)
    att = (wq, wk, wv)
    mine = tile_at(d, wrows)
    side = tile_at(core, wrows)
    other_side = tile_at(1 - core, wrows)

    barrier = pltpu.get_barrier_semaphore()

    def dp_peer(i):
        return lax.rem(d + 1 + i, count)

    def hello(i):
        pl.semaphore_signal(barrier, inc=1, device_id=(dp_peer(i), t), device_id_type=MESH_ID)

    over(count - 1, hello)
    for k in (1, 2, 3):
        pl.semaphore_signal(barrier, inc=1, device_id=(d, lax.rem(t + k, 4)), device_id_type=MESH_ID)
    pl.semaphore_signal(barrier, inc=1, device_id=(flip1(d), flip2(t)), device_id_type=MESH_ID)
    pl.semaphore_wait(barrier, count + 3)

    def b_copy(m):
        return remote_copy(mlp[m], pair.at[m, side, :], b_send.at[m], b_recv.at[core * 3 + m], far)

    def a_copy(m):
        return remote_copy(mlp[m], pair.at[m, side, :], a_send.at[m], a_recv.at[m], (flip1(d), t))

    tok_copy = remote_copy(tok, tok2, tok_send, tok_recv, (d, flip1(t)))
    for m in range(3):
        b_copy(m).start()
    tok_copy.start()

    def oz_copy(k):
        return remote_copy(wo, wo_rows.at[:, tile_at(t, wcols)], oz_send.at[k - 1], oz_recv.at[k - 1], (d, lax.rem(t + k, 4)))

    for k in (1, 2, 3):
        oz_copy(k).start()
    load_o = pltpu.make_async_copy(wo, wo_rows.at[:, tile_at(t, wcols)], load_sem.at[0])
    load_o.start()

    def qkv_copy(i, m):
        return remote_copy(
            att[m], wqkv.at[mine, pl.ds(m * wcols, wcols)], qkv_send.at[i, m], qkv_recv.at[i, m], (dp_peer(i), t)
        )

    def qkv_start(i):
        for m in range(3):
            qkv_copy(i, m).start()

    over(count - 1, qkv_start)

    @pl.when(jnp.logical_not(home))
    def _():
        for m in range(3):
            a_copy(m).start()

    loads = [pltpu.make_async_copy(mlp[m], own_mlp.at[m], load_sem.at[1 + m]) for m in range(3)]
    loads += [pltpu.make_async_copy(att[m], own_att.at[m], load_sem.at[4 + m]) for m in range(3)]
    for copy in loads:
        copy.start()
    for copy in loads:
        copy.wait()
    keeps = [
        pltpu.make_async_copy(own_att.at[m], wqkv.at[mine, pl.ds(m * wcols, wcols)], keep_sem.at[m]) for m in range(3)
    ]
    for copy in keeps:
        copy.start()
    pair_keeps = [pltpu.make_async_copy(own_mlp.at[m], pair.at[m, side, :], keep_sem.at[3 + m]) for m in range(3)]

    @pl.when(home)
    def _():
        for copy in pair_keeps:
            copy.start()

    load_o.wait()
    for k in (1, 2, 3):
        oz_copy(k).wait_recv()
    keep_o = pltpu.make_async_copy(wo_rows, wo_all.at[mine, :], keep_sem.at[6])
    keep_o.start()

    def oq_copy(j):
        return remote_copy(wo_rows, wo_all.at[mine, :], oq_send.at[j], oq_recv.at[j], (lax.rem(d + 2 + 2 * j, count), t))

    def oc_own():
        return remote_copy(wo_rows, wo_all.at[mine, :], oc_send.at[half - 1], oc_recv.at[half - 1], (flip1(d), t))

    def oc_copy(j):
        rows = tile_at(lax.rem(d + count - 2 - 2 * j, count), wrows)
        return remote_copy(wo_all.at[rows, :], wo_all.at[rows, :], oc_send.at[j], oc_recv.at[j], (flip1(d), t))

    over(half - 1, lambda j: oq_copy(j).start())
    oc_own().start()

    def oq_next(j):
        oq_copy(j).wait_recv()
        oc_copy(j).start()

    over(half - 1, oq_next)

    def qkv_wait(i):
        for m in range(3):
            qkv_copy(i, m).wait()

    over(count - 1, qkv_wait)
    over(half - 1, lambda j: oq_copy(j).wait_send())
    over(half - 1, lambda j: oc_copy(j).wait())
    oc_own().wait()
    for k in (1, 2, 3):
        oz_copy(k).wait_send()
    keep_o.wait()
    for copy in keeps:
        copy.wait()
    tok_copy.wait()
    for m in range(3):
        b_copy(m).wait_send()

    @pl.when(home)
    def _():
        for m in range(3):
            pair_keeps[m].wait()
            remote_copy(mlp[m], pair.at[m, other_side, :], a_send.at[m], a_recv.at[m], (flip1(d), t)).wait_recv()

    @pl.when(jnp.logical_not(home))
    def _():
        for m in range(3):
            a_copy(m).wait_send()
            for c in range(2):
                remote_copy(
                    mlp[m], pair.at[m, pl.ds(c * wrows, wrows), :], b_send.at[m], b_recv.at[c * 3 + m], far
                ).wait_recv()


def spread_call(count, tokens, w_up, w_gate, w_down, wq, wk, wv, wo):
    rows, width = tokens.shape
    wrows, wcols = wq.shape
    hid = w_up.shape[1]
    bf = jnp.bfloat16
    anywhere = pl.BlockSpec(memory_space=pl.ANY)
    dma = pltpu.SemaphoreType.DMA
    return pl.pallas_call(
        functools.partial(spread_body, count),
        out_shape=(
            jax.ShapeDtypeStruct((3, 2 * wrows, hid), bf),
            jax.ShapeDtypeStruct((rows, width), bf),
            jax.ShapeDtypeStruct((width, 3 * wcols), bf),
            jax.ShapeDtypeStruct((width, width), bf),
        ),
        in_specs=[anywhere] * 8,
        out_specs=(anywhere,) * 4,
        scratch_shapes=[
            pltpu.VMEM((3, wrows, hid), bf),
            pltpu.VMEM((3, wrows, wcols), bf),
            pltpu.VMEM((wrows, width), bf),
            dma((7,)), dma((7,)), dma((3,)), dma((3,)), dma((3,)), dma((6,)), dma, dma,
            dma((count - 1, 3)), dma((count - 1, 3)), dma((3,)), dma((3,)),
            dma((count // 2,)), dma((count // 2,)), dma((count // 2,)), dma((count // 2,)),
        ],
        compiler_params=pltpu.CompilerParams(vmem_limit_bytes=VMEM_LIMIT, collective_id=2, has_side_effects=True),
        name="spread",
    )(tokens, w_up, w_gate, w_down, wq, wk, wv, wo)


def head_sums(value):
    width = value.shape[1]
    same = (
        lax.broadcasted_iota(jnp.int32, (width, width), 0) // HD == lax.broadcasted_iota(jnp.int32, (width, width), 1) // HD
    )
    ones = jnp.where(same, 1.0, 0.0).astype(jnp.bfloat16)
    high = value.astype(jnp.bfloat16)
    low = (value - high.astype(jnp.float32)).astype(jnp.bfloat16)
    return dot_ab(high, ones) + dot_ab(low, ones)


def swap_halves(value):
    width = value.shape[1]
    lane = lax.broadcasted_iota(jnp.int32, value.shape, 1) % HD
    return jnp.where(lane < HD // 2, pltpu.roll(value, width - HD // 2, 1), pltpu.roll(value, HD // 2, 1))


def project_body(
    tok, tok2, wqkv, cos_ref, sin_ref, order_col, gain_ref, q_ref, k_ref, v_ref, raw_ref, x_hbm,
    xs, plain, load_sem, keep_sem, mid_send, recv, on_send,
):
    t = lax.axis_index("tensor")
    d = lax.axis_index("dp")
    _, rows, width = xs.shape
    group, cols = q_ref.shape
    near = flip1(t)
    across = 3 - t
    inner = (t + 1) // 2 == 1
    arrive = (2 - t // 2, 3 - 3 * (t // 2))
    part = rows // 2
    greet([(d, near), (d, across)])

    def mid_copy(k):
        src = (tok, tok2)[k // 2].at[pl.ds((k % 2) * part, part), :]
        dst = xs.at[(t, near)[k // 2], pl.ds((k % 2) * part, part), :]
        return remote_copy(src, dst, mid_send.at[k], recv.at[k], (d, across))

    def on_copy(k):
        ref = xs.at[arrive[k // 2], pl.ds((k % 2) * part, part), :]
        return remote_copy(ref, ref, on_send.at[k], recv.at[k], (d, near))

    @pl.when(inner)
    def _():
        for k in range(4):
            mid_copy(k).start()

    loads = [
        pltpu.make_async_copy(tok, xs.at[t], load_sem.at[0]),
        pltpu.make_async_copy(tok2, xs.at[near], load_sem.at[1]),
    ]
    for copy in loads:
        copy.start()

    def keep(index, slot):
        return pltpu.make_async_copy(xs.at[slot], x_hbm.at[tile_at(slot, rows), :], keep_sem.at[index])

    def work(index, slot):
        keep(index, slot).start()
        at = tile_at(slot, rows)
        x = xs[slot]
        cos = jnp.concatenate([cos_ref[at, :]] * (cols // cos_ref.shape[1]), axis=1)
        sin = jnp.concatenate([sin_ref[at, :]] * (cols // sin_ref.shape[1]), axis=1)
        for m in range(2):
            raw = dot_ab(x, wqkv[:, m * cols : (m + 1) * cols])
            raw_ref[at, m * cols : (m + 1) * cols] = raw.astype(jnp.bfloat16)
            normed = raw * lax.rsqrt(head_sums(raw * raw) + EPS) * gain_ref[...]
            plain[at, m * cols : (m + 1) * cols] = (normed * cos + swap_halves(normed) * sin).astype(jnp.bfloat16)
        plain[at, 2 * cols : 3 * cols] = dot_ab(x, wqkv[:, 2 * cols : 3 * cols]).astype(jnp.bfloat16)

    loads[0].wait()
    work(0, t)
    loads[1].wait()
    work(1, near)
    for k in range(4):
        slot = arrive[k // 2]
        ref = xs.at[slot, pl.ds((k % 2) * part, part), :]
        remote_copy(ref, ref, on_send.at[k], recv.at[k], (d, near)).wait_recv()

        @pl.when(inner)
        def _():
            on_copy(k).start()

        if k % 2:
            work(2 + k // 2, slot)

    def permute(b):
        at = tile_at(b, BLK)
        hot = (lax.broadcasted_iota(jnp.int32, (BLK, group), 1) == order_col[at, :]).astype(jnp.float32)
        value = dot_ab(hot.astype(jnp.bfloat16), plain[...])
        for m, ref in enumerate((q_ref, k_ref, v_ref)):
            ref[at, :] = value[:, m * cols : (m + 1) * cols].astype(jnp.bfloat16)

    over(group // BLK, permute)
    for index, slot in enumerate((t, near, *arrive)):
        keep(index, slot).wait()

    @pl.when(inner)
    def _():
        for k in range(4):
            mid_copy(k).wait_send()
            on_copy(k).wait_send()


def project_call(tokens, tok2, wqkv, cos, sin, order_col, gains):
    rows, width = tokens.shape
    group = order_col.shape[0]
    cols = wqkv.shape[1] // 3
    bf = jnp.bfloat16
    anywhere = pl.BlockSpec(memory_space=pl.ANY)
    dma = pltpu.SemaphoreType.DMA
    return pl.pallas_call(
        project_body,
        out_shape=(jax.ShapeDtypeStruct((group, cols), bf),) * 3
        + (jax.ShapeDtypeStruct((group, 2 * cols), bf), jax.ShapeDtypeStruct((group, width), bf)),
        in_specs=[anywhere, anywhere] + [vmem()] * 5,
        out_specs=(vmem(),) * 4 + (anywhere,),
        scratch_shapes=[
            pltpu.VMEM((group // rows, rows, width), bf),
            pltpu.VMEM((group, 3 * cols), bf),
            dma((2,)), dma((4,)), dma((4,)), dma((4,)), dma((4,)),
        ],
        compiler_params=pltpu.CompilerParams(vmem_limit_bytes=VMEM_LIMIT, collective_id=3, has_side_effects=True),
        cost_estimate=pl.CostEstimate(flops=6 * 10**10, bytes_accessed=10**7, transcendentals=10**6),
        name="project",
    )(tokens, tok2, wqkv, cos, sin, order_col, gains)


def tail_body(
    count, grad_ref, raw_ref, cos_ref, sin_ref, wqkv, x_hbm, gwo_hbm, kept_ref, gain_ref, gaa_ref, gam_ref, gsu_ref, gsg_ref,
    tok_out, qkv_out, wo_out, gain_out, aa_out, am_out, su_out, sg_out,
    xs, x_t, draw, part_far, part_mid, part_near, own_part, from_a, from_b, from_c, from_d, from_e, from_f,
    gq, got_q, got_w, wo_mid, got_z, vec, got_v, vec_mid, got_s, load_sem,
    hop_send, hop_recv, q_send, q_recv, w_send, w_recv, z_send, z_recv, v_send, v_recv, s_send, s_recv,
):
    d = lax.axis_index("dp")
    t = lax.axis_index("tensor")
    rows, width = tok_out.shape
    group = draw.shape[0]
    cols = draw.shape[1] // 3
    wrows = qkv_out.shape[0]
    near = flip1(t)
    inner = (t + 1) // 2 == 1
    outer = jnp.logical_not(inner)
    far, mid = 3 - 3 * (t // 2), 2 - t // 2
    chunk = rows // 2

    def dp_peer(i):
        return lax.rem(d + 1 + i, count)

    def line_peer(k):
        return lax.rem(t + k, 4)

    barrier = pltpu.get_barrier_semaphore()
    over(
        count - 1,
        lambda i: pl.semaphore_signal(barrier, inc=1, device_id=(dp_peer(i), t), device_id_type=MESH_ID),
    )
    for k in (1, 2, 3):
        pl.semaphore_signal(barrier, inc=1, device_id=(d, line_peer(k)), device_id_type=MESH_ID)
    pl.semaphore_wait(barrier, count + 2)

    def w_copy(i):
        return remote_copy(
            gwo_hbm.at[tile_at(dp_peer(i), wrows), :], got_w.at[d], w_send.at[i], w_recv.at[i], (dp_peer(i), t)
        )

    over(count - 1, lambda i: w_copy(i).start())
    load_w = pltpu.make_async_copy(gwo_hbm.at[tile_at(d, wrows), :], got_w.at[d], load_sem.at[0])
    load_x = pltpu.make_async_copy(x_hbm, xs, load_sem.at[1])
    load_w.start()
    load_x.start()

    def hop(kind, ch):
        src, dst, to = (
            (part_far, from_a, near),
            (part_mid, from_b, near),
            (part_near, from_c, near),
            (part_far, from_d, 3 - t),
            (part_mid, from_e, 3 - t),
            (part_near, from_f, near),
        )[kind]
        part = pl.ds(ch * chunk, chunk)
        return remote_copy(src.at[part, :], dst.at[part, :], hop_send.at[kind, ch], hop_recv.at[kind, ch], (d, to))

    vec[...] = jnp.zeros_like(vec)

    def work(slot, store):
        at = tile_at(slot, rows)
        cos = jnp.concatenate([cos_ref[at, :]] * (cols // cos_ref.shape[1]), axis=1)
        sin = jnp.concatenate([sin_ref[at, :]] * (cols // sin_ref.shape[1]), axis=1)
        gain = gain_ref[...]
        for m in range(2):
            grad = grad_ref[at, m * cols : (m + 1) * cols].astype(jnp.float32)
            raw = raw_ref[at, m * cols : (m + 1) * cols].astype(jnp.float32)
            back = grad * cos - swap_halves(grad) * sin
            factor = lax.rsqrt(head_sums(raw * raw) + EPS)
            normed = raw * factor
            vec[4:5, 0:cols] += jnp.sum(back * normed, axis=0, keepdims=True)
            scaled = back * gain
            draw[at, m * cols : (m + 1) * cols] = (factor * (scaled - normed * head_sums(normed * scaled))).astype(
                jnp.bfloat16
            )
        draw[at, 2 * cols : 3 * cols] = grad_ref[at, 2 * cols : 3 * cols]

        def product(n):
            tile = tile_at(n, TILE)
            store(tile, dot_abt(draw[at, :], wqkv[tile, :]))

        over(width // TILE, product)

    def into(ref):
        def store(tile, value):
            ref[:, tile] = value.astype(ref.dtype)

        return store

    for kind, (slot, ref) in enumerate(((far, part_far), (mid, part_mid), (near, part_near))):
        work(slot, into(ref))

        @pl.when(outer)
        def _():
            for ch in range(2):
                hop(kind, ch).start()

    work(t, into(own_part))

    for row, ref in enumerate((gaa_ref, gam_ref, gsu_ref, gsg_ref)):
        vec[row : row + 1, :] = ref[...]
    got_v[d] = vec[...]

    def v_copy(i):
        return remote_copy(vec, got_v.at[d], v_send.at[i], v_recv.at[i], (dp_peer(i), t))

    over(count - 1, lambda i: v_copy(i).start())

    def pass_on(kind, ch, own, got, then):
        @pl.when(inner)
        def _():
            part = pl.ds(ch * chunk, chunk)
            hop(kind, ch).wait_recv()
            own[part, :] = (own[part, :].astype(jnp.float32) + got[part, :].astype(jnp.float32)).astype(jnp.bfloat16)
            hop(then, ch).start()

    pass_on(0, 0, part_far, from_a, 3)
    pass_on(0, 1, part_far, from_a, 3)

    load_x.wait()

    def flip_block(b):
        at = tile_at(b, 128)
        for n in range(width // TILE):
            x_t[n * TILE : (n + 1) * TILE, at] = xs[at, n * TILE : (n + 1) * TILE].T

    over(group // 128, flip_block)
    pass_on(3, 0, part_near, from_d, 5)

    def weight_grad(n):
        tile = tile_at(n, TILE)
        gq[tile, :] = dot_ab(x_t[tile, :], draw[...]).astype(jnp.bfloat16)

    over(width // TILE, weight_grad)

    def q_copy(i):
        return remote_copy(gq.at[tile_at(dp_peer(i), wrows), :], got_q.at[d], q_send.at[i], q_recv.at[i], (dp_peer(i), t))

    over(count - 1, lambda i: q_copy(i).start())
    got_q[d] = gq[tile_at(d, wrows), :]
    pass_on(1, 0, part_mid, from_b, 4)
    pass_on(3, 1, part_near, from_d, 5)
    pass_on(1, 1, part_mid, from_b, 4)

    load_w.wait()
    over(count - 1, lambda i: w_copy(i).wait_recv())
    wo_mid[...] = lax.fori_loop(
        1, count, lambda i, total: total + got_w[i].astype(jnp.float32), got_w[0].astype(jnp.float32)
    ).astype(jnp.bfloat16)

    def z_copy(k):
        return remote_copy(
            wo_mid.at[:, tile_at(line_peer(k), cols)], got_z.at[t], z_send.at[k - 1], z_recv.at[k - 1], (d, line_peer(k))
        )

    for k in (1, 2, 3):
        z_copy(k).start()
    got_z[t] = wo_mid[:, tile_at(t, cols)]

    over(count - 1, lambda i: v_copy(i).wait_recv())
    even, odd = lax.fori_loop(
        1, count // 2, lambda i, total: (total[0] + got_v[2 * i], total[1] + got_v[2 * i + 1]), (got_v[0], got_v[1])
    )
    both = even + odd
    vec_mid[...] = jnp.concatenate([both[0:2], even[2:3], odd[2:3], even[3:4], odd[3:4], both[4:5], both[4:5]], axis=0)

    def s_copy(k):
        return remote_copy(vec_mid, got_s.at[t], s_send.at[k - 1], s_recv.at[k - 1], (d, line_peer(k)))

    for k in (1, 2, 3):
        s_copy(k).start()
    got_s[t] = vec_mid[...]

    over(count - 1, lambda i: q_copy(i).wait_recv())
    qkv_out[...] = lax.fori_loop(
        1, count, lambda i, total: total + got_q[i].astype(jnp.float32), got_q[0].astype(jnp.float32)
    )

    for k in (1, 2, 3):
        z_copy(k).wait_recv()
        s_copy(k).wait_recv()
    wo_out[...] = (
        got_z[0].astype(jnp.float32)
        + got_z[1].astype(jnp.float32)
        + got_z[2].astype(jnp.float32)
        + got_z[3].astype(jnp.float32)
    )
    shared = got_s[0] + got_s[1] + got_s[2] + got_s[3]
    aa_out[...] = shared[0:1]
    am_out[...] = shared[1:2]
    pairs = (got_s[0] + got_s[2], got_s[1] + got_s[3])
    for s in range(4):
        su_out[s : s + 1, :] = pairs[s % 2][2 + s // 2 : 3 + s // 2]
        sg_out[s : s + 1, :] = pairs[s % 2][4 + s // 2 : 5 + s // 2] * math.sqrt(D)
        gain_out[s : s + 1, :] = got_s[s][6:7, 0:cols]

    for ch in range(2):
        part = pl.ds(ch * chunk, chunk)

        @pl.when(inner)
        def _():
            hop(2, ch).wait_recv()
            hop(4, ch).wait_recv()
            tok_out[part, :] = (
                kept_ref[part, :]
                + own_part[part, :]
                + from_c[part, :].astype(jnp.float32)
                + from_e[part, :].astype(jnp.float32)
            )

        @pl.when(outer)
        def _():
            hop(5, ch).wait_recv()
            tok_out[part, :] = kept_ref[part, :] + own_part[part, :] + from_f[part, :].astype(jnp.float32)

    for ch in range(2):

        @pl.when(inner)
        def _():
            for kind in (3, 4, 5):
                hop(kind, ch).wait_send()

        @pl.when(outer)
        def _():
            for kind in (0, 1, 2):
                hop(kind, ch).wait_send()

    def drain(i):
        w_copy(i).wait_send()
        v_copy(i).wait_send()
        q_copy(i).wait_send()

    over(count - 1, drain)
    for k in (1, 2, 3):
        z_copy(k).wait_send()
        s_copy(k).wait_send()


def tail_call(count, grad_qkv, raw, cos, sin, wqkv, all_tokens, wo_grads, kept, gains, gaa, gam, gsu, gsg):
    rows, width = kept.shape
    group, three = grad_qkv.shape
    cols = three // 3
    wrows = width // count
    bf, f32 = jnp.bfloat16, jnp.float32
    anywhere = pl.BlockSpec(memory_space=pl.ANY)
    dma = pltpu.SemaphoreType.DMA
    shape = jax.ShapeDtypeStruct
    return pl.pallas_call(
        functools.partial(tail_body, count),
        out_shape=(
            shape((rows, width), f32),
            shape((wrows, three), f32),
            shape((wrows, cols), f32),
            shape((4, cols), f32),
            shape((1, width), f32),
            shape((1, width), f32),
            shape((4, width), f32),
            shape((4, width), f32),
        ),
        in_specs=[vmem()] * 5 + [anywhere, anywhere] + [vmem()] * 6,
        out_specs=(vmem(),) * 8,
        scratch_shapes=[
            pltpu.VMEM((group, width), bf),
            pltpu.VMEM((width, group), bf),
            pltpu.VMEM((group, three), bf),
            pltpu.VMEM((rows, width), bf),
            pltpu.VMEM((rows, width), bf),
            pltpu.VMEM((rows, width), bf),
            pltpu.VMEM((rows, width), f32),
        ]
        + [pltpu.VMEM((rows, width), bf)] * 6
        + [
            pltpu.VMEM((width, three), bf),
            pltpu.VMEM((count, wrows, three), bf),
            pltpu.VMEM((count, wrows, width), bf),
            pltpu.VMEM((wrows, width), bf),
            pltpu.VMEM((4, wrows, cols), bf),
            pltpu.VMEM((8, width), f32),
            pltpu.VMEM((count, 8, width), f32),
            pltpu.VMEM((8, width), f32),
            pltpu.VMEM((4, 8, width), f32),
            dma((2,)),
            dma((6, 2)), dma((6, 2)),
            dma((count - 1,)), dma((count - 1,)), dma((count - 1,)), dma((count - 1,)),
            dma((3,)), dma((3,)),
            dma((count - 1,)), dma((count - 1,)),
            dma((3,)), dma((3,)),
        ],
        compiler_params=pltpu.CompilerParams(vmem_limit_bytes=VMEM_LIMIT, collective_id=4, has_side_effects=True),
        cost_estimate=pl.CostEstimate(flops=6 * 10**10, bytes_accessed=10**7, transcendentals=10**6),
        name="tail",
    )(grad_qkv, raw, cos, sin, wqkv, all_tokens, wo_grads, kept, gains, gaa, gam, gsu, gsg)


def flat(dp_index, tensor_index, tensor_count):
    return dp_index * tensor_count + tensor_index


def hidden_routes(dp_count, tensor_count):
    near, far = [], []
    for d in range(dp_count):
        for t in range(tensor_count):
            own = flat(d, t, tensor_count)
            if d % 2 != t // 2:
                near.append((own, flat(d ^ 1, t, tensor_count)))
                far.append((own, flat(d ^ 1, t ^ 2, tensor_count)))
            else:
                near.append((own, flat(d, t ^ 2, tensor_count)))
    return near, far


def same_core_groups(dp_count):
    return [list(range(parity, dp_count, 2)) for parity in range(2)]


def scatter_hidden(parts, dp_count, tensor_count):
    near, far = hidden_routes(dp_count, tensor_count)
    axes = ("dp", "tensor")
    core = lax.rem(lax.axis_index("dp"), 2)
    home = core == lax.axis_index("tensor") // 2
    summed = lax.psum_scatter(
        parts, "dp", scatter_dimension=0, tiled=False, axis_index_groups=same_core_groups(dp_count)
    )
    kinds, rows, cols = summed.shape
    halves = summed.reshape(kinds, 2, rows // 2, cols)
    mine = jnp.where(core == 0, halves[:, 0], halves[:, 1])
    other = jnp.where(core == 0, halves[:, 1], halves[:, 0])
    first = lax.ppermute(jnp.where(home, other, mine), axes, [(b, a) for a, b in near])
    second = lax.ppermute(other, axes, [(b, a) for a, b in far])
    f32 = jnp.float32
    return jnp.where(home, mine.astype(f32), second.astype(f32)) + first.astype(f32)


def layout(order_row, length_row):
    group_rows = order_row.shape[0]
    places = jnp.arange(group_rows, dtype=jnp.int32)
    seg_ends = jnp.cumsum(length_row, dtype=jnp.int32)
    seg_starts = seg_ends - length_row
    seg_first = jnp.max(
        jnp.where(seg_starts[None, :] <= places[:, None], seg_starts[None, :], 0), axis=1
    )
    half_width = HD // 2
    inv_freq = jnp.exp(
        jnp.arange(half_width, dtype=jnp.float32) * (-math.log(10000.0) / half_width)
    )
    depth = jnp.sum(
        jnp.where(order_row[None, :] == places[:, None], (places - seg_first)[None, :], 0), axis=1, dtype=jnp.int32
    )
    angles = depth.astype(jnp.float32)[:, None] * inv_freq[None, :]
    return (seg_first, angles)


def on_device(
    tokens,
    w_query,
    w_key,
    w_value,
    w_out_t,
    w_up,
    w_gate,
    w_down_t,
    scale_qk,
    alpha_attn,
    scale_up,
    scale_gate,
    alpha_mlp,
    order,
    lengths,
    cotangent,
):
    tensor_rank = lax.axis_index("tensor")
    head_cols = w_query.shape[1]
    hidden_cols = w_up.shape[1]
    qk_gains = lax.dynamic_slice_in_dim(scale_qk, tensor_rank * head_cols, head_cols)
    dp_count, tensor_count = lax.axis_size("dp"), lax.axis_size("tensor")
    hidden_rank = lax.rem(tensor_rank, 2) + 2 * lax.rem(lax.axis_index("dp"), 2)
    up_gains = lax.dynamic_slice_in_dim(scale_up, hidden_rank * hidden_cols, hidden_cols)[None, :]
    gate_gains = lax.dynamic_slice_in_dim(
        scale_gate, hidden_rank * hidden_cols, hidden_cols
    )[None, :] * math.sqrt(D)
    order_row = order[0]
    seg_first, angles = layout(order_row, lengths[0])
    group_rows = order_row.shape[0]
    low = lax.slice(seg_first, (0,), (group_rows,), (BLK,)) // BLK
    start = seg_first[None, :]
    order_col = order_row[:, None]
    cosine, sine = jnp.cos(angles), jnp.sin(angles)
    cos_table = jnp.concatenate([cosine] * 4, axis=1)
    sin_table = jnp.concatenate([-sine, sine] * 2, axis=1)

    pair, near_tokens, wqkv, wo_every = spread_call(
        dp_count, tokens, w_up, w_gate, w_down_t, w_query, w_key, w_value, w_out_t
    )
    mlp_parts = lax.all_gather(
        pair, "dp", axis=0, tiled=False, axis_index_groups=same_core_groups(dp_count)
    )
    queries, key_rows, value_rows, raw, all_tokens = project_call(
        tokens, near_tokens, wqkv, cos_table, sin_table, order_col, qk_gains[None, :]
    )
    attended, log_totals, attended_plain = attn_fwd(low, start, order, queries, key_rows, value_rows)
    out_rows, grad_att_rows, mlp_grads, wo_grads, grad_h1_kept, grad_alpha_a, grad_alpha_m, grad_su, grad_sv = middle_call(
        2,
        attended_plain,
        wo_every,
        mlp_parts,
        tokens,
        cotangent,
        alpha_attn[None, :],
        alpha_mlp[None, :],
        up_gains,
        gate_gains,
    )
    grad_qkv = attn_bwd(
        low, start, order, order_col, log_totals, queries, key_rows, value_rows, attended, grad_att_rows
    )
    grad_tokens, qkv_sums, wo_sums, grad_gain, sum_aa, sum_am, sum_su, sum_sv = tail_call(
        dp_count,
        grad_qkv,
        raw,
        cos_table,
        sin_table,
        wqkv,
        all_tokens,
        wo_grads,
        grad_h1_kept,
        qk_gains[None, :],
        grad_alpha_a,
        grad_alpha_m,
        grad_su,
        grad_sv,
    )
    mlp_sums = scatter_hidden(mlp_grads, dp_count, tensor_count)
    weight_sums = [qkv_sums[:, i * head_cols : (i + 1) * head_cols] for i in range(3)] + [wo_sums, *mlp_sums]
    return (
        out_rows,
        grad_tokens,
        weight_sums[0],
        weight_sums[1],
        weight_sums[2],
        weight_sums[3],
        weight_sums[4],
        weight_sums[5],
        weight_sums[6],
        grad_gain.reshape(-1),
        sum_aa.reshape(-1),
        sum_su.reshape(-1),
        sum_sv.reshape(-1),
        sum_am.reshape(-1),
    )


def solution(mesh):
    return jax.shard_map(
        on_device,
        mesh=mesh,
        in_specs=(
            P(("dp", "tensor"), None),
            P("dp", "tensor"),
            P("dp", "tensor"),
            P("dp", "tensor"),
            P("dp", "tensor"),
            P("dp", "tensor"),
            P("dp", "tensor"),
            P("dp", "tensor"),
            P(),
            P(),
            P(),
            P(),
            P(),
            P("dp", None),
            P("dp", None),
            P(("dp", "tensor"), None),
        ),
        out_specs=(
            P(("dp", "tensor"), None),
            P(("dp", "tensor"), None),
            P("dp", "tensor"),
            P("dp", "tensor"),
            P("dp", "tensor"),
            P("dp", "tensor"),
            P("dp", "tensor"),
            P("dp", "tensor"),
            P("dp", "tensor"),
            P(),
            P(),
            P(),
            P(),
            P(),
        ),
        check_vma=False,
    )
```

```python
import functools
import math

import jax
import jax.numpy as jnp
from jax import lax
from jax.experimental import pallas as pl
from jax.experimental.pallas import tpu as pltpu
from jax.sharding import PartitionSpec as P

D = 1024
HD = 64
BLK = 256
LOG2E = 1.4426950408889634
VMEM_LIMIT = 60 * 1024 * 1024


def dot_ab(a, b):
    return lax.dot_general(a, b, (((1,), (0,)), ((), ())), preferred_element_type=jnp.float32)


def dot_abt(a, b):
    return lax.dot_general(a, b, (((1,), (1,)), ((), ())), preferred_element_type=jnp.float32)


def split_heads(block, heads):
    lane_head = lax.broadcasted_iota(jnp.int32, block.shape, 1) // HD
    zero = jnp.zeros_like(block)
    return jnp.concatenate([jnp.where(lane_head == h, block, zero) for h in range(heads)], axis=0)


def attn_fwd_body(
    low_ref, start_ref, order_row, q_ref, k_ref, v_ref, out_ref, lse_ref, plain_ref, vt_ref, qs_ref, acc_ref, sum_ref
):
    rows, cols = q_ref.shape
    heads = cols // HD
    scale = math.sqrt(HD) * LOG2E
    for b in range(rows // BLK):
        vt_ref[:, b * BLK : (b + 1) * BLK] = v_ref[b * BLK : (b + 1) * BLK, :].T

    def one_block(i, _):
        base = pl.multiple_of(i * BLK, BLK)
        qs_ref[...] = split_heads(q_ref[pl.ds(base, BLK), :], heads)
        acc_ref[...] = jnp.zeros_like(acc_ref)
        sum_ref[...] = jnp.zeros_like(sum_ref)
        start = jnp.concatenate([start_ref[:, pl.ds(base, BLK)]] * heads, axis=1)
        own = lax.broadcasted_iota(jnp.int32, (1, heads * BLK), 1) % BLK + base

        def step(j, causal):
            at = pl.multiple_of(j * BLK, BLK)
            scores = dot_abt(k_ref[pl.ds(at, BLK), :], qs_ref[...])
            place = lax.broadcasted_iota(jnp.int32, scores.shape, 0) + at
            keep = place >= start
            if causal:
                keep = keep & (place <= own)
            probs = jnp.where(keep, jnp.exp2(scores * scale), 0.0)
            sum_ref[...] += jnp.sum(probs, axis=0, keepdims=True)
            probs_b = probs.astype(jnp.bfloat16)
            for h in range(heads):
                acc_ref[h * HD : (h + 1) * HD, :] += dot_ab(
                    vt_ref[h * HD : (h + 1) * HD, pl.ds(at, BLK)], probs_b[:, h * BLK : (h + 1) * BLK]
                )

        lax.fori_loop(low_ref[i], i, lambda j, c: (step(j, False), c)[1], 0)
        step(i, True)
        total = sum_ref[...]
        inv = 1.0 / total
        logs = jnp.log2(total)
        for h in range(heads):
            lse_ref[h : h + 1, pl.ds(base, BLK)] = logs[:, h * BLK : (h + 1) * BLK]
            acc_ref[h * HD : (h + 1) * HD, :] *= inv[:, h * BLK : (h + 1) * BLK]
        out_ref[pl.ds(base, BLK), :] = acc_ref[...].T.astype(jnp.bfloat16)
        return 0

    lax.fori_loop(0, rows // BLK, one_block, 0)
    over(rows // BLK, lambda b: to_token_order(b, order_row, out_ref, plain_ref))


def to_token_order(b, order_row, src, dst):
    at = pl.ds(pl.multiple_of(b * BLK, BLK), BLK)
    hot = lax.broadcasted_iota(jnp.int32, (BLK, src.shape[0]), 0) + b * BLK == order_row[...]
    dst[at, :] = dot_ab(hot.astype(jnp.float32).astype(jnp.bfloat16), src[...]).astype(dst.dtype)


def to_packed_order(b, order_col, src, dst):
    at = pl.ds(pl.multiple_of(b * BLK, BLK), BLK)
    hot = lax.broadcasted_iota(jnp.int32, (BLK, src.shape[0]), 1) == order_col[at, :]
    dst[at, :] = dot_ab(hot.astype(jnp.float32).astype(jnp.bfloat16), src[...]).astype(dst.dtype)


def over(count, body):
    lax.fori_loop(0, count, lambda i, carry: (body(i), carry)[1], 0)


def vmem():
    return pl.BlockSpec(memory_space=pltpu.VMEM)


def attn_fwd(low, start, order_row, q, k, v):
    rows, cols = q.shape
    heads = cols // HD
    return pl.pallas_call(
        attn_fwd_body,
        out_shape=(
            jax.ShapeDtypeStruct((rows, cols), jnp.bfloat16),
            jax.ShapeDtypeStruct((8, rows), jnp.float32),
            jax.ShapeDtypeStruct((rows, cols), jnp.bfloat16),
        ),
        in_specs=[pl.BlockSpec(memory_space=pltpu.SMEM)] + [vmem()] * 5,
        out_specs=(vmem(),) * 3,
        scratch_shapes=[
            pltpu.VMEM((cols, rows), jnp.bfloat16),
            pltpu.VMEM((heads * BLK, cols), jnp.bfloat16),
            pltpu.VMEM((cols, BLK), jnp.float32),
            pltpu.VMEM((1, heads * BLK), jnp.float32),
        ],
        compiler_params=pltpu.CompilerParams(vmem_limit_bytes=VMEM_LIMIT),
        cost_estimate=pl.CostEstimate(flops=4 * rows * rows * cols, bytes_accessed=8 * rows * cols, transcendentals=rows * rows * heads),
        name="attn_fwd",
    )(low, start, order_row, q, k, v)


def attn_bwd_body(
    low_ref, start_ref, order_row, order_col, lse_ref, q_ref, k_ref, v_ref, o_ref, grad_ref,
    plain_ref, kt_ref, qs_ref, gs_ref, dqt_ref, dk_acc, dv_acc, g_ref, packed,
):
    rows, cols = q_ref.shape
    heads = cols // HD
    root = math.sqrt(HD)
    scale = root * LOG2E
    for b in range(rows // BLK):
        kt_ref[:, b * BLK : (b + 1) * BLK] = k_ref[b * BLK : (b + 1) * BLK, :].T
    over(rows // BLK, lambda b: to_packed_order(b, order_col, grad_ref, g_ref))
    dk_acc[...] = jnp.zeros_like(dk_acc)
    dv_acc[...] = jnp.zeros_like(dv_acc)

    def one_block(i, _):
        base = pl.multiple_of(i * BLK, BLK)
        qs_ref[...] = split_heads(q_ref[pl.ds(base, BLK), :], heads)
        grads = g_ref[pl.ds(base, BLK), :]
        gs_ref[...] = split_heads(grads, heads)
        dqt_ref[...] = jnp.zeros_like(dqt_ref)
        start = jnp.concatenate([start_ref[:, pl.ds(base, BLK)]] * heads, axis=1)
        own = lax.broadcasted_iota(jnp.int32, (1, heads * BLK), 1) % BLK + base
        prod = (grads.astype(jnp.float32) * o_ref[pl.ds(base, BLK), :].astype(jnp.float32)).T
        delta = jnp.concatenate(
            [jnp.sum(prod[h * HD : (h + 1) * HD, :], axis=0, keepdims=True) for h in range(heads)], axis=1
        )
        lse = jnp.concatenate([lse_ref[h : h + 1, pl.ds(base, BLK)] for h in range(heads)], axis=1)

        def step(j, causal):
            at = pl.multiple_of(j * BLK, BLK)
            scores = dot_abt(k_ref[pl.ds(at, BLK), :], qs_ref[...])
            dprobs = dot_abt(v_ref[pl.ds(at, BLK), :], gs_ref[...])
            place = lax.broadcasted_iota(jnp.int32, scores.shape, 0) + at
            keep = place >= start
            if causal:
                keep = keep & (place <= own)
            probs = jnp.where(keep, jnp.exp2(scores * scale - lse), 0.0)
            dsc = (probs * (dprobs - delta)).astype(jnp.bfloat16)
            dv_acc[pl.ds(at, BLK), :] += dot_ab(probs.astype(jnp.bfloat16), gs_ref[...])
            dk_acc[pl.ds(at, BLK), :] += dot_ab(dsc, qs_ref[...])
            for h in range(heads):
                dqt_ref[h * HD : (h + 1) * HD, :] += dot_ab(
                    kt_ref[h * HD : (h + 1) * HD, pl.ds(at, BLK)], dsc[:, h * BLK : (h + 1) * BLK]
                )

        lax.fori_loop(low_ref[i], i, lambda j, c: (step(j, False), c)[1], 0)
        step(i, True)
        packed[pl.ds(base, BLK), 0:cols] = (dqt_ref[...].T * root).astype(packed.dtype)
        return 0

    lax.fori_loop(0, rows // BLK, one_block, 0)
    packed[:, cols : 2 * cols] = (dk_acc[...] * root).astype(packed.dtype)
    packed[:, 2 * cols : 3 * cols] = dv_acc[...].astype(packed.dtype)
    over(rows // BLK, lambda b: to_token_order(b, order_row, packed, plain_ref))


def attn_bwd(low, start, order_row, order_col, lse, q, k, v, o, g):
    rows, cols = q.shape
    heads = cols // HD
    return pl.pallas_call(
        attn_bwd_body,
        out_shape=jax.ShapeDtypeStruct((rows, 3 * cols), jnp.bfloat16),
        in_specs=[pl.BlockSpec(memory_space=pltpu.SMEM)] + [vmem()] * 9,
        out_specs=vmem(),
        scratch_shapes=[
            pltpu.VMEM((cols, rows), jnp.bfloat16),
            pltpu.VMEM((heads * BLK, cols), jnp.bfloat16),
            pltpu.VMEM((heads * BLK, cols), jnp.bfloat16),
            pltpu.VMEM((cols, BLK), jnp.float32),
            pltpu.VMEM((rows, cols), jnp.float32),
            pltpu.VMEM((rows, cols), jnp.float32),
            pltpu.VMEM((rows, cols), jnp.bfloat16),
            pltpu.VMEM((rows, 3 * cols), jnp.bfloat16),
        ],
        compiler_params=pltpu.CompilerParams(vmem_limit_bytes=VMEM_LIMIT),
        cost_estimate=pl.CostEstimate(flops=10 * rows * rows * cols, bytes_accessed=16 * rows * cols, transcendentals=rows * rows * heads),
        name="attn_bwd",
    )(low, start, order_row, order_col, lse, q, k, v, o, g)


MESH_ID = pl.DeviceIdType.MESH
EPS = 1e-06
TILE = 256
STRIP = 64
WIDE_STRIP = 192


def flip1(index):
    return index + 1 - 2 * lax.rem(index, 2)


def flip2(index):
    return index + 2 - 4 * (index // 2)


def tile_at(index, size):
    if isinstance(index, int):
        return pl.ds(index * size, size)
    return pl.ds(pl.multiple_of(index * size, size), size)


def row_sum(value):
    return jnp.sum(value, axis=-1, keepdims=True)


def middle_body(
    att_ref, wo_hbm, w_hbm, tok_hbm, cot_hbm, aa_ref, am_ref, su_ref, sg_ref,
    out_ref, datt_ref, gw_hbm, gwo_hbm, dh1_ref, gaa_ref, gam_ref, gsu_ref, gsg_ref,
    wo, wall, tok, cot, parts, mids, dbms, mid_t, dbm_t, ups, gates, mixed,
    middle, branch, dh2, own_part, send_a, recv_a, send_d, recv_d, send_z, recv_z,
    gw, gwo, dparts, load_sems, store_sems, hop_send, hop_recv, a2a_send, a2a_recv, d2a_send, d2a_recv, part_send, part_recv,
):
    d = lax.axis_index("dp")
    t = lax.axis_index("tensor")
    rows, width = tok.shape
    heads_w = att_ref.shape[1]
    hid = wall.shape[2]
    nq = w_hbm.shape[0]
    qrows = w_hbm.shape[2]
    chunks = hop_send.shape[0] // 6
    crow = rows // chunks
    core_peer = (flip1(d), t)
    z_peer = (d, flip1(t))
    line = [t, flip1(t), flip2(t), 3 - t]

    barrier = pltpu.get_barrier_semaphore()
    for peer in [core_peer] + [(d, line[k]) for k in (1, 2, 3)]:
        pl.semaphore_signal(barrier, inc=1, device_id=peer, device_id_type=MESH_ID)
    pl.semaphore_wait(barrier, 4)

    def remote(src, dst, ssem, rsem, peer):
        return pltpu.make_async_remote_copy(
            src_ref=src, dst_ref=dst, send_sem=ssem, recv_sem=rsem, device_id=peer, device_id_type=MESH_ID
        )

    a2a = [
        remote(att_ref.at[tile_at(line[k], rows), :], parts.at[k - 1], a2a_send.at[k - 1], a2a_recv.at[k - 1], (d, line[k]))
        for k in (1, 2, 3)
    ]
    for copy in a2a:
        copy.start()
    loads = [
        pltpu.make_async_copy(wo_hbm, wo, load_sems.at[0]),
        pltpu.make_async_copy(tok_hbm, tok, load_sems.at[1]),
        pltpu.make_async_copy(cot_hbm, cot, load_sems.at[2]),
    ]
    wloads = [
        [
            pltpu.make_async_copy(w_hbm.at[q, m], wall.at[m, pl.ds(q * qrows, qrows), :], load_sems.at[3 + m * nq + q])
            for q in range(nq)
        ]
        for m in range(3)
    ]
    for copy in loads + wloads[0] + wloads[1] + wloads[2]:
        copy.start()

    gsu_ref[...] = jnp.zeros_like(gsu_ref)
    gsg_ref[...] = jnp.zeros_like(gsg_ref)
    gam_ref[...] = jnp.zeros_like(gam_ref)
    gaa_ref[...] = jnp.zeros_like(gaa_ref)

    loads[0].wait()
    for copy in a2a:
        copy.wait_recv()

    def project(n):
        cols = tile_at(n, TILE)
        total = dot_abt(att_ref[tile_at(t, rows), :], wo[cols, tile_at(t, heads_w)])
        for k in (1, 2, 3):
            total += dot_abt(parts[k - 1], wo[cols, tile_at(line[k], heads_w)])
        branch[:, cols] = total

    over(width // TILE, project)
    loads[1].wait()

    def hop(buf, phase, ch, kind):
        part = tile_at(ch, crow)
        index = (phase * chunks + ch) * 3 + kind
        src, dst, peer = ((0, 2, z_peer), (0, 1, core_peer), (2, 3, core_peer))[kind]
        return remote(buf.at[src, part, :], buf.at[dst, part, :], hop_send.at[index], hop_recv.at[index], peer)

    def strips(ch, body):
        over(crow // STRIP, lambda i: body(tile_at(i + ch * (crow // STRIP), STRIP)))

    def unit_of(value):
        factor = lax.rsqrt(row_sum(value * value) + EPS)
        return value * factor, factor

    def make_middle(at):
        inputs = tok[at, :].astype(jnp.float32)
        norm_a, factor_a = unit_of(branch[at, :])
        mid, factor_mid = unit_of(inputs + aa_ref[...] * (norm_a - inputs))
        return inputs, norm_a, factor_a, mid, factor_mid

    def first(at):
        mid = make_middle(at)[3]
        middle[at, :] = mid
        mids[0, at, :] = mid.astype(jnp.bfloat16)

    for ch in range(chunks):
        strips(ch, first)
        hop(mids, 0, ch, 0).start()
        hop(mids, 0, ch, 1).start()

    for m in range(3):
        for copy in wloads[m]:
            copy.wait()

    def within(slot, at):
        return pl.ds(pl.multiple_of(slot * rows + at.start, STRIP), at.size)

    def forward_rows(slot, at, store, ready):
        where = within(slot, at)

        def hidden(n):
            cols = tile_at(n, TILE)
            x = mids[slot, at, :]
            up = dot_ab(x, wall[0, :, cols])
            gate_raw = dot_ab(x, wall[1, :, cols])
            gate = gate_raw * sg_ref[:, cols]
            silu = gate / (1.0 + jnp.exp(-gate))
            ups[where, cols] = up.astype(jnp.bfloat16)
            gates[where, cols] = gate_raw.astype(jnp.bfloat16)
            mixed[where, cols] = (up * su_ref[:, cols] * silu).astype(jnp.bfloat16)

        over(hid // TILE, hidden)
        ready()

        def down(n):
            cols = tile_at(n, TILE)
            store(at, cols, dot_abt(mixed[where, :], wall[2, cols, :]))

        over(width // TILE, down)

    def backward_rows(slot, at, store, ready):
        where = within(slot, at)

        def hidden(n):
            cols = tile_at(n, TILE)
            dmix = dot_ab(dbms[slot, at, :], wall[2, :, cols])
            up_raw = ups[where, cols].astype(jnp.float32)
            gate_raw = gates[where, cols].astype(jnp.float32)
            gate = gate_raw * sg_ref[:, cols]
            sig = 1.0 / (1.0 + jnp.exp(-gate))
            d_up = dmix * (gate * sig)
            d_gate = dmix * (up_raw * su_ref[:, cols]) * (sig * (1.0 + gate * (1.0 - sig)))
            gsu_ref[:, cols] += jnp.sum(d_up * up_raw, axis=0, keepdims=True)
            gsg_ref[:, cols] += jnp.sum(d_gate * gate_raw, axis=0, keepdims=True)
            ups[where, cols] = (d_up * su_ref[:, cols]).astype(jnp.bfloat16)
            gates[where, cols] = (d_gate * sg_ref[:, cols]).astype(jnp.bfloat16)

        over(hid // TILE, hidden)
        ready()

        def down(n):
            cols = tile_at(n, TILE)
            store(at, cols, dot_abt(ups[where, :], wall[0, cols, :]) + dot_abt(gates[where, :], wall[1, cols, :]))

        over(width // TILE, down)

    def part_copy(phase, kind, ch):
        part = tile_at(ch, crow)
        index = (phase * 3 + kind) * chunks + ch
        src, dst, peer = ((send_a, recv_a, core_peer), (send_d, recv_d, core_peer), (send_z, recv_z, z_peer))[kind]
        return remote(src.at[part, :], dst.at[part, :], part_send.at[index], part_recv.at[index], peer)

    def nothing():
        pass

    def tensor_pass(phase, buf, rows_fn, fillers):
        def keep_own(at, cols, value):
            own_part[at, cols] = value

        def to(ref):
            def store(at, cols, value):
                ref[at, cols] = value.astype(jnp.bfloat16)

            return store

        def to_z(at, cols, value):
            send_z[at, cols] = (value + recv_d[at, cols].astype(jnp.float32)).astype(jnp.bfloat16)

        over(chunks, lambda i: rows_fn(0, tile_at(i, crow), keep_own, nothing))
        for ch in range(chunks):
            hop(buf, phase, ch, 1).wait_recv()
        if phase == 1:
            for ch in range(chunks):
                part_copy(0, 0, ch).wait_send()
        over(chunks, lambda i: rows_fn(1, tile_at(i, crow), to(send_a), nothing))
        for ch in range(chunks):
            part_copy(phase, 0, ch).start()
        fillers[0]()
        def chunk(ch):
            hop(buf, phase, ch, 0).wait_recv()
            hop(buf, phase, ch, 2).start()
            at = tile_at(ch, crow)
            hop(buf, phase, ch, 2).wait_recv()
            if phase == 1:
                part_copy(0, 1, ch).wait_send()
            rows_fn(3, at, to(send_d), nothing)
            part_copy(phase, 1, ch).start()

            def ready():
                part_copy(phase, 1, ch).wait_recv()
                if phase == 1:
                    part_copy(0, 2, ch).wait_send()

            rows_fn(2, at, to_z, ready)
            part_copy(phase, 2, ch).start()

        over(chunks, chunk)
        fillers[1]()

    def transpose_into(dst, buf, slots):
        per_slot = rows // 128

        def one(i):
            slot = slots[0] + i // per_slot
            at = tile_at(lax.rem(i, per_slot), 128)
            to = tile_at(slots[0] * per_slot + i, 128)
            for n in range(width // TILE):
                dst[n * TILE : (n + 1) * TILE, to] = buf[slot, at, n * TILE : (n + 1) * TILE].T

        over(len(slots) * per_slot, one)

    tensor_pass(
        0, mids, forward_rows,
        [lambda: transpose_into(mid_t, mids, (0, 1)), lambda: transpose_into(mid_t, mids, (2, 3))],
    )

    loads[2].wait()

    def turn(at):
        mid = middle[at, :]
        branch_m = own_part[at, :] + recv_a[at, :].astype(jnp.float32) + recv_z[at, :].astype(jnp.float32)
        norm_m, factor_m = unit_of(branch_m)
        alpha = am_ref[...]
        y, factor_y = unit_of(mid + alpha * (norm_m - mid))
        out_ref[at, :] = y.astype(jnp.bfloat16)
        dy = cot[at, :].astype(jnp.float32)
        grad = factor_y * (dy - y * row_sum(y * dy))
        gam_ref[...] += jnp.sum(grad * (norm_m - mid), axis=0, keepdims=True)
        back = alpha * grad
        dbms[0, at, :] = (factor_m * (back - norm_m * row_sum(norm_m * back))).astype(jnp.bfloat16)
        dh2[at, :] = grad - back

    for ch in range(chunks):
        part_copy(0, 0, ch).wait_recv()
        part_copy(0, 2, ch).wait_recv()
        strips(ch, turn)
        hop(dbms, 1, ch, 0).start()
        hop(dbms, 1, ch, 1).start()

    def weight_grads():
        transpose_into(dbm_t, dbms, (2, 3))
        for m, (lhs, rhs) in enumerate(((mid_t, ups), (mid_t, gates), (dbm_t, mixed))):

            def block(i):
                q = i // (hid // TILE)
                cols = tile_at(lax.rem(i, hid // TILE), TILE)
                value = dot_ab(lhs[tile_at(q, TILE), :], rhs[:, cols])
                gw[m, tile_at(q, TILE), cols] = value.astype(jnp.bfloat16)

            over((width // TILE) * (hid // TILE), block)
            for q in range(nq):
                grad_store(m, q).start()

    def grad_store(m, q):
        return pltpu.make_async_copy(gw.at[m, pl.ds(q * qrows, qrows), :], gw_hbm.at[q, m], store_sems.at[m * nq + q])

    tensor_pass(1, dbms, backward_rows, [lambda: transpose_into(dbm_t, dbms, (0, 1)), weight_grads])

    def last(at):
        inputs, norm_a, factor_a, mid, factor_mid = make_middle(at)
        grad_mid = dh2[at, :] + own_part[at, :] + recv_a[at, :].astype(jnp.float32) + recv_z[at, :].astype(jnp.float32)
        grad = factor_mid * (grad_mid - mid * row_sum(mid * grad_mid))
        gaa_ref[...] += jnp.sum(grad * (norm_a - inputs), axis=0, keepdims=True)
        back = aa_ref[...] * grad
        dh1_ref[at, :] = grad - back
        mids[0, at, :] = (factor_a * (back - norm_a * row_sum(norm_a * back))).astype(jnp.bfloat16)

    for ch in range(chunks):
        hop(mids, 0, ch, 0).wait_send()
        hop(mids, 0, ch, 1).wait_send()
        part_copy(1, 0, ch).wait_recv()
        part_copy(1, 2, ch).wait_recv()
        strips(ch, last)

    dback = [
        remote(dparts.at[k], datt_ref.at[tile_at(t, rows), :], d2a_send.at[k - 1], d2a_recv.at[k - 1], (d, line[k]))
        for k in (1, 2, 3)
    ]
    for k in (3, 2, 1, 0):
        value = dot_ab(mids[0], wo[:, tile_at(line[k], heads_w)]).astype(jnp.bfloat16)
        if k:
            dparts[k] = value
            dback[k - 1].start()
        else:
            datt_ref[tile_at(t, rows), :] = value

    transpose_into(mid_t, mids, (0,))

    def out_grad(n):
        at = tile_at(n, TILE)
        lhs = mid_t[at, 0:rows]
        gwo[at, tile_at(t, heads_w)] = dot_ab(lhs, att_ref[tile_at(t, rows), :]).astype(jnp.bfloat16)
        for k in (1, 2, 3):
            gwo[at, tile_at(line[k], heads_w)] = dot_ab(lhs, parts[k - 1]).astype(jnp.bfloat16)

    over(width // TILE, out_grad)
    wo_store = pltpu.make_async_copy(gwo, gwo_hbm, store_sems.at[3 * nq])
    wo_store.start()

    for k in (1, 2, 3):
        remote(
            dparts.at[k], datt_ref.at[tile_at(line[k], rows), :], d2a_send.at[k - 1], d2a_recv.at[k - 1], (d, line[k])
        ).wait()
    for copy in a2a:
        copy.wait_send()
    for ch in range(chunks):
        hop(mids, 0, ch, 2).wait_send()
        for kind in range(3):
            hop(dbms, 1, ch, kind).wait_send()
            part_copy(1, kind, ch).wait_send()
    for m in range(3):
        for q in range(nq):
            grad_store(m, q).wait()
    wo_store.wait()


def middle_call(chunks, attended, wo, w_parts, tokens, cotangent, alpha_a, alpha_m, su, sg):
    rows, width = tokens.shape
    group, heads_w = attended.shape
    nq, _, qrows, hid = w_parts.shape
    bf, f32 = jnp.bfloat16, jnp.float32
    anywhere = pl.BlockSpec(memory_space=pl.ANY)
    dma = pltpu.SemaphoreType.DMA
    return pl.pallas_call(
        middle_body,
        out_shape=(
            jax.ShapeDtypeStruct((rows, width), bf),
            jax.ShapeDtypeStruct((group, heads_w), bf),
            jax.ShapeDtypeStruct((nq, 3, qrows, hid), bf),
            jax.ShapeDtypeStruct((width, width), bf),
            jax.ShapeDtypeStruct((rows, width), f32),
            jax.ShapeDtypeStruct((1, width), f32),
            jax.ShapeDtypeStruct((1, width), f32),
            jax.ShapeDtypeStruct((1, hid), f32),
            jax.ShapeDtypeStruct((1, hid), f32),
        ),
        in_specs=[vmem(), anywhere, anywhere, anywhere, anywhere] + [vmem()] * 4,
        out_specs=(vmem(), vmem(), anywhere, anywhere) + (vmem(),) * 5,
        scratch_shapes=[
            pltpu.VMEM((width, width), bf),
            pltpu.VMEM((3, width, hid), bf),
            pltpu.VMEM((rows, width), bf),
            pltpu.VMEM((rows, width), bf),
            pltpu.VMEM((3, rows, heads_w), bf),
            pltpu.VMEM((4, rows, width), bf),
            pltpu.VMEM((4, rows, width), bf),
            pltpu.VMEM((width, 4 * rows), bf),
            pltpu.VMEM((width, 4 * rows), bf),
            pltpu.VMEM((4 * rows, hid), bf),
            pltpu.VMEM((4 * rows, hid), bf),
            pltpu.VMEM((4 * rows, hid), bf),
            pltpu.VMEM((rows, width), f32),
            pltpu.VMEM((rows, width), f32),
            pltpu.VMEM((rows, width), f32),
            pltpu.VMEM((rows, width), f32),
        ]
        + [pltpu.VMEM((rows, width), bf)] * 6
        + [
            pltpu.VMEM((3, width, hid), bf),
            pltpu.VMEM((width, width), bf),
            pltpu.VMEM((4, rows, heads_w), bf),
            dma((3 + 3 * nq,)),
            dma((3 * nq + 1,)),
            dma((6 * chunks,)),
            dma((6 * chunks,)),
            dma((3,)),
            dma((3,)),
            dma((3,)),
            dma((3,)),
            dma((6 * chunks,)),
            dma((6 * chunks,)),
        ],
        compiler_params=pltpu.CompilerParams(vmem_limit_bytes=67000000, collective_id=1, has_side_effects=True),
        cost_estimate=pl.CostEstimate(flops=10**11, bytes_accessed=10**8, transcendentals=10**6),
        name="middle",
    )(attended, wo, w_parts, tokens, cotangent, alpha_a, alpha_m, su, sg)


def remote_copy(src, dst, send_sem, recv_sem, peer):
    return pltpu.make_async_remote_copy(
        src_ref=src, dst_ref=dst, send_sem=send_sem, recv_sem=recv_sem, device_id=peer, device_id_type=MESH_ID
    )


def greet(peers):
    barrier = pltpu.get_barrier_semaphore()
    for peer in peers:
        pl.semaphore_signal(barrier, inc=1, device_id=peer, device_id_type=MESH_ID)
    pl.semaphore_wait(barrier, len(peers))


def spread_body(
    count, tok, w_up, w_gate, w_down, wq, wk, wv, wo, pair, tok2, wqkv, wo_all,
    own_mlp, own_att, wo_rows, load_sem, keep_sem, a_send, a_recv, b_send, b_recv, tok_send, tok_recv,
    qkv_send, qkv_recv, oz_send, oz_recv, oq_send, oq_recv, oc_send, oc_recv,
):
    d = lax.axis_index("dp")
    t = lax.axis_index("tensor")
    core = lax.rem(d, 2)
    home = core == t // 2
    far = (d - core + t // 2, flip2(t))
    wrows, wcols = wq.shape
    half = count // 2
    mlp = (w_up, w_gate, w_down)
    att = (wq, wk, wv)
    mine = tile_at(d, wrows)
    side = tile_at(core, wrows)
    other_side = tile_at(1 - core, wrows)

    barrier = pltpu.get_barrier_semaphore()

    def dp_peer(i):
        return lax.rem(d + 1 + i, count)

    def hello(i):
        pl.semaphore_signal(barrier, inc=1, device_id=(dp_peer(i), t), device_id_type=MESH_ID)

    over(count - 1, hello)
    for k in (1, 2, 3):
        pl.semaphore_signal(barrier, inc=1, device_id=(d, lax.rem(t + k, 4)), device_id_type=MESH_ID)
    pl.semaphore_signal(barrier, inc=1, device_id=(flip1(d), flip2(t)), device_id_type=MESH_ID)
    pl.semaphore_wait(barrier, count + 3)

    def b_copy(m):
        return remote_copy(mlp[m], pair.at[m, side, :], b_send.at[m], b_recv.at[core * 3 + m], far)

    def a_copy(m):
        return remote_copy(mlp[m], pair.at[m, side, :], a_send.at[m], a_recv.at[m], (flip1(d), t))

    tok_copy = remote_copy(tok, tok2, tok_send, tok_recv, (d, flip1(t)))
    for m in range(3):
        b_copy(m).start()
    tok_copy.start()

    def oz_copy(k):
        return remote_copy(wo, wo_rows.at[:, tile_at(t, wcols)], oz_send.at[k - 1], oz_recv.at[k - 1], (d, lax.rem(t + k, 4)))

    for k in (1, 2, 3):
        oz_copy(k).start()
    load_o = pltpu.make_async_copy(wo, wo_rows.at[:, tile_at(t, wcols)], load_sem.at[0])
    load_o.start()

    def qkv_copy(i, m):
        return remote_copy(
            att[m], wqkv.at[mine, pl.ds(m * wcols, wcols)], qkv_send.at[i, m], qkv_recv.at[i, m], (dp_peer(i), t)
        )

    def qkv_start(i):
        for m in range(3):
            qkv_copy(i, m).start()

    over(count - 1, qkv_start)

    @pl.when(jnp.logical_not(home))
    def _():
        for m in range(3):
            a_copy(m).start()

    loads = [pltpu.make_async_copy(mlp[m], own_mlp.at[m], load_sem.at[1 + m]) for m in range(3)]
    loads += [pltpu.make_async_copy(att[m], own_att.at[m], load_sem.at[4 + m]) for m in range(3)]
    for copy in loads:
        copy.start()
    for copy in loads:
        copy.wait()
    keeps = [
        pltpu.make_async_copy(own_att.at[m], wqkv.at[mine, pl.ds(m * wcols, wcols)], keep_sem.at[m]) for m in range(3)
    ]
    for copy in keeps:
        copy.start()
    pair_keeps = [pltpu.make_async_copy(own_mlp.at[m], pair.at[m, side, :], keep_sem.at[3 + m]) for m in range(3)]

    @pl.when(home)
    def _():
        for copy in pair_keeps:
            copy.start()

    load_o.wait()
    for k in (1, 2, 3):
        oz_copy(k).wait_recv()
    keep_o = pltpu.make_async_copy(wo_rows, wo_all.at[mine, :], keep_sem.at[6])
    keep_o.start()

    def oq_copy(j):
        return remote_copy(wo_rows, wo_all.at[mine, :], oq_send.at[j], oq_recv.at[j], (lax.rem(d + 2 + 2 * j, count), t))

    def oc_own():
        return remote_copy(wo_rows, wo_all.at[mine, :], oc_send.at[half - 1], oc_recv.at[half - 1], (flip1(d), t))

    def oc_copy(j):
        rows = tile_at(lax.rem(d + count - 2 - 2 * j, count), wrows)
        return remote_copy(wo_all.at[rows, :], wo_all.at[rows, :], oc_send.at[j], oc_recv.at[j], (flip1(d), t))

    over(half - 1, lambda j: oq_copy(j).start())
    oc_own().start()

    def oq_next(j):
        oq_copy(j).wait_recv()
        oc_copy(j).start()

    over(half - 1, oq_next)

    def qkv_wait(i):
        for m in range(3):
            qkv_copy(i, m).wait()

    over(count - 1, qkv_wait)
    over(half - 1, lambda j: oq_copy(j).wait_send())
    over(half - 1, lambda j: oc_copy(j).wait())
    oc_own().wait()
    for k in (1, 2, 3):
        oz_copy(k).wait_send()
    keep_o.wait()
    for copy in keeps:
        copy.wait()
    tok_copy.wait()
    for m in range(3):
        b_copy(m).wait_send()

    @pl.when(home)
    def _():
        for m in range(3):
            pair_keeps[m].wait()
            remote_copy(mlp[m], pair.at[m, other_side, :], a_send.at[m], a_recv.at[m], (flip1(d), t)).wait_recv()

    @pl.when(jnp.logical_not(home))
    def _():
        for m in range(3):
            a_copy(m).wait_send()
            for c in range(2):
                remote_copy(
                    mlp[m], pair.at[m, pl.ds(c * wrows, wrows), :], b_send.at[m], b_recv.at[c * 3 + m], far
                ).wait_recv()


def spread_call(count, tokens, w_up, w_gate, w_down, wq, wk, wv, wo):
    rows, width = tokens.shape
    wrows, wcols = wq.shape
    hid = w_up.shape[1]
    bf = jnp.bfloat16
    anywhere = pl.BlockSpec(memory_space=pl.ANY)
    dma = pltpu.SemaphoreType.DMA
    return pl.pallas_call(
        functools.partial(spread_body, count),
        out_shape=(
            jax.ShapeDtypeStruct((3, 2 * wrows, hid), bf),
            jax.ShapeDtypeStruct((rows, width), bf),
            jax.ShapeDtypeStruct((width, 3 * wcols), bf),
            jax.ShapeDtypeStruct((width, width), bf),
        ),
        in_specs=[anywhere] * 8,
        out_specs=(anywhere,) * 4,
        scratch_shapes=[
            pltpu.VMEM((3, wrows, hid), bf),
            pltpu.VMEM((3, wrows, wcols), bf),
            pltpu.VMEM((wrows, width), bf),
            dma((7,)), dma((7,)), dma((3,)), dma((3,)), dma((3,)), dma((6,)), dma, dma,
            dma((count - 1, 3)), dma((count - 1, 3)), dma((3,)), dma((3,)),
            dma((count // 2,)), dma((count // 2,)), dma((count // 2,)), dma((count // 2,)),
        ],
        compiler_params=pltpu.CompilerParams(vmem_limit_bytes=VMEM_LIMIT, collective_id=2, has_side_effects=True),
        name="spread",
    )(tokens, w_up, w_gate, w_down, wq, wk, wv, wo)


def head_sums(value):
    width = value.shape[1]
    same = (
        lax.broadcasted_iota(jnp.int32, (width, width), 0) // HD == lax.broadcasted_iota(jnp.int32, (width, width), 1) // HD
    )
    ones = jnp.where(same, 1.0, 0.0).astype(jnp.bfloat16)
    high = value.astype(jnp.bfloat16)
    low = (value - high.astype(jnp.float32)).astype(jnp.bfloat16)
    return dot_ab(high, ones) + dot_ab(low, ones)


def swap_halves(value):
    width = value.shape[1]
    lane = lax.broadcasted_iota(jnp.int32, value.shape, 1) % HD
    return jnp.where(lane < HD // 2, pltpu.roll(value, width - HD // 2, 1), pltpu.roll(value, HD // 2, 1))


def project_body(
    tok, tok2, wqkv, cos_ref, sin_ref, order_col, gain_ref, q_ref, k_ref, v_ref, raw_ref, x_hbm,
    xs, plain, load_sem, keep_sem, mid_send, recv, on_send,
):
    t = lax.axis_index("tensor")
    d = lax.axis_index("dp")
    _, rows, width = xs.shape
    group, cols = q_ref.shape
    near = flip1(t)
    across = 3 - t
    inner = (t + 1) // 2 == 1
    arrive = (2 - t // 2, 3 - 3 * (t // 2))
    part = rows // 2
    greet([(d, near), (d, across)])

    def mid_copy(k):
        src = (tok, tok2)[k // 2].at[pl.ds((k % 2) * part, part), :]
        dst = xs.at[(t, near)[k // 2], pl.ds((k % 2) * part, part), :]
        return remote_copy(src, dst, mid_send.at[k], recv.at[k], (d, across))

    def on_copy(k):
        ref = xs.at[arrive[k // 2], pl.ds((k % 2) * part, part), :]
        return remote_copy(ref, ref, on_send.at[k], recv.at[k], (d, near))

    @pl.when(inner)
    def _():
        for k in range(4):
            mid_copy(k).start()

    loads = [
        pltpu.make_async_copy(tok, xs.at[t], load_sem.at[0]),
        pltpu.make_async_copy(tok2, xs.at[near], load_sem.at[1]),
    ]
    for copy in loads:
        copy.start()

    def keep(index, slot):
        return pltpu.make_async_copy(xs.at[slot], x_hbm.at[tile_at(slot, rows), :], keep_sem.at[index])

    def work(index, slot):
        keep(index, slot).start()

        def strip(i):
            at = tile_at(slot * (rows // WIDE_STRIP) + i, WIDE_STRIP)
            x = xs[slot, tile_at(i, WIDE_STRIP), :]
            cos = jnp.concatenate([cos_ref[at, :]] * (cols // cos_ref.shape[1]), axis=1)
            sin = jnp.concatenate([sin_ref[at, :]] * (cols // sin_ref.shape[1]), axis=1)
            for m in range(2):
                raw = dot_ab(x, wqkv[:, m * cols : (m + 1) * cols])
                raw_ref[at, m * cols : (m + 1) * cols] = raw.astype(jnp.bfloat16)
                normed = raw * lax.rsqrt(head_sums(raw * raw) + EPS) * gain_ref[...]
                plain[at, m * cols : (m + 1) * cols] = (normed * cos + swap_halves(normed) * sin).astype(jnp.bfloat16)
            plain[at, 2 * cols : 3 * cols] = dot_ab(x, wqkv[:, 2 * cols : 3 * cols]).astype(jnp.bfloat16)

        over(rows // WIDE_STRIP, strip)

    loads[0].wait()
    work(0, t)
    loads[1].wait()
    work(1, near)
    for k in range(4):
        slot = arrive[k // 2]
        ref = xs.at[slot, pl.ds((k % 2) * part, part), :]
        remote_copy(ref, ref, on_send.at[k], recv.at[k], (d, near)).wait_recv()

        @pl.when(inner)
        def _():
            on_copy(k).start()

        if k % 2:
            work(2 + k // 2, slot)

    def permute(b):
        at = tile_at(b, BLK)
        hot = (lax.broadcasted_iota(jnp.int32, (BLK, group), 1) == order_col[at, :]).astype(jnp.float32)
        value = dot_ab(hot.astype(jnp.bfloat16), plain[...])
        for m, ref in enumerate((q_ref, k_ref, v_ref)):
            ref[at, :] = value[:, m * cols : (m + 1) * cols].astype(jnp.bfloat16)

    over(group // BLK, permute)
    for index, slot in enumerate((t, near, *arrive)):
        keep(index, slot).wait()

    @pl.when(inner)
    def _():
        for k in range(4):
            mid_copy(k).wait_send()
            on_copy(k).wait_send()


def project_call(tokens, tok2, wqkv, cos, sin, order_col, gains):
    rows, width = tokens.shape
    group = order_col.shape[0]
    cols = wqkv.shape[1] // 3
    bf = jnp.bfloat16
    anywhere = pl.BlockSpec(memory_space=pl.ANY)
    dma = pltpu.SemaphoreType.DMA
    return pl.pallas_call(
        project_body,
        out_shape=(jax.ShapeDtypeStruct((group, cols), bf),) * 3
        + (jax.ShapeDtypeStruct((group, 2 * cols), bf), jax.ShapeDtypeStruct((group, width), bf)),
        in_specs=[anywhere, anywhere] + [vmem()] * 5,
        out_specs=(vmem(),) * 4 + (anywhere,),
        scratch_shapes=[
            pltpu.VMEM((group // rows, rows, width), bf),
            pltpu.VMEM((group, 3 * cols), bf),
            dma((2,)), dma((4,)), dma((4,)), dma((4,)), dma((4,)),
        ],
        compiler_params=pltpu.CompilerParams(vmem_limit_bytes=VMEM_LIMIT, collective_id=3, has_side_effects=True),
        cost_estimate=pl.CostEstimate(flops=6 * 10**10, bytes_accessed=10**7, transcendentals=10**6),
        name="project",
    )(tokens, tok2, wqkv, cos, sin, order_col, gains)


def tail_body(
    grad_ref, raw_ref, cos_ref, sin_ref, wqkv, x_hbm, kept_ref, gain_ref, tok_out, gq, gain_sum,
    xs, x_t, draw, part_far, part_mid, part_near, own_part, from_a, from_b, from_c, from_d, from_e, from_f,
    load_sem, hop_send, hop_recv,
):
    d = lax.axis_index("dp")
    t = lax.axis_index("tensor")
    rows, width = tok_out.shape
    group = draw.shape[0]
    cols = draw.shape[1] // 3
    near = flip1(t)
    inner = (t + 1) // 2 == 1
    outer = jnp.logical_not(inner)
    far, mid = 3 - 3 * (t // 2), 2 - t // 2
    chunk = rows // 2
    greet([(d, near), (d, 3 - t)])
    load_x = pltpu.make_async_copy(x_hbm, xs, load_sem)
    load_x.start()

    def hop(kind, ch):
        src, dst, to = (
            (part_far, from_a, near),
            (part_mid, from_b, near),
            (part_near, from_c, near),
            (part_far, from_d, 3 - t),
            (part_mid, from_e, 3 - t),
            (part_near, from_f, near),
        )[kind]
        part = pl.ds(ch * chunk, chunk)
        return remote_copy(src.at[part, :], dst.at[part, :], hop_send.at[kind, ch], hop_recv.at[kind, ch], (d, to))

    gain_sum[...] = jnp.zeros_like(gain_sum)

    def work(slot, store):
        def strip(i):
            at = tile_at(slot * (rows // WIDE_STRIP) + i, WIDE_STRIP)
            cos = jnp.concatenate([cos_ref[at, :]] * (cols // cos_ref.shape[1]), axis=1)
            sin = jnp.concatenate([sin_ref[at, :]] * (cols // sin_ref.shape[1]), axis=1)
            gain = gain_ref[...]
            for m in range(2):
                grad = grad_ref[at, m * cols : (m + 1) * cols].astype(jnp.float32)
                raw = raw_ref[at, m * cols : (m + 1) * cols].astype(jnp.float32)
                back = grad * cos - swap_halves(grad) * sin
                factor = lax.rsqrt(head_sums(raw * raw) + EPS)
                normed = raw * factor
                gain_sum[...] += jnp.sum(back * normed, axis=0, keepdims=True)
                scaled = back * gain
                draw[at, m * cols : (m + 1) * cols] = (
                    factor * (scaled - normed * head_sums(normed * scaled))
                ).astype(jnp.bfloat16)
            draw[at, 2 * cols : 3 * cols] = grad_ref[at, 2 * cols : 3 * cols]

        over(rows // WIDE_STRIP, strip)
        everything = tile_at(slot, rows)

        def product(n):
            tile = tile_at(n, TILE)
            store(tile, dot_abt(draw[everything, :], wqkv[tile, :]))

        over(width // TILE, product)

    def into(ref):
        def store(tile, value):
            ref[:, tile] = value.astype(ref.dtype)

        return store

    for kind, (slot, ref) in enumerate(((far, part_far), (mid, part_mid), (near, part_near))):
        work(slot, into(ref))

        @pl.when(outer)
        def _():
            for ch in range(2):
                hop(kind, ch).start()

    work(t, into(own_part))

    def pass_on(kind, ch, own, got, then):
        @pl.when(inner)
        def _():
            part = pl.ds(ch * chunk, chunk)
            hop(kind, ch).wait_recv()
            own[part, :] = (own[part, :].astype(jnp.float32) + got[part, :].astype(jnp.float32)).astype(jnp.bfloat16)
            hop(then, ch).start()

    pass_on(0, 0, part_far, from_a, 3)
    pass_on(0, 1, part_far, from_a, 3)

    load_x.wait()

    def flip_block(b):
        at = tile_at(b, 128)
        for n in range(width // TILE):
            x_t[n * TILE : (n + 1) * TILE, at] = xs[at, n * TILE : (n + 1) * TILE].T

    over(group // 128, flip_block)
    pass_on(3, 0, part_near, from_d, 5)

    def weight_grad(n):
        tile = tile_at(n, TILE)
        gq[tile, :] = dot_ab(x_t[tile, :], draw[...]).astype(jnp.bfloat16)

    over(width // TILE, weight_grad)
    pass_on(1, 0, part_mid, from_b, 4)
    pass_on(3, 1, part_near, from_d, 5)
    pass_on(1, 1, part_mid, from_b, 4)

    for ch in range(2):
        part = pl.ds(ch * chunk, chunk)

        @pl.when(inner)
        def _():
            hop(2, ch).wait_recv()
            hop(4, ch).wait_recv()
            tok_out[part, :] = (
                kept_ref[part, :]
                + own_part[part, :]
                + from_c[part, :].astype(jnp.float32)
                + from_e[part, :].astype(jnp.float32)
            )

        @pl.when(outer)
        def _():
            hop(5, ch).wait_recv()
            tok_out[part, :] = kept_ref[part, :] + own_part[part, :] + from_f[part, :].astype(jnp.float32)

    for ch in range(2):

        @pl.when(inner)
        def _():
            for kind in (3, 4, 5):
                hop(kind, ch).wait_send()

        @pl.when(outer)
        def _():
            for kind in (0, 1, 2):
                hop(kind, ch).wait_send()


def tail_call(grad_qkv, raw, cos, sin, wqkv, all_tokens, kept, gains):
    rows, width = kept.shape
    group, three = grad_qkv.shape
    bf, f32 = jnp.bfloat16, jnp.float32
    anywhere = pl.BlockSpec(memory_space=pl.ANY)
    dma = pltpu.SemaphoreType.DMA
    shape = jax.ShapeDtypeStruct
    return pl.pallas_call(
        tail_body,
        out_shape=(shape((rows, width), f32), shape((width, three), bf), shape((1, three // 3), f32)),
        in_specs=[vmem()] * 5 + [anywhere] + [vmem()] * 2,
        out_specs=(vmem(),) * 3,
        scratch_shapes=[
            pltpu.VMEM((group, width), bf),
            pltpu.VMEM((width, group), bf),
            pltpu.VMEM((group, three), bf),
            pltpu.VMEM((rows, width), bf),
            pltpu.VMEM((rows, width), bf),
            pltpu.VMEM((rows, width), bf),
            pltpu.VMEM((rows, width), f32),
        ]
        + [pltpu.VMEM((rows, width), bf)] * 6
        + [dma, dma((6, 2)), dma((6, 2))],
        compiler_params=pltpu.CompilerParams(vmem_limit_bytes=VMEM_LIMIT, collective_id=4, has_side_effects=True),
        cost_estimate=pl.CostEstimate(flops=6 * 10**10, bytes_accessed=10**7, transcendentals=10**6),
        name="tail",
    )(grad_qkv, raw, cos, sin, wqkv, all_tokens, kept, gains)


def settle_body(
    count, gq_hbm, gwo_hbm, mlp_hbm, gain_ref, gaa_ref, gam_ref, gsu_ref, gsg_ref,
    q_out, k_out, v_out, wo_out, up_out, gate_out, down_out, gain_out, aa_out, am_out, su_out, sg_out,
    own_q, core_q, got_q, own_w, core_w, got_w, wo_mid, got_z, near_mlp, far_mlp, vec, got_v, vec_mid, got_s,
    load_sem, core_send, core_recv, q_send, q_recv, w_send, w_recv, z_send, z_recv, v_send, v_recv, s_send, s_recv,
    mlp_send, mlp_recv,
):
    d = lax.axis_index("dp")
    t = lax.axis_index("tensor")
    half, wrows, three = got_q.shape
    cols = three // 3
    width = gaa_ref.shape[1]
    chip, core = d // 2, lax.rem(d, 2)
    home = core == t // 2
    away = jnp.logical_not(home)
    f32, bf = jnp.float32, jnp.bfloat16

    def dp_peer(i):
        return lax.rem(d + 1 + i, count)

    def line_peer(k):
        return lax.rem(t + k, 4)

    def chip_peer(i):
        return lax.rem(chip + 1 + i, half)

    barrier = pltpu.get_barrier_semaphore()
    over(
        count - 1,
        lambda i: pl.semaphore_signal(barrier, inc=1, device_id=(dp_peer(i), t), device_id_type=MESH_ID),
    )
    for k in (1, 2, 3):
        pl.semaphore_signal(barrier, inc=1, device_id=(d, line_peer(k)), device_id_type=MESH_ID)
    pl.semaphore_signal(barrier, inc=1, device_id=(flip1(d), flip2(t)), device_id_type=MESH_ID)
    pl.semaphore_wait(barrier, count + 3)

    near_copy = remote_copy(mlp_hbm.at[:, 1 - core], near_mlp, mlp_send.at[0], mlp_recv.at[0], (flip1(d), t))
    far_same = remote_copy(mlp_hbm.at[:, core], far_mlp, mlp_send.at[1], mlp_recv.at[1], (d, flip2(t)))
    far_cross = remote_copy(mlp_hbm.at[:, 1 - core], far_mlp, mlp_send.at[2], mlp_recv.at[1], (flip1(d), flip2(t)))
    keep_mlp = pltpu.make_async_copy(mlp_hbm.at[:, core], near_mlp, load_sem.at[0])

    @pl.when(home)
    def _():
        near_copy.start()
        keep_mlp.start()

    @pl.when(away)
    def _():
        far_same.start()
        far_cross.start()

    core_w_copy = remote_copy(gwo_hbm.at[:, 1 - core], core_w, core_send.at[0], core_recv.at[0], (flip1(d), t))
    core_q_copy = remote_copy(gq_hbm.at[:, 1 - core], core_q, core_send.at[1], core_recv.at[1], (flip1(d), t))
    load_w = pltpu.make_async_copy(gwo_hbm.at[:, core], own_w, load_sem.at[1])
    load_q = pltpu.make_async_copy(gq_hbm.at[:, core], own_q, load_sem.at[2])
    core_w_copy.start()
    core_q_copy.start()
    load_w.start()
    load_q.start()

    vec[...] = jnp.zeros_like(vec)
    for row, ref in enumerate((gaa_ref, gam_ref, gsu_ref, gsg_ref)):
        vec[row : row + 1, :] = ref[...]
    vec[4:5, 0:cols] = gain_ref[...]
    got_v[d] = vec[...]

    def v_copy(i):
        return remote_copy(vec, got_v.at[d], v_send.at[i], v_recv.at[i], (dp_peer(i), t))

    over(count - 1, lambda i: v_copy(i).start())

    def chip_copy(own, got, sends, recvs, i):
        return remote_copy(own.at[chip_peer(i)], got.at[chip], sends.at[i], recvs.at[i], (2 * chip_peer(i) + core, t))

    def w_copy(i):
        return chip_copy(own_w, got_w, w_send, w_recv, i)

    def q_copy(i):
        return chip_copy(own_q, got_q, q_send, q_recv, i)

    def join(own, other, got):
        def one(e):
            own[e] = (own[e].astype(f32) + other[e].astype(f32)).astype(bf)

        over(half, one)
        got[chip] = own[chip]

    load_w.wait()
    core_w_copy.wait_recv()
    join(own_w, core_w, got_w)
    over(half - 1, lambda i: w_copy(i).start())
    load_q.wait()
    core_q_copy.wait_recv()
    join(own_q, core_q, got_q)
    over(half - 1, lambda i: q_copy(i).start())

    def total_of(got):
        return lax.fori_loop(1, half, lambda i, total: total + got[i].astype(f32), got[0].astype(f32))

    over(half - 1, lambda i: w_copy(i).wait_recv())
    wo_mid[...] = total_of(got_w).astype(bf)

    def z_copy(k):
        return remote_copy(
            wo_mid.at[:, tile_at(line_peer(k), cols)], got_z.at[t], z_send.at[k - 1], z_recv.at[k - 1], (d, line_peer(k))
        )

    for k in (1, 2, 3):
        z_copy(k).start()
    got_z[t] = wo_mid[:, tile_at(t, cols)]

    over(count - 1, lambda i: v_copy(i).wait_recv())
    even, odd = lax.fori_loop(
        1, half, lambda i, total: (total[0] + got_v[2 * i], total[1] + got_v[2 * i + 1]), (got_v[0], got_v[1])
    )
    both = even + odd
    vec_mid[...] = jnp.concatenate([both[0:2], even[2:3], odd[2:3], even[3:4], odd[3:4], both[4:5], both[4:5]], axis=0)

    def s_copy(k):
        return remote_copy(vec_mid, got_s.at[t], s_send.at[k - 1], s_recv.at[k - 1], (d, line_peer(k)))

    for k in (1, 2, 3):
        s_copy(k).start()
    got_s[t] = vec_mid[...]

    over(half - 1, lambda i: q_copy(i).wait_recv())
    total = total_of(got_q)
    for m, ref in enumerate((q_out, k_out, v_out)):
        ref[...] = total[:, m * cols : (m + 1) * cols]

    for k in (1, 2, 3):
        z_copy(k).wait_recv()
        s_copy(k).wait_recv()
    wo_out[...] = got_z[0].astype(f32) + got_z[1].astype(f32) + got_z[2].astype(f32) + got_z[3].astype(f32)
    shared = got_s[0] + got_s[1] + got_s[2] + got_s[3]
    aa_out[...] = shared[0:1]
    am_out[...] = shared[1:2]
    pairs = (got_s[0] + got_s[2], got_s[1] + got_s[3])
    for s in range(4):
        su_out[:, s * width : (s + 1) * width] = pairs[s % 2][2 + s // 2 : 3 + s // 2]
        sg_out[:, s * width : (s + 1) * width] = pairs[s % 2][4 + s // 2 : 5 + s // 2] * math.sqrt(D)
        gain_out[:, s * cols : (s + 1) * cols] = got_s[s][6:7, 0:cols]

    far_same.wait_recv()

    @pl.when(home)
    def _():
        keep_mlp.wait()
        near_copy.wait_send()

    @pl.when(away)
    def _():
        near_copy.wait_recv()
        far_same.wait_send()
        far_cross.wait_send()

    for m, ref in enumerate((up_out, gate_out, down_out)):
        ref[...] = near_mlp[m].astype(f32) + far_mlp[m].astype(f32)

    core_w_copy.wait_send()
    core_q_copy.wait_send()
    over(count - 1, lambda i: v_copy(i).wait_send())

    def drain(i):
        w_copy(i).wait_send()
        q_copy(i).wait_send()

    over(half - 1, drain)
    for k in (1, 2, 3):
        z_copy(k).wait_send()
        s_copy(k).wait_send()


def settle_call(count, gq, gwo, mlp, gain_sum, gaa, gam, gsu, gsg):
    width, three = gq.shape
    half = count // 2
    cols = three // 3
    wrows = width // count
    hid = mlp.shape[2]
    bf, f32 = jnp.bfloat16, jnp.float32
    anywhere = pl.BlockSpec(memory_space=pl.ANY)
    dma = pltpu.SemaphoreType.DMA
    shape = jax.ShapeDtypeStruct
    return pl.pallas_call(
        functools.partial(settle_body, count),
        out_shape=(shape((wrows, cols), f32),) * 4
        + (shape((wrows, hid), f32),) * 3
        + (
            shape((1, 4 * cols), f32),
            shape((1, width), f32),
            shape((1, width), f32),
            shape((1, 4 * hid), f32),
            shape((1, 4 * hid), f32),
        ),
        in_specs=[anywhere] * 3 + [vmem()] * 5,
        out_specs=(vmem(),) * 12,
        scratch_shapes=[pltpu.VMEM((half, wrows, three), bf)] * 3
        + [pltpu.VMEM((half, wrows, width), bf)] * 3
        + [
            pltpu.VMEM((wrows, width), bf),
            pltpu.VMEM((4, wrows, cols), bf),
            pltpu.VMEM((3, wrows, hid), bf),
            pltpu.VMEM((3, wrows, hid), bf),
            pltpu.VMEM((8, width), f32),
            pltpu.VMEM((count, 8, width), f32),
            pltpu.VMEM((8, width), f32),
            pltpu.VMEM((4, 8, width), f32),
            dma((3,)),
            dma((2,)), dma((2,)),
            dma((half - 1,)), dma((half - 1,)), dma((half - 1,)), dma((half - 1,)),
            dma((3,)), dma((3,)),
            dma((count - 1,)), dma((count - 1,)),
            dma((3,)), dma((3,)),
            dma((3,)), dma((2,)),
        ],
        compiler_params=pltpu.CompilerParams(vmem_limit_bytes=VMEM_LIMIT, collective_id=5, has_side_effects=True),
        cost_estimate=pl.CostEstimate(flops=10**9, bytes_accessed=10**7, transcendentals=0),
        name="settle",
    )(
        gq.reshape(half, 2, wrows, three),
        gwo.reshape(half, 2, wrows, width),
        mlp.reshape(3, 2, wrows, hid),
        gain_sum, gaa, gam, gsu, gsg,
    )


def same_core_groups(dp_count):
    return [list(range(parity, dp_count, 2)) for parity in range(2)]


def layout(order_row, length_row):
    group_rows = order_row.shape[0]
    places = jnp.arange(group_rows, dtype=jnp.int32)
    seg_ends = jnp.cumsum(length_row, dtype=jnp.int32)
    seg_starts = seg_ends - length_row
    seg_first = jnp.max(
        jnp.where(seg_starts[None, :] <= places[:, None], seg_starts[None, :], 0), axis=1
    )
    half_width = HD // 2
    inv_freq = jnp.exp(
        jnp.arange(half_width, dtype=jnp.float32) * (-math.log(10000.0) / half_width)
    )
    depth = jnp.sum(
        jnp.where(order_row[None, :] == places[:, None], (places - seg_first)[None, :], 0), axis=1, dtype=jnp.int32
    )
    angles = depth.astype(jnp.float32)[:, None] * inv_freq[None, :]
    return (seg_first, angles)


def on_device(
    tokens,
    w_query,
    w_key,
    w_value,
    w_out_t,
    w_up,
    w_gate,
    w_down_t,
    scale_qk,
    alpha_attn,
    scale_up,
    scale_gate,
    alpha_mlp,
    order,
    lengths,
    cotangent,
):
    tensor_rank = lax.axis_index("tensor")
    head_cols = w_query.shape[1]
    hidden_cols = w_up.shape[1]
    qk_gains = lax.dynamic_slice_in_dim(scale_qk, tensor_rank * head_cols, head_cols)
    dp_count, tensor_count = lax.axis_size("dp"), lax.axis_size("tensor")
    hidden_rank = lax.rem(tensor_rank, 2) + 2 * lax.rem(lax.axis_index("dp"), 2)
    up_gains = lax.dynamic_slice_in_dim(scale_up, hidden_rank * hidden_cols, hidden_cols)[None, :]
    gate_gains = lax.dynamic_slice_in_dim(
        scale_gate, hidden_rank * hidden_cols, hidden_cols
    )[None, :] * math.sqrt(D)
    order_row = order[0]
    seg_first, angles = layout(order_row, lengths[0])
    group_rows = order_row.shape[0]
    low = lax.slice(seg_first, (0,), (group_rows,), (BLK,)) // BLK
    start = seg_first[None, :]
    order_col = order_row[:, None]
    cosine, sine = jnp.cos(angles), jnp.sin(angles)
    cos_table = jnp.concatenate([cosine] * 4, axis=1)
    sin_table = jnp.concatenate([-sine, sine] * 2, axis=1)

    pair, near_tokens, wqkv, wo_every = spread_call(
        dp_count, tokens, w_up, w_gate, w_down_t, w_query, w_key, w_value, w_out_t
    )
    mlp_parts = lax.all_gather(
        pair, "dp", axis=0, tiled=False, axis_index_groups=same_core_groups(dp_count)
    )
    queries, key_rows, value_rows, raw, all_tokens = project_call(
        tokens, near_tokens, wqkv, cos_table, sin_table, order_col, qk_gains[None, :]
    )
    attended, log_totals, attended_plain = attn_fwd(low, start, order, queries, key_rows, value_rows)
    out_rows, grad_att_rows, mlp_grads, wo_grads, grad_h1_kept, grad_alpha_a, grad_alpha_m, grad_su, grad_sv = middle_call(
        2,
        attended_plain,
        wo_every,
        mlp_parts,
        tokens,
        cotangent,
        alpha_attn[None, :],
        alpha_mlp[None, :],
        up_gains,
        gate_gains,
    )
    grad_qkv = attn_bwd(
        low, start, order, order_col, log_totals, queries, key_rows, value_rows, attended, grad_att_rows
    )
    mlp_sums = lax.psum_scatter(
        mlp_grads, "dp", scatter_dimension=0, tiled=False, axis_index_groups=same_core_groups(dp_count)
    )
    grad_tokens, grad_q, gain_sum = tail_call(
        grad_qkv, raw, cos_table, sin_table, wqkv, all_tokens, grad_h1_kept, qk_gains[None, :]
    )
    settled = settle_call(
        dp_count, grad_q, wo_grads, mlp_sums, gain_sum, grad_alpha_a, grad_alpha_m, grad_su, grad_sv
    )
    weights, vectors = settled[:7], [v.reshape(-1) for v in settled[7:]]
    grad_gain, sum_aa, sum_am, sum_su, sum_sv = vectors
    return (out_rows, grad_tokens, *weights, grad_gain, sum_aa, sum_su, sum_sv, sum_am)


def solution(mesh):
    return jax.shard_map(
        on_device,
        mesh=mesh,
        in_specs=(
            P(("dp", "tensor"), None),
            P("dp", "tensor"),
            P("dp", "tensor"),
            P("dp", "tensor"),
            P("dp", "tensor"),
            P("dp", "tensor"),
            P("dp", "tensor"),
            P("dp", "tensor"),
            P(),
            P(),
            P(),
            P(),
            P(),
            P("dp", None),
            P("dp", None),
            P(("dp", "tensor"), None),
        ),
        out_specs=(
            P(("dp", "tensor"), None),
            P(("dp", "tensor"), None),
            P("dp", "tensor"),
            P("dp", "tensor"),
            P("dp", "tensor"),
            P("dp", "tensor"),
            P("dp", "tensor"),
            P("dp", "tensor"),
            P("dp", "tensor"),
            P(),
            P(),
            P(),
            P(),
            P(),
        ),
        check_vma=False,
    )
```

```python
import functools
import math

import jax
import jax.numpy as jnp
from jax import lax
from jax.experimental import pallas as pl
from jax.experimental.pallas import tpu as pltpu
from jax.sharding import PartitionSpec as P

D = 1024
HD = 64
BLK = 256
LOG2E = 1.4426950408889634
VMEM_LIMIT = 60 * 1024 * 1024


def dot_ab(a, b):
    return lax.dot_general(a, b, (((1,), (0,)), ((), ())), preferred_element_type=jnp.float32)


def dot_abt(a, b):
    return lax.dot_general(a, b, (((1,), (1,)), ((), ())), preferred_element_type=jnp.float32)


def split_heads(block, heads):
    lane_head = lax.broadcasted_iota(jnp.int32, block.shape, 1) // HD
    zero = jnp.zeros_like(block)
    return jnp.concatenate([jnp.where(lane_head == h, block, zero) for h in range(heads)], axis=0)


def attn_fwd_body(
    low_ref, start_ref, order_row, q_ref, k_ref, v_ref, out_ref, lse_ref, plain_ref, vt_ref, qs_ref, acc_ref, sum_ref
):
    rows, cols = q_ref.shape
    heads = cols // HD
    scale = math.sqrt(HD) * LOG2E
    for b in range(rows // BLK):
        vt_ref[:, b * BLK : (b + 1) * BLK] = v_ref[b * BLK : (b + 1) * BLK, :].T

    def one_block(i, _):
        base = pl.multiple_of(i * BLK, BLK)
        qs_ref[...] = split_heads(q_ref[pl.ds(base, BLK), :], heads)
        acc_ref[...] = jnp.zeros_like(acc_ref)
        sum_ref[...] = jnp.zeros_like(sum_ref)
        start = jnp.concatenate([start_ref[:, pl.ds(base, BLK)]] * heads, axis=1)
        own = lax.broadcasted_iota(jnp.int32, (1, heads * BLK), 1) % BLK + base

        def step(j, causal):
            at = pl.multiple_of(j * BLK, BLK)
            scores = dot_abt(k_ref[pl.ds(at, BLK), :], qs_ref[...])
            place = lax.broadcasted_iota(jnp.int32, scores.shape, 0) + at
            keep = place >= start
            if causal:
                keep = keep & (place <= own)
            probs = jnp.where(keep, jnp.exp2(scores * scale), 0.0)
            sum_ref[...] += jnp.sum(probs, axis=0, keepdims=True)
            probs_b = probs.astype(jnp.bfloat16)
            for h in range(heads):
                acc_ref[h * HD : (h + 1) * HD, :] += dot_ab(
                    vt_ref[h * HD : (h + 1) * HD, pl.ds(at, BLK)], probs_b[:, h * BLK : (h + 1) * BLK]
                )

        lax.fori_loop(low_ref[i], i, lambda j, c: (step(j, False), c)[1], 0)
        step(i, True)
        total = sum_ref[...]
        inv = 1.0 / total
        logs = jnp.log2(total)
        for h in range(heads):
            lse_ref[h : h + 1, pl.ds(base, BLK)] = logs[:, h * BLK : (h + 1) * BLK]
            acc_ref[h * HD : (h + 1) * HD, :] *= inv[:, h * BLK : (h + 1) * BLK]
        out_ref[pl.ds(base, BLK), :] = acc_ref[...].T.astype(jnp.bfloat16)
        return 0

    lax.fori_loop(0, rows // BLK, one_block, 0)
    over(rows // BLK, lambda b: to_token_order(b, order_row, out_ref, plain_ref))


def to_token_order(b, order_row, src, dst):
    at = pl.ds(pl.multiple_of(b * BLK, BLK), BLK)
    hot = lax.broadcasted_iota(jnp.int32, (BLK, src.shape[0]), 0) + b * BLK == order_row[...]
    dst[at, :] = dot_ab(hot.astype(jnp.float32).astype(jnp.bfloat16), src[...]).astype(dst.dtype)


def to_packed_order(b, order_col, src, dst):
    at = pl.ds(pl.multiple_of(b * BLK, BLK), BLK)
    hot = lax.broadcasted_iota(jnp.int32, (BLK, src.shape[0]), 1) == order_col[at, :]
    dst[at, :] = dot_ab(hot.astype(jnp.float32).astype(jnp.bfloat16), src[...]).astype(dst.dtype)


def over(count, body):
    lax.fori_loop(0, count, lambda i, carry: (body(i), carry)[1], 0)


def vmem():
    return pl.BlockSpec(memory_space=pltpu.VMEM)


def attn_fwd(low, start, order_row, q, k, v):
    rows, cols = q.shape
    heads = cols // HD
    return pl.pallas_call(
        attn_fwd_body,
        out_shape=(
            jax.ShapeDtypeStruct((rows, cols), jnp.bfloat16),
            jax.ShapeDtypeStruct((8, rows), jnp.float32),
            jax.ShapeDtypeStruct((rows, cols), jnp.bfloat16),
        ),
        in_specs=[pl.BlockSpec(memory_space=pltpu.SMEM)] + [vmem()] * 5,
        out_specs=(vmem(),) * 3,
        scratch_shapes=[
            pltpu.VMEM((cols, rows), jnp.bfloat16),
            pltpu.VMEM((heads * BLK, cols), jnp.bfloat16),
            pltpu.VMEM((cols, BLK), jnp.float32),
            pltpu.VMEM((1, heads * BLK), jnp.float32),
        ],
        compiler_params=pltpu.CompilerParams(vmem_limit_bytes=VMEM_LIMIT),
        cost_estimate=pl.CostEstimate(flops=4 * rows * rows * cols, bytes_accessed=8 * rows * cols, transcendentals=rows * rows * heads),
        name="attn_fwd",
    )(low, start, order_row, q, k, v)


def attn_bwd_body(
    low_ref, start_ref, order_row, order_col, lse_ref, q_ref, k_ref, v_ref, o_ref, grad_ref,
    plain_ref, kt_ref, qs_ref, gs_ref, dqt_ref, dk_acc, dv_acc, g_ref, packed,
):
    rows, cols = q_ref.shape
    heads = cols // HD
    root = math.sqrt(HD)
    scale = root * LOG2E
    for b in range(rows // BLK):
        kt_ref[:, b * BLK : (b + 1) * BLK] = k_ref[b * BLK : (b + 1) * BLK, :].T
    over(rows // BLK, lambda b: to_packed_order(b, order_col, grad_ref, g_ref))
    dk_acc[...] = jnp.zeros_like(dk_acc)
    dv_acc[...] = jnp.zeros_like(dv_acc)

    def one_block(i, _):
        base = pl.multiple_of(i * BLK, BLK)
        qs_ref[...] = split_heads(q_ref[pl.ds(base, BLK), :], heads)
        grads = g_ref[pl.ds(base, BLK), :]
        gs_ref[...] = split_heads(grads, heads)
        dqt_ref[...] = jnp.zeros_like(dqt_ref)
        start = jnp.concatenate([start_ref[:, pl.ds(base, BLK)]] * heads, axis=1)
        own = lax.broadcasted_iota(jnp.int32, (1, heads * BLK), 1) % BLK + base
        prod = (grads.astype(jnp.float32) * o_ref[pl.ds(base, BLK), :].astype(jnp.float32)).T
        delta = jnp.concatenate(
            [jnp.sum(prod[h * HD : (h + 1) * HD, :], axis=0, keepdims=True) for h in range(heads)], axis=1
        )
        lse = jnp.concatenate([lse_ref[h : h + 1, pl.ds(base, BLK)] for h in range(heads)], axis=1)

        def step(j, causal):
            at = pl.multiple_of(j * BLK, BLK)
            scores = dot_abt(k_ref[pl.ds(at, BLK), :], qs_ref[...])
            dprobs = dot_abt(v_ref[pl.ds(at, BLK), :], gs_ref[...])
            place = lax.broadcasted_iota(jnp.int32, scores.shape, 0) + at
            keep = place >= start
            if causal:
                keep = keep & (place <= own)
            probs = jnp.where(keep, jnp.exp2(scores * scale - lse), 0.0)
            dsc = (probs * (dprobs - delta)).astype(jnp.bfloat16)
            dv_acc[pl.ds(at, BLK), :] += dot_ab(probs.astype(jnp.bfloat16), gs_ref[...])
            dk_acc[pl.ds(at, BLK), :] += dot_ab(dsc, qs_ref[...])
            for h in range(heads):
                dqt_ref[h * HD : (h + 1) * HD, :] += dot_ab(
                    kt_ref[h * HD : (h + 1) * HD, pl.ds(at, BLK)], dsc[:, h * BLK : (h + 1) * BLK]
                )

        lax.fori_loop(low_ref[i], i, lambda j, c: (step(j, False), c)[1], 0)
        step(i, True)
        packed[pl.ds(base, BLK), 0:cols] = (dqt_ref[...].T * root).astype(packed.dtype)
        return 0

    lax.fori_loop(0, rows // BLK, one_block, 0)
    packed[:, cols : 2 * cols] = (dk_acc[...] * root).astype(packed.dtype)
    packed[:, 2 * cols : 3 * cols] = dv_acc[...].astype(packed.dtype)
    over(rows // BLK, lambda b: to_token_order(b, order_row, packed, plain_ref))


def attn_bwd(low, start, order_row, order_col, lse, q, k, v, o, g):
    rows, cols = q.shape
    heads = cols // HD
    return pl.pallas_call(
        attn_bwd_body,
        out_shape=jax.ShapeDtypeStruct((rows, 3 * cols), jnp.bfloat16),
        in_specs=[pl.BlockSpec(memory_space=pltpu.SMEM)] + [vmem()] * 9,
        out_specs=vmem(),
        scratch_shapes=[
            pltpu.VMEM((cols, rows), jnp.bfloat16),
            pltpu.VMEM((heads * BLK, cols), jnp.bfloat16),
            pltpu.VMEM((heads * BLK, cols), jnp.bfloat16),
            pltpu.VMEM((cols, BLK), jnp.float32),
            pltpu.VMEM((rows, cols), jnp.float32),
            pltpu.VMEM((rows, cols), jnp.float32),
            pltpu.VMEM((rows, cols), jnp.bfloat16),
            pltpu.VMEM((rows, 3 * cols), jnp.bfloat16),
        ],
        compiler_params=pltpu.CompilerParams(vmem_limit_bytes=VMEM_LIMIT),
        cost_estimate=pl.CostEstimate(flops=10 * rows * rows * cols, bytes_accessed=16 * rows * cols, transcendentals=rows * rows * heads),
        name="attn_bwd",
    )(low, start, order_row, order_col, lse, q, k, v, o, g)


MESH_ID = pl.DeviceIdType.MESH
EPS = 1e-06
TILE = 256
STRIP = 64
WIDE_STRIP = 192


def flip1(index):
    return index + 1 - 2 * lax.rem(index, 2)


def flip2(index):
    return index + 2 - 4 * (index // 2)


def tile_at(index, size):
    if isinstance(index, int):
        return pl.ds(index * size, size)
    return pl.ds(pl.multiple_of(index * size, size), size)


def row_sum(value):
    return jnp.sum(value, axis=-1, keepdims=True)


def middle_body(
    att_ref, wo_hbm, w_hbm, tok_hbm, cot_hbm, aa_ref, am_ref, su_all, sg_all,
    out_ref, datt_ref, gw_hbm, gwo_hbm, dh1_ref, gaa_ref, gam_ref, gsu_ref, gsg_ref,
    wo, wall, tok, cot, parts, mids, dbms, mid_t, dbm_t, ups, gates, mixed,
    middle, branch, dh2, own_part, send_a, recv_a, send_d, recv_d, send_z, recv_z,
    gw, gwo, dparts, su_ref, sg_ref, load_sems, store_sems, hop_send, hop_recv, a2a_send, a2a_recv, d2a_send, d2a_recv, part_send, part_recv,
):
    d = lax.axis_index("dp")
    t = lax.axis_index("tensor")
    rows, width = tok.shape
    heads_w = att_ref.shape[1]
    hid = wall.shape[2]
    nq = w_hbm.shape[0]
    qrows = w_hbm.shape[2]
    chunks = hop_send.shape[0] // 6
    crow = rows // chunks
    core_peer = (flip1(d), t)
    z_peer = (d, flip1(t))
    line = [t, flip1(t), flip2(t), 3 - t]

    barrier = pltpu.get_barrier_semaphore()
    for peer in [core_peer] + [(d, line[k]) for k in (1, 2, 3)]:
        pl.semaphore_signal(barrier, inc=1, device_id=peer, device_id_type=MESH_ID)
    pl.semaphore_wait(barrier, 4)

    def remote(src, dst, ssem, rsem, peer):
        return pltpu.make_async_remote_copy(
            src_ref=src, dst_ref=dst, send_sem=ssem, recv_sem=rsem, device_id=peer, device_id_type=MESH_ID
        )

    a2a = [
        remote(att_ref.at[tile_at(line[k], rows), :], parts.at[k - 1], a2a_send.at[k - 1], a2a_recv.at[k - 1], (d, line[k]))
        for k in (1, 2, 3)
    ]
    for copy in a2a:
        copy.start()
    loads = [
        pltpu.make_async_copy(wo_hbm, wo, load_sems.at[0]),
        pltpu.make_async_copy(tok_hbm, tok, load_sems.at[1]),
        pltpu.make_async_copy(cot_hbm, cot, load_sems.at[2]),
    ]
    wloads = [
        [
            pltpu.make_async_copy(w_hbm.at[q, m], wall.at[m, pl.ds(q * qrows, qrows), :], load_sems.at[3 + m * nq + q])
            for q in range(nq)
        ]
        for m in range(3)
    ]
    for copy in loads + wloads[0] + wloads[1] + wloads[2]:
        copy.start()

    shard = lax.rem(t, 2) + 2 * lax.rem(d, 2)
    su_ref[...] = su_all[:, tile_at(shard, hid)]
    sg_ref[...] = sg_all[:, tile_at(shard, hid)] * math.sqrt(D)
    gsu_ref[...] = jnp.zeros_like(gsu_ref)
    gsg_ref[...] = jnp.zeros_like(gsg_ref)
    gam_ref[...] = jnp.zeros_like(gam_ref)
    gaa_ref[...] = jnp.zeros_like(gaa_ref)

    loads[0].wait()
    for copy in a2a:
        copy.wait_recv()

    def project(n):
        cols = tile_at(n, TILE)
        total = dot_abt(att_ref[tile_at(t, rows), :], wo[cols, tile_at(t, heads_w)])
        for k in (1, 2, 3):
            total += dot_abt(parts[k - 1], wo[cols, tile_at(line[k], heads_w)])
        branch[:, cols] = total

    over(width // TILE, project)
    loads[1].wait()

    def hop(buf, phase, ch, kind):
        part = tile_at(ch, crow)
        index = (phase * chunks + ch) * 3 + kind
        src, dst, peer = ((0, 2, z_peer), (0, 1, core_peer), (2, 3, core_peer))[kind]
        return remote(buf.at[src, part, :], buf.at[dst, part, :], hop_send.at[index], hop_recv.at[index], peer)

    def strips(ch, body):
        over(crow // STRIP, lambda i: body(tile_at(i + ch * (crow // STRIP), STRIP)))

    def unit_of(value):
        factor = lax.rsqrt(row_sum(value * value) + EPS)
        return value * factor, factor

    def make_middle(at):
        inputs = tok[at, :].astype(jnp.float32)
        norm_a, factor_a = unit_of(branch[at, :])
        mid, factor_mid = unit_of(inputs + aa_ref[...] * (norm_a - inputs))
        return inputs, norm_a, factor_a, mid, factor_mid

    def first(at):
        mid = make_middle(at)[3]
        middle[at, :] = mid
        mids[0, at, :] = mid.astype(jnp.bfloat16)

    for ch in range(chunks):
        strips(ch, first)
        hop(mids, 0, ch, 0).start()
        hop(mids, 0, ch, 1).start()

    for m in range(3):
        for copy in wloads[m]:
            copy.wait()

    def within(slot, at):
        return pl.ds(pl.multiple_of(slot * rows + at.start, STRIP), at.size)

    def forward_rows(slot, at, store, ready):
        where = within(slot, at)

        def hidden(n):
            cols = tile_at(n, TILE)
            x = mids[slot, at, :]
            up = dot_ab(x, wall[0, :, cols])
            gate_raw = dot_ab(x, wall[1, :, cols])
            gate = gate_raw * sg_ref[:, cols]
            silu = gate / (1.0 + jnp.exp(-gate))
            ups[where, cols] = up.astype(jnp.bfloat16)
            gates[where, cols] = gate_raw.astype(jnp.bfloat16)
            mixed[where, cols] = (up * su_ref[:, cols] * silu).astype(jnp.bfloat16)

        over(hid // TILE, hidden)
        ready()

        def down(n):
            cols = tile_at(n, TILE)
            store(at, cols, dot_abt(mixed[where, :], wall[2, cols, :]))

        over(width // TILE, down)

    def backward_rows(slot, at, store, ready):
        where = within(slot, at)

        def hidden(n):
            cols = tile_at(n, TILE)
            dmix = dot_ab(dbms[slot, at, :], wall[2, :, cols])
            up_raw = ups[where, cols].astype(jnp.float32)
            gate_raw = gates[where, cols].astype(jnp.float32)
            gate = gate_raw * sg_ref[:, cols]
            sig = 1.0 / (1.0 + jnp.exp(-gate))
            d_up = dmix * (gate * sig)
            d_gate = dmix * (up_raw * su_ref[:, cols]) * (sig * (1.0 + gate * (1.0 - sig)))
            gsu_ref[:, cols] += jnp.sum(d_up * up_raw, axis=0, keepdims=True)
            gsg_ref[:, cols] += jnp.sum(d_gate * gate_raw, axis=0, keepdims=True)
            ups[where, cols] = (d_up * su_ref[:, cols]).astype(jnp.bfloat16)
            gates[where, cols] = (d_gate * sg_ref[:, cols]).astype(jnp.bfloat16)

        over(hid // TILE, hidden)
        ready()

        def down(n):
            cols = tile_at(n, TILE)
            store(at, cols, dot_abt(ups[where, :], wall[0, cols, :]) + dot_abt(gates[where, :], wall[1, cols, :]))

        over(width // TILE, down)

    def part_copy(phase, kind, ch):
        part = tile_at(ch, crow)
        index = (phase * 3 + kind) * chunks + ch
        src, dst, peer = ((send_a, recv_a, core_peer), (send_d, recv_d, core_peer), (send_z, recv_z, z_peer))[kind]
        return remote(src.at[part, :], dst.at[part, :], part_send.at[index], part_recv.at[index], peer)

    def nothing():
        pass

    def tensor_pass(phase, buf, rows_fn, fillers):
        def keep_own(at, cols, value):
            own_part[at, cols] = value

        def to(ref):
            def store(at, cols, value):
                ref[at, cols] = value.astype(jnp.bfloat16)

            return store

        def to_z(at, cols, value):
            send_z[at, cols] = (value + recv_d[at, cols].astype(jnp.float32)).astype(jnp.bfloat16)

        rows_fn(0, tile_at(0, rows), keep_own, nothing)
        for ch in range(chunks):
            hop(buf, phase, ch, 1).wait_recv()
        if phase == 1:
            for ch in range(chunks):
                part_copy(0, 0, ch).wait_send()
        rows_fn(1, tile_at(0, rows), to(send_a), nothing)
        for ch in range(chunks):
            part_copy(phase, 0, ch).start()
        fillers[0]()
        def chunk(ch):
            hop(buf, phase, ch, 0).wait_recv()
            hop(buf, phase, ch, 2).start()
            at = tile_at(ch, crow)
            hop(buf, phase, ch, 2).wait_recv()
            if phase == 1:
                part_copy(0, 1, ch).wait_send()
            rows_fn(3, at, to(send_d), nothing)
            part_copy(phase, 1, ch).start()

            def ready():
                part_copy(phase, 1, ch).wait_recv()
                if phase == 1:
                    part_copy(0, 2, ch).wait_send()

            rows_fn(2, at, to_z, ready)
            part_copy(phase, 2, ch).start()

        over(chunks, chunk)
        fillers[1]()

    def transpose_into(dst, buf, slots):
        per_slot = rows // 128

        def one(i):
            slot = slots[0] + i // per_slot
            at = tile_at(lax.rem(i, per_slot), 128)
            to = tile_at(slots[0] * per_slot + i, 128)
            for n in range(width // TILE):
                dst[n * TILE : (n + 1) * TILE, to] = buf[slot, at, n * TILE : (n + 1) * TILE].T

        over(len(slots) * per_slot, one)

    tensor_pass(
        0, mids, forward_rows,
        [lambda: transpose_into(mid_t, mids, (0, 1)), lambda: transpose_into(mid_t, mids, (2, 3))],
    )

    loads[2].wait()

    def turn(at):
        mid = middle[at, :]
        branch_m = own_part[at, :] + recv_a[at, :].astype(jnp.float32) + recv_z[at, :].astype(jnp.float32)
        norm_m, factor_m = unit_of(branch_m)
        alpha = am_ref[...]
        y, factor_y = unit_of(mid + alpha * (norm_m - mid))
        out_ref[at, :] = y.astype(jnp.bfloat16)
        dy = cot[at, :].astype(jnp.float32)
        grad = factor_y * (dy - y * row_sum(y * dy))
        gam_ref[...] += jnp.sum(grad * (norm_m - mid), axis=0, keepdims=True)
        back = alpha * grad
        dbms[0, at, :] = (factor_m * (back - norm_m * row_sum(norm_m * back))).astype(jnp.bfloat16)
        dh2[at, :] = grad - back

    for ch in range(chunks):
        part_copy(0, 0, ch).wait_recv()
        part_copy(0, 2, ch).wait_recv()
        strips(ch, turn)
        hop(dbms, 1, ch, 0).start()
        hop(dbms, 1, ch, 1).start()

    def weight_grads():
        transpose_into(dbm_t, dbms, (2, 3))
        for m, (lhs, rhs) in enumerate(((mid_t, ups), (mid_t, gates), (dbm_t, mixed))):

            def block(i):
                q = i // (hid // TILE)
                cols = tile_at(lax.rem(i, hid // TILE), TILE)
                value = dot_ab(lhs[tile_at(q, TILE), :], rhs[:, cols])
                gw[m, tile_at(q, TILE), cols] = value.astype(jnp.bfloat16)

            over((width // TILE) * (hid // TILE), block)
            for q in range(nq):
                grad_store(m, q).start()

    def grad_store(m, q):
        return pltpu.make_async_copy(gw.at[m, pl.ds(q * qrows, qrows), :], gw_hbm.at[q, m], store_sems.at[m * nq + q])

    tensor_pass(1, dbms, backward_rows, [lambda: transpose_into(dbm_t, dbms, (0, 1)), weight_grads])

    def last(at):
        inputs, norm_a, factor_a, mid, factor_mid = make_middle(at)
        grad_mid = dh2[at, :] + own_part[at, :] + recv_a[at, :].astype(jnp.float32) + recv_z[at, :].astype(jnp.float32)
        grad = factor_mid * (grad_mid - mid * row_sum(mid * grad_mid))
        gaa_ref[...] += jnp.sum(grad * (norm_a - inputs), axis=0, keepdims=True)
        back = aa_ref[...] * grad
        dh1_ref[at, :] = grad - back
        mids[0, at, :] = (factor_a * (back - norm_a * row_sum(norm_a * back))).astype(jnp.bfloat16)

    for ch in range(chunks):
        hop(mids, 0, ch, 0).wait_send()
        hop(mids, 0, ch, 1).wait_send()
        part_copy(1, 0, ch).wait_recv()
        part_copy(1, 2, ch).wait_recv()
        strips(ch, last)

    dback = [
        remote(dparts.at[k], datt_ref.at[tile_at(t, rows), :], d2a_send.at[k - 1], d2a_recv.at[k - 1], (d, line[k]))
        for k in (1, 2, 3)
    ]
    for k in (3, 2, 1, 0):
        value = dot_ab(mids[0], wo[:, tile_at(line[k], heads_w)]).astype(jnp.bfloat16)
        if k:
            dparts[k] = value
            dback[k - 1].start()
        else:
            datt_ref[tile_at(t, rows), :] = value

    transpose_into(mid_t, mids, (0,))

    def out_grad(n):
        at = tile_at(n, TILE)
        lhs = mid_t[at, 0:rows]
        gwo[at, tile_at(t, heads_w)] = dot_ab(lhs, att_ref[tile_at(t, rows), :]).astype(jnp.bfloat16)
        for k in (1, 2, 3):
            gwo[at, tile_at(line[k], heads_w)] = dot_ab(lhs, parts[k - 1]).astype(jnp.bfloat16)

    over(width // TILE, out_grad)
    wo_store = pltpu.make_async_copy(gwo, gwo_hbm, store_sems.at[3 * nq])
    wo_store.start()

    for k in (1, 2, 3):
        remote(
            dparts.at[k], datt_ref.at[tile_at(line[k], rows), :], d2a_send.at[k - 1], d2a_recv.at[k - 1], (d, line[k])
        ).wait()
    for copy in a2a:
        copy.wait_send()
    for ch in range(chunks):
        hop(mids, 0, ch, 2).wait_send()
        for kind in range(3):
            hop(dbms, 1, ch, kind).wait_send()
            part_copy(1, kind, ch).wait_send()
    for m in range(3):
        for q in range(nq):
            grad_store(m, q).wait()
    wo_store.wait()


def middle_call(chunks, attended, wo, w_parts, tokens, cotangent, alpha_a, alpha_m, su, sg):
    rows, width = tokens.shape
    group, heads_w = attended.shape
    nq, _, qrows, hid = w_parts.shape
    bf, f32 = jnp.bfloat16, jnp.float32
    anywhere = pl.BlockSpec(memory_space=pl.ANY)
    dma = pltpu.SemaphoreType.DMA
    return pl.pallas_call(
        middle_body,
        out_shape=(
            jax.ShapeDtypeStruct((rows, width), bf),
            jax.ShapeDtypeStruct((group, heads_w), bf),
            jax.ShapeDtypeStruct((nq, 3, qrows, hid), bf),
            jax.ShapeDtypeStruct((width, width), bf),
            jax.ShapeDtypeStruct((rows, width), f32),
            jax.ShapeDtypeStruct((1, width), f32),
            jax.ShapeDtypeStruct((1, width), f32),
            jax.ShapeDtypeStruct((1, hid), f32),
            jax.ShapeDtypeStruct((1, hid), f32),
        ),
        in_specs=[vmem(), anywhere, anywhere, anywhere, anywhere] + [vmem()] * 4,
        out_specs=(vmem(), vmem(), anywhere, anywhere) + (vmem(),) * 5,
        scratch_shapes=[
            pltpu.VMEM((width, width), bf),
            pltpu.VMEM((3, width, hid), bf),
            pltpu.VMEM((rows, width), bf),
            pltpu.VMEM((rows, width), bf),
            pltpu.VMEM((3, rows, heads_w), bf),
            pltpu.VMEM((4, rows, width), bf),
            pltpu.VMEM((4, rows, width), bf),
            pltpu.VMEM((width, 4 * rows), bf),
            pltpu.VMEM((width, 4 * rows), bf),
            pltpu.VMEM((4 * rows, hid), bf),
            pltpu.VMEM((4 * rows, hid), bf),
            pltpu.VMEM((4 * rows, hid), bf),
            pltpu.VMEM((rows, width), f32),
            pltpu.VMEM((rows, width), f32),
            pltpu.VMEM((rows, width), f32),
            pltpu.VMEM((rows, width), f32),
        ]
        + [pltpu.VMEM((rows, width), bf)] * 6
        + [
            pltpu.VMEM((3, width, hid), bf),
            pltpu.VMEM((width, width), bf),
            pltpu.VMEM((4, rows, heads_w), bf),
            pltpu.VMEM((1, hid), f32),
            pltpu.VMEM((1, hid), f32),
            dma((3 + 3 * nq,)),
            dma((3 * nq + 1,)),
            dma((6 * chunks,)),
            dma((6 * chunks,)),
            dma((3,)),
            dma((3,)),
            dma((3,)),
            dma((3,)),
            dma((6 * chunks,)),
            dma((6 * chunks,)),
        ],
        compiler_params=pltpu.CompilerParams(vmem_limit_bytes=67000000, collective_id=1, has_side_effects=True),
        cost_estimate=pl.CostEstimate(flops=10**11, bytes_accessed=10**8, transcendentals=10**6),
        name="middle",
    )(attended, wo, w_parts, tokens, cotangent, alpha_a, alpha_m, su, sg)


def remote_copy(src, dst, send_sem, recv_sem, peer):
    return pltpu.make_async_remote_copy(
        src_ref=src, dst_ref=dst, send_sem=send_sem, recv_sem=recv_sem, device_id=peer, device_id_type=MESH_ID
    )


def greet(peers):
    barrier = pltpu.get_barrier_semaphore()
    for peer in peers:
        pl.semaphore_signal(barrier, inc=1, device_id=peer, device_id_type=MESH_ID)
    pl.semaphore_wait(barrier, len(peers))


def rope_tables(order_ref, length_ref, cos_out, sin_out, col_out, start_out):
    group = order_ref.shape[1]
    lanes = cos_out.shape[1]
    places = lax.broadcasted_iota(jnp.int32, (1, group), 1)
    first = jnp.zeros((1, group), jnp.int32)
    begin = jnp.int32(0)
    for s in range(1, length_ref.shape[1]):
        begin = begin + length_ref[0, s - 1]
        first = jnp.where(places >= begin, begin, first)
    start_out[...] = first
    depth = (places - first).astype(jnp.float32)
    order = order_ref[...]
    order_f = order.astype(jnp.float32)
    lane = lax.broadcasted_iota(jnp.int32, (1, lanes), 1)
    half_width = HD // 2
    freq = jnp.exp((lane % half_width).astype(jnp.float32) * (-math.log(10000.0) / half_width))
    sign = jnp.where(lane % HD < half_width, -1.0, 1.0)

    def block(b):
        at = tile_at(b, 128)
        own = lax.broadcasted_iota(jnp.int32, (128, group), 0) + b * 128
        col_out[at, :] = row_sum(jnp.where(own == places, order_f, 0.0)).astype(jnp.int32)
        angles = row_sum(jnp.where(own == order, depth, 0.0)) * freq
        cos_out[at, :] = jnp.cos(angles)
        sin_out[at, :] = jnp.sin(angles) * sign

    over(group // 128, block)


def spread_body(
    count, tok, w_up, w_gate, w_down, wq, wk, wv, wo, order_ref, length_ref,
    pair, tok2, wqkv, wo_all, cos_out, sin_out, col_out, start_out,
    own_mlp, own_att, wo_rows, load_sem, keep_sem, a_send, a_recv, b_send, b_recv, tok_send, tok_recv,
    qkv_send, qkv_recv, oz_send, oz_recv, oq_send, oq_recv, oc_send, oc_recv,
):
    d = lax.axis_index("dp")
    t = lax.axis_index("tensor")
    core = lax.rem(d, 2)
    home = core == t // 2
    far = (d - core + t // 2, flip2(t))
    wrows, wcols = wq.shape
    half = count // 2
    mlp = (w_up, w_gate, w_down)
    att = (wq, wk, wv)
    mine = tile_at(d, wrows)
    side = tile_at(core, wrows)
    other_side = tile_at(1 - core, wrows)

    barrier = pltpu.get_barrier_semaphore()

    def dp_peer(i):
        return lax.rem(d + 1 + i, count)

    def hello(i):
        pl.semaphore_signal(barrier, inc=1, device_id=(dp_peer(i), t), device_id_type=MESH_ID)

    over(count - 1, hello)
    for k in (1, 2, 3):
        pl.semaphore_signal(barrier, inc=1, device_id=(d, lax.rem(t + k, 4)), device_id_type=MESH_ID)
    pl.semaphore_signal(barrier, inc=1, device_id=(flip1(d), flip2(t)), device_id_type=MESH_ID)
    pl.semaphore_wait(barrier, count + 3)

    def b_copy(m):
        return remote_copy(mlp[m], pair.at[m, side, :], b_send.at[m], b_recv.at[core * 3 + m], far)

    def a_copy(m):
        return remote_copy(mlp[m], pair.at[m, side, :], a_send.at[m], a_recv.at[m], (flip1(d), t))

    tok_copy = remote_copy(tok, tok2, tok_send, tok_recv, (d, flip1(t)))
    def oz_copy(k):
        return remote_copy(wo, wo_rows.at[:, tile_at(t, wcols)], oz_send.at[k - 1], oz_recv.at[k - 1], (d, lax.rem(t + k, 4)))

    for k in (1, 2, 3):
        oz_copy(k).start()
    for m in range(3):
        b_copy(m).start()
    tok_copy.start()
    load_o = pltpu.make_async_copy(wo, wo_rows.at[:, tile_at(t, wcols)], load_sem.at[0])
    load_o.start()

    def qkv_copy(i, m):
        return remote_copy(
            att[m], wqkv.at[mine, pl.ds(m * wcols, wcols)], qkv_send.at[i, m], qkv_recv.at[i, m], (dp_peer(i), t)
        )

    def qkv_start(i):
        for m in range(3):
            qkv_copy(i, m).start()

    over(count - 1, qkv_start)

    @pl.when(jnp.logical_not(home))
    def _():
        for m in range(3):
            a_copy(m).start()

    loads = [pltpu.make_async_copy(mlp[m], own_mlp.at[m], load_sem.at[1 + m]) for m in range(3)]
    loads += [pltpu.make_async_copy(att[m], own_att.at[m], load_sem.at[4 + m]) for m in range(3)]
    for copy in loads:
        copy.start()
    for copy in loads:
        copy.wait()
    keeps = [
        pltpu.make_async_copy(own_att.at[m], wqkv.at[mine, pl.ds(m * wcols, wcols)], keep_sem.at[m]) for m in range(3)
    ]
    for copy in keeps:
        copy.start()
    pair_keeps = [pltpu.make_async_copy(own_mlp.at[m], pair.at[m, side, :], keep_sem.at[3 + m]) for m in range(3)]

    @pl.when(home)
    def _():
        for copy in pair_keeps:
            copy.start()

    load_o.wait()
    for k in (1, 2, 3):
        oz_copy(k).wait_recv()
    keep_o = pltpu.make_async_copy(wo_rows, wo_all.at[mine, :], keep_sem.at[6])
    keep_o.start()

    def oq_copy(j):
        return remote_copy(wo_rows, wo_all.at[mine, :], oq_send.at[j], oq_recv.at[j], (lax.rem(d + 2 + 2 * j, count), t))

    def oc_own():
        return remote_copy(wo_rows, wo_all.at[mine, :], oc_send.at[half - 1], oc_recv.at[half - 1], (flip1(d), t))

    def oc_copy(j):
        rows = tile_at(lax.rem(d + count - 2 - 2 * j, count), wrows)
        return remote_copy(wo_all.at[rows, :], wo_all.at[rows, :], oc_send.at[j], oc_recv.at[j], (flip1(d), t))

    over(half - 1, lambda j: oq_copy(j).start())
    oc_own().start()
    rope_tables(order_ref, length_ref, cos_out, sin_out, col_out, start_out)

    def oq_next(j):
        oq_copy(j).wait_recv()
        oc_copy(j).start()

    over(half - 1, oq_next)

    def qkv_wait(i):
        for m in range(3):
            qkv_copy(i, m).wait()

    over(count - 1, qkv_wait)
    over(half - 1, lambda j: oq_copy(j).wait_send())
    over(half - 1, lambda j: oc_copy(j).wait())
    oc_own().wait()
    for k in (1, 2, 3):
        oz_copy(k).wait_send()
    keep_o.wait()
    for copy in keeps:
        copy.wait()
    tok_copy.wait()
    for m in range(3):
        b_copy(m).wait_send()

    @pl.when(home)
    def _():
        for m in range(3):
            pair_keeps[m].wait()
            remote_copy(mlp[m], pair.at[m, other_side, :], a_send.at[m], a_recv.at[m], (flip1(d), t)).wait_recv()

    @pl.when(jnp.logical_not(home))
    def _():
        for m in range(3):
            a_copy(m).wait_send()
            for c in range(2):
                remote_copy(
                    mlp[m], pair.at[m, pl.ds(c * wrows, wrows), :], b_send.at[m], b_recv.at[c * 3 + m], far
                ).wait_recv()


def spread_call(count, tokens, w_up, w_gate, w_down, wq, wk, wv, wo, order, lengths):
    rows, width = tokens.shape
    group = order.shape[1]
    wrows, wcols = wq.shape
    hid = w_up.shape[1]
    bf = jnp.bfloat16
    anywhere = pl.BlockSpec(memory_space=pl.ANY)
    dma = pltpu.SemaphoreType.DMA
    return pl.pallas_call(
        functools.partial(spread_body, count),
        out_shape=(
            jax.ShapeDtypeStruct((3, 2 * wrows, hid), bf),
            jax.ShapeDtypeStruct((rows, width), bf),
            jax.ShapeDtypeStruct((width, 3 * wcols), bf),
            jax.ShapeDtypeStruct((width, width), bf),
            jax.ShapeDtypeStruct((group, 2 * HD), jnp.float32),
            jax.ShapeDtypeStruct((group, 2 * HD), jnp.float32),
            jax.ShapeDtypeStruct((group, 1), jnp.int32),
            jax.ShapeDtypeStruct((1, group), jnp.int32),
        ),
        in_specs=[anywhere] * 8 + [vmem(), pl.BlockSpec(memory_space=pltpu.SMEM)],
        out_specs=(anywhere,) * 4 + (vmem(),) * 4,
        scratch_shapes=[
            pltpu.VMEM((3, wrows, hid), bf),
            pltpu.VMEM((3, wrows, wcols), bf),
            pltpu.VMEM((wrows, width), bf),
            dma((7,)), dma((7,)), dma((3,)), dma((3,)), dma((3,)), dma((6,)), dma, dma,
            dma((count - 1, 3)), dma((count - 1, 3)), dma((3,)), dma((3,)),
            dma((count // 2,)), dma((count // 2,)), dma((count // 2,)), dma((count // 2,)),
        ],
        compiler_params=pltpu.CompilerParams(vmem_limit_bytes=VMEM_LIMIT, collective_id=2, has_side_effects=True),
        name="spread",
    )(tokens, w_up, w_gate, w_down, wq, wk, wv, wo, order, lengths)


def head_sums(value):
    width = value.shape[1]
    same = (
        lax.broadcasted_iota(jnp.int32, (width, width), 0) // HD == lax.broadcasted_iota(jnp.int32, (width, width), 1) // HD
    )
    ones = jnp.where(same, 1.0, 0.0).astype(jnp.bfloat16)
    high = value.astype(jnp.bfloat16)
    low = (value - high.astype(jnp.float32)).astype(jnp.bfloat16)
    return dot_ab(high, ones) + dot_ab(low, ones)


def swap_halves(value):
    width = value.shape[1]
    lane = lax.broadcasted_iota(jnp.int32, value.shape, 1) % HD
    return jnp.where(lane < HD // 2, pltpu.roll(value, width - HD // 2, 1), pltpu.roll(value, HD // 2, 1))


def project_body(
    tok, tok2, wqkv, cos_ref, sin_ref, order_col, gain_ref, q_ref, k_ref, v_ref, raw_ref, x_hbm,
    xs, plain, load_sem, keep_sem, mid_send, recv, on_send,
):
    t = lax.axis_index("tensor")
    d = lax.axis_index("dp")
    _, rows, width = xs.shape
    group, cols = q_ref.shape
    near = flip1(t)
    across = 3 - t
    inner = (t + 1) // 2 == 1
    arrive = (2 - t // 2, 3 - 3 * (t // 2))
    part = rows // 2
    greet([(d, near), (d, across)])

    def mid_copy(k):
        src = (tok, tok2)[k // 2].at[pl.ds((k % 2) * part, part), :]
        dst = xs.at[(t, near)[k // 2], pl.ds((k % 2) * part, part), :]
        return remote_copy(src, dst, mid_send.at[k], recv.at[k], (d, across))

    def on_copy(k):
        ref = xs.at[arrive[k // 2], pl.ds((k % 2) * part, part), :]
        return remote_copy(ref, ref, on_send.at[k], recv.at[k], (d, near))

    @pl.when(inner)
    def _():
        for k in range(4):
            mid_copy(k).start()

    loads = [
        pltpu.make_async_copy(tok, xs.at[t], load_sem.at[0]),
        pltpu.make_async_copy(tok2, xs.at[near], load_sem.at[1]),
    ]
    for copy in loads:
        copy.start()

    def keep(index, slot):
        return pltpu.make_async_copy(xs.at[slot], x_hbm.at[tile_at(slot, rows), :], keep_sem.at[index])

    def work(index, slot):
        keep(index, slot).start()

        def strip(i):
            at = tile_at(slot * (rows // WIDE_STRIP) + i, WIDE_STRIP)
            x = xs[slot, tile_at(i, WIDE_STRIP), :]
            cos = jnp.concatenate([cos_ref[at, :]] * (cols // cos_ref.shape[1]), axis=1)
            sin = jnp.concatenate([sin_ref[at, :]] * (cols // sin_ref.shape[1]), axis=1)
            for m in range(2):
                raw = dot_ab(x, wqkv[:, m * cols : (m + 1) * cols])
                raw_ref[at, m * cols : (m + 1) * cols] = raw.astype(jnp.bfloat16)
                normed = raw * lax.rsqrt(head_sums(raw * raw) + EPS) * gain_ref[:, tile_at(t, cols)]
                plain[at, m * cols : (m + 1) * cols] = (normed * cos + swap_halves(normed) * sin).astype(jnp.bfloat16)
            plain[at, 2 * cols : 3 * cols] = dot_ab(x, wqkv[:, 2 * cols : 3 * cols]).astype(jnp.bfloat16)

        over(rows // WIDE_STRIP, strip)

    loads[0].wait()
    work(0, t)
    loads[1].wait()
    work(1, near)
    for k in range(4):
        slot = arrive[k // 2]
        ref = xs.at[slot, pl.ds((k % 2) * part, part), :]
        remote_copy(ref, ref, on_send.at[k], recv.at[k], (d, near)).wait_recv()

        @pl.when(inner)
        def _():
            on_copy(k).start()

        if k % 2:
            work(2 + k // 2, slot)

    def permute(b):
        at = tile_at(b, BLK)
        hot = (lax.broadcasted_iota(jnp.int32, (BLK, group), 1) == order_col[at, :]).astype(jnp.float32)
        value = dot_ab(hot.astype(jnp.bfloat16), plain[...])
        for m, ref in enumerate((q_ref, k_ref, v_ref)):
            ref[at, :] = value[:, m * cols : (m + 1) * cols].astype(jnp.bfloat16)

    over(group // BLK, permute)
    for index, slot in enumerate((t, near, *arrive)):
        keep(index, slot).wait()

    @pl.when(inner)
    def _():
        for k in range(4):
            mid_copy(k).wait_send()
            on_copy(k).wait_send()


def project_call(tokens, tok2, wqkv, cos, sin, order_col, gains):
    rows, width = tokens.shape
    group = order_col.shape[0]
    cols = wqkv.shape[1] // 3
    bf = jnp.bfloat16
    anywhere = pl.BlockSpec(memory_space=pl.ANY)
    dma = pltpu.SemaphoreType.DMA
    return pl.pallas_call(
        project_body,
        out_shape=(jax.ShapeDtypeStruct((group, cols), bf),) * 3
        + (jax.ShapeDtypeStruct((group, 2 * cols), bf), jax.ShapeDtypeStruct((group, width), bf)),
        in_specs=[anywhere, anywhere] + [vmem()] * 5,
        out_specs=(vmem(),) * 4 + (anywhere,),
        scratch_shapes=[
            pltpu.VMEM((group // rows, rows, width), bf),
            pltpu.VMEM((group, 3 * cols), bf),
            dma((2,)), dma((4,)), dma((4,)), dma((4,)), dma((4,)),
        ],
        compiler_params=pltpu.CompilerParams(vmem_limit_bytes=VMEM_LIMIT, collective_id=3, has_side_effects=True),
        cost_estimate=pl.CostEstimate(flops=6 * 10**10, bytes_accessed=10**7, transcendentals=10**6),
        name="project",
    )(tokens, tok2, wqkv, cos, sin, order_col, gains)


def tail_body(
    grad_ref, raw_ref, cos_ref, sin_ref, wqkv, x_hbm, kept_ref, gain_ref, tok_out, gq, gain_sum,
    xs, x_t, draw, part_far, part_mid, part_near, own_part, from_a, from_b, from_c, from_d, from_e, from_f,
    load_sem, hop_send, hop_recv,
):
    d = lax.axis_index("dp")
    t = lax.axis_index("tensor")
    rows, width = tok_out.shape
    group = draw.shape[0]
    cols = draw.shape[1] // 3
    near = flip1(t)
    inner = (t + 1) // 2 == 1
    outer = jnp.logical_not(inner)
    far, mid = 3 - 3 * (t // 2), 2 - t // 2
    chunk = rows // 2
    greet([(d, near), (d, 3 - t)])
    load_x = pltpu.make_async_copy(x_hbm, xs, load_sem)
    load_x.start()

    def hop(kind, ch):
        src, dst, to = (
            (part_far, from_a, near),
            (part_mid, from_b, near),
            (part_near, from_c, near),
            (part_far, from_d, 3 - t),
            (part_mid, from_e, 3 - t),
            (part_near, from_f, near),
        )[kind]
        part = pl.ds(ch * chunk, chunk)
        return remote_copy(src.at[part, :], dst.at[part, :], hop_send.at[kind, ch], hop_recv.at[kind, ch], (d, to))

    gain_sum[...] = jnp.zeros_like(gain_sum)

    def work(slot, store):
        def strip(i):
            at = tile_at(slot * (rows // WIDE_STRIP) + i, WIDE_STRIP)
            cos = jnp.concatenate([cos_ref[at, :]] * (cols // cos_ref.shape[1]), axis=1)
            sin = jnp.concatenate([sin_ref[at, :]] * (cols // sin_ref.shape[1]), axis=1)
            gain = gain_ref[:, tile_at(t, cols)]
            for m in range(2):
                grad = grad_ref[at, m * cols : (m + 1) * cols].astype(jnp.float32)
                raw = raw_ref[at, m * cols : (m + 1) * cols].astype(jnp.float32)
                back = grad * cos - swap_halves(grad) * sin
                factor = lax.rsqrt(head_sums(raw * raw) + EPS)
                normed = raw * factor
                gain_sum[...] += jnp.sum(back * normed, axis=0, keepdims=True)
                scaled = back * gain
                draw[at, m * cols : (m + 1) * cols] = (
                    factor * (scaled - normed * head_sums(normed * scaled))
                ).astype(jnp.bfloat16)
            draw[at, 2 * cols : 3 * cols] = grad_ref[at, 2 * cols : 3 * cols]

        over(rows // WIDE_STRIP, strip)
        everything = tile_at(slot, rows)

        def product(n):
            tile = tile_at(n, TILE)
            store(tile, dot_abt(draw[everything, :], wqkv[tile, :]))

        over(width // TILE, product)

    def into(ref):
        def store(tile, value):
            ref[:, tile] = value.astype(ref.dtype)

        return store

    for kind, (slot, ref) in enumerate(((far, part_far), (mid, part_mid), (near, part_near))):
        work(slot, into(ref))

        @pl.when(outer)
        def _():
            for ch in range(2):
                hop(kind, ch).start()

    work(t, into(own_part))

    def pass_on(kind, ch, own, got, then):
        @pl.when(inner)
        def _():
            part = pl.ds(ch * chunk, chunk)
            hop(kind, ch).wait_recv()
            own[part, :] = (own[part, :].astype(jnp.float32) + got[part, :].astype(jnp.float32)).astype(jnp.bfloat16)
            hop(then, ch).start()

    pass_on(0, 0, part_far, from_a, 3)
    pass_on(0, 1, part_far, from_a, 3)

    load_x.wait()

    def flip_block(b):
        at = tile_at(b, 128)
        for n in range(width // TILE):
            x_t[n * TILE : (n + 1) * TILE, at] = xs[at, n * TILE : (n + 1) * TILE].T

    over(group // 128, flip_block)
    pass_on(3, 0, part_near, from_d, 5)

    def weight_grad(n):
        tile = tile_at(n, TILE)
        gq[tile, :] = dot_ab(x_t[tile, :], draw[...]).astype(jnp.bfloat16)

    over(width // TILE, weight_grad)
    pass_on(1, 0, part_mid, from_b, 4)
    pass_on(3, 1, part_near, from_d, 5)
    pass_on(1, 1, part_mid, from_b, 4)

    for ch in range(2):
        part = pl.ds(ch * chunk, chunk)

        @pl.when(inner)
        def _():
            hop(2, ch).wait_recv()
            hop(4, ch).wait_recv()
            tok_out[part, :] = (
                kept_ref[part, :]
                + own_part[part, :]
                + from_c[part, :].astype(jnp.float32)
                + from_e[part, :].astype(jnp.float32)
            )

        @pl.when(outer)
        def _():
            hop(5, ch).wait_recv()
            tok_out[part, :] = kept_ref[part, :] + own_part[part, :] + from_f[part, :].astype(jnp.float32)

    for ch in range(2):

        @pl.when(inner)
        def _():
            for kind in (3, 4, 5):
                hop(kind, ch).wait_send()

        @pl.when(outer)
        def _():
            for kind in (0, 1, 2):
                hop(kind, ch).wait_send()


def tail_call(grad_qkv, raw, cos, sin, wqkv, all_tokens, kept, gains):
    rows, width = kept.shape
    group, three = grad_qkv.shape
    bf, f32 = jnp.bfloat16, jnp.float32
    anywhere = pl.BlockSpec(memory_space=pl.ANY)
    dma = pltpu.SemaphoreType.DMA
    shape = jax.ShapeDtypeStruct
    return pl.pallas_call(
        tail_body,
        out_shape=(shape((rows, width), f32), shape((width, three), bf), shape((1, three // 3), f32)),
        in_specs=[vmem()] * 5 + [anywhere] + [vmem()] * 2,
        out_specs=(vmem(),) * 3,
        scratch_shapes=[
            pltpu.VMEM((group, width), bf),
            pltpu.VMEM((width, group), bf),
            pltpu.VMEM((group, three), bf),
            pltpu.VMEM((rows, width), bf),
            pltpu.VMEM((rows, width), bf),
            pltpu.VMEM((rows, width), bf),
            pltpu.VMEM((rows, width), f32),
        ]
        + [pltpu.VMEM((rows, width), bf)] * 6
        + [dma, dma((6, 2)), dma((6, 2))],
        compiler_params=pltpu.CompilerParams(vmem_limit_bytes=VMEM_LIMIT, collective_id=4, has_side_effects=True),
        cost_estimate=pl.CostEstimate(flops=6 * 10**10, bytes_accessed=10**7, transcendentals=10**6),
        name="tail",
    )(grad_qkv, raw, cos, sin, wqkv, all_tokens, kept, gains)


def settle_body(
    count, gq_hbm, gwo_hbm, mlp_hbm, gain_ref, gaa_ref, gam_ref, gsu_ref, gsg_ref,
    q_out, k_out, v_out, wo_out, up_out, gate_out, down_out, gain_out, aa_out, su_out, sg_out, am_out,
    own_q, core_q, got_q, own_w, core_w, got_w, wo_mid, got_z, near_mlp, far_mlp, vec, got_v, vec_mid, got_s,
    load_sem, core_send, core_recv, q_send, q_recv, w_send, w_recv, z_send, z_recv, v_send, v_recv, s_send, s_recv,
    near_send, near_recv, mlp_send, mlp_recv,
):
    d = lax.axis_index("dp")
    t = lax.axis_index("tensor")
    half, wrows, three = got_q.shape
    cols = three // 3
    width = gaa_ref.shape[1]
    chip, core = d // 2, lax.rem(d, 2)
    home = core == t // 2
    away = jnp.logical_not(home)
    f32, bf = jnp.float32, jnp.bfloat16

    def dp_peer(i):
        return lax.rem(d + 1 + i, count)

    def line_peer(k):
        return lax.rem(t + k, 4)

    def chip_peer(i):
        return lax.rem(chip + 1 + i, half)

    barrier = pltpu.get_barrier_semaphore()
    over(
        count - 1,
        lambda i: pl.semaphore_signal(barrier, inc=1, device_id=(dp_peer(i), t), device_id_type=MESH_ID),
    )
    for k in (1, 2, 3):
        pl.semaphore_signal(barrier, inc=1, device_id=(d, line_peer(k)), device_id_type=MESH_ID)
    pl.semaphore_signal(barrier, inc=1, device_id=(flip1(d), flip2(t)), device_id_type=MESH_ID)
    pl.semaphore_wait(barrier, count + 3)

    near_copy = remote_copy(mlp_hbm.at[:, 1 - core], near_mlp, near_send, near_recv, (flip1(d), t))
    keep_mlp = pltpu.make_async_copy(mlp_hbm.at[:, core], near_mlp, load_sem.at[0])

    def far_same(m):
        return remote_copy(mlp_hbm.at[m, core], far_mlp.at[m], mlp_send.at[m], mlp_recv.at[m], (d, flip2(t)))

    def far_cross(m):
        return remote_copy(
            mlp_hbm.at[m, 1 - core], far_mlp.at[m], mlp_send.at[3 + m], mlp_recv.at[m], (flip1(d), flip2(t))
        )

    def far_start(m):
        @pl.when(away)
        def _():
            far_same(m).start()
            far_cross(m).start()

    @pl.when(home)
    def _():
        near_copy.start()
        keep_mlp.start()

    far_start(0)
    far_start(1)

    core_w_copy = remote_copy(gwo_hbm.at[:, 1 - core], core_w, core_send.at[0], core_recv.at[0], (flip1(d), t))
    core_q_copy = remote_copy(gq_hbm.at[:, 1 - core], core_q, core_send.at[1], core_recv.at[1], (flip1(d), t))
    load_w = pltpu.make_async_copy(gwo_hbm.at[:, core], own_w, load_sem.at[1])
    load_q = pltpu.make_async_copy(gq_hbm.at[:, core], own_q, load_sem.at[2])
    core_w_copy.start()
    core_q_copy.start()
    load_w.start()
    load_q.start()

    vec[...] = jnp.zeros_like(vec)
    for row, ref in enumerate((gaa_ref, gam_ref, gsu_ref, gsg_ref)):
        vec[row : row + 1, :] = ref[...]
    vec[4:5, 0:cols] = gain_ref[...]
    got_v[d] = vec[...]

    def v_copy(i):
        return remote_copy(vec, got_v.at[d], v_send.at[i], v_recv.at[i], (dp_peer(i), t))

    over(count - 1, lambda i: v_copy(i).start())

    def chip_copy(own, got, sends, recvs, i):
        return remote_copy(own.at[chip_peer(i)], got.at[chip], sends.at[i], recvs.at[i], (2 * chip_peer(i) + core, t))

    def w_copy(i):
        return chip_copy(own_w, got_w, w_send, w_recv, i)

    def q_copy(i):
        return chip_copy(own_q, got_q, q_send, q_recv, i)

    def join(own, other, got):
        def one(e):
            own[e] = (own[e].astype(f32) + other[e].astype(f32)).astype(bf)

        over(half, one)
        got[chip] = own[chip]

    load_w.wait()
    core_w_copy.wait_recv()
    join(own_w, core_w, got_w)
    over(half - 1, lambda i: w_copy(i).start())
    load_q.wait()
    core_q_copy.wait_recv()
    join(own_q, core_q, got_q)
    over(half - 1, lambda i: q_copy(i).start())

    def total_of(got):
        return lax.fori_loop(1, half, lambda i, total: total + got[i].astype(f32), got[0].astype(f32))

    over(half - 1, lambda i: w_copy(i).wait_recv())
    wo_mid[...] = total_of(got_w).astype(bf)

    def z_copy(k):
        return remote_copy(
            wo_mid.at[:, tile_at(line_peer(k), cols)], got_z.at[t], z_send.at[k - 1], z_recv.at[k - 1], (d, line_peer(k))
        )

    for k in (1, 2, 3):
        z_copy(k).start()
    got_z[t] = wo_mid[:, tile_at(t, cols)]

    over(count - 1, lambda i: v_copy(i).wait_recv())
    even, odd = lax.fori_loop(
        1, half, lambda i, total: (total[0] + got_v[2 * i], total[1] + got_v[2 * i + 1]), (got_v[0], got_v[1])
    )
    both = even + odd
    vec_mid[...] = jnp.concatenate([both[0:2], even[2:3], odd[2:3], even[3:4], odd[3:4], both[4:5], both[4:5]], axis=0)

    def s_copy(k):
        return remote_copy(vec_mid, got_s.at[t], s_send.at[k - 1], s_recv.at[k - 1], (d, line_peer(k)))

    for k in (1, 2, 3):
        s_copy(k).start()
    got_s[t] = vec_mid[...]
    far_start(2)

    over(half - 1, lambda i: q_copy(i).wait_recv())
    total = total_of(got_q)
    for m, ref in enumerate((q_out, k_out, v_out)):
        ref[...] = total[:, m * cols : (m + 1) * cols]

    for k in (1, 2, 3):
        z_copy(k).wait_recv()
        s_copy(k).wait_recv()
    wo_out[...] = got_z[0].astype(f32) + got_z[1].astype(f32) + got_z[2].astype(f32) + got_z[3].astype(f32)
    shared = got_s[0] + got_s[1] + got_s[2] + got_s[3]
    aa_out[...] = shared[0:1]
    am_out[...] = shared[1:2]
    pairs = (got_s[0] + got_s[2], got_s[1] + got_s[3])
    for s in range(4):
        su_out[:, s * width : (s + 1) * width] = pairs[s % 2][2 + s // 2 : 3 + s // 2]
        sg_out[:, s * width : (s + 1) * width] = pairs[s % 2][4 + s // 2 : 5 + s // 2] * math.sqrt(D)
        gain_out[:, s * cols : (s + 1) * cols] = got_s[s][6:7, 0:cols]

    @pl.when(home)
    def _():
        keep_mlp.wait()
        near_copy.wait_send()

    @pl.when(away)
    def _():
        near_copy.wait_recv()

    for m, ref in enumerate((up_out, gate_out, down_out)):
        far_same(m).wait_recv()
        ref[...] = near_mlp[m].astype(f32) + far_mlp[m].astype(f32)

    @pl.when(away)
    def _():
        for m in range(3):
            far_same(m).wait_send()
            far_cross(m).wait_send()

    core_w_copy.wait_send()
    core_q_copy.wait_send()
    over(count - 1, lambda i: v_copy(i).wait_send())

    def drain(i):
        w_copy(i).wait_send()
        q_copy(i).wait_send()

    over(half - 1, drain)
    for k in (1, 2, 3):
        z_copy(k).wait_send()
        s_copy(k).wait_send()


def settle_call(count, gq, gwo, mlp, gain_sum, gaa, gam, gsu, gsg):
    width, three = gq.shape
    half = count // 2
    cols = three // 3
    wrows = width // count
    hid = mlp.shape[2]
    bf, f32 = jnp.bfloat16, jnp.float32
    anywhere = pl.BlockSpec(memory_space=pl.ANY)
    dma = pltpu.SemaphoreType.DMA
    shape = jax.ShapeDtypeStruct
    return pl.pallas_call(
        functools.partial(settle_body, count),
        out_shape=(shape((wrows, cols), f32),) * 4
        + (shape((wrows, hid), f32),) * 3
        + (
            shape((1, 4 * cols), f32),
            shape((1, width), f32),
            shape((1, 4 * hid), f32),
            shape((1, 4 * hid), f32),
            shape((1, width), f32),
        ),
        in_specs=[anywhere] * 3 + [vmem()] * 5,
        out_specs=(vmem(),) * 12,
        scratch_shapes=[pltpu.VMEM((half, wrows, three), bf)] * 3
        + [pltpu.VMEM((half, wrows, width), bf)] * 3
        + [
            pltpu.VMEM((wrows, width), bf),
            pltpu.VMEM((4, wrows, cols), bf),
            pltpu.VMEM((3, wrows, hid), bf),
            pltpu.VMEM((3, wrows, hid), bf),
            pltpu.VMEM((8, width), f32),
            pltpu.VMEM((count, 8, width), f32),
            pltpu.VMEM((8, width), f32),
            pltpu.VMEM((4, 8, width), f32),
            dma((3,)),
            dma((2,)), dma((2,)),
            dma((half - 1,)), dma((half - 1,)), dma((half - 1,)), dma((half - 1,)),
            dma((3,)), dma((3,)),
            dma((count - 1,)), dma((count - 1,)),
            dma((3,)), dma((3,)),
            dma, dma, dma((6,)), dma((3,)),
        ],
        compiler_params=pltpu.CompilerParams(vmem_limit_bytes=VMEM_LIMIT, collective_id=5, has_side_effects=True),
        cost_estimate=pl.CostEstimate(flops=10**9, bytes_accessed=10**7, transcendentals=0),
        name="settle",
    )(
        gq.reshape(half, 2, wrows, three),
        gwo.reshape(half, 2, wrows, width),
        mlp.reshape(3, 2, wrows, hid),
        gain_sum, gaa, gam, gsu, gsg,
    )


def deliver_body(count, total, *refs):
    ins, outs, rest = refs[:total], refs[total : 2 * total], refs[2 * total :]
    held, load_sem, store_sem = rest[:count], rest[count], rest[count + 1]
    loads = [pltpu.make_async_copy(ins[i], held[i], load_sem.at[i]) for i in range(count)]
    stores = [pltpu.make_async_copy(held[i], outs[i], store_sem.at[i]) for i in range(count)]
    for copy in loads:
        copy.start()
    for i in range(count, total):
        outs[i][...] = ins[i][0, :]
    for load, store in zip(loads, stores):
        load.wait()
        store.start()
    for copy in stores:
        copy.wait()


def deliver_call(arrays, vectors):
    total = len(arrays) + len(vectors)
    specs = [pl.BlockSpec(memory_space=pl.ANY)] * len(arrays) + [vmem()] * len(vectors)
    return pl.pallas_call(
        functools.partial(deliver_body, len(arrays), total),
        out_shape=tuple(jax.ShapeDtypeStruct(a.shape, a.dtype) for a in arrays)
        + tuple(jax.ShapeDtypeStruct((v.shape[1],), v.dtype) for v in vectors),
        in_specs=specs,
        out_specs=tuple(specs),
        scratch_shapes=[pltpu.VMEM(a.shape, a.dtype) for a in arrays] + [pltpu.SemaphoreType.DMA((len(arrays),))] * 2,
        compiler_params=pltpu.CompilerParams(vmem_limit_bytes=VMEM_LIMIT),
        name="deliver",
    )(*arrays, *vectors)


def same_core_groups(dp_count):
    return [list(range(parity, dp_count, 2)) for parity in range(2)]


def on_device(
    tokens,
    w_query,
    w_key,
    w_value,
    w_out_t,
    w_up,
    w_gate,
    w_down_t,
    scale_qk,
    alpha_attn,
    scale_up,
    scale_gate,
    alpha_mlp,
    order,
    lengths,
    cotangent,
):
    dp_count = lax.axis_size("dp")
    pair, near_tokens, wqkv, wo_every, cos_table, sin_table, order_col, start = spread_call(
        dp_count, tokens, w_up, w_gate, w_down_t, w_query, w_key, w_value, w_out_t, order, lengths
    )
    low = lax.slice(start[0], (0,), (start.shape[1],), (BLK,)) // BLK
    mlp_parts = lax.all_gather(
        pair, "dp", axis=0, tiled=False, axis_index_groups=same_core_groups(dp_count)
    )
    queries, key_rows, value_rows, raw, all_tokens = project_call(
        tokens, near_tokens, wqkv, cos_table, sin_table, order_col, scale_qk[None, :]
    )
    attended, log_totals, attended_plain = attn_fwd(low, start, order, queries, key_rows, value_rows)
    out_rows, grad_att_rows, mlp_grads, wo_grads, grad_h1_kept, grad_alpha_a, grad_alpha_m, grad_su, grad_sv = middle_call(
        2,
        attended_plain,
        wo_every,
        mlp_parts,
        tokens,
        cotangent,
        alpha_attn[None, :],
        alpha_mlp[None, :],
        scale_up[None, :],
        scale_gate[None, :],
    )
    grad_qkv = attn_bwd(
        low, start, order, order_col, log_totals, queries, key_rows, value_rows, attended, grad_att_rows
    )
    mlp_sums = lax.psum_scatter(
        mlp_grads, "dp", scatter_dimension=0, tiled=False, axis_index_groups=same_core_groups(dp_count)
    )
    grad_tokens, grad_q, gain_sum = tail_call(
        grad_qkv, raw, cos_table, sin_table, wqkv, all_tokens, grad_h1_kept, scale_qk[None, :]
    )
    settled = settle_call(
        dp_count, grad_q, wo_grads, mlp_sums, gain_sum, grad_alpha_a, grad_alpha_m, grad_su, grad_sv
    )
    return deliver_call([out_rows, grad_tokens, *settled[:7]], settled[7:])


def solution(mesh):
    return jax.shard_map(
        on_device,
        mesh=mesh,
        in_specs=(
            P(("dp", "tensor"), None),
            P("dp", "tensor"),
            P("dp", "tensor"),
            P("dp", "tensor"),
            P("dp", "tensor"),
            P("dp", "tensor"),
            P("dp", "tensor"),
            P("dp", "tensor"),
            P(),
            P(),
            P(),
            P(),
            P(),
            P("dp", None),
            P("dp", None),
            P(("dp", "tensor"), None),
        ),
        out_specs=(
            P(("dp", "tensor"), None),
            P(("dp", "tensor"), None),
            P("dp", "tensor"),
            P("dp", "tensor"),
            P("dp", "tensor"),
            P("dp", "tensor"),
            P("dp", "tensor"),
            P("dp", "tensor"),
            P("dp", "tensor"),
            P(),
            P(),
            P(),
            P(),
            P(),
        ),
        check_vma=False,
    )
```

```python
import functools
import math

import jax
import jax.numpy as jnp
from jax import lax
from jax.experimental import pallas as pl
from jax.experimental.pallas import tpu as pltpu
from jax.sharding import PartitionSpec as P

D = 1024
HD = 64
BLK = 256
LOG2E = 1.4426950408889634
VMEM_LIMIT = 60 * 1024 * 1024


def dot_ab(a, b):
    return lax.dot_general(a, b, (((1,), (0,)), ((), ())), preferred_element_type=jnp.float32)


def dot_abt(a, b):
    return lax.dot_general(a, b, (((1,), (1,)), ((), ())), preferred_element_type=jnp.float32)


def split_heads(block, heads):
    lane_head = lax.broadcasted_iota(jnp.int32, block.shape, 1) // HD
    zero = jnp.zeros_like(block)
    return jnp.concatenate([jnp.where(lane_head == h, block, zero) for h in range(heads)], axis=0)


def attn_fwd_body(
    low_ref, start_ref, order_row, q_ref, k_ref, v_ref, out_ref, lse_ref, plain_ref, vt_ref, qs_ref, acc_ref, sum_ref
):
    rows, cols = q_ref.shape
    heads = cols // HD
    scale = math.sqrt(HD) * LOG2E
    for b in range(rows // BLK):
        vt_ref[:, b * BLK : (b + 1) * BLK] = v_ref[b * BLK : (b + 1) * BLK, :].T

    def one_block(i, _):
        base = pl.multiple_of(i * BLK, BLK)
        qs_ref[...] = split_heads(q_ref[pl.ds(base, BLK), :], heads)
        acc_ref[...] = jnp.zeros_like(acc_ref)
        sum_ref[...] = jnp.zeros_like(sum_ref)
        start = jnp.concatenate([start_ref[:, pl.ds(base, BLK)]] * heads, axis=1)
        own = lax.broadcasted_iota(jnp.int32, (1, heads * BLK), 1) % BLK + base

        def step(j, causal):
            at = pl.multiple_of(j * BLK, BLK)
            scores = dot_abt(k_ref[pl.ds(at, BLK), :], qs_ref[...])
            place = lax.broadcasted_iota(jnp.int32, scores.shape, 0) + at
            keep = place >= start
            if causal:
                keep = keep & (place <= own)
            probs = jnp.where(keep, jnp.exp2(scores * scale), 0.0)
            sum_ref[...] += jnp.sum(probs, axis=0, keepdims=True)
            probs_b = probs.astype(jnp.bfloat16)
            for h in range(heads):
                acc_ref[h * HD : (h + 1) * HD, :] += dot_ab(
                    vt_ref[h * HD : (h + 1) * HD, pl.ds(at, BLK)], probs_b[:, h * BLK : (h + 1) * BLK]
                )

        lax.fori_loop(low_ref[i], i, lambda j, c: (step(j, False), c)[1], 0)
        step(i, True)
        total = sum_ref[...]
        inv = 1.0 / total
        logs = jnp.log2(total)
        for h in range(heads):
            lse_ref[h : h + 1, pl.ds(base, BLK)] = logs[:, h * BLK : (h + 1) * BLK]
            acc_ref[h * HD : (h + 1) * HD, :] *= inv[:, h * BLK : (h + 1) * BLK]
        out_ref[pl.ds(base, BLK), :] = acc_ref[...].T.astype(jnp.bfloat16)
        return 0

    lax.fori_loop(0, rows // BLK, one_block, 0)
    over(rows // BLK, lambda b: to_token_order(b, order_row, out_ref, plain_ref))


def to_token_order(b, order_row, src, dst):
    at = pl.ds(pl.multiple_of(b * BLK, BLK), BLK)
    hot = lax.broadcasted_iota(jnp.int32, (BLK, src.shape[0]), 0) + b * BLK == order_row[...]
    dst[at, :] = dot_ab(hot.astype(jnp.float32).astype(jnp.bfloat16), src[...]).astype(dst.dtype)


def to_packed_order(b, order_col, src, dst):
    at = pl.ds(pl.multiple_of(b * BLK, BLK), BLK)
    hot = lax.broadcasted_iota(jnp.int32, (BLK, src.shape[0]), 1) == order_col[at, :]
    dst[at, :] = dot_ab(hot.astype(jnp.float32).astype(jnp.bfloat16), src[...]).astype(dst.dtype)


def over(count, body):
    lax.fori_loop(0, count, lambda i, carry: (body(i), carry)[1], 0)


def vmem():
    return pl.BlockSpec(memory_space=pltpu.VMEM)


def attn_fwd(low, start, order_row, q, k, v):
    rows, cols = q.shape
    heads = cols // HD
    return pl.pallas_call(
        attn_fwd_body,
        out_shape=(
            jax.ShapeDtypeStruct((rows, cols), jnp.bfloat16),
            jax.ShapeDtypeStruct((8, rows), jnp.float32),
            jax.ShapeDtypeStruct((rows, cols), jnp.bfloat16),
        ),
        in_specs=[pl.BlockSpec(memory_space=pltpu.SMEM)] + [vmem()] * 5,
        out_specs=(vmem(),) * 3,
        scratch_shapes=[
            pltpu.VMEM((cols, rows), jnp.bfloat16),
            pltpu.VMEM((heads * BLK, cols), jnp.bfloat16),
            pltpu.VMEM((cols, BLK), jnp.float32),
            pltpu.VMEM((1, heads * BLK), jnp.float32),
        ],
        compiler_params=pltpu.CompilerParams(vmem_limit_bytes=VMEM_LIMIT),
        cost_estimate=pl.CostEstimate(flops=4 * rows * rows * cols, bytes_accessed=8 * rows * cols, transcendentals=rows * rows * heads),
        name="attn_fwd",
    )(low, start, order_row, q, k, v)


def attn_bwd_body(
    low_ref, start_ref, order_row, order_col, lse_ref, q_ref, k_ref, v_ref, o_ref, grad_ref,
    plain_ref, kt_ref, qs_ref, gs_ref, dqt_ref, dk_acc, dv_acc, g_ref, packed,
):
    rows, cols = q_ref.shape
    heads = cols // HD
    root = math.sqrt(HD)
    scale = root * LOG2E
    for b in range(rows // BLK):
        kt_ref[:, b * BLK : (b + 1) * BLK] = k_ref[b * BLK : (b + 1) * BLK, :].T
    over(rows // BLK, lambda b: to_packed_order(b, order_col, grad_ref, g_ref))
    dk_acc[...] = jnp.zeros_like(dk_acc)
    dv_acc[...] = jnp.zeros_like(dv_acc)

    def one_block(i, _):
        base = pl.multiple_of(i * BLK, BLK)
        qs_ref[...] = split_heads(q_ref[pl.ds(base, BLK), :], heads)
        grads = g_ref[pl.ds(base, BLK), :]
        gs_ref[...] = split_heads(grads, heads)
        dqt_ref[...] = jnp.zeros_like(dqt_ref)
        start = jnp.concatenate([start_ref[:, pl.ds(base, BLK)]] * heads, axis=1)
        own = lax.broadcasted_iota(jnp.int32, (1, heads * BLK), 1) % BLK + base
        prod = (grads.astype(jnp.float32) * o_ref[pl.ds(base, BLK), :].astype(jnp.float32)).T
        delta = jnp.concatenate(
            [jnp.sum(prod[h * HD : (h + 1) * HD, :], axis=0, keepdims=True) for h in range(heads)], axis=1
        )
        lse = jnp.concatenate([lse_ref[h : h + 1, pl.ds(base, BLK)] for h in range(heads)], axis=1)

        def step(j, causal):
            at = pl.multiple_of(j * BLK, BLK)
            scores = dot_abt(k_ref[pl.ds(at, BLK), :], qs_ref[...])
            dprobs = dot_abt(v_ref[pl.ds(at, BLK), :], gs_ref[...])
            place = lax.broadcasted_iota(jnp.int32, scores.shape, 0) + at
            keep = place >= start
            if causal:
                keep = keep & (place <= own)
            probs = jnp.where(keep, jnp.exp2(scores * scale - lse), 0.0)
            dsc = (probs * (dprobs - delta)).astype(jnp.bfloat16)
            dv_acc[pl.ds(at, BLK), :] += dot_ab(probs.astype(jnp.bfloat16), gs_ref[...])
            dk_acc[pl.ds(at, BLK), :] += dot_ab(dsc, qs_ref[...])
            for h in range(heads):
                dqt_ref[h * HD : (h + 1) * HD, :] += dot_ab(
                    kt_ref[h * HD : (h + 1) * HD, pl.ds(at, BLK)], dsc[:, h * BLK : (h + 1) * BLK]
                )

        lax.fori_loop(low_ref[i], i, lambda j, c: (step(j, False), c)[1], 0)
        step(i, True)
        packed[pl.ds(base, BLK), 0:cols] = (dqt_ref[...].T * root).astype(packed.dtype)
        return 0

    lax.fori_loop(0, rows // BLK, one_block, 0)
    packed[:, cols : 2 * cols] = (dk_acc[...] * root).astype(packed.dtype)
    packed[:, 2 * cols : 3 * cols] = dv_acc[...].astype(packed.dtype)
    over(rows // BLK, lambda b: to_token_order(b, order_row, packed, plain_ref))


def attn_bwd(low, start, order_row, order_col, lse, q, k, v, o, g):
    rows, cols = q.shape
    heads = cols // HD
    return pl.pallas_call(
        attn_bwd_body,
        out_shape=jax.ShapeDtypeStruct((rows, 3 * cols), jnp.bfloat16),
        in_specs=[pl.BlockSpec(memory_space=pltpu.SMEM)] + [vmem()] * 9,
        out_specs=vmem(),
        scratch_shapes=[
            pltpu.VMEM((cols, rows), jnp.bfloat16),
            pltpu.VMEM((heads * BLK, cols), jnp.bfloat16),
            pltpu.VMEM((heads * BLK, cols), jnp.bfloat16),
            pltpu.VMEM((cols, BLK), jnp.float32),
            pltpu.VMEM((rows, cols), jnp.float32),
            pltpu.VMEM((rows, cols), jnp.float32),
            pltpu.VMEM((rows, cols), jnp.bfloat16),
            pltpu.VMEM((rows, 3 * cols), jnp.bfloat16),
        ],
        compiler_params=pltpu.CompilerParams(vmem_limit_bytes=VMEM_LIMIT),
        cost_estimate=pl.CostEstimate(flops=10 * rows * rows * cols, bytes_accessed=16 * rows * cols, transcendentals=rows * rows * heads),
        name="attn_bwd",
    )(low, start, order_row, order_col, lse, q, k, v, o, g)


MESH_ID = pl.DeviceIdType.MESH
EPS = 1e-06
TILE = 256
STRIP = 64
WIDE_STRIP = 192


def flip1(index):
    return index + 1 - 2 * lax.rem(index, 2)


def flip2(index):
    return index + 2 - 4 * (index // 2)


def tile_at(index, size):
    if isinstance(index, int):
        return pl.ds(index * size, size)
    return pl.ds(pl.multiple_of(index * size, size), size)


def row_sum(value):
    return jnp.sum(value, axis=-1, keepdims=True)


def middle_body(
    att_ref, wo_hbm, w_hbm, tok_hbm, cot_hbm, aa_ref, am_ref, su_all, sg_all,
    out_ref, datt_ref, gwu_hbm, gwd_hbm, gwo_hbm, dh1_ref, gaa_ref, gam_ref, gsu_ref, gsg_ref,
    wo, wall, tok, cot, parts, mids, dbms, mid_t, dbm_t, ups, gates, mixed,
    middle, branch, dh2, own_part, send_a, recv_a, send_d, recv_d, send_z, recv_z,
    gw, gwo, dparts, su_ref, sg_ref, load_sems, store_sems, hop_send, hop_recv, a2a_send, a2a_recv, d2a_send, d2a_recv, part_send, part_recv,
):
    d = lax.axis_index("dp")
    t = lax.axis_index("tensor")
    rows, width = tok.shape
    heads_w = att_ref.shape[1]
    hid = wall.shape[2]
    nq = w_hbm.shape[0]
    qrows = w_hbm.shape[2]
    chunks = hop_send.shape[0] // 6
    crow = rows // chunks
    core_peer = (flip1(d), t)
    z_peer = (d, flip1(t))
    line = [t, flip1(t), flip2(t), 3 - t]

    barrier = pltpu.get_barrier_semaphore()
    for peer in [core_peer] + [(d, line[k]) for k in (1, 2, 3)]:
        pl.semaphore_signal(barrier, inc=1, device_id=peer, device_id_type=MESH_ID)
    pl.semaphore_wait(barrier, 4)

    def remote(src, dst, ssem, rsem, peer):
        return pltpu.make_async_remote_copy(
            src_ref=src, dst_ref=dst, send_sem=ssem, recv_sem=rsem, device_id=peer, device_id_type=MESH_ID
        )

    a2a = [
        remote(att_ref.at[tile_at(line[k], rows), :], parts.at[k - 1], a2a_send.at[k - 1], a2a_recv.at[k - 1], (d, line[k]))
        for k in (1, 2, 3)
    ]
    for copy in a2a:
        copy.start()
    loads = [
        pltpu.make_async_copy(wo_hbm, wo, load_sems.at[0]),
        pltpu.make_async_copy(tok_hbm, tok, load_sems.at[1]),
        pltpu.make_async_copy(cot_hbm, cot, load_sems.at[2]),
    ]
    wloads = [
        [
            pltpu.make_async_copy(w_hbm.at[q, m], wall.at[m, pl.ds(q * qrows, qrows), :], load_sems.at[3 + m * nq + q])
            for q in range(nq)
        ]
        for m in range(3)
    ]
    for copy in loads + wloads[0] + wloads[1] + wloads[2]:
        copy.start()

    shard = lax.rem(t, 2) + 2 * lax.rem(d, 2)
    su_ref[...] = su_all[:, tile_at(shard, hid)]
    sg_ref[...] = sg_all[:, tile_at(shard, hid)] * math.sqrt(D)
    gsu_ref[...] = jnp.zeros_like(gsu_ref)
    gsg_ref[...] = jnp.zeros_like(gsg_ref)
    gam_ref[...] = jnp.zeros_like(gam_ref)
    gaa_ref[...] = jnp.zeros_like(gaa_ref)

    loads[0].wait()
    for copy in a2a:
        copy.wait_recv()

    def project(n):
        cols = tile_at(n, TILE)
        total = dot_abt(att_ref[tile_at(t, rows), :], wo[cols, tile_at(t, heads_w)])
        for k in (1, 2, 3):
            total += dot_abt(parts[k - 1], wo[cols, tile_at(line[k], heads_w)])
        branch[:, cols] = total

    over(width // TILE, project)
    loads[1].wait()

    def hop(buf, phase, ch, kind):
        part = tile_at(ch, crow)
        index = (phase * chunks + ch) * 3 + kind
        src, dst, peer = ((0, 2, z_peer), (0, 1, core_peer), (2, 3, core_peer))[kind]
        return remote(buf.at[src, part, :], buf.at[dst, part, :], hop_send.at[index], hop_recv.at[index], peer)

    def strips(ch, body):
        over(crow // STRIP, lambda i: body(tile_at(i + ch * (crow // STRIP), STRIP)))

    def unit_of(value):
        factor = lax.rsqrt(row_sum(value * value) + EPS)
        return value * factor, factor

    def make_middle(at):
        inputs = tok[at, :].astype(jnp.float32)
        norm_a, factor_a = unit_of(branch[at, :])
        mid, factor_mid = unit_of(inputs + aa_ref[...] * (norm_a - inputs))
        return inputs, norm_a, factor_a, mid, factor_mid

    def first(at):
        mid = make_middle(at)[3]
        middle[at, :] = mid
        mids[0, at, :] = mid.astype(jnp.bfloat16)

    for ch in range(chunks):
        strips(ch, first)
        hop(mids, 0, ch, 0).start()
        hop(mids, 0, ch, 1).start()

    for m in range(3):
        for copy in wloads[m]:
            copy.wait()

    def within(slot, at):
        return pl.ds(pl.multiple_of(slot * rows + at.start, STRIP), at.size)

    def forward_rows(slot, at, store, ready):
        where = within(slot, at)

        def hidden(n):
            cols = tile_at(n, TILE)
            x = mids[slot, at, :]
            up = dot_ab(x, wall[0, :, cols])
            gate_raw = dot_ab(x, wall[1, :, cols])
            gate = gate_raw * sg_ref[:, cols]
            silu = gate / (1.0 + jnp.exp(-gate))
            ups[where, cols] = up.astype(jnp.bfloat16)
            gates[where, cols] = gate_raw.astype(jnp.bfloat16)
            mixed[where, cols] = (up * su_ref[:, cols] * silu).astype(jnp.bfloat16)

        over(hid // TILE, hidden)
        ready()

        def down(n):
            cols = tile_at(n, TILE)
            store(at, cols, dot_abt(mixed[where, :], wall[2, cols, :]))

        over(width // TILE, down)

    def backward_rows(slot, at, store, ready):
        where = within(slot, at)

        def hidden(n):
            cols = tile_at(n, TILE)
            dmix = dot_ab(dbms[slot, at, :], wall[2, :, cols])
            up_raw = ups[where, cols].astype(jnp.float32)
            gate_raw = gates[where, cols].astype(jnp.float32)
            gate = gate_raw * sg_ref[:, cols]
            sig = 1.0 / (1.0 + jnp.exp(-gate))
            d_up = dmix * (gate * sig)
            d_gate = dmix * (up_raw * su_ref[:, cols]) * (sig * (1.0 + gate * (1.0 - sig)))
            gsu_ref[:, cols] += jnp.sum(d_up * up_raw, axis=0, keepdims=True)
            gsg_ref[:, cols] += jnp.sum(d_gate * gate_raw, axis=0, keepdims=True)
            ups[where, cols] = (d_up * su_ref[:, cols]).astype(jnp.bfloat16)
            gates[where, cols] = (d_gate * sg_ref[:, cols]).astype(jnp.bfloat16)

        over(hid // TILE, hidden)
        ready()

        def down(n):
            cols = tile_at(n, TILE)
            store(at, cols, dot_abt(ups[where, :], wall[0, cols, :]) + dot_abt(gates[where, :], wall[1, cols, :]))

        over(width // TILE, down)

    def part_copy(phase, kind, ch):
        part = tile_at(ch, crow)
        index = (phase * 3 + kind) * chunks + ch
        src, dst, peer = ((send_a, recv_a, core_peer), (send_d, recv_d, core_peer), (send_z, recv_z, z_peer))[kind]
        return remote(src.at[part, :], dst.at[part, :], part_send.at[index], part_recv.at[index], peer)

    def nothing():
        pass

    def tensor_pass(phase, buf, rows_fn, fillers):
        def keep_own(at, cols, value):
            own_part[at, cols] = value

        def to(ref):
            def store(at, cols, value):
                ref[at, cols] = value.astype(jnp.bfloat16)

            return store

        def to_z(at, cols, value):
            send_z[at, cols] = (value + recv_d[at, cols].astype(jnp.float32)).astype(jnp.bfloat16)

        rows_fn(0, tile_at(0, rows), keep_own, nothing)
        for ch in range(chunks):
            hop(buf, phase, ch, 1).wait_recv()
        if phase == 1:
            for ch in range(chunks):
                part_copy(0, 0, ch).wait_send()
        rows_fn(1, tile_at(0, rows), to(send_a), nothing)
        for ch in range(chunks):
            part_copy(phase, 0, ch).start()
        fillers[0]()
        def chunk(ch):
            hop(buf, phase, ch, 0).wait_recv()
            hop(buf, phase, ch, 2).start()
            at = tile_at(ch, crow)
            hop(buf, phase, ch, 2).wait_recv()
            if phase == 1:
                part_copy(0, 1, ch).wait_send()
            rows_fn(3, at, to(send_d), nothing)
            part_copy(phase, 1, ch).start()

            def ready():
                part_copy(phase, 1, ch).wait_recv()
                if phase == 1:
                    part_copy(0, 2, ch).wait_send()

            rows_fn(2, at, to_z, ready)
            part_copy(phase, 2, ch).start()

        over(chunks, chunk)
        fillers[1]()

    def transpose_into(dst, buf, slots):
        per_slot = rows // 128

        def one(i):
            slot = slots[0] + i // per_slot
            at = tile_at(lax.rem(i, per_slot), 128)
            to = tile_at(slots[0] * per_slot + i, 128)
            for n in range(width // TILE):
                dst[n * TILE : (n + 1) * TILE, to] = buf[slot, at, n * TILE : (n + 1) * TILE].T

        over(len(slots) * per_slot, one)

    tensor_pass(
        0, mids, forward_rows,
        [lambda: transpose_into(mid_t, mids, (0, 1)), lambda: transpose_into(mid_t, mids, (2, 3))],
    )

    loads[2].wait()

    def turn(at):
        mid = middle[at, :]
        branch_m = own_part[at, :] + recv_a[at, :].astype(jnp.float32) + recv_z[at, :].astype(jnp.float32)
        norm_m, factor_m = unit_of(branch_m)
        alpha = am_ref[...]
        y, factor_y = unit_of(mid + alpha * (norm_m - mid))
        out_ref[at, :] = y.astype(jnp.bfloat16)
        dy = cot[at, :].astype(jnp.float32)
        grad = factor_y * (dy - y * row_sum(y * dy))
        gam_ref[...] += jnp.sum(grad * (norm_m - mid), axis=0, keepdims=True)
        back = alpha * grad
        dbms[0, at, :] = (factor_m * (back - norm_m * row_sum(norm_m * back))).astype(jnp.bfloat16)
        dh2[at, :] = grad - back

    for ch in range(chunks):
        part_copy(0, 0, ch).wait_recv()
        part_copy(0, 2, ch).wait_recv()
        strips(ch, turn)
        hop(dbms, 1, ch, 0).start()
        hop(dbms, 1, ch, 1).start()

    def grad_store(m, q):
        dst = gwd_hbm.at[q] if m == 2 else gwu_hbm.at[q, m]
        return pltpu.make_async_copy(gw.at[m, pl.ds(q * qrows, qrows), :], dst, store_sems.at[m * nq + q])

    def weight_grad(m):
        lhs, rhs = ((mid_t, ups), (mid_t, gates), (dbm_t, mixed))[m]

        def block(i):
            q = i // (hid // TILE)
            cols = tile_at(lax.rem(i, hid // TILE), TILE)
            value = dot_ab(lhs[tile_at(q, TILE), :], rhs[:, cols])
            gw[m, tile_at(q, TILE), cols] = value.astype(jnp.bfloat16)

        over((width // TILE) * (hid // TILE), block)
        for q in range(nq):
            grad_store(m, q).start()

    def down_grad():
        transpose_into(dbm_t, dbms, (2, 3))
        weight_grad(2)

    tensor_pass(1, dbms, backward_rows, [lambda: transpose_into(dbm_t, dbms, (0, 1)), down_grad])

    def last(at):
        inputs, norm_a, factor_a, mid, factor_mid = make_middle(at)
        grad_mid = dh2[at, :] + own_part[at, :] + recv_a[at, :].astype(jnp.float32) + recv_z[at, :].astype(jnp.float32)
        grad = factor_mid * (grad_mid - mid * row_sum(mid * grad_mid))
        gaa_ref[...] += jnp.sum(grad * (norm_a - inputs), axis=0, keepdims=True)
        back = aa_ref[...] * grad
        dh1_ref[at, :] = grad - back
        mids[0, at, :] = (factor_a * (back - norm_a * row_sum(norm_a * back))).astype(jnp.bfloat16)

    for ch in range(chunks):
        hop(mids, 0, ch, 0).wait_send()
        hop(mids, 0, ch, 1).wait_send()
        part_copy(1, 0, ch).wait_recv()
        part_copy(1, 2, ch).wait_recv()
        strips(ch, last)

    dback = [
        remote(dparts.at[k], datt_ref.at[tile_at(t, rows), :], d2a_send.at[k - 1], d2a_recv.at[k - 1], (d, line[k]))
        for k in (1, 2, 3)
    ]
    for k in (3, 2, 1, 0):
        value = dot_ab(mids[0], wo[:, tile_at(line[k], heads_w)]).astype(jnp.bfloat16)
        if k:
            dparts[k] = value
            dback[k - 1].start()
        else:
            datt_ref[tile_at(t, rows), :] = value

    weight_grad(0)
    weight_grad(1)
    transpose_into(dbm_t, mids, (0,))

    def out_grad(n):
        at = tile_at(n, TILE)
        lhs = dbm_t[at, 0:rows]
        gwo[at, tile_at(t, heads_w)] = dot_ab(lhs, att_ref[tile_at(t, rows), :]).astype(jnp.bfloat16)
        for k in (1, 2, 3):
            gwo[at, tile_at(line[k], heads_w)] = dot_ab(lhs, parts[k - 1]).astype(jnp.bfloat16)

    over(width // TILE, out_grad)
    wo_store = pltpu.make_async_copy(gwo, gwo_hbm, store_sems.at[3 * nq])
    wo_store.start()

    for k in (1, 2, 3):
        remote(
            dparts.at[k], datt_ref.at[tile_at(line[k], rows), :], d2a_send.at[k - 1], d2a_recv.at[k - 1], (d, line[k])
        ).wait()
    for copy in a2a:
        copy.wait_send()
    for ch in range(chunks):
        hop(mids, 0, ch, 2).wait_send()
        for kind in range(3):
            hop(dbms, 1, ch, kind).wait_send()
            part_copy(1, kind, ch).wait_send()
    for m in range(3):
        for q in range(nq):
            grad_store(m, q).wait()
    wo_store.wait()


def middle_call(chunks, attended, wo, w_parts, tokens, cotangent, alpha_a, alpha_m, su, sg):
    rows, width = tokens.shape
    group, heads_w = attended.shape
    nq, _, qrows, hid = w_parts.shape
    bf, f32 = jnp.bfloat16, jnp.float32
    anywhere = pl.BlockSpec(memory_space=pl.ANY)
    dma = pltpu.SemaphoreType.DMA
    return pl.pallas_call(
        middle_body,
        out_shape=(
            jax.ShapeDtypeStruct((rows, width), bf),
            jax.ShapeDtypeStruct((group, heads_w), bf),
            jax.ShapeDtypeStruct((nq, 2, qrows, hid), bf),
            jax.ShapeDtypeStruct((nq, qrows, hid), bf),
            jax.ShapeDtypeStruct((width, width), bf),
            jax.ShapeDtypeStruct((rows, width), f32),
            jax.ShapeDtypeStruct((1, width), f32),
            jax.ShapeDtypeStruct((1, width), f32),
            jax.ShapeDtypeStruct((1, hid), f32),
            jax.ShapeDtypeStruct((1, hid), f32),
        ),
        in_specs=[vmem(), anywhere, anywhere, anywhere, anywhere] + [vmem()] * 4,
        out_specs=(vmem(), vmem(), anywhere, anywhere, anywhere) + (vmem(),) * 5,
        scratch_shapes=[
            pltpu.VMEM((width, width), bf),
            pltpu.VMEM((3, width, hid), bf),
            pltpu.VMEM((rows, width), bf),
            pltpu.VMEM((rows, width), bf),
            pltpu.VMEM((3, rows, heads_w), bf),
            pltpu.VMEM((4, rows, width), bf),
            pltpu.VMEM((4, rows, width), bf),
            pltpu.VMEM((width, 4 * rows), bf),
            pltpu.VMEM((width, 4 * rows), bf),
            pltpu.VMEM((4 * rows, hid), bf),
            pltpu.VMEM((4 * rows, hid), bf),
            pltpu.VMEM((4 * rows, hid), bf),
            pltpu.VMEM((rows, width), f32),
            pltpu.VMEM((rows, width), f32),
            pltpu.VMEM((rows, width), f32),
            pltpu.VMEM((rows, width), f32),
        ]
        + [pltpu.VMEM((rows, width), bf)] * 6
        + [
            pltpu.VMEM((3, width, hid), bf),
            pltpu.VMEM((width, width), bf),
            pltpu.VMEM((4, rows, heads_w), bf),
            pltpu.VMEM((1, hid), f32),
            pltpu.VMEM((1, hid), f32),
            dma((3 + 3 * nq,)),
            dma((3 * nq + 1,)),
            dma((6 * chunks,)),
            dma((6 * chunks,)),
            dma((3,)),
            dma((3,)),
            dma((3,)),
            dma((3,)),
            dma((6 * chunks,)),
            dma((6 * chunks,)),
        ],
        compiler_params=pltpu.CompilerParams(vmem_limit_bytes=67000000, collective_id=1, has_side_effects=True),
        cost_estimate=pl.CostEstimate(flops=10**11, bytes_accessed=10**8, transcendentals=10**6),
        name="middle",
    )(attended, wo, w_parts, tokens, cotangent, alpha_a, alpha_m, su, sg)


def remote_copy(src, dst, send_sem, recv_sem, peer):
    return pltpu.make_async_remote_copy(
        src_ref=src, dst_ref=dst, send_sem=send_sem, recv_sem=recv_sem, device_id=peer, device_id_type=MESH_ID
    )


def greet(peers):
    barrier = pltpu.get_barrier_semaphore()
    for peer in peers:
        pl.semaphore_signal(barrier, inc=1, device_id=peer, device_id_type=MESH_ID)
    pl.semaphore_wait(barrier, len(peers))


def rope_tables(order_ref, length_ref, cos_out, sin_out, col_out, start_out):
    group = order_ref.shape[1]
    lanes = cos_out.shape[1]
    places = lax.broadcasted_iota(jnp.int32, (1, group), 1)
    first = jnp.zeros((1, group), jnp.int32)
    begin = jnp.int32(0)
    for s in range(1, length_ref.shape[1]):
        begin = begin + length_ref[0, s - 1]
        first = jnp.where(places >= begin, begin, first)
    start_out[...] = first
    depth = (places - first).astype(jnp.float32)
    order = order_ref[...]
    order_f = order.astype(jnp.float32)
    lane = lax.broadcasted_iota(jnp.int32, (1, lanes), 1)
    half_width = HD // 2
    freq = jnp.exp((lane % half_width).astype(jnp.float32) * (-math.log(10000.0) / half_width))
    sign = jnp.where(lane % HD < half_width, -1.0, 1.0)

    def block(b):
        at = tile_at(b, 128)
        own = lax.broadcasted_iota(jnp.int32, (128, group), 0) + b * 128
        col_out[at, :] = row_sum(jnp.where(own == places, order_f, 0.0)).astype(jnp.int32)
        angles = row_sum(jnp.where(own == order, depth, 0.0)) * freq
        cos_out[at, :] = jnp.cos(angles)
        sin_out[at, :] = jnp.sin(angles) * sign

    over(group // 128, block)


def spread_body(
    count, tok, w_up, w_gate, w_down, wq, wk, wv, wo, order_ref, length_ref,
    pair, tok2, wqkv, wo_all, cos_out, sin_out, col_out, start_out,
    own_mlp, own_att, wo_rows, load_sem, keep_sem, a_send, a_recv, b_send, b_recv, tok_send, tok_recv,
    qkv_send, qkv_recv, oz_send, oz_recv, oq_send, oq_recv, oc_send, oc_recv,
):
    d = lax.axis_index("dp")
    t = lax.axis_index("tensor")
    core = lax.rem(d, 2)
    home = core == t // 2
    far = (d - core + t // 2, flip2(t))
    wrows, wcols = wq.shape
    half = count // 2
    mlp = (w_up, w_gate, w_down)
    att = (wq, wk, wv)
    mine = tile_at(d, wrows)
    side = tile_at(core, wrows)
    other_side = tile_at(1 - core, wrows)

    barrier = pltpu.get_barrier_semaphore()

    def dp_peer(i):
        return lax.rem(d + 1 + i, count)

    def hello(i):
        pl.semaphore_signal(barrier, inc=1, device_id=(dp_peer(i), t), device_id_type=MESH_ID)

    over(count - 1, hello)
    for k in (1, 2, 3):
        pl.semaphore_signal(barrier, inc=1, device_id=(d, lax.rem(t + k, 4)), device_id_type=MESH_ID)
    pl.semaphore_signal(barrier, inc=1, device_id=(flip1(d), flip2(t)), device_id_type=MESH_ID)
    pl.semaphore_wait(barrier, count + 3)

    def b_copy(m):
        return remote_copy(mlp[m], pair.at[m, side, :], b_send.at[m], b_recv.at[core * 3 + m], far)

    def a_copy(m):
        return remote_copy(mlp[m], pair.at[m, side, :], a_send.at[m], a_recv.at[m], (flip1(d), t))

    tok_copy = remote_copy(tok, tok2, tok_send, tok_recv, (d, flip1(t)))
    def oz_copy(k):
        return remote_copy(wo, wo_rows.at[:, tile_at(t, wcols)], oz_send.at[k - 1], oz_recv.at[k - 1], (d, lax.rem(t + k, 4)))

    for k in (1, 2, 3):
        oz_copy(k).start()
    tok_copy.start()
    for m in range(3):
        b_copy(m).start()
    load_o = pltpu.make_async_copy(wo, wo_rows.at[:, tile_at(t, wcols)], load_sem.at[0])
    load_o.start()

    def qkv_copy(i, m):
        return remote_copy(
            att[m], wqkv.at[mine, pl.ds(m * wcols, wcols)], qkv_send.at[i, m], qkv_recv.at[i, m], (dp_peer(i), t)
        )

    def qkv_start(i):
        for m in range(3):
            qkv_copy(i, m).start()

    over(count - 1, qkv_start)

    @pl.when(jnp.logical_not(home))
    def _():
        for m in range(3):
            a_copy(m).start()

    loads = [pltpu.make_async_copy(mlp[m], own_mlp.at[m], load_sem.at[1 + m]) for m in range(3)]
    loads += [pltpu.make_async_copy(att[m], own_att.at[m], load_sem.at[4 + m]) for m in range(3)]
    for copy in loads:
        copy.start()
    for copy in loads:
        copy.wait()
    keeps = [
        pltpu.make_async_copy(own_att.at[m], wqkv.at[mine, pl.ds(m * wcols, wcols)], keep_sem.at[m]) for m in range(3)
    ]
    for copy in keeps:
        copy.start()
    pair_keeps = [pltpu.make_async_copy(own_mlp.at[m], pair.at[m, side, :], keep_sem.at[3 + m]) for m in range(3)]

    @pl.when(home)
    def _():
        for copy in pair_keeps:
            copy.start()

    load_o.wait()
    for k in (1, 2, 3):
        oz_copy(k).wait_recv()
    keep_o = pltpu.make_async_copy(wo_rows, wo_all.at[mine, :], keep_sem.at[6])
    keep_o.start()

    def oq_copy(j):
        return remote_copy(wo_rows, wo_all.at[mine, :], oq_send.at[j], oq_recv.at[j], (lax.rem(d + 2 + 2 * j, count), t))

    def oc_own():
        return remote_copy(wo_rows, wo_all.at[mine, :], oc_send.at[half - 1], oc_recv.at[half - 1], (flip1(d), t))

    def oc_copy(j):
        rows = tile_at(lax.rem(d + count - 2 - 2 * j, count), wrows)
        return remote_copy(wo_all.at[rows, :], wo_all.at[rows, :], oc_send.at[j], oc_recv.at[j], (flip1(d), t))

    over(half - 1, lambda j: oq_copy(j).start())
    oc_own().start()
    rope_tables(order_ref, length_ref, cos_out, sin_out, col_out, start_out)

    def oq_next(j):
        oq_copy(j).wait_recv()
        oc_copy(j).start()

    over(half - 1, oq_next)

    def qkv_wait(i):
        for m in range(3):
            qkv_copy(i, m).wait()

    over(count - 1, qkv_wait)
    over(half - 1, lambda j: oq_copy(j).wait_send())
    over(half - 1, lambda j: oc_copy(j).wait())
    oc_own().wait()
    for k in (1, 2, 3):
        oz_copy(k).wait_send()
    keep_o.wait()
    for copy in keeps:
        copy.wait()
    tok_copy.wait()
    for m in range(3):
        b_copy(m).wait_send()

    @pl.when(home)
    def _():
        for m in range(3):
            pair_keeps[m].wait()
            remote_copy(mlp[m], pair.at[m, other_side, :], a_send.at[m], a_recv.at[m], (flip1(d), t)).wait_recv()

    @pl.when(jnp.logical_not(home))
    def _():
        for m in range(3):
            a_copy(m).wait_send()
            for c in range(2):
                remote_copy(
                    mlp[m], pair.at[m, pl.ds(c * wrows, wrows), :], b_send.at[m], b_recv.at[c * 3 + m], far
                ).wait_recv()


def spread_call(count, tokens, w_up, w_gate, w_down, wq, wk, wv, wo, order, lengths):
    rows, width = tokens.shape
    group = order.shape[1]
    wrows, wcols = wq.shape
    hid = w_up.shape[1]
    bf = jnp.bfloat16
    anywhere = pl.BlockSpec(memory_space=pl.ANY)
    dma = pltpu.SemaphoreType.DMA
    return pl.pallas_call(
        functools.partial(spread_body, count),
        out_shape=(
            jax.ShapeDtypeStruct((3, 2 * wrows, hid), bf),
            jax.ShapeDtypeStruct((rows, width), bf),
            jax.ShapeDtypeStruct((width, 3 * wcols), bf),
            jax.ShapeDtypeStruct((width, width), bf),
            jax.ShapeDtypeStruct((group, 2 * HD), jnp.float32),
            jax.ShapeDtypeStruct((group, 2 * HD), jnp.float32),
            jax.ShapeDtypeStruct((group, 1), jnp.int32),
            jax.ShapeDtypeStruct((1, group), jnp.int32),
        ),
        in_specs=[anywhere] * 8 + [vmem(), pl.BlockSpec(memory_space=pltpu.SMEM)],
        out_specs=(anywhere,) * 4 + (vmem(),) * 4,
        scratch_shapes=[
            pltpu.VMEM((3, wrows, hid), bf),
            pltpu.VMEM((3, wrows, wcols), bf),
            pltpu.VMEM((wrows, width), bf),
            dma((7,)), dma((7,)), dma((3,)), dma((3,)), dma((3,)), dma((6,)), dma, dma,
            dma((count - 1, 3)), dma((count - 1, 3)), dma((3,)), dma((3,)),
            dma((count // 2,)), dma((count // 2,)), dma((count // 2,)), dma((count // 2,)),
        ],
        compiler_params=pltpu.CompilerParams(vmem_limit_bytes=VMEM_LIMIT, collective_id=2, has_side_effects=True),
        name="spread",
    )(tokens, w_up, w_gate, w_down, wq, wk, wv, wo, order, lengths)


def head_sums(value):
    width = value.shape[1]
    same = (
        lax.broadcasted_iota(jnp.int32, (width, width), 0) // HD == lax.broadcasted_iota(jnp.int32, (width, width), 1) // HD
    )
    ones = jnp.where(same, 1.0, 0.0).astype(jnp.bfloat16)
    high = value.astype(jnp.bfloat16)
    low = (value - high.astype(jnp.float32)).astype(jnp.bfloat16)
    return dot_ab(high, ones) + dot_ab(low, ones)


def swap_halves(value):
    width = value.shape[1]
    lane = lax.broadcasted_iota(jnp.int32, value.shape, 1) % HD
    return jnp.where(lane < HD // 2, pltpu.roll(value, width - HD // 2, 1), pltpu.roll(value, HD // 2, 1))


def project_body(
    tok, tok2, wqkv, cos_ref, sin_ref, order_col, gain_ref, q_ref, k_ref, v_ref, raw_ref, x_hbm,
    xs, plain, load_sem, keep_sem, mid_send, recv, on_send,
):
    t = lax.axis_index("tensor")
    d = lax.axis_index("dp")
    _, rows, width = xs.shape
    group, cols = q_ref.shape
    near = flip1(t)
    across = 3 - t
    inner = (t + 1) // 2 == 1
    arrive = (2 - t // 2, 3 - 3 * (t // 2))
    part = rows // 2
    greet([(d, near), (d, across)])

    def mid_copy(k):
        src = (tok, tok2)[k // 2].at[pl.ds((k % 2) * part, part), :]
        dst = xs.at[(t, near)[k // 2], pl.ds((k % 2) * part, part), :]
        return remote_copy(src, dst, mid_send.at[k], recv.at[k], (d, across))

    def on_copy(k):
        ref = xs.at[arrive[k // 2], pl.ds((k % 2) * part, part), :]
        return remote_copy(ref, ref, on_send.at[k], recv.at[k], (d, near))

    @pl.when(inner)
    def _():
        for k in range(4):
            mid_copy(k).start()

    loads = [
        pltpu.make_async_copy(tok, xs.at[t], load_sem.at[0]),
        pltpu.make_async_copy(tok2, xs.at[near], load_sem.at[1]),
    ]
    for copy in loads:
        copy.start()

    def keep(index, slot):
        return pltpu.make_async_copy(xs.at[slot], x_hbm.at[tile_at(slot, rows), :], keep_sem.at[index])

    def work(index, slot):
        keep(index, slot).start()

        def strip(i):
            at = tile_at(slot * (rows // WIDE_STRIP) + i, WIDE_STRIP)
            x = xs[slot, tile_at(i, WIDE_STRIP), :]
            cos = jnp.concatenate([cos_ref[at, :]] * (cols // cos_ref.shape[1]), axis=1)
            sin = jnp.concatenate([sin_ref[at, :]] * (cols // sin_ref.shape[1]), axis=1)
            for m in range(2):
                raw = dot_ab(x, wqkv[:, m * cols : (m + 1) * cols])
                raw_ref[at, m * cols : (m + 1) * cols] = raw.astype(jnp.bfloat16)
                normed = raw * lax.rsqrt(head_sums(raw * raw) + EPS) * gain_ref[:, tile_at(t, cols)]
                plain[at, m * cols : (m + 1) * cols] = (normed * cos + swap_halves(normed) * sin).astype(jnp.bfloat16)
            plain[at, 2 * cols : 3 * cols] = dot_ab(x, wqkv[:, 2 * cols : 3 * cols]).astype(jnp.bfloat16)

        over(rows // WIDE_STRIP, strip)

    loads[0].wait()
    work(0, t)
    loads[1].wait()
    work(1, near)
    for k in range(4):
        slot = arrive[k // 2]
        ref = xs.at[slot, pl.ds((k % 2) * part, part), :]
        remote_copy(ref, ref, on_send.at[k], recv.at[k], (d, near)).wait_recv()

        @pl.when(inner)
        def _():
            on_copy(k).start()

        if k % 2:
            work(2 + k // 2, slot)

    def permute(b):
        at = tile_at(b, BLK)
        hot = (lax.broadcasted_iota(jnp.int32, (BLK, group), 1) == order_col[at, :]).astype(jnp.float32)
        value = dot_ab(hot.astype(jnp.bfloat16), plain[...])
        for m, ref in enumerate((q_ref, k_ref, v_ref)):
            ref[at, :] = value[:, m * cols : (m + 1) * cols].astype(jnp.bfloat16)

    over(group // BLK, permute)
    for index, slot in enumerate((t, near, *arrive)):
        keep(index, slot).wait()

    @pl.when(inner)
    def _():
        for k in range(4):
            mid_copy(k).wait_send()
            on_copy(k).wait_send()


def project_call(tokens, tok2, wqkv, cos, sin, order_col, gains):
    rows, width = tokens.shape
    group = order_col.shape[0]
    cols = wqkv.shape[1] // 3
    bf = jnp.bfloat16
    anywhere = pl.BlockSpec(memory_space=pl.ANY)
    dma = pltpu.SemaphoreType.DMA
    return pl.pallas_call(
        project_body,
        out_shape=(jax.ShapeDtypeStruct((group, cols), bf),) * 3
        + (jax.ShapeDtypeStruct((group, 2 * cols), bf), jax.ShapeDtypeStruct((group, width), bf)),
        in_specs=[anywhere, anywhere] + [vmem()] * 5,
        out_specs=(vmem(),) * 4 + (anywhere,),
        scratch_shapes=[
            pltpu.VMEM((group // rows, rows, width), bf),
            pltpu.VMEM((group, 3 * cols), bf),
            dma((2,)), dma((4,)), dma((4,)), dma((4,)), dma((4,)),
        ],
        compiler_params=pltpu.CompilerParams(vmem_limit_bytes=VMEM_LIMIT, collective_id=3, has_side_effects=True),
        cost_estimate=pl.CostEstimate(flops=6 * 10**10, bytes_accessed=10**7, transcendentals=10**6),
        name="project",
    )(tokens, tok2, wqkv, cos, sin, order_col, gains)


def tail_body(
    grad_ref, raw_ref, cos_ref, sin_ref, wqkv, x_hbm, down_hbm, kept_ref, gain_ref, tok_out, gq, gain_sum, down_out,
    xs, x_t, draw, part_far, part_mid, part_near, own_part, from_a, from_b, from_c, from_d, from_e, from_f,
    near_mlp, far_mlp, load_sem, hop_send, hop_recv, keep_sem, near_send, near_recv, far_send, far_recv,
):
    d = lax.axis_index("dp")
    t = lax.axis_index("tensor")
    rows, width = tok_out.shape
    group = draw.shape[0]
    cols = draw.shape[1] // 3
    near = flip1(t)
    inner = (t + 1) // 2 == 1
    outer = jnp.logical_not(inner)
    far, mid = 3 - 3 * (t // 2), 2 - t // 2
    chunk = rows // 2
    greet([(d, near), (d, 3 - t), (d, flip2(t)), (flip1(d), t), (flip1(d), flip2(t))])

    core = lax.rem(d, 2)
    home = core == t // 2
    away = jnp.logical_not(home)
    near_copy = remote_copy(down_hbm.at[1 - core], near_mlp, near_send, near_recv, (flip1(d), t))
    far_same = remote_copy(down_hbm.at[core], far_mlp, far_send.at[0], far_recv, (d, flip2(t)))
    far_cross = remote_copy(down_hbm.at[1 - core], far_mlp, far_send.at[1], far_recv, (flip1(d), flip2(t)))
    keep_mlp = pltpu.make_async_copy(down_hbm.at[core], near_mlp, keep_sem)

    @pl.when(home)
    def _():
        near_copy.start()
        keep_mlp.start()

    @pl.when(away)
    def _():
        far_same.start()
        far_cross.start()

    load_x = pltpu.make_async_copy(x_hbm, xs, load_sem)
    load_x.start()

    def hop(kind, ch):
        src, dst, to = (
            (part_far, from_a, near),
            (part_mid, from_b, near),
            (part_near, from_c, near),
            (part_far, from_d, 3 - t),
            (part_mid, from_e, 3 - t),
            (part_near, from_f, near),
        )[kind]
        part = tile_at(ch, chunk)
        return remote_copy(src.at[part, :], dst.at[part, :], hop_send.at[kind, ch], hop_recv.at[kind, ch], (d, to))

    gain_sum[...] = jnp.zeros_like(gain_sum)

    def work(slot, ch, ref):
        at = tile_at(2 * slot + ch, chunk)
        to = tile_at(ch, chunk)
        cos = jnp.concatenate([cos_ref[at, :]] * (cols // cos_ref.shape[1]), axis=1)
        sin = jnp.concatenate([sin_ref[at, :]] * (cols // sin_ref.shape[1]), axis=1)
        gain = gain_ref[:, tile_at(t, cols)]
        for m in range(2):
            grad = grad_ref[at, m * cols : (m + 1) * cols].astype(jnp.float32)
            raw = raw_ref[at, m * cols : (m + 1) * cols].astype(jnp.float32)
            back = grad * cos - swap_halves(grad) * sin
            factor = lax.rsqrt(head_sums(raw * raw) + EPS)
            normed = raw * factor
            gain_sum[...] += jnp.sum(back * normed, axis=0, keepdims=True)
            scaled = back * gain
            draw[at, m * cols : (m + 1) * cols] = (factor * (scaled - normed * head_sums(normed * scaled))).astype(
                jnp.bfloat16
            )
        draw[at, 2 * cols : 3 * cols] = grad_ref[at, 2 * cols : 3 * cols]

        def product(n):
            tile = tile_at(n, TILE)
            ref[to, tile] = dot_abt(draw[at, :], wqkv[tile, :]).astype(ref.dtype)

        over(width // TILE, product)

    def send_part(kind, slot, ref):
        def one(ch):
            work(slot, ch, ref)

            @pl.when(outer)
            def _():
                hop(kind, ch).start()

        over(2, one)

    send_part(0, far, part_far)
    send_part(1, mid, part_mid)
    send_part(2, near, part_near)
    over(2, lambda ch: work(t, ch, own_part))

    def pass_on(kind, ch, own, got, then):
        @pl.when(inner)
        def _():
            part = pl.ds(ch * chunk, chunk)
            hop(kind, ch).wait_recv()
            own[part, :] = (own[part, :].astype(jnp.float32) + got[part, :].astype(jnp.float32)).astype(jnp.bfloat16)
            hop(then, ch).start()

    pass_on(0, 0, part_far, from_a, 3)
    pass_on(0, 1, part_far, from_a, 3)

    load_x.wait()

    def flip_block(b):
        at = tile_at(b, 128)
        for n in range(width // TILE):
            x_t[n * TILE : (n + 1) * TILE, at] = xs[at, n * TILE : (n + 1) * TILE].T

    over(group // 128, flip_block)
    pass_on(3, 0, part_near, from_d, 5)

    def weight_grad(n):
        tile = tile_at(n, TILE)
        gq[tile, :] = dot_ab(x_t[tile, :], draw[...]).astype(jnp.bfloat16)

    over(width // TILE, weight_grad)
    pass_on(1, 0, part_mid, from_b, 4)
    pass_on(3, 1, part_near, from_d, 5)
    pass_on(1, 1, part_mid, from_b, 4)

    @pl.when(home)
    def _():
        keep_mlp.wait()
        near_copy.wait_send()

    @pl.when(away)
    def _():
        near_copy.wait_recv()

    far_same.wait_recv()
    down_out[...] = near_mlp[...].astype(jnp.float32) + far_mlp[...].astype(jnp.float32)

    @pl.when(away)
    def _():
        far_same.wait_send()
        far_cross.wait_send()

    for ch in range(2):
        part = pl.ds(ch * chunk, chunk)

        @pl.when(inner)
        def _():
            hop(2, ch).wait_recv()
            hop(4, ch).wait_recv()
            tok_out[part, :] = (
                kept_ref[part, :]
                + own_part[part, :]
                + from_c[part, :].astype(jnp.float32)
                + from_e[part, :].astype(jnp.float32)
            )

        @pl.when(outer)
        def _():
            hop(5, ch).wait_recv()
            tok_out[part, :] = kept_ref[part, :] + own_part[part, :] + from_f[part, :].astype(jnp.float32)

    for ch in range(2):

        @pl.when(inner)
        def _():
            for kind in (3, 4, 5):
                hop(kind, ch).wait_send()

        @pl.when(outer)
        def _():
            for kind in (0, 1, 2):
                hop(kind, ch).wait_send()


def tail_call(count, grad_qkv, raw, cos, sin, wqkv, all_tokens, down, kept, gains):
    rows, width = kept.shape
    wrows, hid = width // count, down.shape[1]
    group, three = grad_qkv.shape
    bf, f32 = jnp.bfloat16, jnp.float32
    anywhere = pl.BlockSpec(memory_space=pl.ANY)
    dma = pltpu.SemaphoreType.DMA
    shape = jax.ShapeDtypeStruct
    return pl.pallas_call(
        tail_body,
        out_shape=(
            shape((rows, width), f32),
            shape((width, three), bf),
            shape((1, three // 3), f32),
            shape((wrows, hid), f32),
        ),
        in_specs=[vmem()] * 5 + [anywhere] * 2 + [vmem()] * 2,
        out_specs=(vmem(),) * 4,
        scratch_shapes=[
            pltpu.VMEM((group, width), bf),
            pltpu.VMEM((width, group), bf),
            pltpu.VMEM((group, three), bf),
            pltpu.VMEM((rows, width), bf),
            pltpu.VMEM((rows, width), bf),
            pltpu.VMEM((rows, width), bf),
            pltpu.VMEM((rows, width), f32),
        ]
        + [pltpu.VMEM((rows, width), bf)] * 6
        + [pltpu.VMEM((wrows, hid), bf)] * 2
        + [dma, dma((6, 2)), dma((6, 2)), dma, dma, dma, dma((2,)), dma],
        compiler_params=pltpu.CompilerParams(vmem_limit_bytes=VMEM_LIMIT, collective_id=4, has_side_effects=True),
        cost_estimate=pl.CostEstimate(flops=6 * 10**10, bytes_accessed=10**7, transcendentals=10**6),
        name="tail",
    )(grad_qkv, raw, cos, sin, wqkv, all_tokens, down.reshape(2, wrows, hid), kept, gains)


def settle_body(
    count, gq_hbm, gwo_hbm, mlp_hbm, gain_ref, gaa_ref, gam_ref, gsu_ref, gsg_ref,
    q_out, k_out, v_out, wo_out, up_out, gate_out, gain_out, aa_out, su_out, sg_out, am_out,
    own_q, core_q, got_q, own_w, core_w, got_w, wo_mid, got_z, near_mlp, far_mlp, vec, got_v, vec_mid, got_s,
    load_sem, core_send, core_recv, q_send, q_recv, w_send, w_recv, z_send, z_recv, v_send, v_recv, s_send, s_recv,
    near_send, near_recv, mlp_send, mlp_recv,
):
    d = lax.axis_index("dp")
    t = lax.axis_index("tensor")
    half, wrows, three = got_q.shape
    cols = three // 3
    width = gaa_ref.shape[1]
    chip, core = d // 2, lax.rem(d, 2)
    home = core == t // 2
    away = jnp.logical_not(home)
    f32, bf = jnp.float32, jnp.bfloat16

    def dp_peer(i):
        return lax.rem(d + 1 + i, count)

    def line_peer(k):
        return lax.rem(t + k, 4)

    def chip_peer(i):
        return lax.rem(chip + 1 + i, half)

    barrier = pltpu.get_barrier_semaphore()
    over(
        count - 1,
        lambda i: pl.semaphore_signal(barrier, inc=1, device_id=(dp_peer(i), t), device_id_type=MESH_ID),
    )
    for k in (1, 2, 3):
        pl.semaphore_signal(barrier, inc=1, device_id=(d, line_peer(k)), device_id_type=MESH_ID)
    pl.semaphore_signal(barrier, inc=1, device_id=(flip1(d), flip2(t)), device_id_type=MESH_ID)
    pl.semaphore_wait(barrier, count + 3)

    near_copy = remote_copy(mlp_hbm.at[:, 1 - core], near_mlp, near_send, near_recv, (flip1(d), t))
    keep_mlp = pltpu.make_async_copy(mlp_hbm.at[:, core], near_mlp, load_sem.at[0])

    hid = near_mlp.shape[2]

    def far_same(u):
        m, part = u // 2, tile_at(u % 2, hid // 2)
        return remote_copy(
            mlp_hbm.at[m, core, :, part], far_mlp.at[m, :, part], mlp_send.at[u], mlp_recv.at[u], (d, flip2(t))
        )

    def far_cross(u):
        m, part = u // 2, tile_at(u % 2, hid // 2)
        return remote_copy(
            mlp_hbm.at[m, 1 - core, :, part], far_mlp.at[m, :, part], mlp_send.at[4 + u], mlp_recv.at[u],
            (flip1(d), flip2(t)),
        )

    def far_start(u):
        @pl.when(away)
        def _():
            far_same(u).start()
            far_cross(u).start()

    @pl.when(home)
    def _():
        near_copy.start()
        keep_mlp.start()

    for u in range(3):
        far_start(u)

    core_w_copy = remote_copy(gwo_hbm.at[:, 1 - core], core_w, core_send.at[0], core_recv.at[0], (flip1(d), t))
    core_q_copy = remote_copy(gq_hbm.at[:, 1 - core], core_q, core_send.at[1], core_recv.at[1], (flip1(d), t))
    load_w = pltpu.make_async_copy(gwo_hbm.at[:, core], own_w, load_sem.at[1])
    load_q = pltpu.make_async_copy(gq_hbm.at[:, core], own_q, load_sem.at[2])
    core_w_copy.start()
    core_q_copy.start()
    load_w.start()
    load_q.start()

    vec[...] = jnp.zeros_like(vec)
    for row, ref in enumerate((gaa_ref, gam_ref, gsu_ref, gsg_ref)):
        vec[row : row + 1, :] = ref[...]
    vec[4:5, 0:cols] = gain_ref[...]
    got_v[d] = vec[...]

    def v_copy(i):
        return remote_copy(vec, got_v.at[d], v_send.at[i], v_recv.at[i], (dp_peer(i), t))

    over(count - 1, lambda i: v_copy(i).start())

    def chip_copy(own, got, sends, recvs, i):
        return remote_copy(own.at[chip_peer(i)], got.at[chip], sends.at[i], recvs.at[i], (2 * chip_peer(i) + core, t))

    def w_copy(i):
        return chip_copy(own_w, got_w, w_send, w_recv, i)

    def q_copy(i):
        return chip_copy(own_q, got_q, q_send, q_recv, i)

    def join(own, other, got):
        def one(e):
            own[e] = (own[e].astype(f32) + other[e].astype(f32)).astype(bf)

        over(half, one)
        got[chip] = own[chip]

    load_w.wait()
    core_w_copy.wait_recv()
    join(own_w, core_w, got_w)
    over(half - 1, lambda i: w_copy(i).start())
    load_q.wait()
    core_q_copy.wait_recv()
    join(own_q, core_q, got_q)
    over(half - 1, lambda i: q_copy(i).start())

    def total_of(got):
        return lax.fori_loop(1, half, lambda i, total: total + got[i].astype(f32), got[0].astype(f32))

    over(half - 1, lambda i: w_copy(i).wait_recv())
    wo_mid[...] = total_of(got_w).astype(bf)

    def z_copy(k):
        return remote_copy(
            wo_mid.at[:, tile_at(line_peer(k), cols)], got_z.at[t], z_send.at[k - 1], z_recv.at[k - 1], (d, line_peer(k))
        )

    for k in (1, 2, 3):
        z_copy(k).start()
    got_z[t] = wo_mid[:, tile_at(t, cols)]

    over(count - 1, lambda i: v_copy(i).wait_recv())
    even, odd = lax.fori_loop(
        1, half, lambda i, total: (total[0] + got_v[2 * i], total[1] + got_v[2 * i + 1]), (got_v[0], got_v[1])
    )
    both = even + odd
    vec_mid[...] = jnp.concatenate([both[0:2], even[2:3], odd[2:3], even[3:4], odd[3:4], both[4:5], both[4:5]], axis=0)

    def s_copy(k):
        return remote_copy(vec_mid, got_s.at[t], s_send.at[k - 1], s_recv.at[k - 1], (d, line_peer(k)))

    for k in (1, 2, 3):
        s_copy(k).start()
    got_s[t] = vec_mid[...]
    far_start(3)

    over(half - 1, lambda i: q_copy(i).wait_recv())
    total = total_of(got_q)
    for m, ref in enumerate((q_out, k_out, v_out)):
        ref[...] = total[:, m * cols : (m + 1) * cols]

    for k in (1, 2, 3):
        z_copy(k).wait_recv()
        s_copy(k).wait_recv()
    wo_out[...] = got_z[0].astype(f32) + got_z[1].astype(f32) + got_z[2].astype(f32) + got_z[3].astype(f32)
    shared = got_s[0] + got_s[1] + got_s[2] + got_s[3]
    aa_out[...] = shared[0:1]
    am_out[...] = shared[1:2]
    pairs = (got_s[0] + got_s[2], got_s[1] + got_s[3])
    for s in range(4):
        su_out[:, s * width : (s + 1) * width] = pairs[s % 2][2 + s // 2 : 3 + s // 2]
        sg_out[:, s * width : (s + 1) * width] = pairs[s % 2][4 + s // 2 : 5 + s // 2] * math.sqrt(D)
        gain_out[:, s * cols : (s + 1) * cols] = got_s[s][6:7, 0:cols]

    @pl.when(home)
    def _():
        keep_mlp.wait()
        near_copy.wait_send()

    @pl.when(away)
    def _():
        near_copy.wait_recv()

    for m, ref in enumerate((up_out, gate_out)):
        far_same(2 * m).wait_recv()
        far_same(2 * m + 1).wait_recv()
        ref[...] = near_mlp[m].astype(f32) + far_mlp[m].astype(f32)

    @pl.when(away)
    def _():
        for u in range(4):
            far_same(u).wait_send()
            far_cross(u).wait_send()

    core_w_copy.wait_send()
    core_q_copy.wait_send()
    over(count - 1, lambda i: v_copy(i).wait_send())

    def drain(i):
        w_copy(i).wait_send()
        q_copy(i).wait_send()

    over(half - 1, drain)
    for k in (1, 2, 3):
        z_copy(k).wait_send()
        s_copy(k).wait_send()


def settle_call(count, gq, gwo, mlp, gain_sum, gaa, gam, gsu, gsg):
    width, three = gq.shape
    half = count // 2
    cols = three // 3
    wrows = width // count
    hid = mlp.shape[2]
    bf, f32 = jnp.bfloat16, jnp.float32
    anywhere = pl.BlockSpec(memory_space=pl.ANY)
    dma = pltpu.SemaphoreType.DMA
    shape = jax.ShapeDtypeStruct
    return pl.pallas_call(
        functools.partial(settle_body, count),
        out_shape=(shape((wrows, cols), f32),) * 4
        + (shape((wrows, hid), f32),) * 2
        + (
            shape((1, 4 * cols), f32),
            shape((1, width), f32),
            shape((1, 4 * hid), f32),
            shape((1, 4 * hid), f32),
            shape((1, width), f32),
        ),
        in_specs=[anywhere] * 3 + [vmem()] * 5,
        out_specs=(vmem(),) * 11,
        scratch_shapes=[pltpu.VMEM((half, wrows, three), bf)] * 3
        + [pltpu.VMEM((half, wrows, width), bf)] * 3
        + [
            pltpu.VMEM((wrows, width), bf),
            pltpu.VMEM((4, wrows, cols), bf),
            pltpu.VMEM((2, wrows, hid), bf),
            pltpu.VMEM((2, wrows, hid), bf),
            pltpu.VMEM((8, width), f32),
            pltpu.VMEM((count, 8, width), f32),
            pltpu.VMEM((8, width), f32),
            pltpu.VMEM((4, 8, width), f32),
            dma((3,)),
            dma((2,)), dma((2,)),
            dma((half - 1,)), dma((half - 1,)), dma((half - 1,)), dma((half - 1,)),
            dma((3,)), dma((3,)),
            dma((count - 1,)), dma((count - 1,)),
            dma((3,)), dma((3,)),
            dma, dma, dma((8,)), dma((4,)),
        ],
        compiler_params=pltpu.CompilerParams(vmem_limit_bytes=VMEM_LIMIT, collective_id=5, has_side_effects=True),
        cost_estimate=pl.CostEstimate(flops=10**9, bytes_accessed=10**7, transcendentals=0),
        name="settle",
    )(
        gq.reshape(half, 2, wrows, three),
        gwo.reshape(half, 2, wrows, width),
        mlp.reshape(2, 2, wrows, hid),
        gain_sum, gaa, gam, gsu, gsg,
    )


def deliver_body(count, total, *refs):
    ins, outs, rest = refs[:total], refs[total : 2 * total], refs[2 * total :]
    held, load_sem, store_sem = rest[:count], rest[count], rest[count + 1]
    loads = [pltpu.make_async_copy(ins[i], held[i], load_sem.at[i]) for i in range(count)]
    stores = [pltpu.make_async_copy(held[i], outs[i], store_sem.at[i]) for i in range(count)]
    for copy in loads:
        copy.start()
    for i in range(count, total):
        outs[i][...] = ins[i][0, :]
    for load, store in zip(loads, stores):
        load.wait()
        store.start()
    for copy in stores:
        copy.wait()


def deliver_call(arrays, vectors):
    total = len(arrays) + len(vectors)
    specs = [pl.BlockSpec(memory_space=pl.ANY)] * len(arrays) + [vmem()] * len(vectors)
    return pl.pallas_call(
        functools.partial(deliver_body, len(arrays), total),
        out_shape=tuple(jax.ShapeDtypeStruct(a.shape, a.dtype) for a in arrays)
        + tuple(jax.ShapeDtypeStruct((v.shape[1],), v.dtype) for v in vectors),
        in_specs=specs,
        out_specs=tuple(specs),
        scratch_shapes=[pltpu.VMEM(a.shape, a.dtype) for a in arrays] + [pltpu.SemaphoreType.DMA((len(arrays),))] * 2,
        compiler_params=pltpu.CompilerParams(vmem_limit_bytes=VMEM_LIMIT),
        name="deliver",
    )(*arrays, *vectors)


def same_core_groups(dp_count):
    return [list(range(parity, dp_count, 2)) for parity in range(2)]


def on_device(
    tokens,
    w_query,
    w_key,
    w_value,
    w_out_t,
    w_up,
    w_gate,
    w_down_t,
    scale_qk,
    alpha_attn,
    scale_up,
    scale_gate,
    alpha_mlp,
    order,
    lengths,
    cotangent,
):
    dp_count = lax.axis_size("dp")
    pair, near_tokens, wqkv, wo_every, cos_table, sin_table, order_col, start = spread_call(
        dp_count, tokens, w_up, w_gate, w_down_t, w_query, w_key, w_value, w_out_t, order, lengths
    )
    low = lax.slice(start[0], (0,), (start.shape[1],), (BLK,)) // BLK
    mlp_parts = lax.all_gather(
        pair, "dp", axis=0, tiled=False, axis_index_groups=same_core_groups(dp_count)
    )
    queries, key_rows, value_rows, raw, all_tokens = project_call(
        tokens, near_tokens, wqkv, cos_table, sin_table, order_col, scale_qk[None, :]
    )
    attended, log_totals, attended_plain = attn_fwd(low, start, order, queries, key_rows, value_rows)
    out_rows, grad_att_rows, up_gate_grads, down_grads, wo_grads, grad_h1_kept, grad_alpha_a, grad_alpha_m, grad_su, grad_sv = middle_call(
        2,
        attended_plain,
        wo_every,
        mlp_parts,
        tokens,
        cotangent,
        alpha_attn[None, :],
        alpha_mlp[None, :],
        scale_up[None, :],
        scale_gate[None, :],
    )
    grad_qkv = attn_bwd(
        low, start, order, order_col, log_totals, queries, key_rows, value_rows, attended, grad_att_rows
    )
    groups = same_core_groups(dp_count)
    down_sums = lax.psum_scatter(down_grads, "dp", scatter_dimension=0, tiled=False, axis_index_groups=groups)
    up_gate_sums = lax.psum_scatter(up_gate_grads, "dp", scatter_dimension=0, tiled=False, axis_index_groups=groups)
    grad_tokens, grad_q, gain_sum, grad_down = tail_call(
        dp_count, grad_qkv, raw, cos_table, sin_table, wqkv, all_tokens, down_sums, grad_h1_kept, scale_qk[None, :]
    )
    settled = settle_call(
        dp_count, grad_q, wo_grads, up_gate_sums, gain_sum, grad_alpha_a, grad_alpha_m, grad_su, grad_sv
    )
    return deliver_call([out_rows, grad_tokens, *settled[:6], grad_down], settled[6:])


def solution(mesh):
    return jax.shard_map(
        on_device,
        mesh=mesh,
        in_specs=(
            P(("dp", "tensor"), None),
            P("dp", "tensor"),
            P("dp", "tensor"),
            P("dp", "tensor"),
            P("dp", "tensor"),
            P("dp", "tensor"),
            P("dp", "tensor"),
            P("dp", "tensor"),
            P(),
            P(),
            P(),
            P(),
            P(),
            P("dp", None),
            P("dp", None),
            P(("dp", "tensor"), None),
        ),
        out_specs=(
            P(("dp", "tensor"), None),
            P(("dp", "tensor"), None),
            P("dp", "tensor"),
            P("dp", "tensor"),
            P("dp", "tensor"),
            P("dp", "tensor"),
            P("dp", "tensor"),
            P("dp", "tensor"),
            P("dp", "tensor"),
            P(),
            P(),
            P(),
            P(),
            P(),
        ),
        check_vma=False,
    )
```

```python
import functools
import math

import jax
import jax.numpy as jnp
from jax import lax
from jax.experimental import pallas as pl
from jax.experimental.pallas import tpu as pltpu
from jax.sharding import PartitionSpec as P

D = 1024
HD = 64
BLK = 256
LOG2E = 1.4426950408889634
VMEM_LIMIT = 60 * 1024 * 1024


def dot_ab(a, b):
    return lax.dot_general(a, b, (((1,), (0,)), ((), ())), preferred_element_type=jnp.float32)


def dot_abt(a, b):
    return lax.dot_general(a, b, (((1,), (1,)), ((), ())), preferred_element_type=jnp.float32)


def split_heads(block, heads):
    lane_head = lax.broadcasted_iota(jnp.int32, block.shape, 1) // HD
    zero = jnp.zeros_like(block)
    return jnp.concatenate([jnp.where(lane_head == h, block, zero) for h in range(heads)], axis=0)


def attn_fwd_body(
    low_ref, start_ref, order_row, q_ref, k_ref, v_ref, out_ref, lse_ref, plain_ref, vt_ref, qs_ref, acc_ref, sum_ref
):
    rows, cols = q_ref.shape
    heads = cols // HD
    scale = math.sqrt(HD) * LOG2E
    for b in range(rows // BLK):
        vt_ref[:, b * BLK : (b + 1) * BLK] = v_ref[b * BLK : (b + 1) * BLK, :].T

    def one_block(i, _):
        base = pl.multiple_of(i * BLK, BLK)
        qs_ref[...] = split_heads(q_ref[pl.ds(base, BLK), :], heads)
        acc_ref[...] = jnp.zeros_like(acc_ref)
        sum_ref[...] = jnp.zeros_like(sum_ref)
        start = jnp.concatenate([start_ref[:, pl.ds(base, BLK)]] * heads, axis=1)
        own = lax.broadcasted_iota(jnp.int32, (1, heads * BLK), 1) % BLK + base

        def step(j, causal):
            at = pl.multiple_of(j * BLK, BLK)
            scores = dot_abt(k_ref[pl.ds(at, BLK), :], qs_ref[...])
            place = lax.broadcasted_iota(jnp.int32, scores.shape, 0) + at
            keep = place >= start
            if causal:
                keep = keep & (place <= own)
            probs = jnp.where(keep, jnp.exp2(scores * scale), 0.0)
            sum_ref[...] += jnp.sum(probs, axis=0, keepdims=True)
            probs_b = probs.astype(jnp.bfloat16)
            for h in range(heads):
                acc_ref[h * HD : (h + 1) * HD, :] += dot_ab(
                    vt_ref[h * HD : (h + 1) * HD, pl.ds(at, BLK)], probs_b[:, h * BLK : (h + 1) * BLK]
                )

        lax.fori_loop(low_ref[i], i, lambda j, c: (step(j, False), c)[1], 0)
        step(i, True)
        total = sum_ref[...]
        inv = 1.0 / total
        logs = jnp.log2(total)
        for h in range(heads):
            lse_ref[h : h + 1, pl.ds(base, BLK)] = logs[:, h * BLK : (h + 1) * BLK]
            acc_ref[h * HD : (h + 1) * HD, :] *= inv[:, h * BLK : (h + 1) * BLK]
        out_ref[pl.ds(base, BLK), :] = acc_ref[...].T.astype(jnp.bfloat16)
        return 0

    lax.fori_loop(0, rows // BLK, one_block, 0)
    over(rows // BLK, lambda b: to_token_order(b, order_row, out_ref, plain_ref))


def to_token_order(b, order_row, src, dst):
    at = pl.ds(pl.multiple_of(b * BLK, BLK), BLK)
    hot = lax.broadcasted_iota(jnp.int32, (BLK, src.shape[0]), 0) + b * BLK == order_row[...]
    dst[at, :] = dot_ab(hot.astype(jnp.float32).astype(jnp.bfloat16), src[...]).astype(dst.dtype)


def to_packed_order(b, order_col, src, dst):
    at = pl.ds(pl.multiple_of(b * BLK, BLK), BLK)
    hot = lax.broadcasted_iota(jnp.int32, (BLK, src.shape[0]), 1) == order_col[at, :]
    dst[at, :] = dot_ab(hot.astype(jnp.float32).astype(jnp.bfloat16), src[...]).astype(dst.dtype)


def over(count, body):
    lax.fori_loop(0, count, lambda i, carry: (body(i), carry)[1], 0)


def vmem():
    return pl.BlockSpec(memory_space=pltpu.VMEM)


def attn_fwd(low, start, order_row, q, k, v):
    rows, cols = q.shape
    heads = cols // HD
    return pl.pallas_call(
        attn_fwd_body,
        out_shape=(
            jax.ShapeDtypeStruct((rows, cols), jnp.bfloat16),
            jax.ShapeDtypeStruct((8, rows), jnp.float32),
            jax.ShapeDtypeStruct((rows, cols), jnp.bfloat16),
        ),
        in_specs=[pl.BlockSpec(memory_space=pltpu.SMEM)] + [vmem()] * 5,
        out_specs=(vmem(),) * 3,
        scratch_shapes=[
            pltpu.VMEM((cols, rows), jnp.bfloat16),
            pltpu.VMEM((heads * BLK, cols), jnp.bfloat16),
            pltpu.VMEM((cols, BLK), jnp.float32),
            pltpu.VMEM((1, heads * BLK), jnp.float32),
        ],
        compiler_params=pltpu.CompilerParams(vmem_limit_bytes=VMEM_LIMIT),
        cost_estimate=pl.CostEstimate(flops=4 * rows * rows * cols, bytes_accessed=8 * rows * cols, transcendentals=rows * rows * heads),
        name="attn_fwd",
    )(low, start, order_row, q, k, v)


def attn_bwd_body(
    low_ref, start_ref, order_row, order_col, lse_ref, q_ref, k_ref, v_ref, o_ref, grad_ref,
    plain_ref, kt_ref, qs_ref, gs_ref, dqt_ref, dk_acc, dv_acc, g_ref, packed,
):
    rows, cols = q_ref.shape
    heads = cols // HD
    root = math.sqrt(HD)
    scale = root * LOG2E
    for b in range(rows // BLK):
        kt_ref[:, b * BLK : (b + 1) * BLK] = k_ref[b * BLK : (b + 1) * BLK, :].T
    over(rows // BLK, lambda b: to_packed_order(b, order_col, grad_ref, g_ref))
    dk_acc[...] = jnp.zeros_like(dk_acc)
    dv_acc[...] = jnp.zeros_like(dv_acc)

    def one_block(i, _):
        base = pl.multiple_of(i * BLK, BLK)
        qs_ref[...] = split_heads(q_ref[pl.ds(base, BLK), :], heads)
        grads = g_ref[pl.ds(base, BLK), :]
        gs_ref[...] = split_heads(grads, heads)
        dqt_ref[...] = jnp.zeros_like(dqt_ref)
        start = jnp.concatenate([start_ref[:, pl.ds(base, BLK)]] * heads, axis=1)
        own = lax.broadcasted_iota(jnp.int32, (1, heads * BLK), 1) % BLK + base
        prod = (grads.astype(jnp.float32) * o_ref[pl.ds(base, BLK), :].astype(jnp.float32)).T
        delta = jnp.concatenate(
            [jnp.sum(prod[h * HD : (h + 1) * HD, :], axis=0, keepdims=True) for h in range(heads)], axis=1
        )
        lse = jnp.concatenate([lse_ref[h : h + 1, pl.ds(base, BLK)] for h in range(heads)], axis=1)

        def step(j, causal):
            at = pl.multiple_of(j * BLK, BLK)
            scores = dot_abt(k_ref[pl.ds(at, BLK), :], qs_ref[...])
            dprobs = dot_abt(v_ref[pl.ds(at, BLK), :], gs_ref[...])
            place = lax.broadcasted_iota(jnp.int32, scores.shape, 0) + at
            keep = place >= start
            if causal:
                keep = keep & (place <= own)
            probs = jnp.where(keep, jnp.exp2(scores * scale - lse), 0.0)
            dsc = (probs * (dprobs - delta)).astype(jnp.bfloat16)
            dv_acc[pl.ds(at, BLK), :] += dot_ab(probs.astype(jnp.bfloat16), gs_ref[...])
            dk_acc[pl.ds(at, BLK), :] += dot_ab(dsc, qs_ref[...])
            for h in range(heads):
                dqt_ref[h * HD : (h + 1) * HD, :] += dot_ab(
                    kt_ref[h * HD : (h + 1) * HD, pl.ds(at, BLK)], dsc[:, h * BLK : (h + 1) * BLK]
                )

        lax.fori_loop(low_ref[i], i, lambda j, c: (step(j, False), c)[1], 0)
        step(i, True)
        packed[pl.ds(base, BLK), 0:cols] = (dqt_ref[...].T * root).astype(packed.dtype)
        return 0

    lax.fori_loop(0, rows // BLK, one_block, 0)
    packed[:, cols : 2 * cols] = (dk_acc[...] * root).astype(packed.dtype)
    packed[:, 2 * cols : 3 * cols] = dv_acc[...].astype(packed.dtype)
    over(rows // BLK, lambda b: to_token_order(b, order_row, packed, plain_ref))


def attn_bwd(low, start, order_row, order_col, lse, q, k, v, o, g):
    rows, cols = q.shape
    heads = cols // HD
    return pl.pallas_call(
        attn_bwd_body,
        out_shape=jax.ShapeDtypeStruct((rows, 3 * cols), jnp.bfloat16),
        in_specs=[pl.BlockSpec(memory_space=pltpu.SMEM)] + [vmem()] * 9,
        out_specs=vmem(),
        scratch_shapes=[
            pltpu.VMEM((cols, rows), jnp.bfloat16),
            pltpu.VMEM((heads * BLK, cols), jnp.bfloat16),
            pltpu.VMEM((heads * BLK, cols), jnp.bfloat16),
            pltpu.VMEM((cols, BLK), jnp.float32),
            pltpu.VMEM((rows, cols), jnp.float32),
            pltpu.VMEM((rows, cols), jnp.float32),
            pltpu.VMEM((rows, cols), jnp.bfloat16),
            pltpu.VMEM((rows, 3 * cols), jnp.bfloat16),
        ],
        compiler_params=pltpu.CompilerParams(vmem_limit_bytes=VMEM_LIMIT),
        cost_estimate=pl.CostEstimate(flops=10 * rows * rows * cols, bytes_accessed=16 * rows * cols, transcendentals=rows * rows * heads),
        name="attn_bwd",
    )(low, start, order_row, order_col, lse, q, k, v, o, g)


MESH_ID = pl.DeviceIdType.MESH
EPS = 1e-06
TILE = 256
STRIP = 64
WIDE_STRIP = 192


def flip1(index):
    return index + 1 - 2 * lax.rem(index, 2)


def flip2(index):
    return index + 2 - 4 * (index // 2)


def tile_at(index, size):
    if isinstance(index, int):
        return pl.ds(index * size, size)
    return pl.ds(pl.multiple_of(index * size, size), size)


def row_sum(value):
    return jnp.sum(value, axis=-1, keepdims=True)


def middle_body(
    count, att_ref, wo_hbm, w_hbm, down_hbm, tok_hbm, cot_hbm, aa_ref, am_ref, su_all, sg_all,
    out_ref, datt_ref, gw_hbm, down_ref, gwo_hbm, dh1_ref, gaa_ref, gam_ref, gsu_ref, gsg_ref,
    wo, wall, tok, cot, parts, mids, dbms, mid_t, dbm_t, ups, gates, mixed,
    middle, branch, dh2, own_part, send_a, recv_a, send_d, recv_d, send_z, recv_z,
    gw, gwo, dparts, su_ref, sg_ref, got_down, gather_send, gather_recv, scatter_send, scatter_recv, load_sems, store_sems, hop_send, hop_recv, a2a_send, a2a_recv, d2a_send, d2a_recv, part_send, part_recv,
):
    d = lax.axis_index("dp")
    t = lax.axis_index("tensor")
    rows, width = tok.shape
    heads_w = att_ref.shape[1]
    hid = wall.shape[2]
    nq = w_hbm.shape[0]
    qrows = w_hbm.shape[2]
    chunks = hop_send.shape[0] // 6
    crow = rows // chunks
    core_peer = (flip1(d), t)
    z_peer = (d, flip1(t))
    line = [t, flip1(t), flip2(t), 3 - t]

    barrier = pltpu.get_barrier_semaphore()
    half, chip, core = count // 2, d // 2, lax.rem(d, 2)

    def chip_peer(i):
        return lax.rem(chip + 1 + i, half)

    for peer in [core_peer] + [(d, line[k]) for k in (1, 2, 3)]:
        pl.semaphore_signal(barrier, inc=1, device_id=peer, device_id_type=MESH_ID)
    over(
        half - 1,
        lambda i: pl.semaphore_signal(barrier, inc=1, device_id=(2 * chip_peer(i) + core, t), device_id_type=MESH_ID),
    )
    pl.semaphore_wait(barrier, half + 3)

    def remote(src, dst, ssem, rsem, peer):
        return pltpu.make_async_remote_copy(
            src_ref=src, dst_ref=dst, send_sem=ssem, recv_sem=rsem, device_id=peer, device_id_type=MESH_ID
        )

    a2a = [
        remote(att_ref.at[tile_at(line[k], rows), :], parts.at[k - 1], a2a_send.at[k - 1], a2a_recv.at[k - 1], (d, line[k]))
        for k in (1, 2, 3)
    ]
    for copy in a2a:
        copy.start()

    chip_rows = tile_at(chip, qrows)

    def gather(i):
        return remote(
            down_hbm, wall.at[2, chip_rows, :], gather_send.at[i], gather_recv.at[i], (2 * chip_peer(i) + core, t)
        )

    def scatter(i):
        return remote(
            gw.at[2, tile_at(chip_peer(i), qrows), :], got_down.at[chip], scatter_send.at[i], scatter_recv.at[i],
            (2 * chip_peer(i) + core, t),
        )

    over(half - 1, lambda i: gather(i).start())
    keep_down = pltpu.make_async_copy(down_hbm, wall.at[2, chip_rows, :], load_sems.at[3 + 2 * nq])
    keep_down.start()
    loads = [
        pltpu.make_async_copy(wo_hbm, wo, load_sems.at[0]),
        pltpu.make_async_copy(tok_hbm, tok, load_sems.at[1]),
        pltpu.make_async_copy(cot_hbm, cot, load_sems.at[2]),
    ]
    wloads = [
        [
            pltpu.make_async_copy(w_hbm.at[q, m], wall.at[m, pl.ds(q * qrows, qrows), :], load_sems.at[3 + m * nq + q])
            for q in range(nq)
        ]
        for m in range(2)
    ]
    for copy in loads + wloads[0] + wloads[1]:
        copy.start()

    shard = lax.rem(t, 2) + 2 * lax.rem(d, 2)
    su_ref[...] = su_all[:, tile_at(shard, hid)]
    sg_ref[...] = sg_all[:, tile_at(shard, hid)] * math.sqrt(D)
    gsu_ref[...] = jnp.zeros_like(gsu_ref)
    gsg_ref[...] = jnp.zeros_like(gsg_ref)
    gam_ref[...] = jnp.zeros_like(gam_ref)
    gaa_ref[...] = jnp.zeros_like(gaa_ref)

    loads[0].wait()
    for copy in a2a:
        copy.wait_recv()

    def project(n):
        cols = tile_at(n, TILE)
        total = dot_abt(att_ref[tile_at(t, rows), :], wo[cols, tile_at(t, heads_w)])
        for k in (1, 2, 3):
            total += dot_abt(parts[k - 1], wo[cols, tile_at(line[k], heads_w)])
        branch[:, cols] = total

    over(width // TILE, project)
    loads[1].wait()

    def hop(buf, phase, ch, kind):
        part = tile_at(ch, crow)
        index = (phase * chunks + ch) * 3 + kind
        src, dst, peer = ((0, 2, z_peer), (0, 1, core_peer), (2, 3, core_peer))[kind]
        return remote(buf.at[src, part, :], buf.at[dst, part, :], hop_send.at[index], hop_recv.at[index], peer)

    def strips(ch, body):
        over(crow // STRIP, lambda i: body(tile_at(i + ch * (crow // STRIP), STRIP)))

    def unit_of(value):
        factor = lax.rsqrt(row_sum(value * value) + EPS)
        return value * factor, factor

    def make_middle(at):
        inputs = tok[at, :].astype(jnp.float32)
        norm_a, factor_a = unit_of(branch[at, :])
        mid, factor_mid = unit_of(inputs + aa_ref[...] * (norm_a - inputs))
        return inputs, norm_a, factor_a, mid, factor_mid

    def first(at):
        mid = make_middle(at)[3]
        middle[at, :] = mid
        mids[0, at, :] = mid.astype(jnp.bfloat16)

    for ch in range(chunks):
        strips(ch, first)
        hop(mids, 0, ch, 0).start()
        hop(mids, 0, ch, 1).start()

    for m in range(2):
        for copy in wloads[m]:
            copy.wait()

    def down_arrived():
        keep_down.wait()
        over(half - 1, lambda i: gather(i).wait_recv())

    def within(slot, at):
        return pl.ds(pl.multiple_of(slot * rows + at.start, STRIP), at.size)

    def forward_rows(slot, at, store, ready):
        where = within(slot, at)

        def hidden(n):
            cols = tile_at(n, TILE)
            x = mids[slot, at, :]
            up = dot_ab(x, wall[0, :, cols])
            gate_raw = dot_ab(x, wall[1, :, cols])
            gate = gate_raw * sg_ref[:, cols]
            silu = gate / (1.0 + jnp.exp(-gate))
            ups[where, cols] = up.astype(jnp.bfloat16)
            gates[where, cols] = gate_raw.astype(jnp.bfloat16)
            mixed[where, cols] = (up * su_ref[:, cols] * silu).astype(jnp.bfloat16)

        over(hid // TILE, hidden)
        ready()

        def down(n):
            cols = tile_at(n, TILE)
            store(at, cols, dot_abt(mixed[where, :], wall[2, cols, :]))

        over(width // TILE, down)

    def backward_rows(slot, at, store, ready):
        where = within(slot, at)

        def hidden(n):
            cols = tile_at(n, TILE)
            dmix = dot_ab(dbms[slot, at, :], wall[2, :, cols])
            up_raw = ups[where, cols].astype(jnp.float32)
            gate_raw = gates[where, cols].astype(jnp.float32)
            gate = gate_raw * sg_ref[:, cols]
            sig = 1.0 / (1.0 + jnp.exp(-gate))
            d_up = dmix * (gate * sig)
            d_gate = dmix * (up_raw * su_ref[:, cols]) * (sig * (1.0 + gate * (1.0 - sig)))
            gsu_ref[:, cols] += jnp.sum(d_up * up_raw, axis=0, keepdims=True)
            gsg_ref[:, cols] += jnp.sum(d_gate * gate_raw, axis=0, keepdims=True)
            ups[where, cols] = (d_up * su_ref[:, cols]).astype(jnp.bfloat16)
            gates[where, cols] = (d_gate * sg_ref[:, cols]).astype(jnp.bfloat16)

        over(hid // TILE, hidden)
        ready()

        def down(n):
            cols = tile_at(n, TILE)
            store(at, cols, dot_abt(ups[where, :], wall[0, cols, :]) + dot_abt(gates[where, :], wall[1, cols, :]))

        over(width // TILE, down)

    def part_copy(phase, kind, ch):
        part = tile_at(ch, crow)
        index = (phase * 3 + kind) * chunks + ch
        src, dst, peer = ((send_a, recv_a, core_peer), (send_d, recv_d, core_peer), (send_z, recv_z, z_peer))[kind]
        return remote(src.at[part, :], dst.at[part, :], part_send.at[index], part_recv.at[index], peer)

    def nothing():
        pass

    def tensor_pass(phase, buf, rows_fn, fillers):
        def keep_own(at, cols, value):
            own_part[at, cols] = value

        def to(ref):
            def store(at, cols, value):
                ref[at, cols] = value.astype(jnp.bfloat16)

            return store

        def to_z(at, cols, value):
            send_z[at, cols] = (value + recv_d[at, cols].astype(jnp.float32)).astype(jnp.bfloat16)

        rows_fn(0, tile_at(0, rows), keep_own, nothing if phase else down_arrived)
        for ch in range(chunks):
            hop(buf, phase, ch, 1).wait_recv()
        if phase == 1:
            for ch in range(chunks):
                part_copy(0, 0, ch).wait_send()
        rows_fn(1, tile_at(0, rows), to(send_a), nothing)
        for ch in range(chunks):
            part_copy(phase, 0, ch).start()
        fillers[0]()
        def chunk(ch):
            hop(buf, phase, ch, 0).wait_recv()
            hop(buf, phase, ch, 2).start()
            at = tile_at(ch, crow)
            hop(buf, phase, ch, 2).wait_recv()
            if phase == 1:
                part_copy(0, 1, ch).wait_send()
            rows_fn(3, at, to(send_d), nothing)
            part_copy(phase, 1, ch).start()

            def ready():
                part_copy(phase, 1, ch).wait_recv()
                if phase == 1:
                    part_copy(0, 2, ch).wait_send()

            rows_fn(2, at, to_z, ready)
            part_copy(phase, 2, ch).start()

        over(chunks, chunk)
        fillers[1]()

    def transpose_into(dst, buf, slots):
        per_slot = rows // 128

        def one(i):
            slot = slots[0] + i // per_slot
            at = tile_at(lax.rem(i, per_slot), 128)
            to = tile_at(slots[0] * per_slot + i, 128)
            for n in range(width // TILE):
                dst[n * TILE : (n + 1) * TILE, to] = buf[slot, at, n * TILE : (n + 1) * TILE].T

        over(len(slots) * per_slot, one)

    tensor_pass(
        0, mids, forward_rows,
        [lambda: transpose_into(mid_t, mids, (0, 1)), lambda: transpose_into(mid_t, mids, (2, 3))],
    )

    loads[2].wait()

    def turn(at):
        mid = middle[at, :]
        branch_m = own_part[at, :] + recv_a[at, :].astype(jnp.float32) + recv_z[at, :].astype(jnp.float32)
        norm_m, factor_m = unit_of(branch_m)
        alpha = am_ref[...]
        y, factor_y = unit_of(mid + alpha * (norm_m - mid))
        out_ref[at, :] = y.astype(jnp.bfloat16)
        dy = cot[at, :].astype(jnp.float32)
        grad = factor_y * (dy - y * row_sum(y * dy))
        gam_ref[...] += jnp.sum(grad * (norm_m - mid), axis=0, keepdims=True)
        back = alpha * grad
        dbms[0, at, :] = (factor_m * (back - norm_m * row_sum(norm_m * back))).astype(jnp.bfloat16)
        dh2[at, :] = grad - back

    for ch in range(chunks):
        part_copy(0, 0, ch).wait_recv()
        part_copy(0, 2, ch).wait_recv()
        strips(ch, turn)
        hop(dbms, 1, ch, 0).start()
        hop(dbms, 1, ch, 1).start()

    def grad_store(m, q):
        return pltpu.make_async_copy(gw.at[m, pl.ds(q * qrows, qrows), :], gw_hbm.at[q, m], store_sems.at[m * nq + q])

    def weight_grad(m):
        lhs, rhs = ((mid_t, ups), (mid_t, gates), (dbm_t, mixed))[m]

        def block(i):
            q = i // (hid // TILE)
            cols = tile_at(lax.rem(i, hid // TILE), TILE)
            value = dot_ab(lhs[tile_at(q, TILE), :], rhs[:, cols])
            gw[m, tile_at(q, TILE), cols] = value.astype(jnp.bfloat16)

        over((width // TILE) * (hid // TILE), block)

    def down_grad():
        transpose_into(dbm_t, dbms, (2, 3))
        weight_grad(2)
        over(half - 1, lambda i: scatter(i).start())
        got_down[chip] = gw[2, chip_rows, :]

    tensor_pass(1, dbms, backward_rows, [lambda: transpose_into(dbm_t, dbms, (0, 1)), down_grad])

    def last(at):
        inputs, norm_a, factor_a, mid, factor_mid = make_middle(at)
        grad_mid = dh2[at, :] + own_part[at, :] + recv_a[at, :].astype(jnp.float32) + recv_z[at, :].astype(jnp.float32)
        grad = factor_mid * (grad_mid - mid * row_sum(mid * grad_mid))
        gaa_ref[...] += jnp.sum(grad * (norm_a - inputs), axis=0, keepdims=True)
        back = aa_ref[...] * grad
        dh1_ref[at, :] = grad - back
        mids[0, at, :] = (factor_a * (back - norm_a * row_sum(norm_a * back))).astype(jnp.bfloat16)

    for ch in range(chunks):
        hop(mids, 0, ch, 0).wait_send()
        hop(mids, 0, ch, 1).wait_send()
        part_copy(1, 0, ch).wait_recv()
        part_copy(1, 2, ch).wait_recv()
        strips(ch, last)

    dback = [
        remote(dparts.at[k], datt_ref.at[tile_at(t, rows), :], d2a_send.at[k - 1], d2a_recv.at[k - 1], (d, line[k]))
        for k in (1, 2, 3)
    ]
    for k in (3, 2, 1, 0):
        value = dot_ab(mids[0], wo[:, tile_at(line[k], heads_w)]).astype(jnp.bfloat16)
        if k:
            dparts[k] = value
            dback[k - 1].start()
        else:
            datt_ref[tile_at(t, rows), :] = value

    for m in range(2):
        weight_grad(m)
        for q in range(nq):
            grad_store(m, q).start()
    transpose_into(dbm_t, mids, (0,))

    def out_grad(n):
        at = tile_at(n, TILE)
        lhs = dbm_t[at, 0:rows]
        gwo[at, tile_at(t, heads_w)] = dot_ab(lhs, att_ref[tile_at(t, rows), :]).astype(jnp.bfloat16)
        for k in (1, 2, 3):
            gwo[at, tile_at(line[k], heads_w)] = dot_ab(lhs, parts[k - 1]).astype(jnp.bfloat16)

    over(width // TILE, out_grad)
    wo_store = pltpu.make_async_copy(gwo, gwo_hbm, store_sems.at[2 * nq])
    wo_store.start()

    over(half - 1, lambda i: scatter(i).wait_recv())

    def down_sum(i):
        at = tile_at(i, qrows // 2)
        total = got_down[0, at, :].astype(jnp.float32)
        total = lax.fori_loop(1, half, lambda e, value: value + got_down[e, at, :].astype(jnp.float32), total)
        down_ref[at, :] = total.astype(jnp.bfloat16)

    over(2, down_sum)
    over(half - 1, lambda i: gather(i).wait_send())
    over(half - 1, lambda i: scatter(i).wait_send())

    for k in (1, 2, 3):
        remote(
            dparts.at[k], datt_ref.at[tile_at(line[k], rows), :], d2a_send.at[k - 1], d2a_recv.at[k - 1], (d, line[k])
        ).wait()
    for copy in a2a:
        copy.wait_send()
    for ch in range(chunks):
        hop(mids, 0, ch, 2).wait_send()
        for kind in range(3):
            hop(dbms, 1, ch, kind).wait_send()
            part_copy(1, kind, ch).wait_send()
    for m in range(2):
        for q in range(nq):
            grad_store(m, q).wait()
    wo_store.wait()


def middle_call(count, chunks, attended, wo, w_parts, down, tokens, cotangent, alpha_a, alpha_m, su, sg):
    rows, width = tokens.shape
    group, heads_w = attended.shape
    nq, _, qrows, hid = w_parts.shape
    bf, f32 = jnp.bfloat16, jnp.float32
    anywhere = pl.BlockSpec(memory_space=pl.ANY)
    dma = pltpu.SemaphoreType.DMA
    return pl.pallas_call(
        functools.partial(middle_body, count),
        out_shape=(
            jax.ShapeDtypeStruct((rows, width), bf),
            jax.ShapeDtypeStruct((group, heads_w), bf),
            jax.ShapeDtypeStruct((nq, 2, qrows, hid), bf),
            jax.ShapeDtypeStruct((qrows, hid), bf),
            jax.ShapeDtypeStruct((width, width), bf),
            jax.ShapeDtypeStruct((rows, width), f32),
            jax.ShapeDtypeStruct((1, width), f32),
            jax.ShapeDtypeStruct((1, width), f32),
            jax.ShapeDtypeStruct((1, hid), f32),
            jax.ShapeDtypeStruct((1, hid), f32),
        ),
        in_specs=[vmem()] + [anywhere] * 5 + [vmem()] * 4,
        out_specs=(vmem(), vmem(), anywhere, vmem(), anywhere) + (vmem(),) * 5,
        scratch_shapes=[
            pltpu.VMEM((width, width), bf),
            pltpu.VMEM((3, width, hid), bf),
            pltpu.VMEM((rows, width), bf),
            pltpu.VMEM((rows, width), bf),
            pltpu.VMEM((3, rows, heads_w), bf),
            pltpu.VMEM((4, rows, width), bf),
            pltpu.VMEM((4, rows, width), bf),
            pltpu.VMEM((width, 4 * rows), bf),
            pltpu.VMEM((width, 4 * rows), bf),
            pltpu.VMEM((4 * rows, hid), bf),
            pltpu.VMEM((4 * rows, hid), bf),
            pltpu.VMEM((4 * rows, hid), bf),
            pltpu.VMEM((rows, width), f32),
            pltpu.VMEM((rows, width), f32),
            pltpu.VMEM((rows, width), f32),
            pltpu.VMEM((rows, width), f32),
        ]
        + [pltpu.VMEM((rows, width), bf)] * 6
        + [
            pltpu.VMEM((3, width, hid), bf),
            pltpu.VMEM((width, width), bf),
            pltpu.VMEM((4, rows, heads_w), bf),
            pltpu.VMEM((1, hid), f32),
            pltpu.VMEM((1, hid), f32),
            pltpu.VMEM((count // 2, qrows, hid), bf),
            dma((count // 2 - 1,)), dma((count // 2 - 1,)), dma((count // 2 - 1,)), dma((count // 2 - 1,)),
            dma((4 + 2 * nq,)),
            dma((2 * nq + 1,)),
            dma((6 * chunks,)),
            dma((6 * chunks,)),
            dma((3,)),
            dma((3,)),
            dma((3,)),
            dma((3,)),
            dma((6 * chunks,)),
            dma((6 * chunks,)),
        ],
        compiler_params=pltpu.CompilerParams(vmem_limit_bytes=67000000, collective_id=1, has_side_effects=True),
        cost_estimate=pl.CostEstimate(flops=10**11, bytes_accessed=10**8, transcendentals=10**6),
        name="middle",
    )(attended, wo, w_parts, down, tokens, cotangent, alpha_a, alpha_m, su, sg)


def remote_copy(src, dst, send_sem, recv_sem, peer):
    return pltpu.make_async_remote_copy(
        src_ref=src, dst_ref=dst, send_sem=send_sem, recv_sem=recv_sem, device_id=peer, device_id_type=MESH_ID
    )


def greet(peers):
    barrier = pltpu.get_barrier_semaphore()
    for peer in peers:
        pl.semaphore_signal(barrier, inc=1, device_id=peer, device_id_type=MESH_ID)
    pl.semaphore_wait(barrier, len(peers))


def rope_tables(order_ref, length_ref, cos_out, sin_out, col_out, start_out):
    group = order_ref.shape[1]
    lanes = cos_out.shape[1]
    places = lax.broadcasted_iota(jnp.int32, (1, group), 1)
    first = jnp.zeros((1, group), jnp.int32)
    begin = jnp.int32(0)
    for s in range(1, length_ref.shape[1]):
        begin = begin + length_ref[0, s - 1]
        first = jnp.where(places >= begin, begin, first)
    start_out[...] = first
    depth = (places - first).astype(jnp.float32)
    order = order_ref[...]
    order_f = order.astype(jnp.float32)
    lane = lax.broadcasted_iota(jnp.int32, (1, lanes), 1)
    half_width = HD // 2
    freq = jnp.exp((lane % half_width).astype(jnp.float32) * (-math.log(10000.0) / half_width))
    sign = jnp.where(lane % HD < half_width, -1.0, 1.0)

    def block(b):
        at = tile_at(b, 128)
        own = lax.broadcasted_iota(jnp.int32, (128, group), 0) + b * 128
        col_out[at, :] = row_sum(jnp.where(own == places, order_f, 0.0)).astype(jnp.int32)
        angles = row_sum(jnp.where(own == order, depth, 0.0)) * freq
        cos_out[at, :] = jnp.cos(angles)
        sin_out[at, :] = jnp.sin(angles) * sign

    over(group // 128, block)


def spread_body(
    count, tok, w_up, w_gate, w_down, wq, wk, wv, wo, order_ref, length_ref,
    pair, pair_down, tok2, wqkv, wo_all, cos_out, sin_out, col_out, start_out,
    own_mlp, own_att, wo_rows, load_sem, keep_sem, a_send, a_recv, b_send, b_recv, tok_send, tok_recv,
    qkv_send, qkv_recv, oz_send, oz_recv, oq_send, oq_recv, oc_send, oc_recv,
):
    d = lax.axis_index("dp")
    t = lax.axis_index("tensor")
    core = lax.rem(d, 2)
    home = core == t // 2
    far = (d - core + t // 2, flip2(t))
    wrows, wcols = wq.shape
    half = count // 2
    mlp = (w_up, w_gate, w_down)
    att = (wq, wk, wv)
    mine = tile_at(d, wrows)
    side = tile_at(core, wrows)
    other_side = tile_at(1 - core, wrows)

    barrier = pltpu.get_barrier_semaphore()

    def dp_peer(i):
        return lax.rem(d + 1 + i, count)

    def hello(i):
        pl.semaphore_signal(barrier, inc=1, device_id=(dp_peer(i), t), device_id_type=MESH_ID)

    over(count - 1, hello)
    for k in (1, 2, 3):
        pl.semaphore_signal(barrier, inc=1, device_id=(d, lax.rem(t + k, 4)), device_id_type=MESH_ID)
    pl.semaphore_signal(barrier, inc=1, device_id=(flip1(d), flip2(t)), device_id_type=MESH_ID)
    pl.semaphore_wait(barrier, count + 3)

    def pair_at(m, rows):
        return pair_down.at[rows, :] if m == 2 else pair.at[m, rows, :]

    def b_copy(m):
        return remote_copy(mlp[m], pair_at(m, side), b_send.at[m], b_recv.at[core * 3 + m], far)

    def a_copy(m):
        return remote_copy(mlp[m], pair_at(m, side), a_send.at[m], a_recv.at[m], (flip1(d), t))

    tok_copy = remote_copy(tok, tok2, tok_send, tok_recv, (d, flip1(t)))
    def oz_copy(k):
        return remote_copy(wo, wo_rows.at[:, tile_at(t, wcols)], oz_send.at[k - 1], oz_recv.at[k - 1], (d, lax.rem(t + k, 4)))

    for k in (1, 2, 3):
        oz_copy(k).start()
    tok_copy.start()
    for m in range(3):
        b_copy(m).start()
    load_o = pltpu.make_async_copy(wo, wo_rows.at[:, tile_at(t, wcols)], load_sem.at[0])
    load_o.start()

    def qkv_copy(i, m):
        return remote_copy(
            att[m], wqkv.at[mine, pl.ds(m * wcols, wcols)], qkv_send.at[i, m], qkv_recv.at[i, m], (dp_peer(i), t)
        )

    def qkv_start(i):
        for m in range(3):
            qkv_copy(i, m).start()

    over(count - 1, qkv_start)

    @pl.when(jnp.logical_not(home))
    def _():
        for m in range(3):
            a_copy(m).start()

    loads = [pltpu.make_async_copy(mlp[m], own_mlp.at[m], load_sem.at[1 + m]) for m in range(3)]
    loads += [pltpu.make_async_copy(att[m], own_att.at[m], load_sem.at[4 + m]) for m in range(3)]
    for copy in loads:
        copy.start()
    for copy in loads:
        copy.wait()
    keeps = [
        pltpu.make_async_copy(own_att.at[m], wqkv.at[mine, pl.ds(m * wcols, wcols)], keep_sem.at[m]) for m in range(3)
    ]
    for copy in keeps:
        copy.start()
    pair_keeps = [pltpu.make_async_copy(own_mlp.at[m], pair_at(m, side), keep_sem.at[3 + m]) for m in range(3)]

    @pl.when(home)
    def _():
        for copy in pair_keeps:
            copy.start()

    load_o.wait()
    for k in (1, 2, 3):
        oz_copy(k).wait_recv()
    keep_o = pltpu.make_async_copy(wo_rows, wo_all.at[mine, :], keep_sem.at[6])
    keep_o.start()

    def oq_copy(j):
        return remote_copy(wo_rows, wo_all.at[mine, :], oq_send.at[j], oq_recv.at[j], (lax.rem(d + 2 + 2 * j, count), t))

    def oc_own():
        return remote_copy(wo_rows, wo_all.at[mine, :], oc_send.at[half - 1], oc_recv.at[half - 1], (flip1(d), t))

    def oc_copy(j):
        rows = tile_at(lax.rem(d + count - 2 - 2 * j, count), wrows)
        return remote_copy(wo_all.at[rows, :], wo_all.at[rows, :], oc_send.at[j], oc_recv.at[j], (flip1(d), t))

    over(half - 1, lambda j: oq_copy(j).start())
    oc_own().start()
    rope_tables(order_ref, length_ref, cos_out, sin_out, col_out, start_out)

    def oq_next(j):
        oq_copy(j).wait_recv()
        oc_copy(j).start()

    over(half - 1, oq_next)

    def qkv_wait(i):
        for m in range(3):
            qkv_copy(i, m).wait()

    over(count - 1, qkv_wait)
    over(half - 1, lambda j: oq_copy(j).wait_send())
    over(half - 1, lambda j: oc_copy(j).wait())
    oc_own().wait()
    for k in (1, 2, 3):
        oz_copy(k).wait_send()
    keep_o.wait()
    for copy in keeps:
        copy.wait()
    tok_copy.wait()
    for m in range(3):
        b_copy(m).wait_send()

    @pl.when(home)
    def _():
        for m in range(3):
            pair_keeps[m].wait()
            remote_copy(mlp[m], pair_at(m, other_side), a_send.at[m], a_recv.at[m], (flip1(d), t)).wait_recv()

    @pl.when(jnp.logical_not(home))
    def _():
        for m in range(3):
            a_copy(m).wait_send()
            for c in range(2):
                remote_copy(
                    mlp[m], pair_at(m, pl.ds(c * wrows, wrows)), b_send.at[m], b_recv.at[c * 3 + m], far
                ).wait_recv()


def spread_call(count, tokens, w_up, w_gate, w_down, wq, wk, wv, wo, order, lengths):
    rows, width = tokens.shape
    group = order.shape[1]
    wrows, wcols = wq.shape
    hid = w_up.shape[1]
    bf = jnp.bfloat16
    anywhere = pl.BlockSpec(memory_space=pl.ANY)
    dma = pltpu.SemaphoreType.DMA
    return pl.pallas_call(
        functools.partial(spread_body, count),
        out_shape=(
            jax.ShapeDtypeStruct((2, 2 * wrows, hid), bf),
            jax.ShapeDtypeStruct((2 * wrows, hid), bf),
            jax.ShapeDtypeStruct((rows, width), bf),
            jax.ShapeDtypeStruct((width, 3 * wcols), bf),
            jax.ShapeDtypeStruct((width, width), bf),
            jax.ShapeDtypeStruct((group, 2 * HD), jnp.float32),
            jax.ShapeDtypeStruct((group, 2 * HD), jnp.float32),
            jax.ShapeDtypeStruct((group, 1), jnp.int32),
            jax.ShapeDtypeStruct((1, group), jnp.int32),
        ),
        in_specs=[anywhere] * 8 + [vmem(), pl.BlockSpec(memory_space=pltpu.SMEM)],
        out_specs=(anywhere,) * 5 + (vmem(),) * 4,
        scratch_shapes=[
            pltpu.VMEM((3, wrows, hid), bf),
            pltpu.VMEM((3, wrows, wcols), bf),
            pltpu.VMEM((wrows, width), bf),
            dma((7,)), dma((7,)), dma((3,)), dma((3,)), dma((3,)), dma((6,)), dma, dma,
            dma((count - 1, 3)), dma((count - 1, 3)), dma((3,)), dma((3,)),
            dma((count // 2,)), dma((count // 2,)), dma((count // 2,)), dma((count // 2,)),
        ],
        compiler_params=pltpu.CompilerParams(vmem_limit_bytes=VMEM_LIMIT, collective_id=2, has_side_effects=True),
        name="spread",
    )(tokens, w_up, w_gate, w_down, wq, wk, wv, wo, order, lengths)


def head_sums(value):
    width = value.shape[1]
    same = (
        lax.broadcasted_iota(jnp.int32, (width, width), 0) // HD == lax.broadcasted_iota(jnp.int32, (width, width), 1) // HD
    )
    ones = jnp.where(same, 1.0, 0.0).astype(jnp.bfloat16)
    high = value.astype(jnp.bfloat16)
    low = (value - high.astype(jnp.float32)).astype(jnp.bfloat16)
    return dot_ab(high, ones) + dot_ab(low, ones)


def swap_halves(value):
    width = value.shape[1]
    lane = lax.broadcasted_iota(jnp.int32, value.shape, 1) % HD
    return jnp.where(lane < HD // 2, pltpu.roll(value, width - HD // 2, 1), pltpu.roll(value, HD // 2, 1))


def project_body(
    tok, tok2, wqkv, cos_ref, sin_ref, order_col, gain_ref, q_ref, k_ref, v_ref, raw_ref, x_hbm,
    xs, plain, load_sem, keep_sem, mid_send, recv, on_send,
):
    t = lax.axis_index("tensor")
    d = lax.axis_index("dp")
    _, rows, width = xs.shape
    group, cols = q_ref.shape
    near = flip1(t)
    across = 3 - t
    inner = (t + 1) // 2 == 1
    arrive = (2 - t // 2, 3 - 3 * (t // 2))
    pieces = mid_send.shape[0] // 2
    part = rows // pieces
    greet([(d, near), (d, across)])

    def mid_copy(k):
        rows_of = pl.ds((k % pieces) * part, part)
        src = (tok, tok2)[k // pieces].at[rows_of, :]
        return remote_copy(src, xs.at[(t, near)[k // pieces], rows_of, :], mid_send.at[k], recv.at[k], (d, across))

    def on_copy(k):
        ref = xs.at[arrive[k // pieces], pl.ds((k % pieces) * part, part), :]
        return remote_copy(ref, ref, on_send.at[k], recv.at[k], (d, near))

    @pl.when(inner)
    def _():
        for k in range(2 * pieces):
            mid_copy(k).start()

    loads = [
        pltpu.make_async_copy(tok, xs.at[t], load_sem.at[0]),
        pltpu.make_async_copy(tok2, xs.at[near], load_sem.at[1]),
    ]
    for copy in loads:
        copy.start()

    def keep(index, slot):
        return pltpu.make_async_copy(xs.at[slot], x_hbm.at[tile_at(slot, rows), :], keep_sem.at[index])

    def strip(slot, i):
        at = tile_at(slot * (rows // WIDE_STRIP) + i, WIDE_STRIP)
        x = xs[slot, tile_at(i, WIDE_STRIP), :]
        cos = jnp.concatenate([cos_ref[at, :]] * (cols // cos_ref.shape[1]), axis=1)
        sin = jnp.concatenate([sin_ref[at, :]] * (cols // sin_ref.shape[1]), axis=1)
        for m in range(2):
            raw = dot_ab(x, wqkv[:, m * cols : (m + 1) * cols])
            raw_ref[at, m * cols : (m + 1) * cols] = raw.astype(jnp.bfloat16)
            normed = raw * lax.rsqrt(head_sums(raw * raw) + EPS) * gain_ref[:, tile_at(t, cols)]
            plain[at, m * cols : (m + 1) * cols] = (normed * cos + swap_halves(normed) * sin).astype(jnp.bfloat16)
        plain[at, 2 * cols : 3 * cols] = dot_ab(x, wqkv[:, 2 * cols : 3 * cols]).astype(jnp.bfloat16)

    def permute(index, size, first):
        base = tile_at(index, size)

        def one(b):
            at = tile_at(b, BLK)
            token = lax.broadcasted_iota(jnp.int32, (BLK, size), 1) + index * size
            hot = (token == order_col[at, :]).astype(jnp.float32)
            value = dot_ab(hot.astype(jnp.bfloat16), plain[base, :])
            for m, ref in enumerate((q_ref, k_ref, v_ref)):
                piece = value[:, m * cols : (m + 1) * cols]
                if not first:
                    piece += ref[at, :].astype(jnp.float32)
                ref[at, :] = piece.astype(jnp.bfloat16)

        over(group // BLK, one)

    loads[0].wait()
    keep(0, t).start()
    over(rows // WIDE_STRIP, lambda i: strip(t, i))
    loads[1].wait()
    keep(1, near).start()
    over(rows // WIDE_STRIP, lambda i: strip(near, i))
    permute(t // 2, 2 * rows, True)
    per_strip = WIDE_STRIP // part
    for k in range(2 * pieces):
        slot = arrive[k // pieces]
        ref = xs.at[slot, pl.ds((k % pieces) * part, part), :]
        remote_copy(ref, ref, on_send.at[k], recv.at[k], (d, near)).wait_recv()

        @pl.when(inner)
        def _():
            on_copy(k).start()

        if k % per_strip == per_strip - 1:
            strip(slot, (k % pieces) // per_strip)
        if k % pieces == pieces - 1:
            keep(2 + k // pieces, slot).start()
            permute(slot, rows, False)

    for index, slot in enumerate((t, near, *arrive)):
        keep(index, slot).wait()

    @pl.when(inner)
    def _():
        for k in range(2 * pieces):
            mid_copy(k).wait_send()
            on_copy(k).wait_send()


def project_call(tokens, tok2, wqkv, cos, sin, order_col, gains):
    rows, width = tokens.shape
    group = order_col.shape[0]
    cols = wqkv.shape[1] // 3
    bf = jnp.bfloat16
    anywhere = pl.BlockSpec(memory_space=pl.ANY)
    dma = pltpu.SemaphoreType.DMA
    return pl.pallas_call(
        project_body,
        out_shape=(jax.ShapeDtypeStruct((group, cols), bf),) * 3
        + (jax.ShapeDtypeStruct((group, 2 * cols), bf), jax.ShapeDtypeStruct((group, width), bf)),
        in_specs=[anywhere, anywhere] + [vmem()] * 5,
        out_specs=(vmem(),) * 4 + (anywhere,),
        scratch_shapes=[
            pltpu.VMEM((group // rows, rows, width), bf),
            pltpu.VMEM((group, 3 * cols), bf),
            dma((2,)), dma((4,)), dma((8,)), dma((8,)), dma((8,)),
        ],
        compiler_params=pltpu.CompilerParams(vmem_limit_bytes=VMEM_LIMIT, collective_id=3, has_side_effects=True),
        cost_estimate=pl.CostEstimate(flops=6 * 10**10, bytes_accessed=10**7, transcendentals=10**6),
        name="project",
    )(tokens, tok2, wqkv, cos, sin, order_col, gains)


def tail_body(
    grad_ref, raw_ref, cos_ref, sin_ref, wqkv, x_hbm, down_hbm, kept_ref, gain_ref, tok_out, gq, gain_sum, down_out,
    xs, x_t, draw, part_far, part_mid, part_near, own_part, from_a, from_b, from_c, from_d, from_e, from_f,
    near_mlp, far_mlp, load_sem, hop_send, hop_recv, keep_sem, near_send, near_recv, far_send, far_recv,
):
    d = lax.axis_index("dp")
    t = lax.axis_index("tensor")
    rows, width = tok_out.shape
    group = draw.shape[0]
    cols = draw.shape[1] // 3
    near = flip1(t)
    inner = (t + 1) // 2 == 1
    outer = jnp.logical_not(inner)
    far, mid = 3 - 3 * (t // 2), 2 - t // 2
    chunk = rows // 2
    greet([(d, near), (d, 3 - t), (d, flip2(t)), (flip1(d), t), (flip1(d), flip2(t))])

    core = lax.rem(d, 2)
    home = core == t // 2
    away = jnp.logical_not(home)
    near_copy = remote_copy(down_hbm.at[1 - core], near_mlp, near_send, near_recv, (flip1(d), t))
    far_same = remote_copy(down_hbm.at[core], far_mlp, far_send.at[0], far_recv, (d, flip2(t)))
    far_cross = remote_copy(down_hbm.at[1 - core], far_mlp, far_send.at[1], far_recv, (flip1(d), flip2(t)))
    keep_mlp = pltpu.make_async_copy(down_hbm.at[core], near_mlp, keep_sem)

    @pl.when(home)
    def _():
        near_copy.start()
        keep_mlp.start()

    @pl.when(away)
    def _():
        far_same.start()
        far_cross.start()

    load_x = pltpu.make_async_copy(x_hbm, xs, load_sem)
    load_x.start()

    def hop(kind, ch):
        src, dst, to = (
            (part_far, from_a, near),
            (part_mid, from_b, near),
            (part_near, from_c, near),
            (part_far, from_d, 3 - t),
            (part_mid, from_e, 3 - t),
            (part_near, from_f, near),
        )[kind]
        part = tile_at(ch, chunk)
        return remote_copy(src.at[part, :], dst.at[part, :], hop_send.at[kind, ch], hop_recv.at[kind, ch], (d, to))

    gain_sum[...] = jnp.zeros_like(gain_sum)

    def work(slot, ch, ref):
        at = tile_at(2 * slot + ch, chunk)
        to = tile_at(ch, chunk)
        cos = jnp.concatenate([cos_ref[at, :]] * (cols // cos_ref.shape[1]), axis=1)
        sin = jnp.concatenate([sin_ref[at, :]] * (cols // sin_ref.shape[1]), axis=1)
        gain = gain_ref[:, tile_at(t, cols)]
        for m in range(2):
            grad = grad_ref[at, m * cols : (m + 1) * cols].astype(jnp.float32)
            raw = raw_ref[at, m * cols : (m + 1) * cols].astype(jnp.float32)
            back = grad * cos - swap_halves(grad) * sin
            factor = lax.rsqrt(head_sums(raw * raw) + EPS)
            normed = raw * factor
            gain_sum[...] += jnp.sum(back * normed, axis=0, keepdims=True)
            scaled = back * gain
            draw[at, m * cols : (m + 1) * cols] = (factor * (scaled - normed * head_sums(normed * scaled))).astype(
                jnp.bfloat16
            )
        draw[at, 2 * cols : 3 * cols] = grad_ref[at, 2 * cols : 3 * cols]

        def product(n):
            tile = tile_at(n, TILE)
            ref[to, tile] = dot_abt(draw[at, :], wqkv[tile, :]).astype(ref.dtype)

        over(width // TILE, product)

    def send_part(kind, slot, ref):
        def one(ch):
            work(slot, ch, ref)

            @pl.when(outer)
            def _():
                hop(kind, ch).start()

        over(2, one)

    send_part(0, far, part_far)
    send_part(1, mid, part_mid)
    send_part(2, near, part_near)
    over(2, lambda ch: work(t, ch, own_part))

    def pass_on(kind, ch, own, got, then):
        @pl.when(inner)
        def _():
            part = pl.ds(ch * chunk, chunk)
            hop(kind, ch).wait_recv()
            own[part, :] = (own[part, :].astype(jnp.float32) + got[part, :].astype(jnp.float32)).astype(jnp.bfloat16)
            hop(then, ch).start()

    pass_on(0, 0, part_far, from_a, 3)
    pass_on(0, 1, part_far, from_a, 3)

    load_x.wait()

    def flip_block(b):
        at = tile_at(b, 128)
        for n in range(width // TILE):
            x_t[n * TILE : (n + 1) * TILE, at] = xs[at, n * TILE : (n + 1) * TILE].T

    over(group // 128, flip_block)
    pass_on(3, 0, part_near, from_d, 5)

    def weight_grad(n):
        tile = tile_at(n, TILE)
        gq[tile, :] = dot_ab(x_t[tile, :], draw[...]).astype(jnp.bfloat16)

    over(width // TILE, weight_grad)
    pass_on(1, 0, part_mid, from_b, 4)
    pass_on(3, 1, part_near, from_d, 5)
    pass_on(1, 1, part_mid, from_b, 4)

    @pl.when(home)
    def _():
        keep_mlp.wait()
        near_copy.wait_send()

    @pl.when(away)
    def _():
        near_copy.wait_recv()

    far_same.wait_recv()
    down_out[...] = near_mlp[...].astype(jnp.float32) + far_mlp[...].astype(jnp.float32)

    @pl.when(away)
    def _():
        far_same.wait_send()
        far_cross.wait_send()

    for ch in range(2):
        part = pl.ds(ch * chunk, chunk)

        @pl.when(inner)
        def _():
            hop(2, ch).wait_recv()
            hop(4, ch).wait_recv()
            tok_out[part, :] = (
                kept_ref[part, :]
                + own_part[part, :]
                + from_c[part, :].astype(jnp.float32)
                + from_e[part, :].astype(jnp.float32)
            )

        @pl.when(outer)
        def _():
            hop(5, ch).wait_recv()
            tok_out[part, :] = kept_ref[part, :] + own_part[part, :] + from_f[part, :].astype(jnp.float32)

    for ch in range(2):

        @pl.when(inner)
        def _():
            for kind in (3, 4, 5):
                hop(kind, ch).wait_send()

        @pl.when(outer)
        def _():
            for kind in (0, 1, 2):
                hop(kind, ch).wait_send()


def tail_call(count, grad_qkv, raw, cos, sin, wqkv, all_tokens, down, kept, gains):
    rows, width = kept.shape
    wrows, hid = width // count, down.shape[1]
    group, three = grad_qkv.shape
    bf, f32 = jnp.bfloat16, jnp.float32
    anywhere = pl.BlockSpec(memory_space=pl.ANY)
    dma = pltpu.SemaphoreType.DMA
    shape = jax.ShapeDtypeStruct
    return pl.pallas_call(
        tail_body,
        out_shape=(
            shape((rows, width), f32),
            shape((width, three), bf),
            shape((1, three // 3), f32),
            shape((wrows, hid), f32),
        ),
        in_specs=[vmem()] * 5 + [anywhere] * 2 + [vmem()] * 2,
        out_specs=(vmem(),) * 4,
        scratch_shapes=[
            pltpu.VMEM((group, width), bf),
            pltpu.VMEM((width, group), bf),
            pltpu.VMEM((group, three), bf),
            pltpu.VMEM((rows, width), bf),
            pltpu.VMEM((rows, width), bf),
            pltpu.VMEM((rows, width), bf),
            pltpu.VMEM((rows, width), f32),
        ]
        + [pltpu.VMEM((rows, width), bf)] * 6
        + [pltpu.VMEM((wrows, hid), bf)] * 2
        + [dma, dma((6, 2)), dma((6, 2)), dma, dma, dma, dma((2,)), dma],
        compiler_params=pltpu.CompilerParams(vmem_limit_bytes=VMEM_LIMIT, collective_id=4, has_side_effects=True),
        cost_estimate=pl.CostEstimate(flops=6 * 10**10, bytes_accessed=10**7, transcendentals=10**6),
        name="tail",
    )(grad_qkv, raw, cos, sin, wqkv, all_tokens, down.reshape(2, wrows, hid), kept, gains)


def settle_body(
    count, gq_hbm, gwo_hbm, mlp_hbm, gain_ref, gaa_ref, gam_ref, gsu_ref, gsg_ref,
    q_out, k_out, v_out, wo_out, up_out, gate_out, gain_out, aa_out, su_out, sg_out, am_out,
    own_q, core_q, got_q, own_w, core_w, got_w, wo_mid, got_z, near_mlp, far_mlp, vec, got_v, vec_mid, got_s,
    load_sem, core_send, core_recv, q_send, q_recv, w_send, w_recv, z_send, z_recv, v_send, v_recv, s_send, s_recv,
    near_send, near_recv, mlp_send, mlp_recv,
):
    d = lax.axis_index("dp")
    t = lax.axis_index("tensor")
    half, wrows, three = got_q.shape
    cols = three // 3
    width = gaa_ref.shape[1]
    chip, core = d // 2, lax.rem(d, 2)
    home = core == t // 2
    away = jnp.logical_not(home)
    f32, bf = jnp.float32, jnp.bfloat16

    def dp_peer(i):
        return lax.rem(d + 1 + i, count)

    def line_peer(k):
        return lax.rem(t + k, 4)

    def chip_peer(i):
        return lax.rem(chip + 1 + i, half)

    barrier = pltpu.get_barrier_semaphore()
    over(
        count - 1,
        lambda i: pl.semaphore_signal(barrier, inc=1, device_id=(dp_peer(i), t), device_id_type=MESH_ID),
    )
    for k in (1, 2, 3):
        pl.semaphore_signal(barrier, inc=1, device_id=(d, line_peer(k)), device_id_type=MESH_ID)
    pl.semaphore_signal(barrier, inc=1, device_id=(flip1(d), flip2(t)), device_id_type=MESH_ID)
    pl.semaphore_wait(barrier, count + 3)

    near_copy = remote_copy(mlp_hbm.at[:, 1 - core], near_mlp, near_send, near_recv, (flip1(d), t))
    keep_mlp = pltpu.make_async_copy(mlp_hbm.at[:, core], near_mlp, load_sem.at[0])

    hid = near_mlp.shape[2]

    def far_same(u):
        m, part = u // 2, tile_at(u % 2, hid // 2)
        return remote_copy(
            mlp_hbm.at[m, core, :, part], far_mlp.at[m, :, part], mlp_send.at[u], mlp_recv.at[u], (d, flip2(t))
        )

    def far_cross(u):
        m, part = u // 2, tile_at(u % 2, hid // 2)
        return remote_copy(
            mlp_hbm.at[m, 1 - core, :, part], far_mlp.at[m, :, part], mlp_send.at[4 + u], mlp_recv.at[u],
            (flip1(d), flip2(t)),
        )

    def far_start(u):
        @pl.when(away)
        def _():
            far_same(u).start()
            far_cross(u).start()

    @pl.when(home)
    def _():
        near_copy.start()
        keep_mlp.start()

    for u in range(3):
        far_start(u)

    core_w_copy = remote_copy(gwo_hbm.at[:, 1 - core], core_w, core_send.at[0], core_recv.at[0], (flip1(d), t))
    core_q_copy = remote_copy(gq_hbm.at[:, 1 - core], core_q, core_send.at[1], core_recv.at[1], (flip1(d), t))
    load_w = pltpu.make_async_copy(gwo_hbm.at[:, core], own_w, load_sem.at[1])
    load_q = pltpu.make_async_copy(gq_hbm.at[:, core], own_q, load_sem.at[2])
    core_w_copy.start()
    core_q_copy.start()
    load_w.start()
    load_q.start()

    vec[...] = jnp.zeros_like(vec)
    for row, ref in enumerate((gaa_ref, gam_ref, gsu_ref, gsg_ref)):
        vec[row : row + 1, :] = ref[...]
    vec[4:5, 0:cols] = gain_ref[...]
    got_v[d] = vec[...]

    def v_copy(i):
        return remote_copy(vec, got_v.at[d], v_send.at[i], v_recv.at[i], (dp_peer(i), t))

    over(count - 1, lambda i: v_copy(i).start())

    def chip_copy(own, got, sends, recvs, i):
        return remote_copy(own.at[chip_peer(i)], got.at[chip], sends.at[i], recvs.at[i], (2 * chip_peer(i) + core, t))

    def w_copy(i):
        return chip_copy(own_w, got_w, w_send, w_recv, i)

    def q_copy(i):
        return chip_copy(own_q, got_q, q_send, q_recv, i)

    def join(own, other, got):
        def one(e):
            own[e] = (own[e].astype(f32) + other[e].astype(f32)).astype(bf)

        over(half, one)
        got[chip] = own[chip]

    load_w.wait()
    core_w_copy.wait_recv()
    join(own_w, core_w, got_w)
    over(half - 1, lambda i: w_copy(i).start())
    load_q.wait()
    core_q_copy.wait_recv()
    join(own_q, core_q, got_q)
    over(half - 1, lambda i: q_copy(i).start())

    def total_of(got):
        return lax.fori_loop(1, half, lambda i, total: total + got[i].astype(f32), got[0].astype(f32))

    over(half - 1, lambda i: w_copy(i).wait_recv())
    wo_mid[...] = total_of(got_w).astype(bf)

    def z_copy(k):
        return remote_copy(
            wo_mid.at[:, tile_at(line_peer(k), cols)], got_z.at[t], z_send.at[k - 1], z_recv.at[k - 1], (d, line_peer(k))
        )

    for k in (1, 2, 3):
        z_copy(k).start()
    got_z[t] = wo_mid[:, tile_at(t, cols)]

    over(count - 1, lambda i: v_copy(i).wait_recv())
    even, odd = lax.fori_loop(
        1, half, lambda i, total: (total[0] + got_v[2 * i], total[1] + got_v[2 * i + 1]), (got_v[0], got_v[1])
    )
    both = even + odd
    vec_mid[...] = jnp.concatenate([both[0:2], even[2:3], odd[2:3], even[3:4], odd[3:4], both[4:5], both[4:5]], axis=0)

    def s_copy(k):
        return remote_copy(vec_mid, got_s.at[t], s_send.at[k - 1], s_recv.at[k - 1], (d, line_peer(k)))

    for k in (1, 2, 3):
        s_copy(k).start()
    got_s[t] = vec_mid[...]
    far_start(3)

    over(half - 1, lambda i: q_copy(i).wait_recv())
    total = total_of(got_q)
    for m, ref in enumerate((q_out, k_out, v_out)):
        ref[...] = total[:, m * cols : (m + 1) * cols]

    for k in (1, 2, 3):
        z_copy(k).wait_recv()
        s_copy(k).wait_recv()
    wo_out[...] = got_z[0].astype(f32) + got_z[1].astype(f32) + got_z[2].astype(f32) + got_z[3].astype(f32)
    shared = got_s[0] + got_s[1] + got_s[2] + got_s[3]
    aa_out[...] = shared[0:1]
    am_out[...] = shared[1:2]
    pairs = (got_s[0] + got_s[2], got_s[1] + got_s[3])
    for s in range(4):
        su_out[:, s * width : (s + 1) * width] = pairs[s % 2][2 + s // 2 : 3 + s // 2]
        sg_out[:, s * width : (s + 1) * width] = pairs[s % 2][4 + s // 2 : 5 + s // 2] * math.sqrt(D)
        gain_out[:, s * cols : (s + 1) * cols] = got_s[s][6:7, 0:cols]

    @pl.when(home)
    def _():
        keep_mlp.wait()
        near_copy.wait_send()

    @pl.when(away)
    def _():
        near_copy.wait_recv()

    for m, ref in enumerate((up_out, gate_out)):
        far_same(2 * m).wait_recv()
        far_same(2 * m + 1).wait_recv()
        ref[...] = near_mlp[m].astype(f32) + far_mlp[m].astype(f32)

    @pl.when(away)
    def _():
        for u in range(4):
            far_same(u).wait_send()
            far_cross(u).wait_send()

    core_w_copy.wait_send()
    core_q_copy.wait_send()
    over(count - 1, lambda i: v_copy(i).wait_send())

    def drain(i):
        w_copy(i).wait_send()
        q_copy(i).wait_send()

    over(half - 1, drain)
    for k in (1, 2, 3):
        z_copy(k).wait_send()
        s_copy(k).wait_send()


def settle_call(count, gq, gwo, mlp, gain_sum, gaa, gam, gsu, gsg):
    width, three = gq.shape
    half = count // 2
    cols = three // 3
    wrows = width // count
    hid = mlp.shape[2]
    bf, f32 = jnp.bfloat16, jnp.float32
    anywhere = pl.BlockSpec(memory_space=pl.ANY)
    dma = pltpu.SemaphoreType.DMA
    shape = jax.ShapeDtypeStruct
    return pl.pallas_call(
        functools.partial(settle_body, count),
        out_shape=(shape((wrows, cols), f32),) * 4
        + (shape((wrows, hid), f32),) * 2
        + (
            shape((1, 4 * cols), f32),
            shape((1, width), f32),
            shape((1, 4 * hid), f32),
            shape((1, 4 * hid), f32),
            shape((1, width), f32),
        ),
        in_specs=[anywhere] * 3 + [vmem()] * 5,
        out_specs=(vmem(),) * 11,
        scratch_shapes=[pltpu.VMEM((half, wrows, three), bf)] * 3
        + [pltpu.VMEM((half, wrows, width), bf)] * 3
        + [
            pltpu.VMEM((wrows, width), bf),
            pltpu.VMEM((4, wrows, cols), bf),
            pltpu.VMEM((2, wrows, hid), bf),
            pltpu.VMEM((2, wrows, hid), bf),
            pltpu.VMEM((8, width), f32),
            pltpu.VMEM((count, 8, width), f32),
            pltpu.VMEM((8, width), f32),
            pltpu.VMEM((4, 8, width), f32),
            dma((3,)),
            dma((2,)), dma((2,)),
            dma((half - 1,)), dma((half - 1,)), dma((half - 1,)), dma((half - 1,)),
            dma((3,)), dma((3,)),
            dma((count - 1,)), dma((count - 1,)),
            dma((3,)), dma((3,)),
            dma, dma, dma((8,)), dma((4,)),
        ],
        compiler_params=pltpu.CompilerParams(vmem_limit_bytes=VMEM_LIMIT, collective_id=5, has_side_effects=True),
        cost_estimate=pl.CostEstimate(flops=10**9, bytes_accessed=10**7, transcendentals=0),
        name="settle",
    )(
        gq.reshape(half, 2, wrows, three),
        gwo.reshape(half, 2, wrows, width),
        mlp.reshape(2, 2, wrows, hid),
        gain_sum, gaa, gam, gsu, gsg,
    )


def deliver_body(count, total, *refs):
    ins, outs, rest = refs[:total], refs[total : 2 * total], refs[2 * total :]
    held, load_sem, store_sem = rest[:count], rest[count], rest[count + 1]
    loads = [pltpu.make_async_copy(ins[i], held[i], load_sem.at[i]) for i in range(count)]
    stores = [pltpu.make_async_copy(held[i], outs[i], store_sem.at[i]) for i in range(count)]
    for copy in loads:
        copy.start()
    for i in range(count, total):
        outs[i][...] = ins[i][0, :]
    for load, store in zip(loads, stores):
        load.wait()
        store.start()
    for copy in stores:
        copy.wait()


def deliver_call(arrays, vectors):
    total = len(arrays) + len(vectors)
    specs = [pl.BlockSpec(memory_space=pl.ANY)] * len(arrays) + [vmem()] * len(vectors)
    return pl.pallas_call(
        functools.partial(deliver_body, len(arrays), total),
        out_shape=tuple(jax.ShapeDtypeStruct(a.shape, a.dtype) for a in arrays)
        + tuple(jax.ShapeDtypeStruct((v.shape[1],), v.dtype) for v in vectors),
        in_specs=specs,
        out_specs=tuple(specs),
        scratch_shapes=[pltpu.VMEM(a.shape, a.dtype) for a in arrays] + [pltpu.SemaphoreType.DMA((len(arrays),))] * 2,
        compiler_params=pltpu.CompilerParams(vmem_limit_bytes=VMEM_LIMIT),
        name="deliver",
    )(*arrays, *vectors)


def same_core_groups(dp_count):
    return [list(range(parity, dp_count, 2)) for parity in range(2)]


def on_device(
    tokens,
    w_query,
    w_key,
    w_value,
    w_out_t,
    w_up,
    w_gate,
    w_down_t,
    scale_qk,
    alpha_attn,
    scale_up,
    scale_gate,
    alpha_mlp,
    order,
    lengths,
    cotangent,
):
    dp_count = lax.axis_size("dp")
    pair, pair_down, near_tokens, wqkv, wo_every, cos_table, sin_table, order_col, start = spread_call(
        dp_count, tokens, w_up, w_gate, w_down_t, w_query, w_key, w_value, w_out_t, order, lengths
    )
    low = lax.slice(start[0], (0,), (start.shape[1],), (BLK,)) // BLK
    mlp_parts = lax.all_gather(
        pair, "dp", axis=0, tiled=False, axis_index_groups=same_core_groups(dp_count)
    )
    queries, key_rows, value_rows, raw, all_tokens = project_call(
        tokens, near_tokens, wqkv, cos_table, sin_table, order_col, scale_qk[None, :]
    )
    attended, log_totals, attended_plain = attn_fwd(low, start, order, queries, key_rows, value_rows)
    out_rows, grad_att_rows, up_gate_grads, down_sums, wo_grads, grad_h1_kept, grad_alpha_a, grad_alpha_m, grad_su, grad_sv = middle_call(
        dp_count,
        2,
        attended_plain,
        wo_every,
        mlp_parts,
        pair_down,
        tokens,
        cotangent,
        alpha_attn[None, :],
        alpha_mlp[None, :],
        scale_up[None, :],
        scale_gate[None, :],
    )
    grad_qkv = attn_bwd(
        low, start, order, order_col, log_totals, queries, key_rows, value_rows, attended, grad_att_rows
    )
    up_gate_sums = lax.psum_scatter(
        up_gate_grads, "dp", scatter_dimension=0, tiled=False, axis_index_groups=same_core_groups(dp_count)
    )
    grad_tokens, grad_q, gain_sum, grad_down = tail_call(
        dp_count, grad_qkv, raw, cos_table, sin_table, wqkv, all_tokens, down_sums, grad_h1_kept, scale_qk[None, :]
    )
    settled = settle_call(
        dp_count, grad_q, wo_grads, up_gate_sums, gain_sum, grad_alpha_a, grad_alpha_m, grad_su, grad_sv
    )
    return deliver_call([out_rows, grad_tokens, *settled[:6], grad_down], settled[6:])


def solution(mesh):
    return jax.shard_map(
        on_device,
        mesh=mesh,
        in_specs=(
            P(("dp", "tensor"), None),
            P("dp", "tensor"),
            P("dp", "tensor"),
            P("dp", "tensor"),
            P("dp", "tensor"),
            P("dp", "tensor"),
            P("dp", "tensor"),
            P("dp", "tensor"),
            P(),
            P(),
            P(),
            P(),
            P(),
            P("dp", None),
            P("dp", None),
            P(("dp", "tensor"), None),
        ),
        out_specs=(
            P(("dp", "tensor"), None),
            P(("dp", "tensor"), None),
            P("dp", "tensor"),
            P("dp", "tensor"),
            P("dp", "tensor"),
            P("dp", "tensor"),
            P("dp", "tensor"),
            P("dp", "tensor"),
            P("dp", "tensor"),
            P(),
            P(),
            P(),
            P(),
            P(),
        ),
        check_vma=False,
    )
```

```python
import functools
import math

import jax
import jax.numpy as jnp
from jax import lax
from jax.experimental import pallas as pl
from jax.experimental.pallas import tpu as pltpu
from jax.sharding import PartitionSpec as P

D = 1024
HD = 64
BLK = 256
LOG2E = 1.4426950408889634
VMEM_LIMIT = 60 * 1024 * 1024


def dot_ab(a, b):
    return lax.dot_general(a, b, (((1,), (0,)), ((), ())), preferred_element_type=jnp.float32)


def dot_abt(a, b):
    return lax.dot_general(a, b, (((1,), (1,)), ((), ())), preferred_element_type=jnp.float32)


def split_heads(block, heads):
    lane_head = lax.broadcasted_iota(jnp.int32, block.shape, 1) // HD
    zero = jnp.zeros_like(block)
    return jnp.concatenate([jnp.where(lane_head == h, block, zero) for h in range(heads)], axis=0)


def attn_fwd_body(
    low_ref, start_ref, order_row, q_ref, k_ref, v_ref, out_ref, lse_ref, plain_ref, vt_ref, qs_ref, acc_ref, sum_ref
):
    rows, cols = q_ref.shape
    heads = cols // HD
    scale = math.sqrt(HD) * LOG2E
    for b in range(rows // BLK):
        vt_ref[:, b * BLK : (b + 1) * BLK] = v_ref[b * BLK : (b + 1) * BLK, :].T

    def one_block(i, _):
        base = pl.multiple_of(i * BLK, BLK)
        qs_ref[...] = split_heads(q_ref[pl.ds(base, BLK), :], heads)
        acc_ref[...] = jnp.zeros_like(acc_ref)
        sum_ref[...] = jnp.zeros_like(sum_ref)
        start = jnp.concatenate([start_ref[:, pl.ds(base, BLK)]] * heads, axis=1)
        own = lax.broadcasted_iota(jnp.int32, (1, heads * BLK), 1) % BLK + base

        def step(j, causal):
            at = pl.multiple_of(j * BLK, BLK)
            scores = dot_abt(k_ref[pl.ds(at, BLK), :], qs_ref[...])
            place = lax.broadcasted_iota(jnp.int32, scores.shape, 0) + at
            keep = place >= start
            if causal:
                keep = keep & (place <= own)
            probs = jnp.where(keep, jnp.exp2(scores * scale), 0.0)
            sum_ref[...] += jnp.sum(probs, axis=0, keepdims=True)
            probs_b = probs.astype(jnp.bfloat16)
            for h in range(heads):
                acc_ref[h * HD : (h + 1) * HD, :] += dot_ab(
                    vt_ref[h * HD : (h + 1) * HD, pl.ds(at, BLK)], probs_b[:, h * BLK : (h + 1) * BLK]
                )

        lax.fori_loop(low_ref[i], i, lambda j, c: (step(j, False), c)[1], 0)
        step(i, True)
        total = sum_ref[...]
        inv = 1.0 / total
        logs = jnp.log2(total)
        for h in range(heads):
            lse_ref[h : h + 1, pl.ds(base, BLK)] = logs[:, h * BLK : (h + 1) * BLK]
            acc_ref[h * HD : (h + 1) * HD, :] *= inv[:, h * BLK : (h + 1) * BLK]
        out_ref[pl.ds(base, BLK), :] = acc_ref[...].T.astype(jnp.bfloat16)
        return 0

    lax.fori_loop(0, rows // BLK, one_block, 0)
    over(rows // BLK, lambda b: to_token_order(b, order_row, out_ref, plain_ref))


def to_token_order(b, order_row, src, dst):
    at = pl.ds(pl.multiple_of(b * BLK, BLK), BLK)
    hot = lax.broadcasted_iota(jnp.int32, (BLK, src.shape[0]), 0) + b * BLK == order_row[...]
    dst[at, :] = dot_ab(hot.astype(jnp.float32).astype(jnp.bfloat16), src[...]).astype(dst.dtype)


def to_packed_order(b, order_col, src, dst):
    at = pl.ds(pl.multiple_of(b * BLK, BLK), BLK)
    hot = lax.broadcasted_iota(jnp.int32, (BLK, src.shape[0]), 1) == order_col[at, :]
    dst[at, :] = dot_ab(hot.astype(jnp.float32).astype(jnp.bfloat16), src[...]).astype(dst.dtype)


def over(count, body):
    lax.fori_loop(0, count, lambda i, carry: (body(i), carry)[1], 0)


def vmem():
    return pl.BlockSpec(memory_space=pltpu.VMEM)


def attn_fwd(low, start, order_row, q, k, v):
    rows, cols = q.shape
    heads = cols // HD
    return pl.pallas_call(
        attn_fwd_body,
        out_shape=(
            jax.ShapeDtypeStruct((rows, cols), jnp.bfloat16),
            jax.ShapeDtypeStruct((8, rows), jnp.float32),
            jax.ShapeDtypeStruct((rows, cols), jnp.bfloat16),
        ),
        in_specs=[pl.BlockSpec(memory_space=pltpu.SMEM)] + [vmem()] * 5,
        out_specs=(vmem(),) * 3,
        scratch_shapes=[
            pltpu.VMEM((cols, rows), jnp.bfloat16),
            pltpu.VMEM((heads * BLK, cols), jnp.bfloat16),
            pltpu.VMEM((cols, BLK), jnp.float32),
            pltpu.VMEM((1, heads * BLK), jnp.float32),
        ],
        compiler_params=pltpu.CompilerParams(vmem_limit_bytes=VMEM_LIMIT),
        cost_estimate=pl.CostEstimate(flops=4 * rows * rows * cols, bytes_accessed=8 * rows * cols, transcendentals=rows * rows * heads),
        name="attn_fwd",
    )(low, start, order_row, q, k, v)


def attn_bwd_body(
    low_ref, start_ref, order_row, order_col, lse_ref, q_ref, k_ref, v_ref, o_ref, grad_ref,
    plain_ref, kt_ref, qs_ref, gs_ref, dqt_ref, dk_acc, dv_acc, g_ref, packed,
):
    rows, cols = q_ref.shape
    heads = cols // HD
    root = math.sqrt(HD)
    scale = root * LOG2E
    for b in range(rows // BLK):
        kt_ref[:, b * BLK : (b + 1) * BLK] = k_ref[b * BLK : (b + 1) * BLK, :].T
    over(rows // BLK, lambda b: to_packed_order(b, order_col, grad_ref, g_ref))
    dk_acc[...] = jnp.zeros_like(dk_acc)
    dv_acc[...] = jnp.zeros_like(dv_acc)

    def one_block(i, _):
        base = pl.multiple_of(i * BLK, BLK)
        qs_ref[...] = split_heads(q_ref[pl.ds(base, BLK), :], heads)
        grads = g_ref[pl.ds(base, BLK), :]
        gs_ref[...] = split_heads(grads, heads)
        dqt_ref[...] = jnp.zeros_like(dqt_ref)
        start = jnp.concatenate([start_ref[:, pl.ds(base, BLK)]] * heads, axis=1)
        own = lax.broadcasted_iota(jnp.int32, (1, heads * BLK), 1) % BLK + base
        prod = (grads.astype(jnp.float32) * o_ref[pl.ds(base, BLK), :].astype(jnp.float32)).T
        delta = jnp.concatenate(
            [jnp.sum(prod[h * HD : (h + 1) * HD, :], axis=0, keepdims=True) for h in range(heads)], axis=1
        )
        lse = jnp.concatenate([lse_ref[h : h + 1, pl.ds(base, BLK)] for h in range(heads)], axis=1)

        def step(j, causal):
            at = pl.multiple_of(j * BLK, BLK)
            scores = dot_abt(k_ref[pl.ds(at, BLK), :], qs_ref[...])
            dprobs = dot_abt(v_ref[pl.ds(at, BLK), :], gs_ref[...])
            place = lax.broadcasted_iota(jnp.int32, scores.shape, 0) + at
            keep = place >= start
            if causal:
                keep = keep & (place <= own)
            probs = jnp.where(keep, jnp.exp2(scores * scale - lse), 0.0)
            dsc = (probs * (dprobs - delta)).astype(jnp.bfloat16)
            dv_acc[pl.ds(at, BLK), :] += dot_ab(probs.astype(jnp.bfloat16), gs_ref[...])
            dk_acc[pl.ds(at, BLK), :] += dot_ab(dsc, qs_ref[...])
            for h in range(heads):
                dqt_ref[h * HD : (h + 1) * HD, :] += dot_ab(
                    kt_ref[h * HD : (h + 1) * HD, pl.ds(at, BLK)], dsc[:, h * BLK : (h + 1) * BLK]
                )

        lax.fori_loop(low_ref[i], i, lambda j, c: (step(j, False), c)[1], 0)
        step(i, True)
        packed[pl.ds(base, BLK), 0:cols] = (dqt_ref[...].T * root).astype(packed.dtype)
        return 0

    lax.fori_loop(0, rows // BLK, one_block, 0)
    packed[:, cols : 2 * cols] = (dk_acc[...] * root).astype(packed.dtype)
    packed[:, 2 * cols : 3 * cols] = dv_acc[...].astype(packed.dtype)
    over(rows // BLK, lambda b: to_token_order(b, order_row, packed, plain_ref))


def attn_bwd(low, start, order_row, order_col, lse, q, k, v, o, g):
    rows, cols = q.shape
    heads = cols // HD
    return pl.pallas_call(
        attn_bwd_body,
        out_shape=jax.ShapeDtypeStruct((rows, 3 * cols), jnp.bfloat16),
        in_specs=[pl.BlockSpec(memory_space=pltpu.SMEM)] + [vmem()] * 9,
        out_specs=vmem(),
        scratch_shapes=[
            pltpu.VMEM((cols, rows), jnp.bfloat16),
            pltpu.VMEM((heads * BLK, cols), jnp.bfloat16),
            pltpu.VMEM((heads * BLK, cols), jnp.bfloat16),
            pltpu.VMEM((cols, BLK), jnp.float32),
            pltpu.VMEM((rows, cols), jnp.float32),
            pltpu.VMEM((rows, cols), jnp.float32),
            pltpu.VMEM((rows, cols), jnp.bfloat16),
            pltpu.VMEM((rows, 3 * cols), jnp.bfloat16),
        ],
        compiler_params=pltpu.CompilerParams(vmem_limit_bytes=VMEM_LIMIT),
        cost_estimate=pl.CostEstimate(flops=10 * rows * rows * cols, bytes_accessed=16 * rows * cols, transcendentals=rows * rows * heads),
        name="attn_bwd",
    )(low, start, order_row, order_col, lse, q, k, v, o, g)


MESH_ID = pl.DeviceIdType.MESH
EPS = 1e-06
TILE = 256
STRIP = 64
WIDE_STRIP = 192


def flip1(index):
    return index + 1 - 2 * lax.rem(index, 2)


def flip2(index):
    return index + 2 - 4 * (index // 2)


def tile_at(index, size):
    if isinstance(index, int):
        return pl.ds(index * size, size)
    return pl.ds(pl.multiple_of(index * size, size), size)


def row_sum(value):
    return jnp.sum(value, axis=-1, keepdims=True)


def middle_body(
    count, att_ref, wo_hbm, w_hbm, down_hbm, tok_hbm, cot_hbm, aa_ref, am_ref, su_all, sg_all,
    out_ref, datt_ref, gw_hbm, down_ref, gwo_hbm, dh1_ref, gaa_ref, gam_ref, gsu_ref, gsg_ref,
    wo, wall, tok, cot, parts, mids, dbms, mid_t, dbm_t, ups, gates, mixed,
    middle, branch, dh2, own_part, send_a, recv_a, send_d, recv_d, send_z, recv_z,
    gw, gwo, dparts, su_ref, sg_ref, got_down, gather_send, gather_recv, scatter_send, scatter_recv, load_sems, store_sems, hop_send, hop_recv, a2a_send, a2a_recv, d2a_send, d2a_recv, part_send, part_recv,
):
    d = lax.axis_index("dp")
    t = lax.axis_index("tensor")
    rows, width = tok.shape
    heads_w = att_ref.shape[1]
    hid = wall.shape[2]
    nq = w_hbm.shape[0]
    qrows = w_hbm.shape[2]
    chunks = hop_send.shape[0] // 6
    crow = rows // chunks
    core_peer = (flip1(d), t)
    z_peer = (d, flip1(t))
    line = [t, flip1(t), flip2(t), 3 - t]

    barrier = pltpu.get_barrier_semaphore()
    half, chip, core = count // 2, d // 2, lax.rem(d, 2)

    def chip_peer(i):
        return lax.rem(chip + 1 + i, half)

    for peer in [core_peer] + [(d, line[k]) for k in (1, 2, 3)]:
        pl.semaphore_signal(barrier, inc=1, device_id=peer, device_id_type=MESH_ID)
    over(
        half - 1,
        lambda i: pl.semaphore_signal(barrier, inc=1, device_id=(2 * chip_peer(i) + core, t), device_id_type=MESH_ID),
    )
    pl.semaphore_wait(barrier, half + 3)

    def remote(src, dst, ssem, rsem, peer):
        return pltpu.make_async_remote_copy(
            src_ref=src, dst_ref=dst, send_sem=ssem, recv_sem=rsem, device_id=peer, device_id_type=MESH_ID
        )

    a2a = [
        remote(att_ref.at[tile_at(line[k], rows), :], parts.at[k - 1], a2a_send.at[k - 1], a2a_recv.at[k - 1], (d, line[k]))
        for k in (1, 2, 3)
    ]
    for copy in a2a:
        copy.start()

    chip_rows = tile_at(chip, qrows)

    def gather(i):
        return remote(
            down_hbm, wall.at[2, chip_rows, :], gather_send.at[i], gather_recv.at[i], (2 * chip_peer(i) + core, t)
        )

    def scatter(i):
        return remote(
            gw.at[2, tile_at(chip_peer(i), qrows), :], got_down.at[chip], scatter_send.at[i], scatter_recv.at[i],
            (2 * chip_peer(i) + core, t),
        )

    over(half - 1, lambda i: gather(i).start())
    keep_down = pltpu.make_async_copy(down_hbm, wall.at[2, chip_rows, :], load_sems.at[3 + 2 * nq])
    keep_down.start()
    loads = [
        pltpu.make_async_copy(wo_hbm, wo, load_sems.at[0]),
        pltpu.make_async_copy(tok_hbm, tok, load_sems.at[1]),
        pltpu.make_async_copy(cot_hbm, cot, load_sems.at[2]),
    ]
    wloads = [
        [
            pltpu.make_async_copy(w_hbm.at[q, m], wall.at[m, pl.ds(q * qrows, qrows), :], load_sems.at[3 + m * nq + q])
            for q in range(nq)
        ]
        for m in range(2)
    ]
    for copy in loads + wloads[0] + wloads[1]:
        copy.start()

    shard = lax.rem(t, 2) + 2 * lax.rem(d, 2)
    su_ref[...] = su_all[:, tile_at(shard, hid)]
    sg_ref[...] = sg_all[:, tile_at(shard, hid)] * math.sqrt(D)
    gsu_ref[...] = jnp.zeros_like(gsu_ref)
    gsg_ref[...] = jnp.zeros_like(gsg_ref)
    gam_ref[...] = jnp.zeros_like(gam_ref)
    gaa_ref[...] = jnp.zeros_like(gaa_ref)

    loads[0].wait()
    for copy in a2a:
        copy.wait_recv()

    def project(n):
        cols = tile_at(n, TILE)
        total = dot_abt(att_ref[tile_at(t, rows), :], wo[cols, tile_at(t, heads_w)])
        for k in (1, 2, 3):
            total += dot_abt(parts[k - 1], wo[cols, tile_at(line[k], heads_w)])
        branch[:, cols] = total

    over(width // TILE, project)
    loads[1].wait()

    def hop(buf, phase, ch, kind):
        part = tile_at(ch, crow)
        index = (phase * chunks + ch) * 3 + kind
        src, dst, peer = ((0, 2, z_peer), (0, 1, core_peer), (2, 3, core_peer))[kind]
        return remote(buf.at[src, part, :], buf.at[dst, part, :], hop_send.at[index], hop_recv.at[index], peer)

    def strips(ch, body):
        over(crow // STRIP, lambda i: body(tile_at(i + ch * (crow // STRIP), STRIP)))

    def unit_of(value):
        factor = lax.rsqrt(row_sum(value * value) + EPS)
        return value * factor, factor

    def make_middle(at):
        inputs = tok[at, :].astype(jnp.float32)
        norm_a, factor_a = unit_of(branch[at, :])
        mid, factor_mid = unit_of(inputs + aa_ref[...] * (norm_a - inputs))
        return inputs, norm_a, factor_a, mid, factor_mid

    def first(at):
        mid = make_middle(at)[3]
        middle[at, :] = mid
        mids[0, at, :] = mid.astype(jnp.bfloat16)

    for ch in range(chunks):
        strips(ch, first)
        hop(mids, 0, ch, 0).start()
        hop(mids, 0, ch, 1).start()

    for m in range(2):
        for copy in wloads[m]:
            copy.wait()

    def down_arrived():
        keep_down.wait()
        over(half - 1, lambda i: gather(i).wait_recv())

    def within(slot, at):
        return pl.ds(pl.multiple_of(slot * rows + at.start, STRIP), at.size)

    def forward_rows(slot, at):
        where = within(slot, at)

        def hidden(n):
            cols = tile_at(n, TILE)
            x = mids[slot, at, :]
            up = dot_ab(x, wall[0, :, cols])
            gate_raw = dot_ab(x, wall[1, :, cols])
            gate = gate_raw * sg_ref[:, cols]
            silu = gate / (1.0 + jnp.exp(-gate))
            ups[where, cols] = up.astype(jnp.bfloat16)
            gates[where, cols] = gate_raw.astype(jnp.bfloat16)
            mixed[where, cols] = (up * su_ref[:, cols] * silu).astype(jnp.bfloat16)

        def down(cols):
            return dot_abt(mixed[where, :], wall[2, cols, :])

        return hidden, down

    def backward_rows(slot, at):
        where = within(slot, at)

        def hidden(n):
            cols = tile_at(n, TILE)
            dmix = dot_ab(dbms[slot, at, :], wall[2, :, cols])
            up_raw = ups[where, cols].astype(jnp.float32)
            gate_raw = gates[where, cols].astype(jnp.float32)
            gate = gate_raw * sg_ref[:, cols]
            sig = 1.0 / (1.0 + jnp.exp(-gate))
            d_up = dmix * (gate * sig)
            d_gate = dmix * (up_raw * su_ref[:, cols]) * (sig * (1.0 + gate * (1.0 - sig)))
            gsu_ref[:, cols] += jnp.sum(d_up * up_raw, axis=0, keepdims=True)
            gsg_ref[:, cols] += jnp.sum(d_gate * gate_raw, axis=0, keepdims=True)
            ups[where, cols] = (d_up * su_ref[:, cols]).astype(jnp.bfloat16)
            gates[where, cols] = (d_gate * sg_ref[:, cols]).astype(jnp.bfloat16)

        def down(cols):
            return dot_abt(ups[where, :], wall[0, cols, :]) + dot_abt(gates[where, :], wall[1, cols, :])

        return hidden, down

    def part_copy(phase, kind, ch):
        part = tile_at(ch, crow)
        index = (phase * 3 + kind) * chunks + ch
        src, dst, peer = ((send_a, recv_a, core_peer), (send_d, recv_d, core_peer), (send_z, recv_z, z_peer))[kind]
        return remote(src.at[part, :], dst.at[part, :], part_send.at[index], part_recv.at[index], peer)

    def tensor_pass(phase, buf, rows_fn, fillers):
        def keep_own(at, cols, value):
            own_part[at, cols] = value

        def to(ref):
            def store(at, cols, value):
                ref[at, cols] = value.astype(jnp.bfloat16)

            return store

        def to_z(at, cols, value):
            send_z[at, cols] = (value + recv_d[at, cols].astype(jnp.float32)).astype(jnp.bfloat16)

        tiles = hid // TILE
        all_rows = tile_at(0, rows)

        def span(low, high, body):
            over(high - low, lambda n: body(n + low))

        def store_all(at, down, store):
            def one(n):
                cols = tile_at(n, TILE)
                store(at, cols, down(cols))

            over(width // TILE, one)

        hidden, down = rows_fn(0, all_rows)
        over(tiles, hidden)
        if phase == 0:
            down_arrived()
        store_all(all_rows, down, keep_own)
        for ch in range(chunks):
            hop(buf, phase, ch, 1).wait_recv()
        if phase == 1:
            for ch in range(chunks):
                part_copy(0, 0, ch).wait_send()
        hidden, down = rows_fn(1, all_rows)
        over(tiles, hidden)
        store_all(all_rows, down, to(send_a))
        for ch in range(chunks):
            part_copy(phase, 0, ch).start()
        fillers[0]()

        def chunk(ch):
            at = tile_at(ch, crow)
            hop(buf, phase, ch, 0).wait_recv()
            hop(buf, phase, ch, 2).start()
            hidden_z, down_z = rows_fn(2, at)
            hidden_d, down_d = rows_fn(3, at)
            span(0, tiles // 2, hidden_z)
            hop(buf, phase, ch, 2).wait_recv()
            if phase == 1:
                part_copy(0, 1, ch).wait_send()
            over(tiles, hidden_d)
            store_all(at, down_d, to(send_d))
            part_copy(phase, 1, ch).start()
            span(tiles // 2, tiles, hidden_z)
            part_copy(phase, 1, ch).wait_recv()
            if phase == 1:
                part_copy(0, 2, ch).wait_send()
            store_all(at, down_z, to_z)
            part_copy(phase, 2, ch).start()

        over(chunks, chunk)
        fillers[1]()

    def transpose_into(dst, buf, slots):
        per_slot = rows // 128

        def one(i):
            slot = slots[0] + i // per_slot
            at = tile_at(lax.rem(i, per_slot), 128)
            to = tile_at(slots[0] * per_slot + i, 128)
            for n in range(width // TILE):
                dst[n * TILE : (n + 1) * TILE, to] = buf[slot, at, n * TILE : (n + 1) * TILE].T

        over(len(slots) * per_slot, one)

    tensor_pass(
        0, mids, forward_rows,
        [lambda: transpose_into(mid_t, mids, (0, 1)), lambda: transpose_into(mid_t, mids, (2, 3))],
    )

    loads[2].wait()

    def turn(at):
        mid = middle[at, :]
        branch_m = own_part[at, :] + recv_a[at, :].astype(jnp.float32) + recv_z[at, :].astype(jnp.float32)
        norm_m, factor_m = unit_of(branch_m)
        alpha = am_ref[...]
        y, factor_y = unit_of(mid + alpha * (norm_m - mid))
        out_ref[at, :] = y.astype(jnp.bfloat16)
        dy = cot[at, :].astype(jnp.float32)
        grad = factor_y * (dy - y * row_sum(y * dy))
        gam_ref[...] += jnp.sum(grad * (norm_m - mid), axis=0, keepdims=True)
        back = alpha * grad
        dbms[0, at, :] = (factor_m * (back - norm_m * row_sum(norm_m * back))).astype(jnp.bfloat16)
        dh2[at, :] = grad - back

    for ch in range(chunks):
        part_copy(0, 0, ch).wait_recv()
        part_copy(0, 2, ch).wait_recv()
        strips(ch, turn)
        hop(dbms, 1, ch, 0).start()
        hop(dbms, 1, ch, 1).start()

    def grad_store(m, q):
        return pltpu.make_async_copy(gw.at[m, pl.ds(q * qrows, qrows), :], gw_hbm.at[q, m], store_sems.at[m * nq + q])

    def weight_grad(m):
        lhs, rhs = ((mid_t, ups), (mid_t, gates), (dbm_t, mixed))[m]

        def block(i):
            q = i // (hid // TILE)
            cols = tile_at(lax.rem(i, hid // TILE), TILE)
            value = dot_ab(lhs[tile_at(q, TILE), :], rhs[:, cols])
            gw[m, tile_at(q, TILE), cols] = value.astype(jnp.bfloat16)

        over((width // TILE) * (hid // TILE), block)

    def down_grad():
        transpose_into(dbm_t, dbms, (2, 3))
        weight_grad(2)
        over(half - 1, lambda i: scatter(i).start())
        got_down[chip] = gw[2, chip_rows, :]

    tensor_pass(1, dbms, backward_rows, [lambda: transpose_into(dbm_t, dbms, (0, 1)), down_grad])

    def last(at):
        inputs, norm_a, factor_a, mid, factor_mid = make_middle(at)
        grad_mid = dh2[at, :] + own_part[at, :] + recv_a[at, :].astype(jnp.float32) + recv_z[at, :].astype(jnp.float32)
        grad = factor_mid * (grad_mid - mid * row_sum(mid * grad_mid))
        gaa_ref[...] += jnp.sum(grad * (norm_a - inputs), axis=0, keepdims=True)
        back = aa_ref[...] * grad
        dh1_ref[at, :] = grad - back
        mids[0, at, :] = (factor_a * (back - norm_a * row_sum(norm_a * back))).astype(jnp.bfloat16)

    for ch in range(chunks):
        hop(mids, 0, ch, 0).wait_send()
        hop(mids, 0, ch, 1).wait_send()
        part_copy(1, 0, ch).wait_recv()
        part_copy(1, 2, ch).wait_recv()
        strips(ch, last)

    dback = [
        remote(dparts.at[k], datt_ref.at[tile_at(t, rows), :], d2a_send.at[k - 1], d2a_recv.at[k - 1], (d, line[k]))
        for k in (1, 2, 3)
    ]
    for k in (3, 2, 1, 0):
        value = dot_ab(mids[0], wo[:, tile_at(line[k], heads_w)]).astype(jnp.bfloat16)
        if k:
            dparts[k] = value
            dback[k - 1].start()
        else:
            datt_ref[tile_at(t, rows), :] = value

    for m in range(2):
        weight_grad(m)
        for q in range(nq):
            grad_store(m, q).start()
    transpose_into(dbm_t, mids, (0,))

    def out_grad(n):
        at = tile_at(n, TILE)
        lhs = dbm_t[at, 0:rows]
        gwo[at, tile_at(t, heads_w)] = dot_ab(lhs, att_ref[tile_at(t, rows), :]).astype(jnp.bfloat16)
        for k in (1, 2, 3):
            gwo[at, tile_at(line[k], heads_w)] = dot_ab(lhs, parts[k - 1]).astype(jnp.bfloat16)

    over(width // TILE, out_grad)
    wo_store = pltpu.make_async_copy(gwo, gwo_hbm, store_sems.at[2 * nq])
    wo_store.start()

    over(half - 1, lambda i: scatter(i).wait_recv())

    def down_sum(i):
        at = tile_at(i, qrows // 2)
        total = got_down[0, at, :].astype(jnp.float32)
        total = lax.fori_loop(1, half, lambda e, value: value + got_down[e, at, :].astype(jnp.float32), total)
        down_ref[at, :] = total.astype(jnp.bfloat16)

    over(2, down_sum)
    over(half - 1, lambda i: gather(i).wait_send())
    over(half - 1, lambda i: scatter(i).wait_send())

    for k in (1, 2, 3):
        remote(
            dparts.at[k], datt_ref.at[tile_at(line[k], rows), :], d2a_send.at[k - 1], d2a_recv.at[k - 1], (d, line[k])
        ).wait()
    for copy in a2a:
        copy.wait_send()
    for ch in range(chunks):
        hop(mids, 0, ch, 2).wait_send()
        for kind in range(3):
            hop(dbms, 1, ch, kind).wait_send()
            part_copy(1, kind, ch).wait_send()
    for m in range(2):
        for q in range(nq):
            grad_store(m, q).wait()
    wo_store.wait()


def middle_call(count, chunks, attended, wo, w_parts, down, tokens, cotangent, alpha_a, alpha_m, su, sg):
    rows, width = tokens.shape
    group, heads_w = attended.shape
    nq, _, qrows, hid = w_parts.shape
    bf, f32 = jnp.bfloat16, jnp.float32
    anywhere = pl.BlockSpec(memory_space=pl.ANY)
    dma = pltpu.SemaphoreType.DMA
    return pl.pallas_call(
        functools.partial(middle_body, count),
        out_shape=(
            jax.ShapeDtypeStruct((rows, width), bf),
            jax.ShapeDtypeStruct((group, heads_w), bf),
            jax.ShapeDtypeStruct((nq, 2, qrows, hid), bf),
            jax.ShapeDtypeStruct((qrows, hid), bf),
            jax.ShapeDtypeStruct((width, width), bf),
            jax.ShapeDtypeStruct((rows, width), f32),
            jax.ShapeDtypeStruct((1, width), f32),
            jax.ShapeDtypeStruct((1, width), f32),
            jax.ShapeDtypeStruct((1, hid), f32),
            jax.ShapeDtypeStruct((1, hid), f32),
        ),
        in_specs=[vmem()] + [anywhere] * 5 + [vmem()] * 4,
        out_specs=(vmem(), vmem(), anywhere, vmem(), anywhere) + (vmem(),) * 5,
        scratch_shapes=[
            pltpu.VMEM((width, width), bf),
            pltpu.VMEM((3, width, hid), bf),
            pltpu.VMEM((rows, width), bf),
            pltpu.VMEM((rows, width), bf),
            pltpu.VMEM((3, rows, heads_w), bf),
            pltpu.VMEM((4, rows, width), bf),
            pltpu.VMEM((4, rows, width), bf),
            pltpu.VMEM((width, 4 * rows), bf),
            pltpu.VMEM((width, 4 * rows), bf),
            pltpu.VMEM((4 * rows, hid), bf),
            pltpu.VMEM((4 * rows, hid), bf),
            pltpu.VMEM((4 * rows, hid), bf),
            pltpu.VMEM((rows, width), f32),
            pltpu.VMEM((rows, width), f32),
            pltpu.VMEM((rows, width), f32),
            pltpu.VMEM((rows, width), f32),
        ]
        + [pltpu.VMEM((rows, width), bf)] * 6
        + [
            pltpu.VMEM((3, width, hid), bf),
            pltpu.VMEM((width, width), bf),
            pltpu.VMEM((4, rows, heads_w), bf),
            pltpu.VMEM((1, hid), f32),
            pltpu.VMEM((1, hid), f32),
            pltpu.VMEM((count // 2, qrows, hid), bf),
            dma((count // 2 - 1,)), dma((count // 2 - 1,)), dma((count // 2 - 1,)), dma((count // 2 - 1,)),
            dma((4 + 2 * nq,)),
            dma((2 * nq + 1,)),
            dma((6 * chunks,)),
            dma((6 * chunks,)),
            dma((3,)),
            dma((3,)),
            dma((3,)),
            dma((3,)),
            dma((6 * chunks,)),
            dma((6 * chunks,)),
        ],
        compiler_params=pltpu.CompilerParams(vmem_limit_bytes=67000000, collective_id=1, has_side_effects=True),
        cost_estimate=pl.CostEstimate(flops=10**11, bytes_accessed=10**8, transcendentals=10**6),
        name="middle",
    )(attended, wo, w_parts, down, tokens, cotangent, alpha_a, alpha_m, su, sg)


def remote_copy(src, dst, send_sem, recv_sem, peer):
    return pltpu.make_async_remote_copy(
        src_ref=src, dst_ref=dst, send_sem=send_sem, recv_sem=recv_sem, device_id=peer, device_id_type=MESH_ID
    )


def greet(peers):
    barrier = pltpu.get_barrier_semaphore()
    for peer in peers:
        pl.semaphore_signal(barrier, inc=1, device_id=peer, device_id_type=MESH_ID)
    pl.semaphore_wait(barrier, len(peers))


def rope_tables(order_ref, length_ref, cos_out, sin_out, col_out, start_out):
    group = order_ref.shape[1]
    lanes = cos_out.shape[1]
    places = lax.broadcasted_iota(jnp.int32, (1, group), 1)
    first = jnp.zeros((1, group), jnp.int32)
    begin = jnp.int32(0)
    for s in range(1, length_ref.shape[1]):
        begin = begin + length_ref[0, s - 1]
        first = jnp.where(places >= begin, begin, first)
    start_out[...] = first
    depth = (places - first).astype(jnp.float32)
    order = order_ref[...]
    order_f = order.astype(jnp.float32)
    lane = lax.broadcasted_iota(jnp.int32, (1, lanes), 1)
    half_width = HD // 2
    freq = jnp.exp((lane % half_width).astype(jnp.float32) * (-math.log(10000.0) / half_width))
    sign = jnp.where(lane % HD < half_width, -1.0, 1.0)

    def block(b):
        at = tile_at(b, 128)
        own = lax.broadcasted_iota(jnp.int32, (128, group), 0) + b * 128
        col_out[at, :] = row_sum(jnp.where(own == places, order_f, 0.0)).astype(jnp.int32)
        angles = row_sum(jnp.where(own == order, depth, 0.0)) * freq
        cos_out[at, :] = jnp.cos(angles)
        sin_out[at, :] = jnp.sin(angles) * sign

    over(group // 128, block)


def spread_body(
    count, tok, w_up, w_gate, wq, wk, wv, wo, order_ref, length_ref,
    pair, tok2, wqkv, wo_all, cos_out, sin_out, col_out, start_out,
    own_mlp, own_att, wo_rows, load_sem, keep_sem, a_send, a_recv, b_send, b_recv, tok_send, tok_recv,
    qkv_send, qkv_recv, relay_send, relay_recv, oz_send, oz_recv, oq_send, oq_recv, oc_send, oc_recv,
):
    d = lax.axis_index("dp")
    t = lax.axis_index("tensor")
    core = lax.rem(d, 2)
    home = core == t // 2
    far = (d - core + t // 2, flip2(t))
    wrows, wcols = wq.shape
    half = count // 2
    mlp = (w_up, w_gate)
    att = (wq, wk, wv)
    mine = tile_at(d, wrows)
    side = tile_at(core, wrows)
    other_side = tile_at(1 - core, wrows)

    barrier = pltpu.get_barrier_semaphore()

    def dp_peer(i):
        return lax.rem(d + 1 + i, count)

    def hello(i):
        pl.semaphore_signal(barrier, inc=1, device_id=(dp_peer(i), t), device_id_type=MESH_ID)

    over(count - 1, hello)
    for k in (1, 2, 3):
        pl.semaphore_signal(barrier, inc=1, device_id=(d, lax.rem(t + k, 4)), device_id_type=MESH_ID)
    pl.semaphore_signal(barrier, inc=1, device_id=(flip1(d), flip2(t)), device_id_type=MESH_ID)
    pl.semaphore_wait(barrier, count + 3)

    def pair_at(m, rows):
        return pair.at[m, rows, :]

    def b_copy(m):
        return remote_copy(mlp[m], pair_at(m, side), b_send.at[m], b_recv.at[core * 3 + m], far)

    def a_copy(m):
        return remote_copy(mlp[m], pair_at(m, side), a_send.at[m], a_recv.at[m], (flip1(d), t))

    tok_copy = remote_copy(tok, tok2, tok_send, tok_recv, (d, flip1(t)))
    def oz_copy(k):
        return remote_copy(wo, wo_rows.at[:, tile_at(t, wcols)], oz_send.at[k - 1], oz_recv.at[k - 1], (d, lax.rem(t + k, 4)))

    for k in (1, 2, 3):
        oz_copy(k).start()
    tok_copy.start()
    for m in range(2):
        b_copy(m).start()
    load_o = pltpu.make_async_copy(wo, wo_rows.at[:, tile_at(t, wcols)], load_sem.at[0])
    load_o.start()

    def qkv_to(i, m, peer):
        return remote_copy(
            att[m], wqkv.at[mine, pl.ds(m * wcols, wcols)], qkv_send.at[i, m], qkv_recv.at[i, m], (peer, t)
        )

    def qkv_copy(j, m):
        return qkv_to(j, m, lax.rem(d + 2 + 2 * j, count))

    def qkv_own(m):
        return qkv_to(half - 1, m, flip1(d))

    def qkv_relay(j):
        rows = tile_at(lax.rem(d + count - 2 - 2 * j, count), wrows)
        return remote_copy(wqkv.at[rows, :], wqkv.at[rows, :], relay_send.at[j], relay_recv.at[j], (flip1(d), t))

    def qkv_start(j):
        for m in range(3):
            qkv_copy(j, m).start()

    over(half - 1, qkv_start)
    for m in range(3):
        qkv_own(m).start()

    @pl.when(jnp.logical_not(home))
    def _():
        for m in range(2):
            a_copy(m).start()

    loads = [pltpu.make_async_copy(mlp[m], own_mlp.at[m], load_sem.at[1 + m]) for m in range(2)]
    loads += [pltpu.make_async_copy(att[m], own_att.at[m], load_sem.at[4 + m]) for m in range(3)]
    for copy in loads:
        copy.start()
    for copy in loads:
        copy.wait()
    keeps = [
        pltpu.make_async_copy(own_att.at[m], wqkv.at[mine, pl.ds(m * wcols, wcols)], keep_sem.at[m]) for m in range(3)
    ]
    for copy in keeps:
        copy.start()
    pair_keeps = [pltpu.make_async_copy(own_mlp.at[m], pair_at(m, side), keep_sem.at[3 + m]) for m in range(2)]

    @pl.when(home)
    def _():
        for copy in pair_keeps:
            copy.start()

    load_o.wait()
    for k in (1, 2, 3):
        oz_copy(k).wait_recv()
    keep_o = pltpu.make_async_copy(wo_rows, wo_all.at[mine, :], keep_sem.at[6])
    keep_o.start()

    def oq_copy(j):
        return remote_copy(wo_rows, wo_all.at[mine, :], oq_send.at[j], oq_recv.at[j], (lax.rem(d + 2 + 2 * j, count), t))

    def oc_own():
        return remote_copy(wo_rows, wo_all.at[mine, :], oc_send.at[half - 1], oc_recv.at[half - 1], (flip1(d), t))

    def oc_copy(j):
        rows = tile_at(lax.rem(d + count - 2 - 2 * j, count), wrows)
        return remote_copy(wo_all.at[rows, :], wo_all.at[rows, :], oc_send.at[j], oc_recv.at[j], (flip1(d), t))

    over(half - 1, lambda j: oq_copy(j).start())
    oc_own().start()
    rope_tables(order_ref, length_ref, cos_out, sin_out, col_out, start_out)

    def qkv_next(j):
        for m in range(3):
            qkv_copy(j, m).wait_recv()
        qkv_relay(j).start()

    over(half - 1, qkv_next)

    def oq_next(j):
        oq_copy(j).wait_recv()
        oc_copy(j).start()

    over(half - 1, oq_next)

    def qkv_wait(j):
        for m in range(3):
            qkv_copy(j, m).wait_send()
        qkv_relay(j).wait()

    over(half - 1, qkv_wait)
    for m in range(3):
        qkv_own(m).wait()
    over(half - 1, lambda j: oq_copy(j).wait_send())
    over(half - 1, lambda j: oc_copy(j).wait())
    oc_own().wait()
    for k in (1, 2, 3):
        oz_copy(k).wait_send()
    keep_o.wait()
    for copy in keeps:
        copy.wait()
    tok_copy.wait()
    for m in range(2):
        b_copy(m).wait_send()

    @pl.when(home)
    def _():
        for m in range(2):
            pair_keeps[m].wait()
            remote_copy(mlp[m], pair_at(m, other_side), a_send.at[m], a_recv.at[m], (flip1(d), t)).wait_recv()

    @pl.when(jnp.logical_not(home))
    def _():
        for m in range(2):
            a_copy(m).wait_send()
            for c in range(2):
                remote_copy(
                    mlp[m], pair_at(m, pl.ds(c * wrows, wrows)), b_send.at[m], b_recv.at[c * 3 + m], far
                ).wait_recv()


def spread_call(count, tokens, w_up, w_gate, wq, wk, wv, wo, order, lengths):
    rows, width = tokens.shape
    group = order.shape[1]
    wrows, wcols = wq.shape
    hid = w_up.shape[1]
    bf = jnp.bfloat16
    anywhere = pl.BlockSpec(memory_space=pl.ANY)
    dma = pltpu.SemaphoreType.DMA
    return pl.pallas_call(
        functools.partial(spread_body, count),
        out_shape=(
            jax.ShapeDtypeStruct((2, 2 * wrows, hid), bf),
            jax.ShapeDtypeStruct((rows, width), bf),
            jax.ShapeDtypeStruct((width, 3 * wcols), bf),
            jax.ShapeDtypeStruct((width, width), bf),
            jax.ShapeDtypeStruct((group, 2 * HD), jnp.float32),
            jax.ShapeDtypeStruct((group, 2 * HD), jnp.float32),
            jax.ShapeDtypeStruct((group, 1), jnp.int32),
            jax.ShapeDtypeStruct((1, group), jnp.int32),
        ),
        in_specs=[anywhere] * 7 + [vmem(), pl.BlockSpec(memory_space=pltpu.SMEM)],
        out_specs=(anywhere,) * 4 + (vmem(),) * 4,
        scratch_shapes=[
            pltpu.VMEM((2, wrows, hid), bf),
            pltpu.VMEM((3, wrows, wcols), bf),
            pltpu.VMEM((wrows, width), bf),
            dma((7,)), dma((7,)), dma((3,)), dma((3,)), dma((3,)), dma((6,)), dma, dma,
            dma((count // 2, 3)), dma((count // 2, 3)), dma((count // 2 - 1,)), dma((count // 2 - 1,)), dma((3,)), dma((3,)),
            dma((count // 2,)), dma((count // 2,)), dma((count // 2,)), dma((count // 2,)),
        ],
        compiler_params=pltpu.CompilerParams(vmem_limit_bytes=VMEM_LIMIT, collective_id=2, has_side_effects=True),
        name="spread",
    )(tokens, w_up, w_gate, wq, wk, wv, wo, order, lengths)


def head_sums(value):
    width = value.shape[1]
    same = (
        lax.broadcasted_iota(jnp.int32, (width, width), 0) // HD == lax.broadcasted_iota(jnp.int32, (width, width), 1) // HD
    )
    ones = jnp.where(same, 1.0, 0.0).astype(jnp.bfloat16)
    high = value.astype(jnp.bfloat16)
    low = (value - high.astype(jnp.float32)).astype(jnp.bfloat16)
    return dot_ab(high, ones) + dot_ab(low, ones)


def swap_halves(value):
    width = value.shape[1]
    lane = lax.broadcasted_iota(jnp.int32, value.shape, 1) % HD
    return jnp.where(lane < HD // 2, pltpu.roll(value, width - HD // 2, 1), pltpu.roll(value, HD // 2, 1))


def project_body(
    tok, tok2, w_down, wqkv, cos_ref, sin_ref, order_col, gain_ref, q_ref, k_ref, v_ref, raw_ref, x_hbm, pair_down,
    xs, plain, own_down, load_sem, keep_sem, mid_send, recv, on_send, down_load, down_keep, a_send, a_recv, b_send, b_recv,
):
    t = lax.axis_index("tensor")
    d = lax.axis_index("dp")
    _, rows, width = xs.shape
    group, cols = q_ref.shape
    near = flip1(t)
    across = 3 - t
    inner = (t + 1) // 2 == 1
    arrive = (2 - t // 2, 3 - 3 * (t // 2))
    pieces = mid_send.shape[0] // 2
    part = rows // pieces
    greet([(d, near), (d, across), (d, flip2(t)), (flip1(d), t), (flip1(d), flip2(t))])

    core = lax.rem(d, 2)
    home = core == t // 2
    wrows = own_down.shape[0]

    def down_at(c):
        return pair_down.at[tile_at(c, wrows), :]

    b_copy = remote_copy(w_down, down_at(core), b_send, b_recv.at[core], (d - core + t // 2, flip2(t)))
    a_copy = remote_copy(w_down, down_at(core), a_send, a_recv, (flip1(d), t))
    load_down = pltpu.make_async_copy(w_down, own_down, down_load)
    keep_down = pltpu.make_async_copy(own_down, down_at(core), down_keep)

    def mid_copy(k):
        rows_of = pl.ds((k % pieces) * part, part)
        src = (tok, tok2)[k // pieces].at[rows_of, :]
        return remote_copy(src, xs.at[(t, near)[k // pieces], rows_of, :], mid_send.at[k], recv.at[k], (d, across))

    def on_copy(k):
        ref = xs.at[arrive[k // pieces], pl.ds((k % pieces) * part, part), :]
        return remote_copy(ref, ref, on_send.at[k], recv.at[k], (d, near))

    @pl.when(inner)
    def _():
        for k in range(2 * pieces):
            mid_copy(k).start()
        b_copy.start()

    load_down.start()

    @pl.when(jnp.logical_not(home))
    def _():
        a_copy.start()

    loads = [
        pltpu.make_async_copy(tok, xs.at[t], load_sem.at[0]),
        pltpu.make_async_copy(tok2, xs.at[near], load_sem.at[1]),
    ]
    for copy in loads:
        copy.start()

    def keep(index, slot):
        return pltpu.make_async_copy(xs.at[slot], x_hbm.at[tile_at(slot, rows), :], keep_sem.at[index])

    def strip(slot, i):
        at = tile_at(slot * (rows // WIDE_STRIP) + i, WIDE_STRIP)
        x = xs[slot, tile_at(i, WIDE_STRIP), :]
        cos = jnp.concatenate([cos_ref[at, :]] * (cols // cos_ref.shape[1]), axis=1)
        sin = jnp.concatenate([sin_ref[at, :]] * (cols // sin_ref.shape[1]), axis=1)
        for m in range(2):
            raw = dot_ab(x, wqkv[:, m * cols : (m + 1) * cols])
            raw_ref[at, m * cols : (m + 1) * cols] = raw.astype(jnp.bfloat16)
            normed = raw * lax.rsqrt(head_sums(raw * raw) + EPS) * gain_ref[:, tile_at(t, cols)]
            plain[at, m * cols : (m + 1) * cols] = (normed * cos + swap_halves(normed) * sin).astype(jnp.bfloat16)
        plain[at, 2 * cols : 3 * cols] = dot_ab(x, wqkv[:, 2 * cols : 3 * cols]).astype(jnp.bfloat16)

    def permute(index, size, first):
        base = tile_at(index, size)

        def one(b):
            at = tile_at(b, BLK)
            token = lax.broadcasted_iota(jnp.int32, (BLK, size), 1) + index * size
            hot = (token == order_col[at, :]).astype(jnp.float32)
            value = dot_ab(hot.astype(jnp.bfloat16), plain[base, :])
            for m, ref in enumerate((q_ref, k_ref, v_ref)):
                piece = value[:, m * cols : (m + 1) * cols]
                if not first:
                    piece += ref[at, :].astype(jnp.float32)
                ref[at, :] = piece.astype(jnp.bfloat16)

        over(group // BLK, one)

    loads[0].wait()
    keep(0, t).start()
    over(rows // WIDE_STRIP, lambda i: strip(t, i))
    loads[1].wait()
    keep(1, near).start()
    over(rows // WIDE_STRIP, lambda i: strip(near, i))
    permute(t // 2, 2 * rows, True)
    load_down.wait()

    @pl.when(home)
    def _():
        keep_down.start()

    per_strip = WIDE_STRIP // part
    for k in range(2 * pieces):
        slot = arrive[k // pieces]
        ref = xs.at[slot, pl.ds((k % pieces) * part, part), :]
        remote_copy(ref, ref, on_send.at[k], recv.at[k], (d, near)).wait_recv()

        @pl.when(inner)
        def _():
            on_copy(k).start()

        if k == 2 * pieces - 3:

            @pl.when(jnp.logical_not(inner))
            def _():
                b_copy.start()

        if k % per_strip == per_strip - 1:
            strip(slot, (k % pieces) // per_strip)
        if k % pieces == pieces - 1:
            keep(2 + k // pieces, slot).start()
            permute(slot, rows, False)

    for index, slot in enumerate((t, near, *arrive)):
        keep(index, slot).wait()

    @pl.when(inner)
    def _():
        for k in range(2 * pieces):
            mid_copy(k).wait_send()
            on_copy(k).wait_send()

    b_copy.wait_send()

    @pl.when(home)
    def _():
        keep_down.wait()
        remote_copy(w_down, down_at(1 - core), a_send, a_recv, (flip1(d), t)).wait_recv()

    @pl.when(jnp.logical_not(home))
    def _():
        a_copy.wait_send()
        for c in range(2):
            remote_copy(w_down, down_at(c), b_send, b_recv.at[c], (d - core + t // 2, flip2(t))).wait_recv()


def project_call(tokens, tok2, w_down, wqkv, cos, sin, order_col, gains):
    rows, width = tokens.shape
    group = order_col.shape[0]
    cols = wqkv.shape[1] // 3
    wrows, hid = w_down.shape
    bf = jnp.bfloat16
    anywhere = pl.BlockSpec(memory_space=pl.ANY)
    dma = pltpu.SemaphoreType.DMA
    return pl.pallas_call(
        project_body,
        out_shape=(jax.ShapeDtypeStruct((group, cols), bf),) * 3
        + (
            jax.ShapeDtypeStruct((group, 2 * cols), bf),
            jax.ShapeDtypeStruct((group, width), bf),
            jax.ShapeDtypeStruct((2 * wrows, hid), bf),
        ),
        in_specs=[anywhere] * 3 + [vmem()] * 5,
        out_specs=(vmem(),) * 4 + (anywhere,) * 2,
        scratch_shapes=[
            pltpu.VMEM((group // rows, rows, width), bf),
            pltpu.VMEM((group, 3 * cols), bf),
            pltpu.VMEM((wrows, hid), bf),
            dma((2,)), dma((4,)), dma((8,)), dma((8,)), dma((8,)),
            dma, dma, dma, dma, dma, dma((2,)),
        ],
        compiler_params=pltpu.CompilerParams(vmem_limit_bytes=VMEM_LIMIT, collective_id=3, has_side_effects=True),
        cost_estimate=pl.CostEstimate(flops=6 * 10**10, bytes_accessed=10**7, transcendentals=10**6),
        name="project",
    )(tokens, tok2, w_down, wqkv, cos, sin, order_col, gains)


def join(own, other, got, chip):
    def one(e):
        own[e] = (own[e].astype(jnp.float32) + other[e].astype(jnp.float32)).astype(own.dtype)

    over(own.shape[0], one)
    got[chip] = own[chip]


def total_of(got):
    return lax.fori_loop(
        1, got.shape[0], lambda i, total: total + got[i].astype(jnp.float32), got[0].astype(jnp.float32)
    )


def tail_body(
    count, grad_ref, raw_ref, cos_ref, sin_ref, wqkv, x_hbm, down_hbm, gwo_hbm, kept_ref, gain_ref,
    tok_out, gq, gain_sum, down_out, wo_mid,
    xs, x_t, draw, part_far, part_mid, part_near, own_part, from_a, from_b, from_c, from_d, from_e, from_f,
    near_mlp, far_mlp, own_w, core_w, got_w, load_sem, hop_send, hop_recv, keep_sem, near_send, near_recv, far_send, far_recv,
    load_w_sem, core_send, core_recv, w_send, w_recv,
):
    d = lax.axis_index("dp")
    t = lax.axis_index("tensor")
    rows, width = tok_out.shape
    group = draw.shape[0]
    cols = draw.shape[1] // 3
    near = flip1(t)
    inner = (t + 1) // 2 == 1
    outer = jnp.logical_not(inner)
    far, mid = 3 - 3 * (t // 2), 2 - t // 2
    chunk = rows // 2
    half, chip, core = count // 2, d // 2, lax.rem(d, 2)

    def chip_peer(i):
        return lax.rem(chip + 1 + i, half)

    barrier = pltpu.get_barrier_semaphore()
    for peer in [(d, near), (d, 3 - t), (d, flip2(t)), (flip1(d), t), (flip1(d), flip2(t))]:
        pl.semaphore_signal(barrier, inc=1, device_id=peer, device_id_type=MESH_ID)
    over(
        half - 1,
        lambda i: pl.semaphore_signal(barrier, inc=1, device_id=(2 * chip_peer(i) + core, t), device_id_type=MESH_ID),
    )
    pl.semaphore_wait(barrier, half + 4)

    home = core == t // 2
    away = jnp.logical_not(home)
    near_copy = remote_copy(down_hbm.at[1 - core], near_mlp, near_send, near_recv, (flip1(d), t))
    far_same = remote_copy(down_hbm.at[core], far_mlp, far_send.at[0], far_recv, (d, flip2(t)))
    far_cross = remote_copy(down_hbm.at[1 - core], far_mlp, far_send.at[1], far_recv, (flip1(d), flip2(t)))
    keep_mlp = pltpu.make_async_copy(down_hbm.at[core], near_mlp, keep_sem)

    @pl.when(home)
    def _():
        near_copy.start()
        keep_mlp.start()

    @pl.when(away)
    def _():
        far_same.start()
        far_cross.start()

    load_x = pltpu.make_async_copy(x_hbm, xs, load_sem)
    load_x.start()

    core_w_copy = remote_copy(gwo_hbm.at[:, 1 - core], core_w, core_send, core_recv, (flip1(d), t))
    load_w = pltpu.make_async_copy(gwo_hbm.at[:, core], own_w, load_w_sem)
    core_w_copy.start()
    load_w.start()

    def w_copy(i):
        return remote_copy(
            own_w.at[chip_peer(i)], got_w.at[chip], w_send.at[i], w_recv.at[i], (2 * chip_peer(i) + core, t)
        )

    def hop(kind, ch):
        src, dst, to = (
            (part_far, from_a, near),
            (part_mid, from_b, near),
            (part_near, from_c, near),
            (part_far, from_d, 3 - t),
            (part_mid, from_e, 3 - t),
            (part_near, from_f, near),
        )[kind]
        part = tile_at(ch, chunk)
        return remote_copy(src.at[part, :], dst.at[part, :], hop_send.at[kind, ch], hop_recv.at[kind, ch], (d, to))

    gain_sum[...] = jnp.zeros_like(gain_sum)

    def work(slot, ch, ref):
        at = tile_at(2 * slot + ch, chunk)
        to = tile_at(ch, chunk)
        cos = jnp.concatenate([cos_ref[at, :]] * (cols // cos_ref.shape[1]), axis=1)
        sin = jnp.concatenate([sin_ref[at, :]] * (cols // sin_ref.shape[1]), axis=1)
        gain = gain_ref[:, tile_at(t, cols)]
        for m in range(2):
            grad = grad_ref[at, m * cols : (m + 1) * cols].astype(jnp.float32)
            raw = raw_ref[at, m * cols : (m + 1) * cols].astype(jnp.float32)
            back = grad * cos - swap_halves(grad) * sin
            factor = lax.rsqrt(head_sums(raw * raw) + EPS)
            normed = raw * factor
            gain_sum[...] += jnp.sum(back * normed, axis=0, keepdims=True)
            scaled = back * gain
            draw[at, m * cols : (m + 1) * cols] = (factor * (scaled - normed * head_sums(normed * scaled))).astype(
                jnp.bfloat16
            )
        draw[at, 2 * cols : 3 * cols] = grad_ref[at, 2 * cols : 3 * cols]

        def product(n):
            tile = tile_at(n, TILE)
            ref[to, tile] = dot_abt(draw[at, :], wqkv[tile, :]).astype(ref.dtype)

        over(width // TILE, product)

    def send_part(kind, slot, ref):
        def one(ch):
            work(slot, ch, ref)

            @pl.when(outer)
            def _():
                hop(kind, ch).start()

        over(2, one)

    send_part(0, far, part_far)
    send_part(1, mid, part_mid)
    send_part(2, near, part_near)
    over(2, lambda ch: work(t, ch, own_part))

    def pass_on(kind, ch, own, got, then):
        @pl.when(inner)
        def _():
            part = pl.ds(ch * chunk, chunk)
            hop(kind, ch).wait_recv()
            own[part, :] = (own[part, :].astype(jnp.float32) + got[part, :].astype(jnp.float32)).astype(jnp.bfloat16)
            hop(then, ch).start()

    pass_on(0, 0, part_far, from_a, 3)
    pass_on(0, 1, part_far, from_a, 3)

    load_w.wait()
    core_w_copy.wait_recv()
    join(own_w, core_w, got_w, chip)
    over(half - 1, lambda i: w_copy(i).start())
    load_x.wait()

    def flip_block(b):
        at = tile_at(b, 128)
        for n in range(width // TILE):
            x_t[n * TILE : (n + 1) * TILE, at] = xs[at, n * TILE : (n + 1) * TILE].T

    over(group // 128, flip_block)
    pass_on(3, 0, part_near, from_d, 5)

    def weight_grad(n):
        tile = tile_at(n, TILE)
        gq[tile, :] = dot_ab(x_t[tile, :], draw[...]).astype(jnp.bfloat16)

    over(width // TILE, weight_grad)
    pass_on(1, 0, part_mid, from_b, 4)
    pass_on(3, 1, part_near, from_d, 5)
    pass_on(1, 1, part_mid, from_b, 4)

    @pl.when(home)
    def _():
        keep_mlp.wait()
        near_copy.wait_send()

    @pl.when(away)
    def _():
        near_copy.wait_recv()

    over(half - 1, lambda i: w_copy(i).wait_recv())
    wo_mid[...] = total_of(got_w).astype(jnp.bfloat16)
    core_w_copy.wait_send()
    over(half - 1, lambda i: w_copy(i).wait_send())
    far_same.wait_recv()
    down_out[...] = near_mlp[...].astype(jnp.float32) + far_mlp[...].astype(jnp.float32)

    @pl.when(away)
    def _():
        far_same.wait_send()
        far_cross.wait_send()

    for ch in range(2):
        part = pl.ds(ch * chunk, chunk)

        @pl.when(inner)
        def _():
            hop(2, ch).wait_recv()
            hop(4, ch).wait_recv()
            tok_out[part, :] = (
                kept_ref[part, :]
                + own_part[part, :]
                + from_c[part, :].astype(jnp.float32)
                + from_e[part, :].astype(jnp.float32)
            )

        @pl.when(outer)
        def _():
            hop(5, ch).wait_recv()
            tok_out[part, :] = kept_ref[part, :] + own_part[part, :] + from_f[part, :].astype(jnp.float32)

    for ch in range(2):

        @pl.when(inner)
        def _():
            for kind in (3, 4, 5):
                hop(kind, ch).wait_send()

        @pl.when(outer)
        def _():
            for kind in (0, 1, 2):
                hop(kind, ch).wait_send()


def tail_call(count, grad_qkv, raw, cos, sin, wqkv, all_tokens, down, gwo, kept, gains):
    rows, width = kept.shape
    wrows, hid = width // count, down.shape[1]
    group, three = grad_qkv.shape
    bf, f32 = jnp.bfloat16, jnp.float32
    anywhere = pl.BlockSpec(memory_space=pl.ANY)
    dma = pltpu.SemaphoreType.DMA
    shape = jax.ShapeDtypeStruct
    return pl.pallas_call(
        functools.partial(tail_body, count),
        out_shape=(
            shape((rows, width), f32),
            shape((width, three), bf),
            shape((1, three // 3), f32),
            shape((wrows, hid), f32),
            shape((wrows, width), bf),
        ),
        in_specs=[vmem()] * 5 + [anywhere] * 3 + [vmem()] * 2,
        out_specs=(vmem(),) * 5,
        scratch_shapes=[
            pltpu.VMEM((group, width), bf),
            pltpu.VMEM((width, group), bf),
            pltpu.VMEM((group, three), bf),
            pltpu.VMEM((rows, width), bf),
            pltpu.VMEM((rows, width), bf),
            pltpu.VMEM((rows, width), bf),
            pltpu.VMEM((rows, width), f32),
        ]
        + [pltpu.VMEM((rows, width), bf)] * 6
        + [pltpu.VMEM((wrows, hid), bf)] * 2
        + [pltpu.VMEM((count // 2, wrows, width), bf)] * 3
        + [dma, dma((6, 2)), dma((6, 2)), dma, dma, dma, dma((2,)), dma]
        + [dma, dma, dma, dma((count // 2 - 1,)), dma((count // 2 - 1,))],
        compiler_params=pltpu.CompilerParams(vmem_limit_bytes=VMEM_LIMIT, collective_id=4, has_side_effects=True),
        cost_estimate=pl.CostEstimate(flops=6 * 10**10, bytes_accessed=10**7, transcendentals=10**6),
        name="tail",
    )(
        grad_qkv, raw, cos, sin, wqkv, all_tokens, down.reshape(2, wrows, hid),
        gwo.reshape(count // 2, 2, wrows, width), kept, gains,
    )


def settle_body(
    count, gq_hbm, mlp_hbm, wo_mid, gain_ref, gaa_ref, gam_ref, gsu_ref, gsg_ref,
    q_out, k_out, v_out, wo_out, up_out, gate_out, gain_out, aa_out, su_out, sg_out, am_out,
    own_q, core_q, got_q, got_z, near_mlp, far_mlp, vec, got_v, vec_mid, got_s,
    load_sem, core_send, core_recv, q_send, q_recv, z_send, z_recv, v_send, v_recv, s_send, s_recv,
    near_send, near_recv, mlp_send, mlp_recv,
):
    d = lax.axis_index("dp")
    t = lax.axis_index("tensor")
    half, wrows, three = got_q.shape
    cols = three // 3
    width = gaa_ref.shape[1]
    chip, core = d // 2, lax.rem(d, 2)
    home = core == t // 2
    away = jnp.logical_not(home)
    f32, bf = jnp.float32, jnp.bfloat16

    def dp_peer(i):
        return lax.rem(d + 1 + i, count)

    def line_peer(k):
        return lax.rem(t + k, 4)

    def chip_peer(i):
        return lax.rem(chip + 1 + i, half)

    barrier = pltpu.get_barrier_semaphore()
    over(
        count - 1,
        lambda i: pl.semaphore_signal(barrier, inc=1, device_id=(dp_peer(i), t), device_id_type=MESH_ID),
    )
    for k in (1, 2, 3):
        pl.semaphore_signal(barrier, inc=1, device_id=(d, line_peer(k)), device_id_type=MESH_ID)
    pl.semaphore_signal(barrier, inc=1, device_id=(flip1(d), flip2(t)), device_id_type=MESH_ID)
    pl.semaphore_wait(barrier, count + 3)

    def z_copy(k):
        return remote_copy(
            wo_mid.at[:, tile_at(line_peer(k), cols)], got_z.at[t], z_send.at[k - 1], z_recv.at[k - 1], (d, line_peer(k))
        )

    for k in (1, 2, 3):
        z_copy(k).start()
    got_z[t] = wo_mid[:, tile_at(t, cols)]

    near_copy = remote_copy(mlp_hbm.at[:, 1 - core], near_mlp, near_send, near_recv, (flip1(d), t))
    keep_mlp = pltpu.make_async_copy(mlp_hbm.at[:, core], near_mlp, load_sem.at[0])

    hid = near_mlp.shape[2]

    def far_same(u):
        m, part = u // 2, tile_at(u % 2, hid // 2)
        return remote_copy(
            mlp_hbm.at[m, core, :, part], far_mlp.at[m, :, part], mlp_send.at[u], mlp_recv.at[u], (d, flip2(t))
        )

    def far_cross(u):
        m, part = u // 2, tile_at(u % 2, hid // 2)
        return remote_copy(
            mlp_hbm.at[m, 1 - core, :, part], far_mlp.at[m, :, part], mlp_send.at[4 + u], mlp_recv.at[u],
            (flip1(d), flip2(t)),
        )

    def far_start(u):
        @pl.when(away)
        def _():
            far_same(u).start()
            far_cross(u).start()

    @pl.when(home)
    def _():
        near_copy.start()
        keep_mlp.start()

    for u in range(3):
        far_start(u)

    core_q_copy = remote_copy(gq_hbm.at[:, 1 - core], core_q, core_send, core_recv, (flip1(d), t))
    load_q = pltpu.make_async_copy(gq_hbm.at[:, core], own_q, load_sem.at[1])
    core_q_copy.start()
    load_q.start()

    vec[...] = jnp.zeros_like(vec)
    for row, ref in enumerate((gaa_ref, gam_ref, gsu_ref, gsg_ref)):
        vec[row : row + 1, :] = ref[...]
    vec[4:5, 0:cols] = gain_ref[...]
    got_v[d] = vec[...]

    def v_copy(i):
        return remote_copy(vec, got_v.at[d], v_send.at[i], v_recv.at[i], (dp_peer(i), t))

    over(count - 1, lambda i: v_copy(i).start())

    def q_copy(i):
        return remote_copy(
            own_q.at[chip_peer(i)], got_q.at[chip], q_send.at[i], q_recv.at[i], (2 * chip_peer(i) + core, t)
        )

    load_q.wait()
    core_q_copy.wait_recv()
    join(own_q, core_q, got_q, chip)
    over(half - 1, lambda i: q_copy(i).start())

    over(count - 1, lambda i: v_copy(i).wait_recv())
    even, odd = lax.fori_loop(
        1, half, lambda i, total: (total[0] + got_v[2 * i], total[1] + got_v[2 * i + 1]), (got_v[0], got_v[1])
    )
    both = even + odd
    vec_mid[...] = jnp.concatenate([both[0:2], even[2:3], odd[2:3], even[3:4], odd[3:4], both[4:5], both[4:5]], axis=0)

    def s_copy(k):
        return remote_copy(vec_mid, got_s.at[t], s_send.at[k - 1], s_recv.at[k - 1], (d, line_peer(k)))

    for k in (1, 2, 3):
        s_copy(k).start()
    got_s[t] = vec_mid[...]
    far_start(3)

    over(half - 1, lambda i: q_copy(i).wait_recv())
    total = total_of(got_q)
    for m, ref in enumerate((q_out, k_out, v_out)):
        ref[...] = total[:, m * cols : (m + 1) * cols]

    for k in (1, 2, 3):
        z_copy(k).wait_recv()
        s_copy(k).wait_recv()
    wo_out[...] = got_z[0].astype(f32) + got_z[1].astype(f32) + got_z[2].astype(f32) + got_z[3].astype(f32)
    shared = got_s[0] + got_s[1] + got_s[2] + got_s[3]
    aa_out[...] = shared[0:1]
    am_out[...] = shared[1:2]
    pairs = (got_s[0] + got_s[2], got_s[1] + got_s[3])
    for s in range(4):
        su_out[:, s * width : (s + 1) * width] = pairs[s % 2][2 + s // 2 : 3 + s // 2]
        sg_out[:, s * width : (s + 1) * width] = pairs[s % 2][4 + s // 2 : 5 + s // 2] * math.sqrt(D)
        gain_out[:, s * cols : (s + 1) * cols] = got_s[s][6:7, 0:cols]

    @pl.when(home)
    def _():
        keep_mlp.wait()
        near_copy.wait_send()

    @pl.when(away)
    def _():
        near_copy.wait_recv()

    for m, ref in enumerate((up_out, gate_out)):
        far_same(2 * m).wait_recv()
        far_same(2 * m + 1).wait_recv()
        ref[...] = near_mlp[m].astype(f32) + far_mlp[m].astype(f32)

    @pl.when(away)
    def _():
        for u in range(4):
            far_same(u).wait_send()
            far_cross(u).wait_send()

    core_q_copy.wait_send()
    over(count - 1, lambda i: v_copy(i).wait_send())
    over(half - 1, lambda i: q_copy(i).wait_send())
    for k in (1, 2, 3):
        z_copy(k).wait_send()
        s_copy(k).wait_send()


def settle_call(count, gq, mlp, wo_mid, gain_sum, gaa, gam, gsu, gsg):
    width, three = gq.shape
    half = count // 2
    cols = three // 3
    wrows = width // count
    hid = mlp.shape[2]
    bf, f32 = jnp.bfloat16, jnp.float32
    anywhere = pl.BlockSpec(memory_space=pl.ANY)
    dma = pltpu.SemaphoreType.DMA
    shape = jax.ShapeDtypeStruct
    return pl.pallas_call(
        functools.partial(settle_body, count),
        out_shape=(shape((wrows, cols), f32),) * 4
        + (shape((wrows, hid), f32),) * 2
        + (
            shape((1, 4 * cols), f32),
            shape((1, width), f32),
            shape((1, 4 * hid), f32),
            shape((1, 4 * hid), f32),
            shape((1, width), f32),
        ),
        in_specs=[anywhere] * 2 + [vmem()] * 6,
        out_specs=(vmem(),) * 11,
        scratch_shapes=[pltpu.VMEM((half, wrows, three), bf)] * 3
        + [
            pltpu.VMEM((4, wrows, cols), bf),
            pltpu.VMEM((2, wrows, hid), bf),
            pltpu.VMEM((2, wrows, hid), bf),
            pltpu.VMEM((8, width), f32),
            pltpu.VMEM((count, 8, width), f32),
            pltpu.VMEM((8, width), f32),
            pltpu.VMEM((4, 8, width), f32),
            dma((2,)),
            dma, dma,
            dma((half - 1,)), dma((half - 1,)),
            dma((3,)), dma((3,)),
            dma((count - 1,)), dma((count - 1,)),
            dma((3,)), dma((3,)),
            dma, dma, dma((8,)), dma((4,)),
        ],
        compiler_params=pltpu.CompilerParams(vmem_limit_bytes=VMEM_LIMIT, collective_id=5, has_side_effects=True),
        cost_estimate=pl.CostEstimate(flops=10**9, bytes_accessed=10**7, transcendentals=0),
        name="settle",
    )(
        gq.reshape(half, 2, wrows, three),
        mlp.reshape(2, 2, wrows, hid),
        wo_mid, gain_sum, gaa, gam, gsu, gsg,
    )


def deliver_body(count, total, *refs):
    ins, outs, rest = refs[:total], refs[total : 2 * total], refs[2 * total :]
    held, load_sem, store_sem = rest[:count], rest[count], rest[count + 1]
    loads = [pltpu.make_async_copy(ins[i], held[i], load_sem.at[i]) for i in range(count)]
    stores = [pltpu.make_async_copy(held[i], outs[i], store_sem.at[i]) for i in range(count)]
    for copy in loads:
        copy.start()
    for i in range(count, total):
        outs[i][...] = ins[i][0, :]
    for load, store in zip(loads, stores):
        load.wait()
        store.start()
    for copy in stores:
        copy.wait()


def deliver_call(arrays, vectors):
    total = len(arrays) + len(vectors)
    specs = [pl.BlockSpec(memory_space=pl.ANY)] * len(arrays) + [vmem()] * len(vectors)
    return pl.pallas_call(
        functools.partial(deliver_body, len(arrays), total),
        out_shape=tuple(jax.ShapeDtypeStruct(a.shape, a.dtype) for a in arrays)
        + tuple(jax.ShapeDtypeStruct((v.shape[1],), v.dtype) for v in vectors),
        in_specs=specs,
        out_specs=tuple(specs),
        scratch_shapes=[pltpu.VMEM(a.shape, a.dtype) for a in arrays] + [pltpu.SemaphoreType.DMA((len(arrays),))] * 2,
        compiler_params=pltpu.CompilerParams(vmem_limit_bytes=VMEM_LIMIT),
        name="deliver",
    )(*arrays, *vectors)


def same_core_groups(dp_count):
    return [list(range(parity, dp_count, 2)) for parity in range(2)]


def on_device(
    tokens,
    w_query,
    w_key,
    w_value,
    w_out_t,
    w_up,
    w_gate,
    w_down_t,
    scale_qk,
    alpha_attn,
    scale_up,
    scale_gate,
    alpha_mlp,
    order,
    lengths,
    cotangent,
):
    dp_count = lax.axis_size("dp")
    pair, near_tokens, wqkv, wo_every, cos_table, sin_table, order_col, start = spread_call(
        dp_count, tokens, w_up, w_gate, w_query, w_key, w_value, w_out_t, order, lengths
    )
    low = lax.slice(start[0], (0,), (start.shape[1],), (BLK,)) // BLK
    mlp_parts = lax.all_gather(
        pair, "dp", axis=0, tiled=False, axis_index_groups=same_core_groups(dp_count)
    )
    queries, key_rows, value_rows, raw, all_tokens, pair_down = project_call(
        tokens, near_tokens, w_down_t, wqkv, cos_table, sin_table, order_col, scale_qk[None, :]
    )
    attended, log_totals, attended_plain = attn_fwd(low, start, order, queries, key_rows, value_rows)
    out_rows, grad_att_rows, up_gate_grads, down_sums, wo_grads, grad_h1_kept, grad_alpha_a, grad_alpha_m, grad_su, grad_sv = middle_call(
        dp_count,
        2,
        attended_plain,
        wo_every,
        mlp_parts,
        pair_down,
        tokens,
        cotangent,
        alpha_attn[None, :],
        alpha_mlp[None, :],
        scale_up[None, :],
        scale_gate[None, :],
    )
    grad_qkv = attn_bwd(
        low, start, order, order_col, log_totals, queries, key_rows, value_rows, attended, grad_att_rows
    )
    up_gate_sums = lax.psum_scatter(
        up_gate_grads, "dp", scatter_dimension=0, tiled=False, axis_index_groups=same_core_groups(dp_count)
    )
    grad_tokens, grad_q, gain_sum, grad_down, wo_sums = tail_call(
        dp_count, grad_qkv, raw, cos_table, sin_table, wqkv, all_tokens, down_sums, wo_grads, grad_h1_kept, scale_qk[None, :]
    )
    settled = settle_call(
        dp_count, grad_q, up_gate_sums, wo_sums, gain_sum, grad_alpha_a, grad_alpha_m, grad_su, grad_sv
    )
    return deliver_call([out_rows, grad_tokens, *settled[:6], grad_down], settled[6:])


def solution(mesh):
    return jax.shard_map(
        on_device,
        mesh=mesh,
        in_specs=(
            P(("dp", "tensor"), None),
            P("dp", "tensor"),
            P("dp", "tensor"),
            P("dp", "tensor"),
            P("dp", "tensor"),
            P("dp", "tensor"),
            P("dp", "tensor"),
            P("dp", "tensor"),
            P(),
            P(),
            P(),
            P(),
            P(),
            P("dp", None),
            P("dp", None),
            P(("dp", "tensor"), None),
        ),
        out_specs=(
            P(("dp", "tensor"), None),
            P(("dp", "tensor"), None),
            P("dp", "tensor"),
            P("dp", "tensor"),
            P("dp", "tensor"),
            P("dp", "tensor"),
            P("dp", "tensor"),
            P("dp", "tensor"),
            P("dp", "tensor"),
            P(),
            P(),
            P(),
            P(),
            P(),
        ),
        check_vma=False,
    )
```

```python
import functools
import math

import jax
import jax.numpy as jnp
from jax import lax
from jax.experimental import pallas as pl
from jax.experimental.pallas import tpu as pltpu
from jax.sharding import PartitionSpec as P

D = 1024
HD = 64
BLK = 256
LOG2E = 1.4426950408889634
VMEM_LIMIT = 60 * 1024 * 1024


def dot_ab(a, b):
    return lax.dot_general(a, b, (((1,), (0,)), ((), ())), preferred_element_type=jnp.float32)


def dot_abt(a, b):
    return lax.dot_general(a, b, (((1,), (1,)), ((), ())), preferred_element_type=jnp.float32)


def split_heads(block, heads):
    lane_head = lax.broadcasted_iota(jnp.int32, block.shape, 1) // HD
    zero = jnp.zeros_like(block)
    return jnp.concatenate([jnp.where(lane_head == h, block, zero) for h in range(heads)], axis=0)


def attn_fwd_body(
    low_ref, start_ref, order_row, q_ref, k_ref, v_ref, out_ref, lse_ref, plain_ref, vt_ref, qs_ref, acc_ref, sum_ref
):
    rows, cols = q_ref.shape
    heads = cols // HD
    scale = math.sqrt(HD) * LOG2E
    for b in range(rows // BLK):
        vt_ref[:, b * BLK : (b + 1) * BLK] = v_ref[b * BLK : (b + 1) * BLK, :].T

    def one_block(i, _):
        base = pl.multiple_of(i * BLK, BLK)
        qs_ref[...] = split_heads(q_ref[pl.ds(base, BLK), :], heads)
        acc_ref[...] = jnp.zeros_like(acc_ref)
        sum_ref[...] = jnp.zeros_like(sum_ref)
        start = jnp.concatenate([start_ref[:, pl.ds(base, BLK)]] * heads, axis=1)
        own = lax.broadcasted_iota(jnp.int32, (1, heads * BLK), 1) % BLK + base

        def step(j, causal):
            at = pl.multiple_of(j * BLK, BLK)
            scores = dot_abt(k_ref[pl.ds(at, BLK), :], qs_ref[...])
            place = lax.broadcasted_iota(jnp.int32, scores.shape, 0) + at
            keep = place >= start
            if causal:
                keep = keep & (place <= own)
            probs = jnp.where(keep, jnp.exp2(scores * scale), 0.0)
            sum_ref[...] += jnp.sum(probs, axis=0, keepdims=True)
            probs_b = probs.astype(jnp.bfloat16)
            for h in range(heads):
                acc_ref[h * HD : (h + 1) * HD, :] += dot_ab(
                    vt_ref[h * HD : (h + 1) * HD, pl.ds(at, BLK)], probs_b[:, h * BLK : (h + 1) * BLK]
                )

        lax.fori_loop(low_ref[i], i, lambda j, c: (step(j, False), c)[1], 0)
        step(i, True)
        total = sum_ref[...]
        inv = 1.0 / total
        logs = jnp.log2(total)
        for h in range(heads):
            lse_ref[h : h + 1, pl.ds(base, BLK)] = logs[:, h * BLK : (h + 1) * BLK]
            acc_ref[h * HD : (h + 1) * HD, :] *= inv[:, h * BLK : (h + 1) * BLK]
        out_ref[pl.ds(base, BLK), :] = acc_ref[...].T.astype(jnp.bfloat16)
        return 0

    lax.fori_loop(0, rows // BLK, one_block, 0)
    over(rows // BLK, lambda b: to_token_order(b, order_row, out_ref, plain_ref))


def to_token_order(b, order_row, src, dst):
    at = pl.ds(pl.multiple_of(b * BLK, BLK), BLK)
    hot = lax.broadcasted_iota(jnp.int32, (BLK, src.shape[0]), 0) + b * BLK == order_row[...]
    dst[at, :] = dot_ab(hot.astype(jnp.float32).astype(jnp.bfloat16), src[...]).astype(dst.dtype)


def to_packed_order(b, order_col, src, dst):
    at = pl.ds(pl.multiple_of(b * BLK, BLK), BLK)
    hot = lax.broadcasted_iota(jnp.int32, (BLK, src.shape[0]), 1) == order_col[at, :]
    dst[at, :] = dot_ab(hot.astype(jnp.float32).astype(jnp.bfloat16), src[...]).astype(dst.dtype)


def over(count, body):
    lax.fori_loop(0, count, lambda i, carry: (body(i), carry)[1], 0)


def vmem():
    return pl.BlockSpec(memory_space=pltpu.VMEM)


def attn_fwd(low, start, order_row, q, k, v):
    rows, cols = q.shape
    heads = cols // HD
    return pl.pallas_call(
        attn_fwd_body,
        out_shape=(
            jax.ShapeDtypeStruct((rows, cols), jnp.bfloat16),
            jax.ShapeDtypeStruct((8, rows), jnp.float32),
            jax.ShapeDtypeStruct((rows, cols), jnp.bfloat16),
        ),
        in_specs=[pl.BlockSpec(memory_space=pltpu.SMEM)] + [vmem()] * 5,
        out_specs=(vmem(),) * 3,
        scratch_shapes=[
            pltpu.VMEM((cols, rows), jnp.bfloat16),
            pltpu.VMEM((heads * BLK, cols), jnp.bfloat16),
            pltpu.VMEM((cols, BLK), jnp.float32),
            pltpu.VMEM((1, heads * BLK), jnp.float32),
        ],
        compiler_params=pltpu.CompilerParams(vmem_limit_bytes=VMEM_LIMIT),
        cost_estimate=pl.CostEstimate(flops=4 * rows * rows * cols, bytes_accessed=8 * rows * cols, transcendentals=rows * rows * heads),
        name="attn_fwd",
    )(low, start, order_row, q, k, v)


def attn_bwd_body(
    low_ref, start_ref, order_row, order_col, lse_ref, q_ref, k_ref, v_ref, o_ref, grad_ref,
    plain_ref, kt_ref, qs_ref, gs_ref, dqt_ref, dk_acc, dv_acc, g_ref, packed,
):
    rows, cols = q_ref.shape
    heads = cols // HD
    root = math.sqrt(HD)
    scale = root * LOG2E
    for b in range(rows // BLK):
        kt_ref[:, b * BLK : (b + 1) * BLK] = k_ref[b * BLK : (b + 1) * BLK, :].T
    over(rows // BLK, lambda b: to_packed_order(b, order_col, grad_ref, g_ref))
    dk_acc[...] = jnp.zeros_like(dk_acc)
    dv_acc[...] = jnp.zeros_like(dv_acc)

    def one_block(i, _):
        base = pl.multiple_of(i * BLK, BLK)
        qs_ref[...] = split_heads(q_ref[pl.ds(base, BLK), :], heads)
        grads = g_ref[pl.ds(base, BLK), :]
        gs_ref[...] = split_heads(grads, heads)
        dqt_ref[...] = jnp.zeros_like(dqt_ref)
        start = jnp.concatenate([start_ref[:, pl.ds(base, BLK)]] * heads, axis=1)
        own = lax.broadcasted_iota(jnp.int32, (1, heads * BLK), 1) % BLK + base
        prod = (grads.astype(jnp.float32) * o_ref[pl.ds(base, BLK), :].astype(jnp.float32)).T
        delta = jnp.concatenate(
            [jnp.sum(prod[h * HD : (h + 1) * HD, :], axis=0, keepdims=True) for h in range(heads)], axis=1
        )
        lse = jnp.concatenate([lse_ref[h : h + 1, pl.ds(base, BLK)] for h in range(heads)], axis=1)

        def step(j, causal):
            at = pl.multiple_of(j * BLK, BLK)
            scores = dot_abt(k_ref[pl.ds(at, BLK), :], qs_ref[...])
            dprobs = dot_abt(v_ref[pl.ds(at, BLK), :], gs_ref[...])
            place = lax.broadcasted_iota(jnp.int32, scores.shape, 0) + at
            keep = place >= start
            if causal:
                keep = keep & (place <= own)
            probs = jnp.where(keep, jnp.exp2(scores * scale - lse), 0.0)
            dsc = (probs * (dprobs - delta)).astype(jnp.bfloat16)
            dv_acc[pl.ds(at, BLK), :] += dot_ab(probs.astype(jnp.bfloat16), gs_ref[...])
            dk_acc[pl.ds(at, BLK), :] += dot_ab(dsc, qs_ref[...])
            for h in range(heads):
                dqt_ref[h * HD : (h + 1) * HD, :] += dot_ab(
                    kt_ref[h * HD : (h + 1) * HD, pl.ds(at, BLK)], dsc[:, h * BLK : (h + 1) * BLK]
                )

        lax.fori_loop(low_ref[i], i, lambda j, c: (step(j, False), c)[1], 0)
        step(i, True)
        packed[pl.ds(base, BLK), 0:cols] = (dqt_ref[...].T * root).astype(packed.dtype)
        return 0

    lax.fori_loop(0, rows // BLK, one_block, 0)
    packed[:, cols : 2 * cols] = (dk_acc[...] * root).astype(packed.dtype)
    packed[:, 2 * cols : 3 * cols] = dv_acc[...].astype(packed.dtype)
    over(rows // BLK, lambda b: to_token_order(b, order_row, packed, plain_ref))


def attn_bwd(low, start, order_row, order_col, lse, q, k, v, o, g):
    rows, cols = q.shape
    heads = cols // HD
    return pl.pallas_call(
        attn_bwd_body,
        out_shape=jax.ShapeDtypeStruct((rows, 3 * cols), jnp.bfloat16),
        in_specs=[pl.BlockSpec(memory_space=pltpu.SMEM)] + [vmem()] * 9,
        out_specs=vmem(),
        scratch_shapes=[
            pltpu.VMEM((cols, rows), jnp.bfloat16),
            pltpu.VMEM((heads * BLK, cols), jnp.bfloat16),
            pltpu.VMEM((heads * BLK, cols), jnp.bfloat16),
            pltpu.VMEM((cols, BLK), jnp.float32),
            pltpu.VMEM((rows, cols), jnp.float32),
            pltpu.VMEM((rows, cols), jnp.float32),
            pltpu.VMEM((rows, cols), jnp.bfloat16),
            pltpu.VMEM((rows, 3 * cols), jnp.bfloat16),
        ],
        compiler_params=pltpu.CompilerParams(vmem_limit_bytes=VMEM_LIMIT),
        cost_estimate=pl.CostEstimate(flops=10 * rows * rows * cols, bytes_accessed=16 * rows * cols, transcendentals=rows * rows * heads),
        name="attn_bwd",
    )(low, start, order_row, order_col, lse, q, k, v, o, g)


MESH_ID = pl.DeviceIdType.MESH
EPS = 1e-06
TILE = 256
STRIP = 64
WIDE_STRIP = 192


def flip1(index):
    return index + 1 - 2 * lax.rem(index, 2)


def flip2(index):
    return index + 2 - 4 * (index // 2)


def tile_at(index, size):
    if isinstance(index, int):
        return pl.ds(index * size, size)
    return pl.ds(pl.multiple_of(index * size, size), size)


def row_sum(value):
    return jnp.sum(value, axis=-1, keepdims=True)


def middle_body(
    count, att_ref, wo_hbm, w_hbm, down_hbm, tok_hbm, cot_hbm, aa_ref, am_ref, su_all, sg_all,
    out_ref, datt_ref, gw_hbm, down_ref, gwo_hbm, dh1_ref, gaa_ref, gam_ref, gsu_ref, gsg_ref,
    wo, wall, tok, cot, parts, mids, dbms, mid_t, dbm_t, ups, gates, mixed,
    middle, branch, dh2, own_part, send_a, recv_a, send_d, recv_d, send_z, recv_z,
    gw, gwo, dparts, su_ref, sg_ref, got_down, gather_send, gather_recv, scatter_send, scatter_recv, load_sems, store_sems, hop_send, hop_recv, a2a_send, a2a_recv, d2a_send, d2a_recv, part_send, part_recv,
):
    d = lax.axis_index("dp")
    t = lax.axis_index("tensor")
    rows, width = tok.shape
    heads_w = att_ref.shape[1]
    hid = wall.shape[2]
    nq = w_hbm.shape[0]
    qrows = w_hbm.shape[2]
    chunks = hop_send.shape[0] // 6
    crow = rows // chunks
    core_peer = (flip1(d), t)
    z_peer = (d, flip1(t))
    line = [t, flip1(t), flip2(t), 3 - t]

    barrier = pltpu.get_barrier_semaphore()
    half, chip, core = count // 2, d // 2, lax.rem(d, 2)

    def chip_peer(i):
        return lax.rem(chip + 1 + i, half)

    for peer in [core_peer] + [(d, line[k]) for k in (1, 2, 3)]:
        pl.semaphore_signal(barrier, inc=1, device_id=peer, device_id_type=MESH_ID)
    over(
        half - 1,
        lambda i: pl.semaphore_signal(barrier, inc=1, device_id=(2 * chip_peer(i) + core, t), device_id_type=MESH_ID),
    )
    pl.semaphore_wait(barrier, half + 3)

    def remote(src, dst, ssem, rsem, peer):
        return pltpu.make_async_remote_copy(
            src_ref=src, dst_ref=dst, send_sem=ssem, recv_sem=rsem, device_id=peer, device_id_type=MESH_ID
        )

    a2a = [
        remote(att_ref.at[tile_at(line[k], rows), :], parts.at[k - 1], a2a_send.at[k - 1], a2a_recv.at[k - 1], (d, line[k]))
        for k in (1, 2, 3)
    ]
    for copy in a2a:
        copy.start()

    chip_rows = tile_at(chip, qrows)

    def gather(i):
        return remote(
            down_hbm, wall.at[2, chip_rows, :], gather_send.at[i], gather_recv.at[i], (2 * chip_peer(i) + core, t)
        )

    def scatter(i):
        return remote(
            gw.at[2, tile_at(chip_peer(i), qrows), :], got_down.at[chip], scatter_send.at[i], scatter_recv.at[i],
            (2 * chip_peer(i) + core, t),
        )

    over(half - 1, lambda i: gather(i).start())
    keep_down = pltpu.make_async_copy(down_hbm, wall.at[2, chip_rows, :], load_sems.at[3 + 2 * nq])
    keep_down.start()
    loads = [
        pltpu.make_async_copy(wo_hbm, wo, load_sems.at[0]),
        pltpu.make_async_copy(tok_hbm, tok, load_sems.at[1]),
        pltpu.make_async_copy(cot_hbm, cot, load_sems.at[2]),
    ]
    wloads = [
        [
            pltpu.make_async_copy(w_hbm.at[q, m], wall.at[m, pl.ds(q * qrows, qrows), :], load_sems.at[3 + m * nq + q])
            for q in range(nq)
        ]
        for m in range(2)
    ]
    for copy in loads + wloads[0] + wloads[1]:
        copy.start()

    shard = lax.rem(t, 2) + 2 * lax.rem(d, 2)
    su_ref[...] = su_all[:, tile_at(shard, hid)]
    sg_ref[...] = sg_all[:, tile_at(shard, hid)] * math.sqrt(D)
    gsu_ref[...] = jnp.zeros_like(gsu_ref)
    gsg_ref[...] = jnp.zeros_like(gsg_ref)
    gam_ref[...] = jnp.zeros_like(gam_ref)
    gaa_ref[...] = jnp.zeros_like(gaa_ref)

    loads[0].wait()
    for copy in a2a:
        copy.wait_recv()

    def project(n):
        cols = tile_at(n, TILE)
        total = dot_abt(att_ref[tile_at(t, rows), :], wo[cols, tile_at(t, heads_w)])
        for k in (1, 2, 3):
            total += dot_abt(parts[k - 1], wo[cols, tile_at(line[k], heads_w)])
        branch[:, cols] = total

    over(width // TILE, project)
    loads[1].wait()

    def hop(buf, phase, ch, kind):
        part = tile_at(ch, crow)
        index = (phase * chunks + ch) * 3 + kind
        src, dst, peer = ((0, 2, z_peer), (0, 1, core_peer), (2, 3, core_peer))[kind]
        return remote(buf.at[src, part, :], buf.at[dst, part, :], hop_send.at[index], hop_recv.at[index], peer)

    def strips(ch, body):
        over(crow // STRIP, lambda i: body(tile_at(i + ch * (crow // STRIP), STRIP)))

    def unit_of(value):
        factor = lax.rsqrt(row_sum(value * value) + EPS)
        return value * factor, factor

    def make_middle(at):
        inputs = tok[at, :].astype(jnp.float32)
        norm_a, factor_a = unit_of(branch[at, :])
        mid, factor_mid = unit_of(inputs + aa_ref[...] * (norm_a - inputs))
        return inputs, norm_a, factor_a, mid, factor_mid

    def first(at):
        mid = make_middle(at)[3]
        middle[at, :] = mid
        mids[0, at, :] = mid.astype(jnp.bfloat16)

    for ch in range(chunks):
        strips(ch, first)
        hop(mids, 0, ch, 0).start()
        hop(mids, 0, ch, 1).start()

    for m in range(2):
        for copy in wloads[m]:
            copy.wait()

    def down_arrived():
        keep_down.wait()
        over(half - 1, lambda i: gather(i).wait_recv())

    def within(slot, at):
        return pl.ds(pl.multiple_of(slot * rows + at.start, STRIP), at.size)

    def forward_rows(slot, at):
        where = within(slot, at)

        def hidden(n):
            cols = tile_at(n, TILE)
            x = mids[slot, at, :]
            up = dot_ab(x, wall[0, :, cols])
            gate_raw = dot_ab(x, wall[1, :, cols])
            gate = gate_raw * sg_ref[:, cols]
            silu = gate / (1.0 + jnp.exp(-gate))
            ups[where, cols] = up.astype(jnp.bfloat16)
            gates[where, cols] = gate_raw.astype(jnp.bfloat16)
            mixed[where, cols] = (up * su_ref[:, cols] * silu).astype(jnp.bfloat16)

        def down(cols):
            return dot_abt(mixed[where, :], wall[2, cols, :])

        return hidden, down

    def backward_rows(slot, at):
        where = within(slot, at)

        def hidden(n):
            cols = tile_at(n, TILE)
            dmix = dot_ab(dbms[slot, at, :], wall[2, :, cols])
            up_raw = ups[where, cols].astype(jnp.float32)
            gate_raw = gates[where, cols].astype(jnp.float32)
            gate = gate_raw * sg_ref[:, cols]
            sig = 1.0 / (1.0 + jnp.exp(-gate))
            d_up = dmix * (gate * sig)
            d_gate = dmix * (up_raw * su_ref[:, cols]) * (sig * (1.0 + gate * (1.0 - sig)))
            gsu_ref[:, cols] += jnp.sum(d_up * up_raw, axis=0, keepdims=True)
            gsg_ref[:, cols] += jnp.sum(d_gate * gate_raw, axis=0, keepdims=True)
            ups[where, cols] = (d_up * su_ref[:, cols]).astype(jnp.bfloat16)
            gates[where, cols] = (d_gate * sg_ref[:, cols]).astype(jnp.bfloat16)

        def down(cols):
            return dot_abt(ups[where, :], wall[0, cols, :]) + dot_abt(gates[where, :], wall[1, cols, :])

        return hidden, down

    def part_copy(phase, kind, ch):
        part = tile_at(ch, crow)
        index = (phase * 3 + kind) * chunks + ch
        src, dst, peer = ((send_a, recv_a, core_peer), (send_d, recv_d, core_peer), (send_z, recv_z, z_peer))[kind]
        return remote(src.at[part, :], dst.at[part, :], part_send.at[index], part_recv.at[index], peer)

    def tensor_pass(phase, buf, rows_fn, fillers):
        def keep_own(at, cols, value):
            own_part[at, cols] = value

        def to(ref):
            def store(at, cols, value):
                ref[at, cols] = value.astype(jnp.bfloat16)

            return store

        def to_z(at, cols, value):
            send_z[at, cols] = (value + recv_d[at, cols].astype(jnp.float32)).astype(jnp.bfloat16)

        tiles = hid // TILE
        all_rows = tile_at(0, rows)

        def span(low, high, body):
            over(high - low, lambda n: body(n + low))

        def store_all(at, down, store):
            def one(n):
                cols = tile_at(n, TILE)
                store(at, cols, down(cols))

            over(width // TILE, one)

        hidden, down = rows_fn(0, all_rows)
        over(tiles, hidden)
        if phase == 0:
            down_arrived()
        store_all(all_rows, down, keep_own)
        for ch in range(chunks):
            hop(buf, phase, ch, 1).wait_recv()
        if phase == 1:
            for ch in range(chunks):
                part_copy(0, 0, ch).wait_send()
        hidden, down = rows_fn(1, all_rows)
        over(tiles, hidden)
        store_all(all_rows, down, to(send_a))
        for ch in range(chunks):
            part_copy(phase, 0, ch).start()
        fillers[0]()

        def chunk(ch):
            at = tile_at(ch, crow)
            hop(buf, phase, ch, 0).wait_recv()
            hop(buf, phase, ch, 2).start()
            hidden_z, down_z = rows_fn(2, at)
            hidden_d, down_d = rows_fn(3, at)
            span(0, tiles // 2, hidden_z)
            hop(buf, phase, ch, 2).wait_recv()
            if phase == 1:
                part_copy(0, 1, ch).wait_send()
            over(tiles, hidden_d)
            store_all(at, down_d, to(send_d))
            part_copy(phase, 1, ch).start()
            span(tiles // 2, tiles, hidden_z)
            part_copy(phase, 1, ch).wait_recv()
            if phase == 1:
                part_copy(0, 2, ch).wait_send()
            store_all(at, down_z, to_z)
            part_copy(phase, 2, ch).start()

        over(chunks, chunk)
        fillers[1]()

    def transpose_into(dst, buf, slots):
        per_slot = rows // 128

        def one(i):
            slot = slots[0] + i // per_slot
            at = tile_at(lax.rem(i, per_slot), 128)
            to = tile_at(slots[0] * per_slot + i, 128)
            for n in range(width // TILE):
                dst[n * TILE : (n + 1) * TILE, to] = buf[slot, at, n * TILE : (n + 1) * TILE].T

        over(len(slots) * per_slot, one)

    tensor_pass(
        0, mids, forward_rows,
        [lambda: transpose_into(mid_t, mids, (0, 1)), lambda: transpose_into(mid_t, mids, (2, 3))],
    )

    loads[2].wait()

    def turn(at):
        mid = middle[at, :]
        branch_m = own_part[at, :] + recv_a[at, :].astype(jnp.float32) + recv_z[at, :].astype(jnp.float32)
        norm_m, factor_m = unit_of(branch_m)
        alpha = am_ref[...]
        y, factor_y = unit_of(mid + alpha * (norm_m - mid))
        out_ref[at, :] = y.astype(jnp.bfloat16)
        dy = cot[at, :].astype(jnp.float32)
        grad = factor_y * (dy - y * row_sum(y * dy))
        gam_ref[...] += jnp.sum(grad * (norm_m - mid), axis=0, keepdims=True)
        back = alpha * grad
        dbms[0, at, :] = (factor_m * (back - norm_m * row_sum(norm_m * back))).astype(jnp.bfloat16)
        dh2[at, :] = grad - back

    for ch in range(chunks):
        part_copy(0, 0, ch).wait_recv()
        part_copy(0, 2, ch).wait_recv()
        strips(ch, turn)
        hop(dbms, 1, ch, 0).start()
        hop(dbms, 1, ch, 1).start()

    def grad_store(m, q):
        return pltpu.make_async_copy(gw.at[m, pl.ds(q * qrows, qrows), :], gw_hbm.at[q, m], store_sems.at[m * nq + q])

    def weight_grad(m):
        lhs, rhs = ((mid_t, ups), (mid_t, gates), (dbm_t, mixed))[m]

        def block(i):
            q = i // (hid // TILE)
            cols = tile_at(lax.rem(i, hid // TILE), TILE)
            value = dot_ab(lhs[tile_at(q, TILE), :], rhs[:, cols])
            gw[m, tile_at(q, TILE), cols] = value.astype(jnp.bfloat16)

        over((width // TILE) * (hid // TILE), block)

    def down_grad():
        transpose_into(dbm_t, dbms, (2, 3))
        weight_grad(2)
        over(half - 1, lambda i: scatter(i).start())
        got_down[chip] = gw[2, chip_rows, :]

    tensor_pass(1, dbms, backward_rows, [lambda: transpose_into(dbm_t, dbms, (0, 1)), down_grad])

    def last(at):
        inputs, norm_a, factor_a, mid, factor_mid = make_middle(at)
        grad_mid = dh2[at, :] + own_part[at, :] + recv_a[at, :].astype(jnp.float32) + recv_z[at, :].astype(jnp.float32)
        grad = factor_mid * (grad_mid - mid * row_sum(mid * grad_mid))
        gaa_ref[...] += jnp.sum(grad * (norm_a - inputs), axis=0, keepdims=True)
        back = aa_ref[...] * grad
        dh1_ref[at, :] = grad - back
        mids[0, at, :] = (factor_a * (back - norm_a * row_sum(norm_a * back))).astype(jnp.bfloat16)

    for ch in range(chunks):
        hop(mids, 0, ch, 0).wait_send()
        hop(mids, 0, ch, 1).wait_send()
        part_copy(1, 0, ch).wait_recv()
        part_copy(1, 2, ch).wait_recv()
        strips(ch, last)

    dback = [
        remote(dparts.at[k], datt_ref.at[tile_at(t, rows), :], d2a_send.at[k - 1], d2a_recv.at[k - 1], (d, line[k]))
        for k in (1, 2, 3)
    ]
    for k in (3, 2, 1, 0):
        value = dot_ab(mids[0], wo[:, tile_at(line[k], heads_w)]).astype(jnp.bfloat16)
        if k:
            dparts[k] = value
            dback[k - 1].start()
        else:
            datt_ref[tile_at(t, rows), :] = value

    for m in range(2):
        weight_grad(m)
        for q in range(nq):
            grad_store(m, q).start()
    transpose_into(dbm_t, mids, (0,))

    def out_grad(n):
        at = tile_at(n, TILE)
        lhs = dbm_t[at, 0:rows]
        gwo[at, tile_at(t, heads_w)] = dot_ab(lhs, att_ref[tile_at(t, rows), :]).astype(jnp.bfloat16)
        for k in (1, 2, 3):
            gwo[at, tile_at(line[k], heads_w)] = dot_ab(lhs, parts[k - 1]).astype(jnp.bfloat16)

    over(width // TILE, out_grad)
    wo_store = pltpu.make_async_copy(gwo, gwo_hbm, store_sems.at[2 * nq])
    wo_store.start()

    over(half - 1, lambda i: scatter(i).wait_recv())

    def down_sum(i):
        at = tile_at(i, qrows // 2)
        total = got_down[0, at, :].astype(jnp.float32)
        total = lax.fori_loop(1, half, lambda e, value: value + got_down[e, at, :].astype(jnp.float32), total)
        down_ref[at, :] = total.astype(jnp.bfloat16)

    over(2, down_sum)
    over(half - 1, lambda i: gather(i).wait_send())
    over(half - 1, lambda i: scatter(i).wait_send())

    for k in (1, 2, 3):
        remote(
            dparts.at[k], datt_ref.at[tile_at(line[k], rows), :], d2a_send.at[k - 1], d2a_recv.at[k - 1], (d, line[k])
        ).wait()
    for copy in a2a:
        copy.wait_send()
    for ch in range(chunks):
        hop(mids, 0, ch, 2).wait_send()
        for kind in range(3):
            hop(dbms, 1, ch, kind).wait_send()
            part_copy(1, kind, ch).wait_send()
    for m in range(2):
        for q in range(nq):
            grad_store(m, q).wait()
    wo_store.wait()


def middle_call(count, chunks, attended, wo, w_parts, down, tokens, cotangent, alpha_a, alpha_m, su, sg):
    rows, width = tokens.shape
    group, heads_w = attended.shape
    nq, _, qrows, hid = w_parts.shape
    bf, f32 = jnp.bfloat16, jnp.float32
    anywhere = pl.BlockSpec(memory_space=pl.ANY)
    dma = pltpu.SemaphoreType.DMA
    return pl.pallas_call(
        functools.partial(middle_body, count),
        out_shape=(
            jax.ShapeDtypeStruct((rows, width), bf),
            jax.ShapeDtypeStruct((group, heads_w), bf),
            jax.ShapeDtypeStruct((nq, 2, qrows, hid), bf),
            jax.ShapeDtypeStruct((qrows, hid), bf),
            jax.ShapeDtypeStruct((width, width), bf),
            jax.ShapeDtypeStruct((rows, width), f32),
            jax.ShapeDtypeStruct((1, width), f32),
            jax.ShapeDtypeStruct((1, width), f32),
            jax.ShapeDtypeStruct((1, hid), f32),
            jax.ShapeDtypeStruct((1, hid), f32),
        ),
        in_specs=[vmem()] + [anywhere] * 5 + [vmem()] * 4,
        out_specs=(vmem(), vmem(), anywhere, vmem(), anywhere) + (vmem(),) * 5,
        scratch_shapes=[
            pltpu.VMEM((width, width), bf),
            pltpu.VMEM((3, width, hid), bf),
            pltpu.VMEM((rows, width), bf),
            pltpu.VMEM((rows, width), bf),
            pltpu.VMEM((3, rows, heads_w), bf),
            pltpu.VMEM((4, rows, width), bf),
            pltpu.VMEM((4, rows, width), bf),
            pltpu.VMEM((width, 4 * rows), bf),
            pltpu.VMEM((width, 4 * rows), bf),
            pltpu.VMEM((4 * rows, hid), bf),
            pltpu.VMEM((4 * rows, hid), bf),
            pltpu.VMEM((4 * rows, hid), bf),
            pltpu.VMEM((rows, width), f32),
            pltpu.VMEM((rows, width), f32),
            pltpu.VMEM((rows, width), f32),
            pltpu.VMEM((rows, width), f32),
        ]
        + [pltpu.VMEM((rows, width), bf)] * 6
        + [
            pltpu.VMEM((3, width, hid), bf),
            pltpu.VMEM((width, width), bf),
            pltpu.VMEM((4, rows, heads_w), bf),
            pltpu.VMEM((1, hid), f32),
            pltpu.VMEM((1, hid), f32),
            pltpu.VMEM((count // 2, qrows, hid), bf),
            dma((count // 2 - 1,)), dma((count // 2 - 1,)), dma((count // 2 - 1,)), dma((count // 2 - 1,)),
            dma((4 + 2 * nq,)),
            dma((2 * nq + 1,)),
            dma((6 * chunks,)),
            dma((6 * chunks,)),
            dma((3,)),
            dma((3,)),
            dma((3,)),
            dma((3,)),
            dma((6 * chunks,)),
            dma((6 * chunks,)),
        ],
        compiler_params=pltpu.CompilerParams(vmem_limit_bytes=67000000, collective_id=1, has_side_effects=True),
        cost_estimate=pl.CostEstimate(flops=10**11, bytes_accessed=10**8, transcendentals=10**6),
        name="middle",
    )(attended, wo, w_parts, down, tokens, cotangent, alpha_a, alpha_m, su, sg)


def remote_copy(src, dst, send_sem, recv_sem, peer):
    return pltpu.make_async_remote_copy(
        src_ref=src, dst_ref=dst, send_sem=send_sem, recv_sem=recv_sem, device_id=peer, device_id_type=MESH_ID
    )


def greet(peers):
    barrier = pltpu.get_barrier_semaphore()
    for peer in peers:
        pl.semaphore_signal(barrier, inc=1, device_id=peer, device_id_type=MESH_ID)
    pl.semaphore_wait(barrier, len(peers))


def rope_tables(order_ref, length_ref, cos_out, sin_out, col_out, start_out):
    group = order_ref.shape[1]
    lanes = cos_out.shape[1]
    places = lax.broadcasted_iota(jnp.int32, (1, group), 1)
    first = jnp.zeros((1, group), jnp.int32)
    begin = jnp.int32(0)
    for s in range(1, length_ref.shape[1]):
        begin = begin + length_ref[0, s - 1]
        first = jnp.where(places >= begin, begin, first)
    start_out[...] = first
    depth = (places - first).astype(jnp.float32)
    order = order_ref[...]
    order_f = order.astype(jnp.float32)
    lane = lax.broadcasted_iota(jnp.int32, (1, lanes), 1)
    half_width = HD // 2
    freq = jnp.exp((lane % half_width).astype(jnp.float32) * (-math.log(10000.0) / half_width))
    sign = jnp.where(lane % HD < half_width, -1.0, 1.0)

    def block(b):
        at = tile_at(b, 128)
        own = lax.broadcasted_iota(jnp.int32, (128, group), 0) + b * 128
        col_out[at, :] = row_sum(jnp.where(own == places, order_f, 0.0)).astype(jnp.int32)
        angles = row_sum(jnp.where(own == order, depth, 0.0)) * freq
        cos_out[at, :] = jnp.cos(angles)
        sin_out[at, :] = jnp.sin(angles) * sign

    over(group // 128, block)


def spread_body(
    count, tok, w_up, w_gate, wq, wk, wv, wo, order_ref, length_ref,
    pair, tok2, wqkv, wo_all, cos_out, sin_out, col_out, start_out,
    own_mlp, own_att, wo_rows, load_sem, keep_sem, a_send, a_recv, b_send, b_recv, tok_send, tok_recv,
    qkv_send, qkv_recv, relay_send, relay_recv, oz_send, oz_recv, oq_send, oq_recv, oc_send, oc_recv,
):
    d = lax.axis_index("dp")
    t = lax.axis_index("tensor")
    core = lax.rem(d, 2)
    home = core == t // 2
    far = (d - core + t // 2, flip2(t))
    wrows, wcols = wq.shape
    half = count // 2
    mlp = (w_up, w_gate)
    att = (wq, wk, wv)
    mine = tile_at(d, wrows)
    side = tile_at(core, wrows)
    other_side = tile_at(1 - core, wrows)

    barrier = pltpu.get_barrier_semaphore()

    def dp_peer(i):
        return lax.rem(d + 1 + i, count)

    def hello(i):
        pl.semaphore_signal(barrier, inc=1, device_id=(dp_peer(i), t), device_id_type=MESH_ID)

    over(count - 1, hello)
    for k in (1, 2, 3):
        pl.semaphore_signal(barrier, inc=1, device_id=(d, lax.rem(t + k, 4)), device_id_type=MESH_ID)
    pl.semaphore_signal(barrier, inc=1, device_id=(flip1(d), flip2(t)), device_id_type=MESH_ID)
    pl.semaphore_wait(barrier, count + 3)

    def pair_at(m, rows):
        return pair.at[m, rows, :]

    def b_copy(m):
        return remote_copy(mlp[m], pair_at(m, side), b_send.at[m], b_recv.at[core * 3 + m], far)

    def a_copy(m):
        return remote_copy(mlp[m], pair_at(m, side), a_send.at[m], a_recv.at[m], (flip1(d), t))

    tok_copy = remote_copy(tok, tok2, tok_send, tok_recv, (d, flip1(t)))
    def oz_copy(k):
        return remote_copy(wo, wo_rows.at[:, tile_at(t, wcols)], oz_send.at[k - 1], oz_recv.at[k - 1], (d, lax.rem(t + k, 4)))

    for k in (1, 2, 3):
        oz_copy(k).start()
    tok_copy.start()
    for m in range(2):
        b_copy(m).start()
    load_o = pltpu.make_async_copy(wo, wo_rows.at[:, tile_at(t, wcols)], load_sem.at[0])
    load_o.start()

    def qkv_to(i, m, peer):
        return remote_copy(
            att[m], wqkv.at[mine, pl.ds(m * wcols, wcols)], qkv_send.at[i, m], qkv_recv.at[i, m], (peer, t)
        )

    def qkv_copy(j, m):
        return qkv_to(j, m, lax.rem(d + 2 + 2 * j, count))

    def qkv_own(m):
        return qkv_to(half - 1, m, flip1(d))

    def qkv_relay(j):
        rows = tile_at(lax.rem(d + count - 2 - 2 * j, count), wrows)
        return remote_copy(wqkv.at[rows, :], wqkv.at[rows, :], relay_send.at[j], relay_recv.at[j], (flip1(d), t))

    def qkv_start(j):
        for m in range(3):
            qkv_copy(j, m).start()

    over(half - 1, qkv_start)
    for m in range(3):
        qkv_own(m).start()

    @pl.when(jnp.logical_not(home))
    def _():
        for m in range(2):
            a_copy(m).start()

    loads = [pltpu.make_async_copy(mlp[m], own_mlp.at[m], load_sem.at[1 + m]) for m in range(2)]
    loads += [pltpu.make_async_copy(att[m], own_att.at[m], load_sem.at[4 + m]) for m in range(3)]
    for copy in loads:
        copy.start()
    for copy in loads:
        copy.wait()
    keeps = [
        pltpu.make_async_copy(own_att.at[m], wqkv.at[mine, pl.ds(m * wcols, wcols)], keep_sem.at[m]) for m in range(3)
    ]
    for copy in keeps:
        copy.start()
    pair_keeps = [pltpu.make_async_copy(own_mlp.at[m], pair_at(m, side), keep_sem.at[3 + m]) for m in range(2)]

    @pl.when(home)
    def _():
        for copy in pair_keeps:
            copy.start()

    load_o.wait()
    for k in (1, 2, 3):
        oz_copy(k).wait_recv()
    keep_o = pltpu.make_async_copy(wo_rows, wo_all.at[mine, :], keep_sem.at[6])
    keep_o.start()

    def oq_copy(j):
        return remote_copy(wo_rows, wo_all.at[mine, :], oq_send.at[j], oq_recv.at[j], (lax.rem(d + 2 + 2 * j, count), t))

    def oc_own():
        return remote_copy(wo_rows, wo_all.at[mine, :], oc_send.at[half - 1], oc_recv.at[half - 1], (flip1(d), t))

    def oc_copy(j):
        rows = tile_at(lax.rem(d + count - 2 - 2 * j, count), wrows)
        return remote_copy(wo_all.at[rows, :], wo_all.at[rows, :], oc_send.at[j], oc_recv.at[j], (flip1(d), t))

    over(half - 1, lambda j: oq_copy(j).start())
    oc_own().start()
    rope_tables(order_ref, length_ref, cos_out, sin_out, col_out, start_out)

    def qkv_next(j):
        for m in range(3):
            qkv_copy(j, m).wait_recv()
        qkv_relay(j).start()

    over(half - 1, qkv_next)

    def oq_next(j):
        oq_copy(j).wait_recv()
        oc_copy(j).start()

    over(half - 1, oq_next)

    def qkv_wait(j):
        for m in range(3):
            qkv_copy(j, m).wait_send()
        qkv_relay(j).wait()

    over(half - 1, qkv_wait)
    for m in range(3):
        qkv_own(m).wait()
    over(half - 1, lambda j: oq_copy(j).wait_send())
    over(half - 1, lambda j: oc_copy(j).wait())
    oc_own().wait()
    for k in (1, 2, 3):
        oz_copy(k).wait_send()
    keep_o.wait()
    for copy in keeps:
        copy.wait()
    tok_copy.wait()
    for m in range(2):
        b_copy(m).wait_send()

    @pl.when(home)
    def _():
        for m in range(2):
            pair_keeps[m].wait()
            remote_copy(mlp[m], pair_at(m, other_side), a_send.at[m], a_recv.at[m], (flip1(d), t)).wait_recv()

    @pl.when(jnp.logical_not(home))
    def _():
        for m in range(2):
            a_copy(m).wait_send()
            for c in range(2):
                remote_copy(
                    mlp[m], pair_at(m, pl.ds(c * wrows, wrows)), b_send.at[m], b_recv.at[c * 3 + m], far
                ).wait_recv()


def spread_call(count, tokens, w_up, w_gate, wq, wk, wv, wo, order, lengths):
    rows, width = tokens.shape
    group = order.shape[1]
    wrows, wcols = wq.shape
    hid = w_up.shape[1]
    bf = jnp.bfloat16
    anywhere = pl.BlockSpec(memory_space=pl.ANY)
    dma = pltpu.SemaphoreType.DMA
    return pl.pallas_call(
        functools.partial(spread_body, count),
        out_shape=(
            jax.ShapeDtypeStruct((2, 2 * wrows, hid), bf),
            jax.ShapeDtypeStruct((rows, width), bf),
            jax.ShapeDtypeStruct((width, 3 * wcols), bf),
            jax.ShapeDtypeStruct((width, width), bf),
            jax.ShapeDtypeStruct((group, 2 * HD), jnp.float32),
            jax.ShapeDtypeStruct((group, 2 * HD), jnp.float32),
            jax.ShapeDtypeStruct((group, 1), jnp.int32),
            jax.ShapeDtypeStruct((1, group), jnp.int32),
        ),
        in_specs=[anywhere] * 7 + [vmem(), pl.BlockSpec(memory_space=pltpu.SMEM)],
        out_specs=(anywhere,) * 4 + (vmem(),) * 4,
        scratch_shapes=[
            pltpu.VMEM((2, wrows, hid), bf),
            pltpu.VMEM((3, wrows, wcols), bf),
            pltpu.VMEM((wrows, width), bf),
            dma((7,)), dma((7,)), dma((3,)), dma((3,)), dma((3,)), dma((6,)), dma, dma,
            dma((count // 2, 3)), dma((count // 2, 3)), dma((count // 2 - 1,)), dma((count // 2 - 1,)), dma((3,)), dma((3,)),
            dma((count // 2,)), dma((count // 2,)), dma((count // 2,)), dma((count // 2,)),
        ],
        compiler_params=pltpu.CompilerParams(vmem_limit_bytes=VMEM_LIMIT, collective_id=2, has_side_effects=True),
        name="spread",
    )(tokens, w_up, w_gate, wq, wk, wv, wo, order, lengths)


def head_sums(value):
    width = value.shape[1]
    same = (
        lax.broadcasted_iota(jnp.int32, (width, width), 0) // HD == lax.broadcasted_iota(jnp.int32, (width, width), 1) // HD
    )
    ones = jnp.where(same, 1.0, 0.0).astype(jnp.bfloat16)
    high = value.astype(jnp.bfloat16)
    low = (value - high.astype(jnp.float32)).astype(jnp.bfloat16)
    return dot_ab(high, ones) + dot_ab(low, ones)


def swap_halves(value):
    width = value.shape[1]
    lane = lax.broadcasted_iota(jnp.int32, value.shape, 1) % HD
    return jnp.where(lane < HD // 2, pltpu.roll(value, width - HD // 2, 1), pltpu.roll(value, HD // 2, 1))


def project_body(
    tok, tok2, w_down, wqkv, cos_ref, sin_ref, order_col, gain_ref, q_ref, k_ref, v_ref, raw_ref, x_hbm, pair_down,
    xs, plain, own_down, load_sem, keep_sem, mid_send, recv, on_send, down_load, down_keep, a_send, a_recv, b_send, b_recv,
):
    t = lax.axis_index("tensor")
    d = lax.axis_index("dp")
    _, rows, width = xs.shape
    group, cols = q_ref.shape
    near = flip1(t)
    across = 3 - t
    inner = (t + 1) // 2 == 1
    arrive = (2 - t // 2, 3 - 3 * (t // 2))
    pieces = mid_send.shape[0] // 2
    part = rows // pieces
    greet([(d, near), (d, across), (d, flip2(t)), (flip1(d), t), (flip1(d), flip2(t))])

    core = lax.rem(d, 2)
    home = core == t // 2
    wrows = own_down.shape[0]

    def down_at(c):
        return pair_down.at[tile_at(c, wrows), :]

    b_copy = remote_copy(w_down, down_at(core), b_send, b_recv.at[core], (d - core + t // 2, flip2(t)))
    a_copy = remote_copy(w_down, down_at(core), a_send, a_recv, (flip1(d), t))
    load_down = pltpu.make_async_copy(w_down, own_down, down_load)
    keep_down = pltpu.make_async_copy(own_down, down_at(core), down_keep)

    def mid_copy(k):
        rows_of = pl.ds((k % pieces) * part, part)
        src = (tok, tok2)[k // pieces].at[rows_of, :]
        return remote_copy(src, xs.at[(t, near)[k // pieces], rows_of, :], mid_send.at[k], recv.at[k], (d, across))

    def on_copy(k):
        ref = xs.at[arrive[k // pieces], pl.ds((k % pieces) * part, part), :]
        return remote_copy(ref, ref, on_send.at[k], recv.at[k], (d, near))

    @pl.when(inner)
    def _():
        for k in range(2 * pieces):
            mid_copy(k).start()
        b_copy.start()

    load_down.start()

    @pl.when(jnp.logical_not(home))
    def _():
        a_copy.start()

    loads = [
        pltpu.make_async_copy(tok, xs.at[t], load_sem.at[0]),
        pltpu.make_async_copy(tok2, xs.at[near], load_sem.at[1]),
    ]
    for copy in loads:
        copy.start()

    def keep(index, slot):
        return pltpu.make_async_copy(xs.at[slot], x_hbm.at[tile_at(slot, rows), :], keep_sem.at[index])

    def strip(slot, i):
        at = tile_at(slot * (rows // WIDE_STRIP) + i, WIDE_STRIP)
        x = xs[slot, tile_at(i, WIDE_STRIP), :]
        cos = jnp.concatenate([cos_ref[at, :]] * (cols // cos_ref.shape[1]), axis=1)
        sin = jnp.concatenate([sin_ref[at, :]] * (cols // sin_ref.shape[1]), axis=1)
        for m in range(2):
            raw = dot_ab(x, wqkv[:, m * cols : (m + 1) * cols])
            raw_ref[at, m * cols : (m + 1) * cols] = raw.astype(jnp.bfloat16)
            normed = raw * lax.rsqrt(head_sums(raw * raw) + EPS) * gain_ref[:, tile_at(t, cols)]
            plain[at, m * cols : (m + 1) * cols] = (normed * cos + swap_halves(normed) * sin).astype(jnp.bfloat16)
        plain[at, 2 * cols : 3 * cols] = dot_ab(x, wqkv[:, 2 * cols : 3 * cols]).astype(jnp.bfloat16)

    def permute(index, size, first):
        base = tile_at(index, size)

        def one(b):
            at = tile_at(b, BLK)
            token = lax.broadcasted_iota(jnp.int32, (BLK, size), 1) + index * size
            hot = (token == order_col[at, :]).astype(jnp.float32)
            value = dot_ab(hot.astype(jnp.bfloat16), plain[base, :])
            for m, ref in enumerate((q_ref, k_ref, v_ref)):
                piece = value[:, m * cols : (m + 1) * cols]
                if not first:
                    piece += ref[at, :].astype(jnp.float32)
                ref[at, :] = piece.astype(jnp.bfloat16)

        over(group // BLK, one)

    loads[0].wait()
    keep(0, t).start()
    over(rows // WIDE_STRIP, lambda i: strip(t, i))
    loads[1].wait()
    keep(1, near).start()
    over(rows // WIDE_STRIP, lambda i: strip(near, i))
    permute(t // 2, 2 * rows, True)
    load_down.wait()

    @pl.when(home)
    def _():
        keep_down.start()

    per_strip = WIDE_STRIP // part
    for k in range(2 * pieces):
        slot = arrive[k // pieces]
        ref = xs.at[slot, pl.ds((k % pieces) * part, part), :]
        remote_copy(ref, ref, on_send.at[k], recv.at[k], (d, near)).wait_recv()

        @pl.when(inner)
        def _():
            on_copy(k).start()

        if k == 2 * pieces - 5:

            @pl.when(jnp.logical_not(inner))
            def _():
                b_copy.start()

        if k % per_strip == per_strip - 1:
            strip(slot, (k % pieces) // per_strip)
        if k % pieces == pieces - 1:
            keep(2 + k // pieces, slot).start()
            permute(slot, rows, False)

    for index, slot in enumerate((t, near, *arrive)):
        keep(index, slot).wait()

    @pl.when(inner)
    def _():
        for k in range(2 * pieces):
            mid_copy(k).wait_send()
            on_copy(k).wait_send()

    b_copy.wait_send()

    @pl.when(home)
    def _():
        keep_down.wait()
        remote_copy(w_down, down_at(1 - core), a_send, a_recv, (flip1(d), t)).wait_recv()

    @pl.when(jnp.logical_not(home))
    def _():
        a_copy.wait_send()
        for c in range(2):
            remote_copy(w_down, down_at(c), b_send, b_recv.at[c], (d - core + t // 2, flip2(t))).wait_recv()


def project_call(tokens, tok2, w_down, wqkv, cos, sin, order_col, gains):
    rows, width = tokens.shape
    group = order_col.shape[0]
    cols = wqkv.shape[1] // 3
    wrows, hid = w_down.shape
    bf = jnp.bfloat16
    anywhere = pl.BlockSpec(memory_space=pl.ANY)
    dma = pltpu.SemaphoreType.DMA
    return pl.pallas_call(
        project_body,
        out_shape=(jax.ShapeDtypeStruct((group, cols), bf),) * 3
        + (
            jax.ShapeDtypeStruct((group, 2 * cols), bf),
            jax.ShapeDtypeStruct((group, width), bf),
            jax.ShapeDtypeStruct((2 * wrows, hid), bf),
        ),
        in_specs=[anywhere] * 3 + [vmem()] * 5,
        out_specs=(vmem(),) * 4 + (anywhere,) * 2,
        scratch_shapes=[
            pltpu.VMEM((group // rows, rows, width), bf),
            pltpu.VMEM((group, 3 * cols), bf),
            pltpu.VMEM((wrows, hid), bf),
            dma((2,)), dma((4,)), dma((8,)), dma((8,)), dma((8,)),
            dma, dma, dma, dma, dma, dma((2,)),
        ],
        compiler_params=pltpu.CompilerParams(vmem_limit_bytes=VMEM_LIMIT, collective_id=3, has_side_effects=True),
        cost_estimate=pl.CostEstimate(flops=6 * 10**10, bytes_accessed=10**7, transcendentals=10**6),
        name="project",
    )(tokens, tok2, w_down, wqkv, cos, sin, order_col, gains)


def join(own, other, got, chip):
    def one(e):
        own[e] = (own[e].astype(jnp.float32) + other[e].astype(jnp.float32)).astype(own.dtype)

    over(own.shape[0], one)
    got[chip] = own[chip]


def total_of(got):
    return lax.fori_loop(
        1, got.shape[0], lambda i, total: total + got[i].astype(jnp.float32), got[0].astype(jnp.float32)
    )


def tail_body(
    count, grad_ref, raw_ref, cos_ref, sin_ref, wqkv, x_hbm, down_hbm, gwo_hbm, kept_ref, gain_ref,
    tok_out, gq, gain_sum, down_out, wo_mid,
    xs, x_t, draw, part_far, part_mid, part_near, own_part, from_a, from_b, from_c, from_d, from_e, from_f,
    near_mlp, far_mlp, own_w, core_w, got_w, load_sem, hop_send, hop_recv, keep_sem, near_send, near_recv, far_send, far_recv,
    load_w_sem, core_send, core_recv, w_send, w_recv,
):
    d = lax.axis_index("dp")
    t = lax.axis_index("tensor")
    rows, width = tok_out.shape
    group = draw.shape[0]
    cols = draw.shape[1] // 3
    near = flip1(t)
    inner = (t + 1) // 2 == 1
    outer = jnp.logical_not(inner)
    far, mid = 3 - 3 * (t // 2), 2 - t // 2
    chunk = rows // 2
    half, chip, core = count // 2, d // 2, lax.rem(d, 2)

    def chip_peer(i):
        return lax.rem(chip + 1 + i, half)

    barrier = pltpu.get_barrier_semaphore()
    for peer in [(d, near), (d, 3 - t), (d, flip2(t)), (flip1(d), t), (flip1(d), flip2(t))]:
        pl.semaphore_signal(barrier, inc=1, device_id=peer, device_id_type=MESH_ID)
    over(
        half - 1,
        lambda i: pl.semaphore_signal(barrier, inc=1, device_id=(2 * chip_peer(i) + core, t), device_id_type=MESH_ID),
    )
    pl.semaphore_wait(barrier, half + 4)

    home = core == t // 2
    away = jnp.logical_not(home)
    near_copy = remote_copy(down_hbm.at[1 - core], near_mlp, near_send, near_recv, (flip1(d), t))
    far_same = remote_copy(down_hbm.at[core], far_mlp, far_send.at[0], far_recv, (d, flip2(t)))
    far_cross = remote_copy(down_hbm.at[1 - core], far_mlp, far_send.at[1], far_recv, (flip1(d), flip2(t)))
    keep_mlp = pltpu.make_async_copy(down_hbm.at[core], near_mlp, keep_sem)

    @pl.when(home)
    def _():
        near_copy.start()
        keep_mlp.start()

    @pl.when(away)
    def _():
        far_same.start()
        far_cross.start()

    load_x = pltpu.make_async_copy(x_hbm, xs, load_sem)
    load_x.start()

    core_w_copy = remote_copy(gwo_hbm.at[:, 1 - core], core_w, core_send, core_recv, (flip1(d), t))
    load_w = pltpu.make_async_copy(gwo_hbm.at[:, core], own_w, load_w_sem)
    core_w_copy.start()
    load_w.start()

    def w_copy(i):
        return remote_copy(
            own_w.at[chip_peer(i)], got_w.at[chip], w_send.at[i], w_recv.at[i], (2 * chip_peer(i) + core, t)
        )

    def hop(kind, ch):
        src, dst, to = (
            (part_far, from_a, near),
            (part_mid, from_b, near),
            (part_near, from_c, near),
            (part_far, from_d, 3 - t),
            (part_mid, from_e, 3 - t),
            (part_near, from_f, near),
        )[kind]
        part = tile_at(ch, chunk)
        return remote_copy(src.at[part, :], dst.at[part, :], hop_send.at[kind, ch], hop_recv.at[kind, ch], (d, to))

    gain_sum[...] = jnp.zeros_like(gain_sum)

    def work(slot, ch, ref):
        at = tile_at(2 * slot + ch, chunk)
        to = tile_at(ch, chunk)
        cos = jnp.concatenate([cos_ref[at, :]] * (cols // cos_ref.shape[1]), axis=1)
        sin = jnp.concatenate([sin_ref[at, :]] * (cols // sin_ref.shape[1]), axis=1)
        gain = gain_ref[:, tile_at(t, cols)]
        for m in range(2):
            grad = grad_ref[at, m * cols : (m + 1) * cols].astype(jnp.float32)
            raw = raw_ref[at, m * cols : (m + 1) * cols].astype(jnp.float32)
            back = grad * cos - swap_halves(grad) * sin
            factor = lax.rsqrt(head_sums(raw * raw) + EPS)
            normed = raw * factor
            gain_sum[...] += jnp.sum(back * normed, axis=0, keepdims=True)
            scaled = back * gain
            draw[at, m * cols : (m + 1) * cols] = (factor * (scaled - normed * head_sums(normed * scaled))).astype(
                jnp.bfloat16
            )
        draw[at, 2 * cols : 3 * cols] = grad_ref[at, 2 * cols : 3 * cols]

        def product(n):
            tile = tile_at(n, TILE)
            ref[to, tile] = dot_abt(draw[at, :], wqkv[tile, :]).astype(ref.dtype)

        over(width // TILE, product)

    def send_part(kind, slot, ref):
        def one(ch):
            work(slot, ch, ref)

            @pl.when(outer)
            def _():
                hop(kind, ch).start()

        over(2, one)

    send_part(0, far, part_far)
    send_part(1, mid, part_mid)
    send_part(2, near, part_near)
    over(2, lambda ch: work(t, ch, own_part))

    def pass_on(kind, ch, own, got, then):
        @pl.when(inner)
        def _():
            part = pl.ds(ch * chunk, chunk)
            hop(kind, ch).wait_recv()
            own[part, :] = (own[part, :].astype(jnp.float32) + got[part, :].astype(jnp.float32)).astype(jnp.bfloat16)
            hop(then, ch).start()

    pass_on(0, 0, part_far, from_a, 3)
    pass_on(0, 1, part_far, from_a, 3)

    load_w.wait()
    core_w_copy.wait_recv()
    join(own_w, core_w, got_w, chip)
    over(half - 1, lambda i: w_copy(i).start())
    load_x.wait()

    def flip_block(b):
        at = tile_at(b, 128)
        for n in range(width // TILE):
            x_t[n * TILE : (n + 1) * TILE, at] = xs[at, n * TILE : (n + 1) * TILE].T

    over(group // 128, flip_block)
    pass_on(3, 0, part_near, from_d, 5)

    def weight_grad(n):
        tile = tile_at(n, TILE)
        gq[tile, :] = dot_ab(x_t[tile, :], draw[...]).astype(jnp.bfloat16)

    over(width // TILE, weight_grad)
    pass_on(1, 0, part_mid, from_b, 4)
    pass_on(3, 1, part_near, from_d, 5)
    pass_on(1, 1, part_mid, from_b, 4)

    @pl.when(home)
    def _():
        keep_mlp.wait()
        near_copy.wait_send()

    @pl.when(away)
    def _():
        near_copy.wait_recv()

    over(half - 1, lambda i: w_copy(i).wait_recv())
    wo_mid[...] = total_of(got_w).astype(jnp.bfloat16)
    core_w_copy.wait_send()
    over(half - 1, lambda i: w_copy(i).wait_send())
    far_same.wait_recv()
    down_out[...] = near_mlp[...].astype(jnp.float32) + far_mlp[...].astype(jnp.float32)

    @pl.when(away)
    def _():
        far_same.wait_send()
        far_cross.wait_send()

    for ch in range(2):
        part = pl.ds(ch * chunk, chunk)

        @pl.when(inner)
        def _():
            hop(2, ch).wait_recv()
            hop(4, ch).wait_recv()
            tok_out[part, :] = (
                kept_ref[part, :]
                + own_part[part, :]
                + from_c[part, :].astype(jnp.float32)
                + from_e[part, :].astype(jnp.float32)
            )

        @pl.when(outer)
        def _():
            hop(5, ch).wait_recv()
            tok_out[part, :] = kept_ref[part, :] + own_part[part, :] + from_f[part, :].astype(jnp.float32)

    for ch in range(2):

        @pl.when(inner)
        def _():
            for kind in (3, 4, 5):
                hop(kind, ch).wait_send()

        @pl.when(outer)
        def _():
            for kind in (0, 1, 2):
                hop(kind, ch).wait_send()


def tail_call(count, grad_qkv, raw, cos, sin, wqkv, all_tokens, down, gwo, kept, gains):
    rows, width = kept.shape
    wrows, hid = width // count, down.shape[1]
    group, three = grad_qkv.shape
    bf, f32 = jnp.bfloat16, jnp.float32
    anywhere = pl.BlockSpec(memory_space=pl.ANY)
    dma = pltpu.SemaphoreType.DMA
    shape = jax.ShapeDtypeStruct
    return pl.pallas_call(
        functools.partial(tail_body, count),
        out_shape=(
            shape((rows, width), f32),
            shape((width, three), bf),
            shape((1, three // 3), f32),
            shape((wrows, hid), f32),
            shape((wrows, width), bf),
        ),
        in_specs=[vmem()] * 5 + [anywhere] * 3 + [vmem()] * 2,
        out_specs=(vmem(),) * 5,
        scratch_shapes=[
            pltpu.VMEM((group, width), bf),
            pltpu.VMEM((width, group), bf),
            pltpu.VMEM((group, three), bf),
            pltpu.VMEM((rows, width), bf),
            pltpu.VMEM((rows, width), bf),
            pltpu.VMEM((rows, width), bf),
            pltpu.VMEM((rows, width), f32),
        ]
        + [pltpu.VMEM((rows, width), bf)] * 6
        + [pltpu.VMEM((wrows, hid), bf)] * 2
        + [pltpu.VMEM((count // 2, wrows, width), bf)] * 3
        + [dma, dma((6, 2)), dma((6, 2)), dma, dma, dma, dma((2,)), dma]
        + [dma, dma, dma, dma((count // 2 - 1,)), dma((count // 2 - 1,))],
        compiler_params=pltpu.CompilerParams(vmem_limit_bytes=VMEM_LIMIT, collective_id=4, has_side_effects=True),
        cost_estimate=pl.CostEstimate(flops=6 * 10**10, bytes_accessed=10**7, transcendentals=10**6),
        name="tail",
    )(
        grad_qkv, raw, cos, sin, wqkv, all_tokens, down.reshape(2, wrows, hid),
        gwo.reshape(count // 2, 2, wrows, width), kept, gains,
    )


def settle_body(
    count, gq_hbm, mlp_hbm, wo_mid, gain_ref, gaa_ref, gam_ref, gsu_ref, gsg_ref,
    q_out, k_out, v_out, wo_out, up_out, gate_out, gain_out, aa_out, su_out, sg_out, am_out,
    own_q, core_q, got_q, got_z, near_mlp, far_mlp, vec, got_v, vec_mid, got_s,
    load_sem, core_send, core_recv, q_send, q_recv, z_send, z_recv, v_send, v_recv, s_send, s_recv,
    near_send, near_recv, mlp_send, mlp_recv,
):
    d = lax.axis_index("dp")
    t = lax.axis_index("tensor")
    half, wrows, three = got_q.shape
    cols = three // 3
    width = gaa_ref.shape[1]
    chip, core = d // 2, lax.rem(d, 2)
    home = core == t // 2
    away = jnp.logical_not(home)
    f32, bf = jnp.float32, jnp.bfloat16

    def dp_peer(i):
        return lax.rem(d + 1 + i, count)

    def line_peer(k):
        return lax.rem(t + k, 4)

    def chip_peer(i):
        return lax.rem(chip + 1 + i, half)

    barrier = pltpu.get_barrier_semaphore()
    over(
        count - 1,
        lambda i: pl.semaphore_signal(barrier, inc=1, device_id=(dp_peer(i), t), device_id_type=MESH_ID),
    )
    for k in (1, 2, 3):
        pl.semaphore_signal(barrier, inc=1, device_id=(d, line_peer(k)), device_id_type=MESH_ID)
    pl.semaphore_signal(barrier, inc=1, device_id=(flip1(d), flip2(t)), device_id_type=MESH_ID)
    pl.semaphore_wait(barrier, count + 3)

    def z_copy(k):
        return remote_copy(
            wo_mid.at[:, tile_at(line_peer(k), cols)], got_z.at[t], z_send.at[k - 1], z_recv.at[k - 1], (d, line_peer(k))
        )

    for k in (1, 2, 3):
        z_copy(k).start()
    got_z[t] = wo_mid[:, tile_at(t, cols)]

    near_copy = remote_copy(mlp_hbm.at[:, 1 - core], near_mlp, near_send, near_recv, (flip1(d), t))
    keep_mlp = pltpu.make_async_copy(mlp_hbm.at[:, core], near_mlp, load_sem.at[0])

    hid = near_mlp.shape[2]

    def far_same(u):
        m, part = u // 2, tile_at(u % 2, hid // 2)
        return remote_copy(
            mlp_hbm.at[m, core, :, part], far_mlp.at[m, :, part], mlp_send.at[u], mlp_recv.at[u], (d, flip2(t))
        )

    def far_cross(u):
        m, part = u // 2, tile_at(u % 2, hid // 2)
        return remote_copy(
            mlp_hbm.at[m, 1 - core, :, part], far_mlp.at[m, :, part], mlp_send.at[4 + u], mlp_recv.at[u],
            (flip1(d), flip2(t)),
        )

    def far_start(u):
        @pl.when(away)
        def _():
            far_same(u).start()
            far_cross(u).start()

    @pl.when(home)
    def _():
        near_copy.start()
        keep_mlp.start()

    for u in range(3):
        far_start(u)

    core_q_copy = remote_copy(gq_hbm.at[:, 1 - core], core_q, core_send, core_recv, (flip1(d), t))
    load_q = pltpu.make_async_copy(gq_hbm.at[:, core], own_q, load_sem.at[1])
    core_q_copy.start()
    load_q.start()

    vec[...] = jnp.zeros_like(vec)
    for row, ref in enumerate((gaa_ref, gam_ref, gsu_ref, gsg_ref)):
        vec[row : row + 1, :] = ref[...]
    vec[4:5, 0:cols] = gain_ref[...]
    got_v[d] = vec[...]

    def v_copy(i):
        return remote_copy(vec, got_v.at[d], v_send.at[i], v_recv.at[i], (dp_peer(i), t))

    over(count - 1, lambda i: v_copy(i).start())

    def q_copy(i):
        return remote_copy(
            own_q.at[chip_peer(i)], got_q.at[chip], q_send.at[i], q_recv.at[i], (2 * chip_peer(i) + core, t)
        )

    load_q.wait()
    core_q_copy.wait_recv()
    join(own_q, core_q, got_q, chip)
    over(half - 1, lambda i: q_copy(i).start())

    over(count - 1, lambda i: v_copy(i).wait_recv())
    even, odd = lax.fori_loop(
        1, half, lambda i, total: (total[0] + got_v[2 * i], total[1] + got_v[2 * i + 1]), (got_v[0], got_v[1])
    )
    both = even + odd
    vec_mid[...] = jnp.concatenate([both[0:2], even[2:3], odd[2:3], even[3:4], odd[3:4], both[4:5], both[4:5]], axis=0)

    def s_copy(k):
        return remote_copy(vec_mid, got_s.at[t], s_send.at[k - 1], s_recv.at[k - 1], (d, line_peer(k)))

    for k in (1, 2, 3):
        s_copy(k).start()
    got_s[t] = vec_mid[...]
    far_start(3)

    over(half - 1, lambda i: q_copy(i).wait_recv())
    total = total_of(got_q)
    for m, ref in enumerate((q_out, k_out, v_out)):
        ref[...] = total[:, m * cols : (m + 1) * cols]

    for k in (1, 2, 3):
        z_copy(k).wait_recv()
        s_copy(k).wait_recv()
    wo_out[...] = got_z[0].astype(f32) + got_z[1].astype(f32) + got_z[2].astype(f32) + got_z[3].astype(f32)
    shared = got_s[0] + got_s[1] + got_s[2] + got_s[3]
    aa_out[...] = shared[0:1]
    am_out[...] = shared[1:2]
    pairs = (got_s[0] + got_s[2], got_s[1] + got_s[3])
    for s in range(4):
        su_out[:, s * width : (s + 1) * width] = pairs[s % 2][2 + s // 2 : 3 + s // 2]
        sg_out[:, s * width : (s + 1) * width] = pairs[s % 2][4 + s // 2 : 5 + s // 2] * math.sqrt(D)
        gain_out[:, s * cols : (s + 1) * cols] = got_s[s][6:7, 0:cols]

    @pl.when(home)
    def _():
        keep_mlp.wait()
        near_copy.wait_send()

    @pl.when(away)
    def _():
        near_copy.wait_recv()

    for m, ref in enumerate((up_out, gate_out)):
        far_same(2 * m).wait_recv()
        far_same(2 * m + 1).wait_recv()
        ref[...] = near_mlp[m].astype(f32) + far_mlp[m].astype(f32)

    @pl.when(away)
    def _():
        for u in range(4):
            far_same(u).wait_send()
            far_cross(u).wait_send()

    core_q_copy.wait_send()
    over(count - 1, lambda i: v_copy(i).wait_send())
    over(half - 1, lambda i: q_copy(i).wait_send())
    for k in (1, 2, 3):
        z_copy(k).wait_send()
        s_copy(k).wait_send()


def settle_call(count, gq, mlp, wo_mid, gain_sum, gaa, gam, gsu, gsg):
    width, three = gq.shape
    half = count // 2
    cols = three // 3
    wrows = width // count
    hid = mlp.shape[2]
    bf, f32 = jnp.bfloat16, jnp.float32
    anywhere = pl.BlockSpec(memory_space=pl.ANY)
    dma = pltpu.SemaphoreType.DMA
    shape = jax.ShapeDtypeStruct
    return pl.pallas_call(
        functools.partial(settle_body, count),
        out_shape=(shape((wrows, cols), f32),) * 4
        + (shape((wrows, hid), f32),) * 2
        + (
            shape((1, 4 * cols), f32),
            shape((1, width), f32),
            shape((1, 4 * hid), f32),
            shape((1, 4 * hid), f32),
            shape((1, width), f32),
        ),
        in_specs=[anywhere] * 2 + [vmem()] * 6,
        out_specs=(vmem(),) * 11,
        scratch_shapes=[pltpu.VMEM((half, wrows, three), bf)] * 3
        + [
            pltpu.VMEM((4, wrows, cols), bf),
            pltpu.VMEM((2, wrows, hid), bf),
            pltpu.VMEM((2, wrows, hid), bf),
            pltpu.VMEM((8, width), f32),
            pltpu.VMEM((count, 8, width), f32),
            pltpu.VMEM((8, width), f32),
            pltpu.VMEM((4, 8, width), f32),
            dma((2,)),
            dma, dma,
            dma((half - 1,)), dma((half - 1,)),
            dma((3,)), dma((3,)),
            dma((count - 1,)), dma((count - 1,)),
            dma((3,)), dma((3,)),
            dma, dma, dma((8,)), dma((4,)),
        ],
        compiler_params=pltpu.CompilerParams(vmem_limit_bytes=VMEM_LIMIT, collective_id=5, has_side_effects=True),
        cost_estimate=pl.CostEstimate(flops=10**9, bytes_accessed=10**7, transcendentals=0),
        name="settle",
    )(
        gq.reshape(half, 2, wrows, three),
        mlp.reshape(2, 2, wrows, hid),
        wo_mid, gain_sum, gaa, gam, gsu, gsg,
    )


def deliver_body(count, total, *refs):
    ins, outs, rest = refs[:total], refs[total : 2 * total], refs[2 * total :]
    held, load_sem, store_sem = rest[:count], rest[count], rest[count + 1]
    loads = [pltpu.make_async_copy(ins[i], held[i], load_sem.at[i]) for i in range(count)]
    stores = [pltpu.make_async_copy(held[i], outs[i], store_sem.at[i]) for i in range(count)]
    for copy in loads:
        copy.start()
    for i in range(count, total):
        outs[i][...] = ins[i][0, :]
    for load, store in zip(loads, stores):
        load.wait()
        store.start()
    for copy in stores:
        copy.wait()


def deliver_call(arrays, vectors):
    total = len(arrays) + len(vectors)
    specs = [pl.BlockSpec(memory_space=pl.ANY)] * len(arrays) + [vmem()] * len(vectors)
    return pl.pallas_call(
        functools.partial(deliver_body, len(arrays), total),
        out_shape=tuple(jax.ShapeDtypeStruct(a.shape, a.dtype) for a in arrays)
        + tuple(jax.ShapeDtypeStruct((v.shape[1],), v.dtype) for v in vectors),
        in_specs=specs,
        out_specs=tuple(specs),
        scratch_shapes=[pltpu.VMEM(a.shape, a.dtype) for a in arrays] + [pltpu.SemaphoreType.DMA((len(arrays),))] * 2,
        compiler_params=pltpu.CompilerParams(vmem_limit_bytes=VMEM_LIMIT),
        name="deliver",
    )(*arrays, *vectors)


def same_core_groups(dp_count):
    return [list(range(parity, dp_count, 2)) for parity in range(2)]


def on_device(
    tokens,
    w_query,
    w_key,
    w_value,
    w_out_t,
    w_up,
    w_gate,
    w_down_t,
    scale_qk,
    alpha_attn,
    scale_up,
    scale_gate,
    alpha_mlp,
    order,
    lengths,
    cotangent,
):
    dp_count = lax.axis_size("dp")
    pair, near_tokens, wqkv, wo_every, cos_table, sin_table, order_col, start = spread_call(
        dp_count, tokens, w_up, w_gate, w_query, w_key, w_value, w_out_t, order, lengths
    )
    low = lax.slice(start[0], (0,), (start.shape[1],), (BLK,)) // BLK
    mlp_parts = lax.all_gather(
        pair, "dp", axis=0, tiled=False, axis_index_groups=same_core_groups(dp_count)
    )
    queries, key_rows, value_rows, raw, all_tokens, pair_down = project_call(
        tokens, near_tokens, w_down_t, wqkv, cos_table, sin_table, order_col, scale_qk[None, :]
    )
    attended, log_totals, attended_plain = attn_fwd(low, start, order, queries, key_rows, value_rows)
    out_rows, grad_att_rows, up_gate_grads, down_sums, wo_grads, grad_h1_kept, grad_alpha_a, grad_alpha_m, grad_su, grad_sv = middle_call(
        dp_count,
        2,
        attended_plain,
        wo_every,
        mlp_parts,
        pair_down,
        tokens,
        cotangent,
        alpha_attn[None, :],
        alpha_mlp[None, :],
        scale_up[None, :],
        scale_gate[None, :],
    )
    grad_qkv = attn_bwd(
        low, start, order, order_col, log_totals, queries, key_rows, value_rows, attended, grad_att_rows
    )
    up_gate_sums = lax.psum_scatter(
        up_gate_grads, "dp", scatter_dimension=0, tiled=False, axis_index_groups=same_core_groups(dp_count)
    )
    grad_tokens, grad_q, gain_sum, grad_down, wo_sums = tail_call(
        dp_count, grad_qkv, raw, cos_table, sin_table, wqkv, all_tokens, down_sums, wo_grads, grad_h1_kept, scale_qk[None, :]
    )
    settled = settle_call(
        dp_count, grad_q, up_gate_sums, wo_sums, gain_sum, grad_alpha_a, grad_alpha_m, grad_su, grad_sv
    )
    return deliver_call([out_rows, grad_tokens, *settled[:6], grad_down], settled[6:])


def solution(mesh):
    return jax.shard_map(
        on_device,
        mesh=mesh,
        in_specs=(
            P(("dp", "tensor"), None),
            P("dp", "tensor"),
            P("dp", "tensor"),
            P("dp", "tensor"),
            P("dp", "tensor"),
            P("dp", "tensor"),
            P("dp", "tensor"),
            P("dp", "tensor"),
            P(),
            P(),
            P(),
            P(),
            P(),
            P("dp", None),
            P("dp", None),
            P(("dp", "tensor"), None),
        ),
        out_specs=(
            P(("dp", "tensor"), None),
            P(("dp", "tensor"), None),
            P("dp", "tensor"),
            P("dp", "tensor"),
            P("dp", "tensor"),
            P("dp", "tensor"),
            P("dp", "tensor"),
            P("dp", "tensor"),
            P("dp", "tensor"),
            P(),
            P(),
            P(),
            P(),
            P(),
        ),
        check_vma=False,
    )
```
